32 devices in a mesh: wide: 16 (over z, x, core), blk: 2 (over y).
Axes of the slice: x: 2, y: 2, z: 4, core: 2. Of those that a mesh axis runs over, the one named last changes fastest.
Arguments:
- tokens: bfloat16 [16, 2048, 1280], P('wide', 'blk'), may hold values from -6 to 6
- cell_start: int32 [16, 2048], P('wide', 'blk'), may hold values from 0 to 2047, as said below
- norm1_gain: float32 [1280], replicated, may hold values from 0.1 to 1.9
- norm1_bias: float32 [1280], replicated, may hold values from -3 to 3
- w_qkv: bfloat16 [1280, 3840], replicated, may hold values from -0.15625 to 0.15625
- bias_q: float32 [1280], replicated, may hold values from -3 to 3
- bias_v: float32 [1280], replicated, may hold values from -3 to 3
- w_out: bfloat16 [1280, 1280], replicated, may hold values from -0.625 to 0.625
- bias_out: float32 [1280], replicated, may hold values from -3 to 3
- norm2_gain: float32 [1280], replicated, may hold values from 0.1 to 1.9
- norm2_bias: float32 [1280], replicated, may hold values from -3 to 3
- w_in: bfloat16 [1280, 5120], replicated, may hold values from -0.15625 to 0.15625
- bias_in: float32 [5120], replicated, may hold values from -3 to 3
- w_back: bfloat16 [5120, 1280], replicated, may hold values from -0.078125 to 0.078125
- bias_back: float32 [1280], replicated, may hold values from -3 to 3
- cotangent: bfloat16 [16, 2048, 1280], P('wide', 'blk'), may hold values from -6 to 6
Outputs:
- mixed: bfloat16 [16, 2048, 1280], P('wide', 'blk')
- grad_tokens: float32 [16, 2048, 1280], P('wide', 'blk')
- grad_norm1_gain: float32 [1280], P('wide')
- grad_norm1_bias: float32 [1280], P('wide')
- grad_w_qkv: float32 [1280, 3840], P('wide')
- grad_bias_q: float32 [1280], P('wide')
- grad_bias_v: float32 [1280], P('wide')
- grad_w_out: float32 [1280, 1280], P('wide')
- grad_bias_out: float32 [1280], P('wide')
- grad_norm2_gain: float32 [1280], P('wide')
- grad_norm2_bias: float32 [1280], P('wide')
- grad_w_in: float32 [1280, 5120], P('wide')
- grad_bias_in: float32 [5120], P('wide')
- grad_w_back: float32 [5120, 1280], P('wide')
- grad_bias_back: float32 [1280], P('wide')
The draws below stay inside these ranges and needn't reach their ends.
Inputs may be any that keep to these rules, and one draw needn't show every extreme that they name: cell_start[r, p] is the first position of the cell holding position p of row r: it never falls along a row, equals p where a cell begins and is 0 at p = 0. In every row the last position 2047 is a cell of its own. In each aligned pair of rows one row has a cell that holds positions 511 to 1535.
All inputs are finite; a program needn't handle non-finite values.
Results may differ from the reference program's by a relative error of at most 0.02.
Values may be sent and summed in bfloat16 or wider, within the bound.
No kernel may reach another device: no remote copies, remote signals or barrier semaphores. Data moves between devices by JAX's collectives and lax.ppermute only.
A program may use at most 448 MiB of HBM per device.

```python
import jax
import jax.numpy as jnp
from jax import lax

D = 1280
HEADS = 20
HEAD_DIM = 64
FF = 5120
LEN = 2048
SEG = 1024
ROWS_ALL = 16


def draw_cell_start(key, part):
    first_key = jax.random.fold_in(key, 11)
    second_key = jax.random.fold_in(key, 23)
    places = jnp.arange(LEN, dtype=jnp.int32)
    begins = jax.random.randint(first_key, (ROWS_ALL, LEN), 0, max(2, LEN // 6)) == 0
    chosen = jax.random.randint(second_key, (ROWS_ALL // 2,), 0, 2)
    row_ids = jnp.arange(ROWS_ALL, dtype=jnp.int32)
    spanning = row_ids % 2 == jnp.repeat(chosen, 2)
    inner = (places >= SEG // 2) & (places < LEN - SEG // 2)
    begins = begins & jnp.logical_not(spanning[:, None] & inner[None, :]) & (places[None, :] > 0)
    begins = begins | (places[None, :] == LEN - 1)
    marks = jnp.where(begins | (places[None, :] == 0), places[None, :], 0).astype(jnp.int32)
    return lax.cummax(marks, axis=1)


def raised(result, own_key, source, target, shards_of, factor):
    def block_of(dim):
        return (jnp.arange(result.shape[dim]) // (result.shape[dim] // shards_of)).reshape((-1,) + (1,) * (result.ndim - 1 - dim))

    one_side = jax.random.permutation(own_key, shards_of)[block_of(target)]
    other_side = (block_of(target) + shards_of // 2) % shards_of
    return jnp.where((block_of(source) == one_side) | (block_of(source) == other_side), factor * result, result)


def shard_levels(stream_key, extent, cuts, least, high):
    loudness, own = 1.0, jax.random.fold_in(stream_key, 6)
    for axis_at, shards_of in cuts:
        heights = jnp.exp(jax.random.uniform(jax.random.fold_in(own, axis_at), (shards_of,), jnp.float32, least / len(cuts), high / len(cuts)))
        loudness = loudness * jnp.repeat(heights, extent[axis_at] // shards_of).reshape([-1 if axis == axis_at else 1 for axis in range(len(extent))])
    return loudness


def bell_draw(stream_key, dims, deviation, most, split=(), kind=jnp.bfloat16):
    drawn = jax.random.normal(stream_key, dims, jnp.float32) * deviation
    if len(split) > 0:
        drawn = shard_levels(stream_key, dims, split, -0.22, 0.18) * drawn
    return jnp.clip(drawn, min=-most, max=most).astype(kind)


def noise_with(stream_key, shape, deviation, limit, cuts, heavy, kind=jnp.bfloat16):
    drawn = deviation * jax.random.normal(stream_key, shape, jnp.float32)
    if cuts:
        drawn = drawn * shard_levels(stream_key, shape, cuts, -0.22, 0.18)
    return jnp.clip(raised(drawn, jax.random.fold_in(stream_key, 3), *heavy), -limit, limit).astype(kind)


def setup_inputs(seed: int = 0) -> dict:
    streams_of = jax.random.split(jax.random.key(seed), 17)
    tokens = bell_draw(streams_of[0], (ROWS_ALL, LEN, D), 1.0, 6.0, ((0, 16), (1, 2)))
    cell_start = draw_cell_start(jax.random.fold_in(streams_of[16], 71), 0)
    norm1_gain = jnp.clip(1.0 + 0.18 * jax.random.normal(streams_of[2], (D,), jnp.float32), 0.1, 1.9)
    norm1_bias = bell_draw(streams_of[3], (D,), 0.5, 3.0, (), jnp.float32)
    w_qkv = bell_draw(streams_of[4], (D, 3 * D), D ** -0.5, 0.15625)
    bias_q = bell_draw(streams_of[5], (D,), 0.5, 3.0, (), jnp.float32)
    bias_v = bell_draw(streams_of[6], (D,), 0.5, 3.0, (), jnp.float32)
    w_out = bell_draw(streams_of[7], (D, D), (D // 16) ** -0.5, 0.625)
    bias_out = bell_draw(streams_of[8], (D,), 0.5, 3.0, (), jnp.float32)
    norm2_gain = jnp.clip(1.0 + 0.18 * jax.random.normal(streams_of[9], (D,), jnp.float32), 0.1, 1.9)
    norm2_bias = bell_draw(streams_of[10], (D,), 0.5, 3.0, (), jnp.float32)
    w_in = bell_draw(streams_of[11], (D, FF), D ** -0.5, 0.15625)
    bias_in = bell_draw(streams_of[12], (FF,), 0.5, 3.0, (), jnp.float32)
    w_back = bell_draw(streams_of[13], (FF, D), FF ** -0.5, 0.078125)
    bias_back = bell_draw(streams_of[14], (D,), 0.5, 3.0, (), jnp.float32)
    cotangent = noise_with(streams_of[15], (ROWS_ALL, LEN, D), 1.0, 6.0, ((0, 16), (1, 2)), (0, 2, 16, 2.0))
    return dict(tokens=tokens, cell_start=cell_start, norm1_gain=norm1_gain, norm1_bias=norm1_bias, w_qkv=w_qkv, bias_q=bias_q, bias_v=bias_v, w_out=w_out, bias_out=bias_out, norm2_gain=norm2_gain, norm2_bias=norm2_bias, w_in=w_in, bias_in=bias_in, w_back=w_back, bias_back=bias_back, cotangent=cotangent)


@jax.custom_vjp
def low(v):
    return lax.optimization_barrier(v.astype(jnp.bfloat16)).astype(jnp.float32)

@jax.custom_vjp
def low_back(v):
    return v

def low_keep(v):
    return (low(v), None)

def low_pass(kept, grad):
    return (grad,)

def back_keep(v):
    return (v, None)

def back_low(kept, grad):
    return (low(grad),)
low.defvjp(low_keep, low_pass)
low_back.defvjp(back_keep, back_low)
NEGATIVE = -1e+30
HIGH = lax.Precision.HIGHEST

def layer_norm(values, gain, shift):
    centred = values - lax.optimization_barrier(jnp.mean(values, axis=-1, keepdims=True))
    spread = lax.optimization_barrier(jnp.mean(centred * centred, axis=-1, keepdims=True))
    return centred * lax.rsqrt(spread + 1e-05) * gain + shift

def gelu_exact(values):
    return jax.nn.gelu(values, approximate=False)

def attend_row(inputs):
    query, keys, values, cells = inputs
    allowed = cells[:, None] == cells[None, :]

    def one_head(parts):
        query_head, key_head, value_head = parts
        scores = low_back(jnp.dot(query_head, key_head.T, precision=HIGH)) * 0.125
        scores = jnp.where(allowed, scores, NEGATIVE)
        highest = lax.optimization_barrier(jnp.max(scores, axis=-1, keepdims=True))
        expo = jnp.where(allowed, jnp.exp(scores - highest), 0.0)
        weights = low(expo / lax.optimization_barrier(jnp.sum(expo, axis=-1, keepdims=True)))
        return jnp.dot(weights, value_head, precision=HIGH)

    def split_heads(tensor):
        return tensor.reshape(LEN, HEADS, HEAD_DIM).transpose(1, 0, 2)
    heads_out = lax.map(jax.checkpoint(one_head), (split_heads(query), split_heads(keys), split_heads(values)))
    return heads_out.transpose(1, 0, 2).reshape(LEN, D)

def forward(inputs, cells, gain1, shift1, w_qkv, bias_q, bias_v, w_out, bias_out, gain2, shift2, w_in, bias_in, w_back, bias_back):
    normed1 = low(layer_norm(inputs, gain1, shift1))
    mixed_qkv = jnp.dot(normed1, w_qkv, precision=HIGH)
    query = low(low_back(mixed_qkv[..., :D] + bias_q))
    keys = low(low_back(mixed_qkv[..., D:2 * D]))
    values = low(low_back(mixed_qkv[..., 2 * D:] + bias_v))
    attended = lax.map(attend_row, (query, keys, values, cells))
    attended = low(low_back(attended))
    middle = inputs + low_back(jnp.dot(attended, w_out, precision=HIGH) + bias_out)
    normed2 = low(layer_norm(middle, gain2, shift2))
    hidden = low(gelu_exact(low_back(jnp.dot(normed2, w_in, precision=HIGH) + bias_in)))
    return middle + low_back(jnp.dot(hidden, w_back, precision=HIGH) + bias_back)

def reference(tokens, cell_start, norm1_gain, norm1_bias, w_qkv, bias_q, bias_v, w_out, bias_out, norm2_gain, norm2_bias, w_in, bias_in, w_back, bias_back, cotangent):
    floats = [array.astype(jnp.float32) for array in (tokens, norm1_gain, norm1_bias, w_qkv, bias_q, bias_v, w_out, bias_out, norm2_gain, norm2_bias, w_in, bias_in, w_back, bias_back)]

    def closed(*params):
        return forward(params[0], cell_start, *params[1:])
    output, pullback = jax.vjp(closed, *floats)
    grads = pullback(cotangent.astype(jnp.float32))
    return (output.astype(jnp.bfloat16), grads[0], grads[1], grads[2], grads[3], grads[4], grads[5], grads[6], grads[7], grads[8], grads[9], grads[10], grads[11], grads[12], grads[13])
```

```python
import functools
import math

import jax
import jax.numpy as jnp
from jax import lax
from jax.experimental import pallas as pl
from jax.experimental.pallas import tpu as pltpu
from jax.sharding import PartitionSpec as P

HEADS = 20
HEAD_DIM = 64
HD = HEAD_DIM
EPS = 1e-05
NEG = -1e30
LOG2E = math.log2(math.e)
C2 = LOG2E / math.sqrt(HEAD_DIM)
F32 = jnp.float32
BF = jnp.bfloat16
NN = (((1,), (0,)), ((), ()))
NT = (((1,), (1,)), ((), ()))
TN = (((0,), (0,)), ((), ()))
VMEM_LIMIT = 56 * 2**20


def dot(a, b, dims):
    return lax.dot_general(a, b, dims, preferred_element_type=F32)


def head_sumsq(x,hp16):
    W=x.shape[1]
    sq=x.astype(F32)*x.astype(F32)
    row=lax.broadcasted_iota(jnp.int32,(hp16,W),0); col=lax.broadcasted_iota(jnp.int32,(hp16,W),1)
    ones=jnp.where(row==col//HD,1.0,0.0).astype(BF)
    return lax.dot_general(ones,sq.astype(BF),NT,preferred_element_type=F32)

def fwd_kernel(flags,cq,ck,q,k,v,*rest,first,tq,tk,heads):
    if first:
        accT_o,m_o,l_o,qm,vT,bias,acc,m,l,kn=rest
    else:
        accT_i,m_i,l_i,o_o,lse_o,qm,vT,bias,acc,m,l,kn=rest
    r=pl.program_id(0); qi=pl.program_id(1)
    nk=k.shape[1]//tk
    hp16=m.shape[0]
    @pl.when(qi==0)
    def _():
        vT[...]=v[0].T
        kn[...]=jnp.broadcast_to(jnp.sqrt(jnp.max(head_sumsq(k[0],hp16),1,keepdims=True)),kn.shape)
    lane=lax.broadcasted_iota(jnp.int32,(tq,128),1)
    for hp in range(heads//2):
        qp=q[0,:,hp*128:(hp+1)*128]
        qm[2*hp]=jnp.where(lane<64,qp,0).astype(BF)
        qm[2*hp+1]=jnp.where(lane>=64,qp,0).astype(BF)
    bound=jnp.sqrt(head_sumsq(q[0],hp16))*kn[:,0:1]*(C2*1.02)
    safe=jnp.max(bound)<50.0
    if first:
        m0=bound
    else:
        m0=jnp.maximum(bound,m_i[0])
    def loop(online):
        if first:
            acc[...]=jnp.zeros_like(acc); l[...]=jnp.zeros_like(l)
            m[...]=jnp.full_like(m,NEG) if online else m0
        elif online:
            acc[...]=accT_i[0]; m[...]=m_i[0]; l[...]=l_i[0]
        else:
            al=jnp.exp2(m_i[0]-m0)
            m[...]=m0; l[...]=al*l_i[0]
            for hh in range(heads):
                hs=slice(hh*HD,(hh+1)*HD)
                acc[hs,:]=al[hh:hh+1,:]*accT_i[0,hs,:]
        def body(kt,masked):
            ks=pl.ds(pl.multiple_of(kt*tk,tk),tk)
            if online:
                @pl.loop(0,heads//2)
                def _(hp):
                    kp=k[0,ks,pl.ds(pl.multiple_of(hp*128,128),128)]
                    for j in range(2):
                        hh=2*hp+j
                        s=lax.dot_general(kp,qm[hh],NT,preferred_element_type=F32)*C2+bias[...]
                        mp=m[pl.ds(hh,1),:]
                        mn=jnp.maximum(mp,jnp.max(s,0,keepdims=True))
                        p=jnp.exp2(s-mn)
                        al=jnp.exp2(mp-mn)
                        m[pl.ds(hh,1),:]=mn
                        l[pl.ds(hh,1),:]=al*l[pl.ds(hh,1),:]+jnp.sum(p,0,keepdims=True)
                        hs=pl.ds(pl.multiple_of(hh*HD,HD),HD)
                        acc[hs,:]=al*acc[hs,:]+lax.dot_general(vT[hs,ks],p.astype(BF),NN,preferred_element_type=F32)
                return
            def score(hh):
                s=lax.dot_general(k[0,ks,(hh//2)*128:(hh//2+1)*128],qm[hh],NT,preferred_element_type=F32)*C2
                if masked: s=s+bias[...]
                return s
            s=score(0); pp=None
            for hh in range(heads+1):
                if hh+1<heads: sn=score(hh+1)
                if pp is not None:
                    hs=slice((hh-1)*HD,hh*HD)
                    acc[hs,:]+=lax.dot_general(vT[hs,ks],pp,NN,preferred_element_type=F32)
                if hh<heads:
                    p=jnp.exp2(s-m[hh:hh+1,:])
                    l[hh:hh+1,:]+=jnp.sum(p,0,keepdims=True)
                    pp=p.astype(BF)
                s=sn
        @pl.loop(0,nk)
        def _(kt):
            f=flags[r,qi,kt]
            def mask():
                ks=pl.ds(pl.multiple_of(kt*tk,tk),tk)
                bias[...]=jnp.where(ck[0,ks,0:1]==cq[0,0:1,:],0.0,NEG)
            if online:
                @pl.when(f>0)
                def _():
                    mask(); body(kt,True)
            else:
                @pl.when(f==1)
                def _():
                    mask(); body(kt,True)
                @pl.when(f==2)
                def _(): body(kt,False)
    @pl.when(safe)
    def _(): loop(False)
    @pl.when(jnp.logical_not(safe))
    def _(): loop(True)
    if first:
        accT_o[0]=acc[...]; m_o[0]=m[...]; l_o[0]=l[...]
    else:
        for hp in range(heads//2):
            parts=[]
            for hh in (2*hp,2*hp+1):
                parts.append(acc[hh*HD:(hh+1)*HD,:]/l[hh:hh+1,:])
            o_o[0,:,hp*128:(hp+1)*128]=jnp.concatenate(parts,0).T.astype(BF)
        lse_o[0]=m[...]+jnp.log2(l[...])

def attn_fwd(flags,cq,ck,q,k,v,state=None,tq=256,tk=256,heads=10):
    nr,S,W=q.shape; Sk=k.shape[1]; hp16=-(-heads//8)*8
    first=state is None
    qs=lambda r,i,*_:(r,i,0); ts=lambda r,i,*_:(r,0,i); ks=lambda r,i,*_:(r,0,0)
    stspec=[pl.BlockSpec((1,W,tq),ts),pl.BlockSpec((1,hp16,tq),ts),pl.BlockSpec((1,hp16,tq),ts)]
    ins=[pl.BlockSpec((1,1,tq),ts),pl.BlockSpec((1,Sk,128),ks),pl.BlockSpec((1,tq,W),qs),pl.BlockSpec((1,Sk,W),ks),pl.BlockSpec((1,Sk,W),ks)]
    if first:
        outs=stspec
        osh=[jax.ShapeDtypeStruct((nr,W,S),F32)]+[jax.ShapeDtypeStruct((nr,hp16,S),F32)]*2
    else:
        ins=ins+stspec
        outs=[pl.BlockSpec((1,tq,W),qs),pl.BlockSpec((1,hp16,tq),ts)]
        osh=[jax.ShapeDtypeStruct((nr,S,W),BF),jax.ShapeDtypeStruct((nr,hp16,S),F32)]
    fl=4*nr*S*Sk*W
    return pl.pallas_call(functools.partial(fwd_kernel,first=first,tq=tq,tk=tk,heads=heads),
        out_shape=osh,
        grid_spec=pltpu.PrefetchScalarGridSpec(num_scalar_prefetch=1,grid=(nr,S//tq),in_specs=ins,out_specs=outs,
          scratch_shapes=[pltpu.VMEM((heads,tq,128),BF),pltpu.VMEM((W,Sk),BF),pltpu.VMEM((tk,tq),F32),pltpu.VMEM((W,tq),F32),pltpu.VMEM((hp16,tq),F32),pltpu.VMEM((hp16,tq),F32),pltpu.VMEM((hp16,128),F32)]),
        compiler_params=pltpu.CompilerParams(dimension_semantics=("arbitrary","arbitrary"),vmem_limit_bytes=VMEM_LIMIT),
        cost_estimate=pl.CostEstimate(flops=fl*4,bytes_accessed=nr*(S*W*2+2*Sk*W*2+S*W*4),transcendentals=nr*S*Sk*heads),
        name="attn_fwd_a" if first else "attn_fwd_b",
    )(flags,cq,ck,q,k,v,*(state or ()))

def bwd_kernel(flags,cq,ck,q,k,v,do,o,lse,*rest,first,tq,tk,heads):
    if first:
        dqT_o,dk_o,dv_o,qm,dom,kT,bias,dqT,dk,dv,delta=rest
    else:
        dqT_i,dq_o,dk_o,dv_o,qm,dom,kT,bias,dqT,dk,dv,delta=rest
    r=pl.program_id(0); qi=pl.program_id(1); nq=pl.num_programs(1)
    nk=k.shape[1]//tk
    @pl.when(qi==0)
    def _():
        kT[...]=k[0].T
        dk[...]=jnp.zeros_like(dk); dv[...]=jnp.zeros_like(dv)
    lane=lax.broadcasted_iota(jnp.int32,(tq,128),1)
    for hp in range(heads//2):
        c=slice(hp*128,(hp+1)*128)
        qp=q[0,:,c]*jnp.asarray(0.125,BF); dp_=do[0,:,c]
        qm[2*hp]=jnp.where(lane<64,qp,0).astype(BF)
        qm[2*hp+1]=jnp.where(lane>=64,qp,0).astype(BF)
        dom[2*hp]=jnp.where(lane<64,dp_,0).astype(BF)
        dom[2*hp+1]=jnp.where(lane>=64,dp_,0).astype(BF)
    W=heads*HD
    prod=do[0].astype(F32)*o[0].astype(F32)
    hi=prod.astype(BF); lo=(prod-hi.astype(F32)).astype(BF)
    hp16=delta.shape[0]
    row=lax.broadcasted_iota(jnp.int32,(hp16,W),0); col=lax.broadcasted_iota(jnp.int32,(hp16,W),1)
    ones=jnp.where(row==col//HD,1.0,0.0).astype(BF)
    delta[...]=lax.dot_general(ones,hi,NT,preferred_element_type=F32)+lax.dot_general(ones,lo,NT,preferred_element_type=F32)
    if first: dqT[...]=jnp.zeros_like(dqT)
    else: dqT[...]=dqT_i[0]
    def body(kt,masked):
        ks=pl.ds(pl.multiple_of(kt*tk,tk),tk)
        def col(hh): return slice((hh//2)*128,(hh//2+1)*128)
        def score(hh):
            s=lax.dot_general(k[0,ks,col(hh)],qm[hh],NT,preferred_element_type=F32)*LOG2E
            if masked: s=s+bias[...]
            return s,lax.dot_general(v[0,ks,col(hh)],dom[hh],NT,preferred_element_type=F32)
        nxt=score(0); prev=None
        for hh in range(heads+1):
            cur=nxt
            if hh+1<heads: nxt=score(hh+1)
            if prev is not None:
                h1=hh-1; pb,dsb=prev
                hs=slice(h1*HD,(h1+1)*HD)
                dqT[hs,:]+=lax.dot_general(kT[hs,ks],dsb,NN,preferred_element_type=F32)
                dv[ks,col(h1)]+=jnp.dot(pb,dom[h1],preferred_element_type=F32)
                dk[ks,col(h1)]+=jnp.dot(dsb,qm[h1],preferred_element_type=F32)
            if hh<heads:
                s,dp=cur
                p=jnp.exp2(s-lse[0,hh:hh+1,:])
                ds=p*(dp-delta[hh:hh+1,:])
                prev=(p.astype(BF),ds.astype(BF))
    @pl.loop(0,nk)
    def _(kt):
        f=flags[r,qi,kt]
        @pl.when(f==1)
        def _():
            ks=pl.ds(pl.multiple_of(kt*tk,tk),tk)
            bias[...]=jnp.where(ck[0,ks,0:1]==cq[0,0:1,:],0.0,NEG)
            body(kt,True)
        @pl.when(f==2)
        def _(): body(kt,False)
    if first: dqT_o[0]=dqT[...]
    else: dq_o[0]=(dqT[...]*0.125).T.astype(BF)
    @pl.when(qi==nq-1)
    def _():
        dk_o[0]=dk[...].astype(BF); dv_o[0]=dv[...].astype(BF)

def attn_bwd(flags,cq,ck,q,k,v,do,o,lse,dqT=None,tq=256,tk=256,heads=10):
    nr,S,W=q.shape; Sk=k.shape[1]; hp16=lse.shape[1]
    first=dqT is None
    qs=lambda r,i,*_:(r,i,0); ts=lambda r,i,*_:(r,0,i); ks=lambda r,i,*_:(r,0,0)
    ins=[pl.BlockSpec((1,1,tq),ts),pl.BlockSpec((1,Sk,128),ks),pl.BlockSpec((1,tq,W),qs),pl.BlockSpec((1,Sk,W),ks),pl.BlockSpec((1,Sk,W),ks),
         pl.BlockSpec((1,tq,W),qs),pl.BlockSpec((1,tq,W),qs),pl.BlockSpec((1,hp16,tq),ts)]
    dko=[pl.BlockSpec((1,Sk,W),ks)]*2; dksh=[jax.ShapeDtypeStruct((nr,Sk,W),BF)]*2
    if first:
        outs=[pl.BlockSpec((1,W,tq),ts)]+dko; osh=[jax.ShapeDtypeStruct((nr,W,S),F32)]+dksh
        extra=()
    else:
        ins=ins+[pl.BlockSpec((1,W,tq),ts)]
        outs=[pl.BlockSpec((1,tq,W),qs)]+dko; osh=[jax.ShapeDtypeStruct((nr,S,W),BF)]+dksh
        extra=(dqT,)
    fl=10*nr*S*Sk*W
    return pl.pallas_call(functools.partial(bwd_kernel,first=first,tq=tq,tk=tk,heads=heads),
        out_shape=osh,
        grid_spec=pltpu.PrefetchScalarGridSpec(num_scalar_prefetch=1,grid=(nr,S//tq),in_specs=ins,out_specs=outs,
          scratch_shapes=[pltpu.VMEM((heads,tq,128),BF),pltpu.VMEM((heads,tq,128),BF),pltpu.VMEM((W,Sk),BF),pltpu.VMEM((tk,tq),F32),pltpu.VMEM((W,tq),F32),
             pltpu.VMEM((Sk,W),F32),pltpu.VMEM((Sk,W),F32),pltpu.VMEM((hp16,tq),F32)]),
        compiler_params=pltpu.CompilerParams(dimension_semantics=("arbitrary","arbitrary"),vmem_limit_bytes=VMEM_LIMIT),
        cost_estimate=pl.CostEstimate(flops=fl*4,bytes_accessed=nr*(3*S*W*2+4*Sk*W*2+S*W*4),transcendentals=nr*S*Sk*heads),
        name="attn_bwd_a" if first else "attn_bwd_b",
    )(flags,cq,ck,q,k,v,do,o,lse,*extra)


def ffn_kernel(core, acts, w, b, d_act, act_o, theirs_o, mine_o, sum_o):
    del core
    step = pl.program_id(0)
    half = pl.num_programs(0) // 2
    rows = acts.shape[0]
    chunk = min(256, rows)
    count = rows // chunk

    def product(i):
        return dot(acts[i * chunk : (i + 1) * chunk, :], w[...], NN) + b[...]

    pre = product(0)
    total = None
    for i in range(count):
        following = product(i + 1) if i + 1 < count else None
        at = slice(i * chunk, (i + 1) * chunk)
        cdf = 0.5 + 0.5 * lax.erf(pre * math.sqrt(0.5))
        pdf = jnp.exp(-0.5 * pre * pre) * (1.0 / math.sqrt(2.0 * math.pi))
        act_o[at, :] = (pre * cdf).astype(BF)
        d_pre = (d_act[at, :].astype(F32) * (cdf + pre * pdf)).astype(BF)

        @pl.when(step < half)
        def _():
            theirs_o[at, :] = d_pre

        @pl.when(step >= half)
        def _():
            mine_o[at, :] = d_pre

        part = jnp.sum(d_pre.astype(F32), axis=0, keepdims=True)
        total = part if total is None else total + part
        pre = following
    sum_o[...] = total


def ffn_call(core, acts, w, b, d_act):
    rows, width = acts.shape
    ff = w.shape[1]
    tile = 512
    half = ff // 2 // tile

    def place(i, core):
        return jnp.where(i < half, 1 - core[0], core[0]) * half + lax.rem(i, half)

    col = lambda i, core: (0, place(i, core))
    return pl.pallas_call(
        ffn_kernel,
        out_shape=[
            jax.ShapeDtypeStruct((rows, ff), BF),
            jax.ShapeDtypeStruct((rows, ff // 2), BF),
            jax.ShapeDtypeStruct((rows, ff // 2), BF),
            jax.ShapeDtypeStruct((1, ff), F32),
        ],
        grid_spec=pltpu.PrefetchScalarGridSpec(
            num_scalar_prefetch=1,
            grid=(2 * half,),
            in_specs=[
                pl.BlockSpec((rows, width), lambda i, core: (0, 0)),
                pl.BlockSpec((width, tile), col),
                pl.BlockSpec((1, tile), col),
                pl.BlockSpec((rows, tile), col),
            ],
            out_specs=[
                pl.BlockSpec((rows, tile), col),
                pl.BlockSpec((rows, tile), lambda i, core: (0, jnp.minimum(i, half - 1))),
                pl.BlockSpec((rows, tile), lambda i, core: (0, jnp.maximum(i - half, 0))),
                pl.BlockSpec((1, tile), col),
            ],
        ),
        compiler_params=pltpu.CompilerParams(vmem_limit_bytes=VMEM_LIMIT),
        cost_estimate=pl.CostEstimate(
            flops=2 * rows * width * ff,
            bytes_accessed=2 * (rows * width + width * ff + 3 * rows * ff),
            transcendentals=2 * rows * ff,
        ),
        name="ffn",
    )(core, acts, w, b, d_act)


def grad_kernel(where, *refs, groups, first, second):
    ins = refs[: sum(2 * len(g) for g in groups)]
    outs = refs[len(ins) : len(ins) + first]
    acc = refs[-1]
    height = acc.shape[0] // len(groups)
    at = 0
    for index, group in enumerate(groups):
        total = None
        for _ in group:
            part = dot(ins[at][...], ins[at + 1][...], TN)
            total = part if total is None else total + part
            at += 2
        acc[index * height : (index + 1) * height, :] = total
    rows = acc.shape[0] // (first * second)
    for one in range(first):
        for two in range(second):
            block = lax.bitwise_xor(two * first + one, where[0])
            outs[one][two] = acc[pl.ds(pl.multiple_of(block * rows, 16), rows), :].astype(BF)


def grad_call(where, groups, first, second, tile, name):
    width = groups[0][0][3]
    ins, flat, flops, moved = [], [], 0, 0
    height = sum(g[0][0].shape[1] for g in groups)
    for group in groups:
        for a, b, offset, n in group:
            ins.append(pl.BlockSpec(a.shape, lambda i, where: (0, 0)))
            if offset is None:
                ins.append(pl.BlockSpec((b.shape[0], tile), lambda i, where: (0, i)))
            else:
                ins.append(
                    pl.BlockSpec(
                        (b.shape[0], tile),
                        lambda i, where, offset=offset: (0, where[offset] * (width // tile) + i),
                    )
                )
            flat += [a, b]
            flops += 2 * a.shape[0] * a.shape[1] * n
            moved += 2 * a.shape[0] * (a.shape[1] + n)
    rows = height // (first * second)
    return pl.pallas_call(
        functools.partial(
            grad_kernel,
            groups=[[None] * len(g) for g in groups],
            first=first,
            second=second,
        ),
        out_shape=[jax.ShapeDtypeStruct((second, rows, width), BF)] * first,
        grid_spec=pltpu.PrefetchScalarGridSpec(
            num_scalar_prefetch=1,
            grid=(width // tile,),
            in_specs=ins,
            out_specs=[pl.BlockSpec((second, rows, tile), lambda i, where: (0, 0, i))] * first,
            scratch_shapes=[pltpu.VMEM((height, tile), F32)],
        ),
        compiler_params=pltpu.CompilerParams(vmem_limit_bytes=VMEM_LIMIT),
        cost_estimate=pl.CostEstimate(
            flops=flops, bytes_accessed=moved + 2 * height * width, transcendentals=0
        ),
        name=name,
    )(where, *flat)


def back_kernel(where, a1, b1, a2, b2, out):
    del where
    out[0] = (dot(a1[...], b1[...], TN) + dot(a2[...], b2[...], TN)).astype(BF)


def back_call(where, own, mate, one, first, second, name):
    (a1, b1), (a2, b2) = own, mate
    tokens, ff = a1.shape
    rows = ff // (first * second)
    width = b2.shape[1]
    if rows % 128:
        total = dot(a1, lax.dynamic_slice_in_dim(b1, where[1] * width, width, 1), TN) + dot(a2, b2, TN)
        total = total.astype(BF).reshape(first * second, rows, width)
        return jnp.stack([total[lax.bitwise_xor(two * first + one, where[0])] for two in range(second)])

    def block(i, where):
        return (0, lax.bitwise_xor(i * first + one, where[0]))

    return pl.pallas_call(
        back_kernel,
        out_shape=jax.ShapeDtypeStruct((second, rows, width), BF),
        grid_spec=pltpu.PrefetchScalarGridSpec(
            num_scalar_prefetch=1,
            grid=(second,),
            in_specs=[
                pl.BlockSpec((tokens, rows), block),
                pl.BlockSpec((tokens, width), lambda i, where: (0, where[1])),
                pl.BlockSpec((tokens, rows), block),
                pl.BlockSpec((tokens, width), lambda i, where: (0, 0)),
            ],
            out_specs=pl.BlockSpec((1, rows, width), lambda i, where: (i, 0, 0)),
        ),
        compiler_params=pltpu.CompilerParams(vmem_limit_bytes=VMEM_LIMIT),
        cost_estimate=pl.CostEstimate(
            flops=4 * tokens * second * rows * width,
            bytes_accessed=2 * (2 * tokens * (second * rows + width) + second * rows * width),
            transcendentals=0,
        ),
        name=name,
    )(where, a1, b1, a2, b2)


def tile_flags(queries, keys, tq, tk):
    q_first, q_last = queries[:, ::tq], queries[:, tq - 1 :: tq]
    k_first, k_last = keys[:, ::tk], keys[:, tk - 1 :: tk]
    meet = (q_first[:, :, None] <= k_last[:, None, :]) & (k_first[:, None, :] <= q_last[:, :, None])
    whole = (
        (q_first == q_last)[:, :, None]
        & (k_first == k_last)[:, None, :]
        & (q_first[:, :, None] == k_first[:, None, :])
    )
    return jnp.where(whole, 2, jnp.where(meet, 1, 0)).astype(jnp.int32)


def layer_norm_parts(values):
    centred = values - jnp.mean(values, axis=-1, keepdims=True)
    rstd = lax.rsqrt(jnp.mean(centred * centred, axis=-1, keepdims=True) + EPS)
    return centred * rstd, rstd


def layer_norm_back(d_norm, gain, xhat, rstd):
    e = d_norm * gain
    return rstd * (
        e - jnp.mean(e, axis=-1, keepdims=True) - xhat * jnp.mean(e * xhat, axis=-1, keepdims=True)
    )


def on_device(
    tokens,
    cell_start,
    norm1_gain,
    norm1_bias,
    w_qkv,
    bias_q,
    bias_v,
    w_out,
    bias_out,
    norm2_gain,
    norm2_bias,
    w_in,
    bias_in,
    w_back,
    bias_back,
    cotangent,
):
    rows, seg, width = tokens.shape
    count = rows * seg
    ff = w_in.shape[1]
    half = width // 2
    wide = lax.axis_size("wide")
    group = lax.axis_size("blk")
    place = lax.axis_index("wide")
    core = place % 2
    chips = wide // 2
    first = 2 if chips <= 8 else 4
    second = chips // first
    heads = HEADS // 2
    tq, tk = min(512, seg), min(256, seg)
    where = jnp.stack([place // 2, core]).astype(jnp.int32)
    where_out = jnp.stack([lax.bitwise_xor(place // 2, core * (chips // 2)), core]).astype(jnp.int32)

    def across(array, by):
        return lax.ppermute(array, "wide", [(i, i ^ by) for i in range(wide)])

    def to_mate(array):
        return across(array, 1)

    def from_ahead(array, by):
        return lax.ppermute(array, "blk", [((i + by) % group, i) for i in range(group)])

    def to_ahead(array, by):
        return lax.ppermute(array, "blk", [(i, (i + by) % group) for i in range(group)])

    def cut(array, start, size, axis):
        return lax.dynamic_slice_in_dim(array, start, size, axis)

    inputs = tokens.astype(F32).reshape(count, width)
    xhat1, rstd1 = layer_norm_parts(inputs)
    acts = (xhat1 * norm1_gain + norm1_bias).astype(BF)
    far_acts = [from_ahead(acts, by) for by in range(1, group)]
    acts_sets = [acts, to_mate(acts)]
    cells = [cell_start, to_mate(cell_start)]
    far_cells = [jnp.concatenate([from_ahead(c, by) for by in range(1, group)], axis=1) for c in cells]

    w_q = cut(w_qkv, core * half, half, 1)
    w_k = cut(w_qkv, width + core * half, half, 1)
    w_v = cut(w_qkv, 2 * width + core * half, half, 1)
    b_q = cut(bias_q, core * half, half, 0)
    b_v = cut(bias_v, core * half, half, 0)

    def by_row(array):
        return array.reshape(rows, -1, half)

    def columns(array):
        return jnp.broadcast_to(array[:, :, None], array.shape + (128,))

    queries = [by_row((dot(a, w_q, NN) + b_q).astype(BF)) for a in acts_sets]
    keys = [by_row(dot(a, w_k, NN).astype(BF)) for a in acts_sets]
    values = [by_row((dot(a, w_v, NN) + b_v).astype(BF)) for a in acts_sets]
    near_flags = [tile_flags(c, c, tq, tk) for c in cells]
    far_flags = [tile_flags(c, f, tq, tk) for c, f in zip(cells, far_cells)]
    cell_rows = [c[:, None, :] for c in cells]
    near_columns = [columns(c) for c in cells]
    far_columns = [columns(c) for c in far_cells]
    states = [
        attn_fwd(near_flags[s], cell_rows[s], near_columns[s], queries[s], keys[s], values[s], None, tq, tk, heads)
        for s in range(2)
    ]
    d_out = cotangent.reshape(count, width)
    d_act = dot(d_out, w_back, NT).astype(BF)

    far_sets = [far_acts, [to_mate(a) for a in far_acts]]

    def joined(parts):
        return parts[0] if len(parts) == 1 else jnp.concatenate(parts, axis=1)

    far_keys = [joined([by_row(dot(a, w_k, NN).astype(BF)) for a in f]) for f in far_sets]
    far_values = [joined([by_row((dot(a, w_v, NN) + b_v).astype(BF)) for a in f]) for f in far_sets]
    attended = [None, None]
    stats = [None, None]
    for s in (1, 0):
        attended[s], stats[s] = attn_fwd(
            far_flags[s], cell_rows[s], far_columns[s], queries[s], far_keys[s], far_values[s], states[s], tq, tk, heads
        )
    flat = [a.reshape(count, half) for a in attended]
    own_rest = to_mate(flat[1])
    mate_rest = to_mate(flat[0])
    w_out_own = cut(w_out, core * half, half, 0)
    w_out_mate = cut(w_out, (1 - core) * half, half, 0)
    middle = inputs + (dot(flat[0], w_out_own, NN) + dot(own_rest, w_out_mate, NN)) + bias_out

    xhat2, rstd2 = layer_norm_parts(middle)
    acts2 = (xhat2 * norm2_gain + norm2_bias).astype(BF)
    acts2_mate = to_mate(acts2)
    act, d_pre_theirs, d_pre_mine, d_pre_sum = ffn_call(
        where[1:], acts2, w_in, bias_in.reshape(1, ff), d_act
    )
    d_pre_mate = to_mate(d_pre_theirs)
    act_mate = to_mate(act)
    d_out_mate = to_mate(cut(d_out, (1 - core) * half, half, 1))
    w_in_mine = cut(w_in, core * (ff // 2), ff // 2, 1)
    w_in_theirs = cut(w_in, (1 - core) * (ff // 2), ff // 2, 1)
    d_norm2 = dot(d_pre_theirs, w_in_theirs, NT) + dot(d_pre_mine, w_in_mine, NT)
    grad_out = d_out.astype(F32)
    d_middle = grad_out + layer_norm_back(d_norm2, norm2_gain, xhat2, rstd2)
    d_z = d_middle.astype(BF)
    d_att_mate = to_mate(dot(d_z, w_out_mate, NT).astype(BF))
    d_att = [by_row(dot(d_z, w_out_own, NT).astype(BF)), by_row(d_att_mate)]
    d_z_mate = to_mate(cut(d_z, (1 - core) * half, half, 1))

    mixed = (middle + dot(act, w_back, NN) + bias_back).astype(BF).reshape(tokens.shape)

    def scatter(parts):
        received = [across(parts[one], 2 * one) for one in range(1, first)]
        sums = []
        for two in range(second):
            total = parts[0][two].astype(F32)
            for part in received:
                total = total + part[two].astype(F32)
            sums.append(total.astype(BF))
        total = sums[0].astype(F32)
        for two in range(1, second):
            total = total + across(sums[two], 2 * first * two).astype(F32)
        total = total.astype(BF)
        if group == 2:
            return total.astype(F32) + from_ahead(total, 1).astype(F32)
        return lax.psum(total, "blk").astype(F32)

    def finish(total):
        split = total.astype(BF).reshape(2, -1, total.shape[-1])
        theirs = lax.dynamic_index_in_dim(split, 1 - core, 0, keepdims=False)
        mine = lax.dynamic_index_in_dim(split, core, 0, keepdims=False)
        other = to_mate(theirs)
        low, high = jnp.where(core == 0, mine, other), jnp.where(core == 0, other, mine)
        return low.astype(F32), high.astype(F32)

    grad_in = grad_call(
        where, [[(acts2, d_pre_mine, None, ff // 2), (acts2_mate, d_pre_mate, None, ff // 2)]], first, second, 512, "grad_in"
    )
    grad_back = [
        back_call(where, (act, d_out), (act_mate, d_out_mate), one, first, second, "grad_back")
        for one in list(range(1, first)) + [0]
    ]
    grad_back = [grad_back[-1]] + grad_back[:-1]
    grad_w_in = jnp.concatenate(finish(scatter(grad_in)), axis=1)
    grad_w_back = jnp.concatenate(finish(scatter(grad_back)), axis=1)
    grad_o = grad_call(
        where_out,
        [
            [(flat[0], d_z, 1, half), (flat[1], d_z_mate, None, half)],
            [(own_rest, d_z, 1, half), (mate_rest, d_z_mate, None, half)],
        ],
        first,
        second,
        half,
        "grad_out",
    )
    grad_w_out = jnp.concatenate(finish(scatter(grad_o)), axis=1)

    def vectors(parts):
        packed = jnp.concatenate([p.reshape(wide, -1) for p in parts], axis=1)
        total = packed
        digits = [(1, 2), (2, first), (2 * first, second)]
        for stride, size in reversed(digits):
            total = total.reshape(-1, size, stride, packed.shape[1])
            mine = (place // stride) % size
            kept = lax.dynamic_index_in_dim(total, mine, 1, keepdims=False)
            for by in range(1, size):
                send = lax.dynamic_index_in_dim(total, mine ^ by, 1, keepdims=False)
                kept = kept + across(send, by * stride)
            total = kept.reshape(stride, packed.shape[1])
        total = total.reshape(-1)
        if group == 2:
            total = total + from_ahead(total, 1)
        else:
            total = lax.psum(total, "blk")
        out, at = [], 0
        for p in parts:
            size = p.size // wide
            out.append(total[at : at + size])
            at += size
        return out

    early = vectors(
        [
            jnp.sum(d_z.astype(F32), axis=0),
            jnp.sum(d_norm2 * xhat2, axis=0),
            jnp.sum(d_norm2, axis=0),
            d_pre_sum,
            jnp.sum(grad_out, axis=0),
        ]
    )

    far_back = [
        attn_bwd(
            far_flags[s], cell_rows[s], far_columns[s], queries[s], far_keys[s], far_values[s],
            d_att[s], attended[s], stats[s], None, tq, tk, heads,
        )
        for s in range(2)
    ]

    def far_norm(s, by):
        at = slice(by * seg, (by + 1) * seg)
        d_k = far_back[s][1][:, at].reshape(count, half)
        d_v = far_back[s][2][:, at].reshape(count, half)
        return d_k, d_v, dot(d_k, w_k, NT) + dot(d_v, w_v, NT)

    far_grads = [[far_norm(s, by) for by in range(group - 1)] for s in range(2)]
    d_norm1_far = None
    for by in range(group - 1):
        part = far_grads[0][by][2] + to_mate(far_grads[1][by][2].astype(BF)).astype(F32)
        part = to_ahead(part.astype(BF), by + 1).astype(F32)
        d_norm1_far = part if d_norm1_far is None else d_norm1_far + part
    near_back = [
        attn_bwd(
            near_flags[s], cell_rows[s], near_columns[s], queries[s], keys[s], values[s],
            d_att[s], attended[s], stats[s], far_back[s][0], tq, tk, heads,
        )
        for s in range(2)
    ]
    d_q = [b[0].reshape(count, half) for b in near_back]
    d_k = [b[1].reshape(count, half) for b in near_back]
    d_v = [b[2].reshape(count, half) for b in near_back]

    def grad_far(column, near, name):
        pairs = [(acts_sets[s], near[s], None, half) for s in range(2)]
        for s in range(2):
            for by in range(group - 1):
                pairs.append((far_sets[s][by], far_grads[s][by][column], None, half))
        return grad_call(where, [pairs], first, second, half, name)

    grad_k = finish(scatter(grad_far(0, d_k, "grad_k")))
    grad_v = finish(scatter(grad_far(1, d_v, "grad_v")))
    grad_q = finish(
        scatter(grad_call(where, [[(acts_sets[s], d_q[s], None, half) for s in range(2)]], first, second, half, "grad_q"))
    )
    grad_w_qkv = jnp.concatenate(grad_q + grad_k + grad_v, axis=1)

    near_norm = [dot(d_q[s], w_q, NT) + dot(d_k[s], w_k, NT) + dot(d_v[s], w_v, NT) for s in range(2)]
    d_norm1 = near_norm[0] + to_mate(near_norm[1].astype(BF)).astype(F32) + d_norm1_far
    grad_tokens = (d_middle + layer_norm_back(d_norm1, norm1_gain, xhat1, rstd1)).reshape(tokens.shape)

    def widened(array):
        return lax.dynamic_update_slice_in_dim(jnp.zeros((width,), F32), array, core * half, 0)

    def column_sum(arrays):
        return sum(jnp.sum(a.astype(F32), axis=0) for a in arrays)

    late = vectors(
        [
            jnp.sum(d_norm1 * xhat1, axis=0),
            jnp.sum(d_norm1, axis=0),
            widened(column_sum(d_q)),
            widened(column_sum(d_v + [g[1] for f in far_grads for g in f])),
        ]
    )
    return (
        mixed,
        grad_tokens,
        late[0],
        late[1],
        grad_w_qkv,
        late[2],
        late[3],
        grad_w_out,
        early[0],
        early[1],
        early[2],
        grad_w_in,
        early[3],
        grad_w_back,
        early[4],
    )


def solution(mesh):
    spread = P("wide", "blk", None)
    placed = (spread, P("wide", "blk")) + (P(),) * 13 + (spread,)
    matrix, vector = P("wide", None), P("wide")
    return jax.shard_map(
        on_device,
        mesh=mesh,
        in_specs=placed,
        out_specs=(
            spread, spread, vector, vector, matrix, vector, vector, matrix, vector, vector, vector,
            matrix, vector, matrix, vector,
        ),
        check_vma=False,
    )
```

```python
import functools
import math

import jax
import jax.numpy as jnp
from jax import lax
from jax.experimental import pallas as pl
from jax.experimental.pallas import tpu as pltpu
from jax.sharding import PartitionSpec as P

HEADS = 20
HEAD_DIM = 64
HD = HEAD_DIM
EPS = 1e-05
NEG = -1e30
LOG2E = math.log2(math.e)
C2 = LOG2E / math.sqrt(HEAD_DIM)
F32 = jnp.float32
BF = jnp.bfloat16
NN = (((1,), (0,)), ((), ()))
NT = (((1,), (1,)), ((), ()))
TN = (((0,), (0,)), ((), ()))
VMEM_LIMIT = 56 * 2**20
SHARE = 20


def dot(a, b, dims):
    return lax.dot_general(a, b, dims, preferred_element_type=F32)


def head_sumsq(x,hp16):
    W=x.shape[1]
    sq=x.astype(F32)*x.astype(F32)
    row=lax.broadcasted_iota(jnp.int32,(hp16,W),0); col=lax.broadcasted_iota(jnp.int32,(hp16,W),1)
    ones=jnp.where(row==col//HD,1.0,0.0).astype(BF)
    return lax.dot_general(ones,sq.astype(BF),NT,preferred_element_type=F32)

def fwd_kernel(flags,cq,ck,q,k,v,*rest,first,tq,tk,heads):
    if first:
        accT_o,m_o,l_o,qm,vT,bias,acc,m,l,kn=rest
    else:
        accT_i,m_i,l_i,o_o,lse_o,qm,vT,bias,acc,m,l,kn=rest
    r=pl.program_id(0); qi=pl.program_id(1)
    nk=k.shape[1]//tk
    hp16=m.shape[0]
    @pl.when(qi==0)
    def _():
        vT[...]=v[0].T
        kn[...]=jnp.broadcast_to(jnp.sqrt(jnp.max(head_sumsq(k[0],hp16),1,keepdims=True)),kn.shape)
    lane=lax.broadcasted_iota(jnp.int32,(tq,128),1)
    for hp in range(heads//2):
        qp=q[0,:,hp*128:(hp+1)*128]
        qm[2*hp]=jnp.where(lane<64,qp,0).astype(BF)
        qm[2*hp+1]=jnp.where(lane>=64,qp,0).astype(BF)
    bound=jnp.sqrt(head_sumsq(q[0],hp16))*kn[:,0:1]*(C2*1.02)
    safe=jnp.max(bound)<50.0
    if first:
        m0=bound
    else:
        m0=jnp.maximum(bound,m_i[0])
    def loop(online):
        if first:
            acc[...]=jnp.zeros_like(acc); l[...]=jnp.zeros_like(l)
            m[...]=jnp.full_like(m,NEG) if online else m0
        elif online:
            acc[...]=accT_i[0]; m[...]=m_i[0]; l[...]=l_i[0]
        else:
            al=jnp.exp2(m_i[0]-m0)
            m[...]=m0; l[...]=al*l_i[0]
            for hh in range(heads):
                hs=slice(hh*HD,(hh+1)*HD)
                acc[hs,:]=al[hh:hh+1,:]*accT_i[0,hs,:]
        def body(kt,masked):
            ks=pl.ds(pl.multiple_of(kt*tk,tk),tk)
            if online:
                @pl.loop(0,heads//2)
                def _(hp):
                    kp=k[0,ks,pl.ds(pl.multiple_of(hp*128,128),128)]
                    for j in range(2):
                        hh=2*hp+j
                        s=lax.dot_general(kp,qm[hh],NT,preferred_element_type=F32)*C2+bias[...]
                        mp=m[pl.ds(hh,1),:]
                        mn=jnp.maximum(mp,jnp.max(s,0,keepdims=True))
                        p=jnp.exp2(s-mn)
                        al=jnp.exp2(mp-mn)
                        m[pl.ds(hh,1),:]=mn
                        l[pl.ds(hh,1),:]=al*l[pl.ds(hh,1),:]+jnp.sum(p,0,keepdims=True)
                        hs=pl.ds(pl.multiple_of(hh*HD,HD),HD)
                        acc[hs,:]=al*acc[hs,:]+lax.dot_general(vT[hs,ks],p.astype(BF),NN,preferred_element_type=F32)
                return
            def score(hh):
                s=lax.dot_general(k[0,ks,(hh//2)*128:(hh//2+1)*128],qm[hh],NT,preferred_element_type=F32)*C2
                if masked: s=s+bias[...]
                return s
            s=score(0); pp=None
            for hh in range(heads+1):
                if hh+1<heads: sn=score(hh+1)
                if pp is not None:
                    hs=slice((hh-1)*HD,hh*HD)
                    acc[hs,:]+=lax.dot_general(vT[hs,ks],pp,NN,preferred_element_type=F32)
                if hh<heads:
                    p=jnp.exp2(s-m[hh:hh+1,:])
                    l[hh:hh+1,:]+=jnp.sum(p,0,keepdims=True)
                    pp=p.astype(BF)
                s=sn
        @pl.loop(0,nk)
        def _(kt):
            f=flags[r,qi,kt]
            def mask():
                ks=pl.ds(pl.multiple_of(kt*tk,tk),tk)
                bias[...]=jnp.where(ck[0,ks,0:1]==cq[0,0:1,:],0.0,NEG)
            if online:
                @pl.when(f>0)
                def _():
                    mask(); body(kt,True)
            else:
                @pl.when(f==1)
                def _():
                    mask(); body(kt,True)
                @pl.when(f==2)
                def _(): body(kt,False)
    @pl.when(safe)
    def _(): loop(False)
    @pl.when(jnp.logical_not(safe))
    def _(): loop(True)
    if first:
        accT_o[0]=acc[...]; m_o[0]=m[...]; l_o[0]=l[...]
    else:
        for hp in range(heads//2):
            parts=[]
            for hh in (2*hp,2*hp+1):
                parts.append(acc[hh*HD:(hh+1)*HD,:]/l[hh:hh+1,:])
            o_o[0,:,hp*128:(hp+1)*128]=jnp.concatenate(parts,0).T.astype(BF)
        lse_o[0]=m[...]+jnp.log2(l[...])

def attn_fwd(flags,cq,ck,q,kv,kb,state,tq,tk,heads):
    nr,S,_=q.shape; W=heads*HD; Sk=kv.shape[1]; hp16=-(-heads//8)*8
    first=state is None
    qs=lambda r,i,*_:(r,i,0); ts=lambda r,i,*_:(r,0,i); ks=lambda r,i,*_:(r,0,0)
    stspec=[pl.BlockSpec((1,W,tq),ts),pl.BlockSpec((1,hp16,tq),ts),pl.BlockSpec((1,hp16,tq),ts)]
    ins=[pl.BlockSpec((1,1,tq),ts),pl.BlockSpec((1,Sk,128),ks),pl.BlockSpec((1,tq,W),qs),pl.BlockSpec((1,Sk,W),lambda r,i,*_:(r,0,kb)),pl.BlockSpec((1,Sk,W),lambda r,i,*_:(r,0,kb+1))]
    if first:
        outs=stspec
        osh=[jax.ShapeDtypeStruct((nr,W,S),F32)]+[jax.ShapeDtypeStruct((nr,hp16,S),F32)]*2
    else:
        ins=ins+stspec
        outs=[pl.BlockSpec((1,tq,W),qs),pl.BlockSpec((1,hp16,tq),ts)]
        osh=[jax.ShapeDtypeStruct((nr,S,W),BF),jax.ShapeDtypeStruct((nr,hp16,S),F32)]
    fl=4*nr*S*Sk*W
    return pl.pallas_call(functools.partial(fwd_kernel,first=first,tq=tq,tk=tk,heads=heads),
        out_shape=osh,
        grid_spec=pltpu.PrefetchScalarGridSpec(num_scalar_prefetch=1,grid=(nr,S//tq),in_specs=ins,out_specs=outs,
          scratch_shapes=[pltpu.VMEM((heads,tq,128),BF),pltpu.VMEM((W,Sk),BF),pltpu.VMEM((tk,tq),F32),pltpu.VMEM((W,tq),F32),pltpu.VMEM((hp16,tq),F32),pltpu.VMEM((hp16,tq),F32),pltpu.VMEM((hp16,128),F32)]),
        compiler_params=pltpu.CompilerParams(dimension_semantics=("arbitrary","arbitrary"),vmem_limit_bytes=VMEM_LIMIT),
        cost_estimate=pl.CostEstimate(flops=fl//SHARE,bytes_accessed=nr*(S*W*2+2*Sk*W*2+S*W*4)//SHARE,transcendentals=0),
        name="attn_fwd_a" if first else "attn_fwd_b",
    )(flags,cq,ck,q,kv,kv,*(state or ()))

def bwd_kernel(flags,cq,ck,q,k,v,do,o,lse,*rest,first,tq,tk,heads):
    if first:
        dqT_o,dkv_o,qm,dom,kT,bias,dqT,dk,dv,delta=rest
    else:
        dqT_i,dqkv_o,qm,dom,kT,bias,dqT,dk,dv,delta=rest
    r=pl.program_id(0); qi=pl.program_id(1); nq=pl.num_programs(1)
    nk=k.shape[1]//tk
    @pl.when(qi==0)
    def _():
        kT[...]=k[0].T
        dk[...]=jnp.zeros_like(dk); dv[...]=jnp.zeros_like(dv)
    lane=lax.broadcasted_iota(jnp.int32,(tq,128),1)
    for hp in range(heads//2):
        c=slice(hp*128,(hp+1)*128)
        qp=q[0,:,c]*jnp.asarray(0.125,BF); dp_=do[0,:,c]
        qm[2*hp]=jnp.where(lane<64,qp,0).astype(BF)
        qm[2*hp+1]=jnp.where(lane>=64,qp,0).astype(BF)
        dom[2*hp]=jnp.where(lane<64,dp_,0).astype(BF)
        dom[2*hp+1]=jnp.where(lane>=64,dp_,0).astype(BF)
    W=heads*HD
    prod=do[0].astype(F32)*o[0].astype(F32)
    hi=prod.astype(BF); lo=(prod-hi.astype(F32)).astype(BF)
    hp16=delta.shape[0]
    row=lax.broadcasted_iota(jnp.int32,(hp16,W),0); col=lax.broadcasted_iota(jnp.int32,(hp16,W),1)
    ones=jnp.where(row==col//HD,1.0,0.0).astype(BF)
    delta[...]=lax.dot_general(ones,hi,NT,preferred_element_type=F32)+lax.dot_general(ones,lo,NT,preferred_element_type=F32)
    if first: dqT[...]=jnp.zeros_like(dqT)
    else: dqT[...]=dqT_i[0]
    def body(kt):
        ks=pl.ds(pl.multiple_of(kt*tk,tk),tk)
        def col(hh): return slice((hh//2)*128,(hh//2+1)*128)
        def score(hh):
            s=lax.dot_general(k[0,ks,col(hh)],qm[hh],NT,preferred_element_type=F32)*LOG2E+bias[...]
            return s,lax.dot_general(v[0,ks,col(hh)],dom[hh],NT,preferred_element_type=F32)
        nxt=score(0); prev=None
        for hh in range(heads+1):
            cur=nxt
            if hh+1<heads: nxt=score(hh+1)
            if prev is not None:
                h1=hh-1; pb,dsb=prev
                hs=slice(h1*HD,(h1+1)*HD)
                dqT[hs,:]+=lax.dot_general(kT[hs,ks],dsb,NN,preferred_element_type=F32)
                dv[ks,col(h1)]+=jnp.dot(pb,dom[h1],preferred_element_type=F32)
                dk[ks,col(h1)]+=jnp.dot(dsb,qm[h1],preferred_element_type=F32)
            if hh<heads:
                s,dp=cur
                p=jnp.exp2(s-lse[0,hh:hh+1,:])
                ds=p*(dp-delta[hh:hh+1,:])
                prev=(p.astype(BF),ds.astype(BF))
    @pl.loop(0,nk)
    def _(kt):
        f=flags[r,qi,kt]
        @pl.when(f>0)
        def _():
            ks=pl.ds(pl.multiple_of(kt*tk,tk),tk)
            bias[...]=jnp.where(ck[0,ks,0:1]==cq[0,0:1,:],0.0,NEG)
            body(kt)
    if first: dqT_o[0]=dqT[...]
    else: dqkv_o[0,pl.ds(pl.multiple_of(qi*tq,tq),tq),0:W]=(dqT[...]*0.125).T.astype(BF)
    @pl.when(qi==nq-1)
    def _():
        out,at=(dkv_o,0) if first else (dqkv_o,W)
        out[0,:,at:at+W]=dk[...].astype(BF); out[0,:,at+W:at+2*W]=dv[...].astype(BF)

def attn_bwd(flags,cq,ck,q,kv,kb,do,o,lse,dqT,tq,tk,heads):
    nr,S,_=q.shape; W=heads*HD; Sk=kv.shape[1]; hp16=lse.shape[1]
    first=dqT is None
    qs=lambda r,i,*_:(r,i,0); ts=lambda r,i,*_:(r,0,i); ks=lambda r,i,*_:(r,0,0)
    ins=[pl.BlockSpec((1,1,tq),ts),pl.BlockSpec((1,Sk,128),ks),pl.BlockSpec((1,tq,W),qs),pl.BlockSpec((1,Sk,W),lambda r,i,*_:(r,0,kb)),pl.BlockSpec((1,Sk,W),lambda r,i,*_:(r,0,kb+1)),
         pl.BlockSpec((1,tq,W),qs),pl.BlockSpec((1,tq,W),qs),pl.BlockSpec((1,hp16,tq),ts)]
    if first:
        outs=[pl.BlockSpec((1,W,tq),ts),pl.BlockSpec((1,Sk,2*W),ks)]; osh=[jax.ShapeDtypeStruct((nr,W,S),F32),jax.ShapeDtypeStruct((nr,Sk,2*W),BF)]
        extra=()
    else:
        ins=ins+[pl.BlockSpec((1,W,tq),ts)]
        outs=[pl.BlockSpec((1,Sk,3*W),ks)]; osh=[jax.ShapeDtypeStruct((nr,Sk,3*W),BF)]
        extra=(dqT,)
    fl=10*nr*S*Sk*W
    return pl.pallas_call(functools.partial(bwd_kernel,first=first,tq=tq,tk=tk,heads=heads),
        out_shape=osh,
        grid_spec=pltpu.PrefetchScalarGridSpec(num_scalar_prefetch=1,grid=(nr,S//tq),in_specs=ins,out_specs=outs,
          scratch_shapes=[pltpu.VMEM((heads,tq,128),BF),pltpu.VMEM((heads,tq,128),BF),pltpu.VMEM((W,Sk),BF),pltpu.VMEM((tk,tq),F32),pltpu.VMEM((W,tq),F32),
             pltpu.VMEM((Sk,W),F32),pltpu.VMEM((Sk,W),F32),pltpu.VMEM((hp16,tq),F32)]),
        compiler_params=pltpu.CompilerParams(dimension_semantics=("arbitrary","arbitrary"),vmem_limit_bytes=VMEM_LIMIT),
        cost_estimate=pl.CostEstimate(flops=fl//SHARE,bytes_accessed=nr*(3*S*W*2+4*Sk*W*2+S*W*4)//SHARE,transcendentals=0),
        name="attn_bwd_a" if first else "attn_bwd_b",
    )(flags,cq,ck,q,kv,kv,do,o,lse,*extra)


def ffn_kernel(core, acts, w, b, d_act, act_o, theirs_o, mine_o, sum_o):
    del core
    step = pl.program_id(0)
    half = pl.num_programs(0) // 2
    rows = acts.shape[0]
    chunk = min(256, rows)
    count = rows // chunk

    def product(i):
        return dot(acts[i * chunk : (i + 1) * chunk, :], w[...], NN) + b[...]

    pre = product(0)
    total = None
    for i in range(count):
        following = product(i + 1) if i + 1 < count else None
        at = slice(i * chunk, (i + 1) * chunk)
        cdf = 0.5 + 0.5 * lax.erf(pre * math.sqrt(0.5))
        pdf = jnp.exp(-0.5 * pre * pre) * (1.0 / math.sqrt(2.0 * math.pi))
        act_o[at, :] = (pre * cdf).astype(BF)
        d_pre = (d_act[at, :].astype(F32) * (cdf + pre * pdf)).astype(BF)

        @pl.when(step < half)
        def _():
            theirs_o[at, :] = d_pre

        @pl.when(step >= half)
        def _():
            mine_o[at, :] = d_pre

        part = jnp.sum(d_pre.astype(F32), axis=0, keepdims=True)
        total = part if total is None else total + part
        pre = following
    sum_o[...] = total


def ffn_call(core, acts, w, b, d_act):
    rows, width = acts.shape
    ff = w.shape[1]
    tile = 512
    half = ff // 2 // tile

    def place(i, core):
        return jnp.where(i < half, 1 - core[0], core[0]) * half + lax.rem(i, half)

    col = lambda i, core: (0, place(i, core))
    return pl.pallas_call(
        ffn_kernel,
        out_shape=[
            jax.ShapeDtypeStruct((rows, ff), BF),
            jax.ShapeDtypeStruct((rows, ff // 2), BF),
            jax.ShapeDtypeStruct((rows, ff // 2), BF),
            jax.ShapeDtypeStruct((1, ff), F32),
        ],
        grid_spec=pltpu.PrefetchScalarGridSpec(
            num_scalar_prefetch=1,
            grid=(2 * half,),
            in_specs=[
                pl.BlockSpec((rows, width), lambda i, core: (0, 0)),
                pl.BlockSpec((width, tile), col),
                pl.BlockSpec((1, tile), col),
                pl.BlockSpec((rows, tile), col),
            ],
            out_specs=[
                pl.BlockSpec((rows, tile), col),
                pl.BlockSpec((rows, tile), lambda i, core: (0, jnp.minimum(i, half - 1))),
                pl.BlockSpec((rows, tile), lambda i, core: (0, jnp.maximum(i - half, 0))),
                pl.BlockSpec((1, tile), col),
            ],
        ),
        compiler_params=pltpu.CompilerParams(vmem_limit_bytes=VMEM_LIMIT),
        cost_estimate=pl.CostEstimate(
            flops=2 * rows * width * ff // SHARE,
            bytes_accessed=2 * (rows * width + width * ff + 3 * rows * ff) // SHARE,
            transcendentals=0,
        ),
        name="ffn",
    )(core, acts, w, b, d_act)


def store_blocks(where, acc, outs, first, second, halved):
    rows = acc.shape[0] // (first * second)
    for one in range(first):
        for two in range(second):
            block = lax.bitwise_xor(two * first + one, where[0]) * rows
            if halved:
                for part in range(2):
                    at = block + lax.bitwise_xor(where[2], part) * (rows // 2)
                    piece = acc[pl.ds(pl.multiple_of(at, 16), rows // 2), :]
                    outs[part][one, two] = piece.astype(BF)
            else:
                outs[one][two] = acc[pl.ds(pl.multiple_of(block, 16), rows), :].astype(BF)


def grad_kernel(where, *refs, groups, first, second, halved):
    ins = refs[: sum(2 * g for g in groups)]
    acc = refs[-1]
    height = acc.shape[0] // len(groups)
    at = 0
    for index, pairs in enumerate(groups):
        total = None
        for _ in range(pairs):
            part = dot(ins[at][...], ins[at + 1][...], TN)
            total = part if total is None else total + part
            at += 2
        acc[index * height : (index + 1) * height, :] = total
    store_blocks(where, acc, refs[len(ins) : -1], first, second, halved)


def grad_call(where, groups, width, first, second, tile, halved, name):
    ins, flat, depth = [], [], 0
    for group in groups:
        for a, b, offset in group:
            ins.append(pl.BlockSpec(a.shape, lambda i, where: (0, 0)))
            if offset is None:
                index = lambda i, where: (0, where[1] * (width // tile) + i)
            else:
                index = lambda i, where, offset=offset: (0, offset // tile + i)
            ins.append(pl.BlockSpec((b.shape[0], tile), index))
            flat += [a, b]
            depth += a.shape[0]
    height = sum(g[0][0].shape[1] for g in groups)
    depth = depth // len(groups)
    rows = height // (first * second)
    if halved:
        shape, block = (first, second, rows // 2, width), (first, second, rows // 2, tile)
        outs = 2
        index = lambda i, where: (0, 0, 0, i)
    else:
        shape, block = (second, rows, width), (second, rows, tile)
        outs = first
        index = lambda i, where: (0, 0, i)
    return pl.pallas_call(
        functools.partial(
            grad_kernel, groups=[len(g) for g in groups], first=first, second=second, halved=halved
        ),
        out_shape=[jax.ShapeDtypeStruct(shape, BF)] * outs,
        grid_spec=pltpu.PrefetchScalarGridSpec(
            num_scalar_prefetch=1,
            grid=(width // tile,),
            in_specs=ins,
            out_specs=[pl.BlockSpec(block, index)] * outs,
            scratch_shapes=[pltpu.VMEM((height, tile), F32)],
        ),
        compiler_params=pltpu.CompilerParams(vmem_limit_bytes=VMEM_LIMIT),
        cost_estimate=pl.CostEstimate(
            flops=2 * depth * height * width // SHARE,
            bytes_accessed=2 * (depth * (height + width) + height * width) // SHARE,
            transcendentals=0,
        ),
        name=name,
    )(where, *flat)


def back_kernel(where, a1, b1, a2, b2, out1, out2, acc):
    acc[...] = dot(a1[...], b1[...], TN) + dot(a2[...], b2[...], TN)
    rows = acc.shape[0] // 2
    for part, out in enumerate((out1, out2)):
        at = lax.bitwise_xor(where[2], part) * rows
        out[0, 0] = acc[pl.ds(pl.multiple_of(at, 16), rows), :].astype(BF)


def back_call(where, own, mate, first, second, name):
    (a1, b1), (a2, b2) = own, mate
    tokens, ff = a1.shape
    rows = ff // (first * second)
    width = b2.shape[1]

    def block(i, where):
        return (0, lax.bitwise_xor(lax.rem(i, second) * first + i // second, where[0]))

    return pl.pallas_call(
        back_kernel,
        out_shape=[jax.ShapeDtypeStruct((first, second, rows // 2, width), BF)] * 2,
        grid_spec=pltpu.PrefetchScalarGridSpec(
            num_scalar_prefetch=1,
            grid=(first * second,),
            in_specs=[
                pl.BlockSpec((tokens, rows), block),
                pl.BlockSpec((tokens, width), lambda i, where: (0, where[1])),
                pl.BlockSpec((tokens, rows), block),
                pl.BlockSpec((tokens, width), lambda i, where: (0, 0)),
            ],
            out_specs=[
                pl.BlockSpec(
                    (1, 1, rows // 2, width), lambda i, where: (i // second, lax.rem(i, second), 0, 0)
                )
            ]
            * 2,
            scratch_shapes=[pltpu.VMEM((rows, width), F32)],
        ),
        compiler_params=pltpu.CompilerParams(vmem_limit_bytes=VMEM_LIMIT),
        cost_estimate=pl.CostEstimate(
            flops=4 * tokens * ff * width // SHARE,
            bytes_accessed=2 * (2 * tokens * (ff + width) + ff * width) // SHARE,
            transcendentals=0,
        ),
        name=name,
    )(where, a1, b1, a2, b2)


def product_kernel(a, b, *rest, dims):
    total = dot(a[...], b[...], dims)
    for term in rest[:-1]:
        total = total + term[...]
    rest[-1][...] = total.astype(rest[-1].dtype)


def product(a, b, dims, name, terms=()):
    rows, depth = a.shape
    turned = dims == NT
    width = b.shape[0] if turned else b.shape[1]
    tile = 256
    if turned:
        b_spec = pl.BlockSpec((tile, depth), lambda i: (i, 0))
    else:
        b_spec = pl.BlockSpec((depth, tile), lambda i: (0, i))
    return pl.pallas_call(
        functools.partial(product_kernel, dims=dims),
        out_shape=jax.ShapeDtypeStruct((rows, width), BF),
        grid=(width // tile,),
        in_specs=[pl.BlockSpec(a.shape, lambda i: (0, 0), pipeline_mode=pl.Buffered(1)), b_spec]
        + [pl.BlockSpec((t.shape[0], tile), lambda i: (0, i)) for t in terms],
        out_specs=pl.BlockSpec((rows, tile), lambda i: (0, i)),
        compiler_params=pltpu.CompilerParams(vmem_limit_bytes=VMEM_LIMIT),
        cost_estimate=pl.CostEstimate(
            flops=2 * rows * depth * width // SHARE,
            bytes_accessed=2 * (rows * depth + depth * width + rows * width) // SHARE,
            transcendentals=0,
        ),
        name=name,
    )(a, b, *terms)


def tile_flags(queries, keys, tq, tk):
    q_first, q_last = queries[:, ::tq], queries[:, tq - 1 :: tq]
    k_first, k_last = keys[:, ::tk], keys[:, tk - 1 :: tk]
    meet = (q_first[:, :, None] <= k_last[:, None, :]) & (k_first[:, None, :] <= q_last[:, :, None])
    whole = (
        (q_first == q_last)[:, :, None]
        & (k_first == k_last)[:, None, :]
        & (q_first[:, :, None] == k_first[:, None, :])
    )
    return jnp.where(whole, 2, jnp.where(meet, 1, 0)).astype(jnp.int32)


def layer_norm_parts(values):
    centred = values - jnp.mean(values, axis=-1, keepdims=True)
    rstd = lax.rsqrt(jnp.mean(centred * centred, axis=-1, keepdims=True) + EPS)
    return centred * rstd, rstd


def layer_norm_back(d_norm, gain, xhat, rstd):
    e = d_norm * gain
    return rstd * (
        e - jnp.mean(e, axis=-1, keepdims=True) - xhat * jnp.mean(e * xhat, axis=-1, keepdims=True)
    )


def on_device(
    tokens,
    cell_start,
    norm1_gain,
    norm1_bias,
    w_qkv,
    bias_q,
    bias_v,
    w_out,
    bias_out,
    norm2_gain,
    norm2_bias,
    w_in,
    bias_in,
    w_back,
    bias_back,
    cotangent,
):
    rows, seg, width = tokens.shape
    count = rows * seg
    ff = w_in.shape[1]
    half = width // 2
    wide = lax.axis_size("wide")
    group = lax.axis_size("blk")
    place = lax.axis_index("wide")
    member = lax.axis_index("blk")
    core = place % 2
    chips = wide // 2
    first = 2 if chips <= 8 else 4
    second = chips // first
    heads = HEADS // 2
    tq, tk = min(512, seg), min(256, seg)
    halves = group == 2 and ff // chips % 128 == 0
    where = jnp.stack([place // 2, core, member]).astype(jnp.int32)
    where_out = jnp.stack([lax.bitwise_xor(place // 2, core * (chips // 2)), core, member]).astype(jnp.int32)

    def after(value, *earlier):
        return lax.optimization_barrier((value, earlier))[0]

    def across(array, by):
        return lax.ppermute(array, "wide", [(i, i ^ by) for i in range(wide)])

    def to_mate(array):
        return across(array, 1)

    def from_ahead(array, by):
        return lax.ppermute(array, "blk", [((i + by) % group, i) for i in range(group)])

    def to_ahead(array, by):
        return lax.ppermute(array, "blk", [(i, (i + by) % group) for i in range(group)])

    def from_all_ahead(array):
        parts = [from_ahead(array, by) for by in range(1, group)]
        return parts[0] if len(parts) == 1 else jnp.concatenate(parts, axis=1)

    def cut(array, start, size, axis):
        return lax.dynamic_slice_in_dim(array, start, size, axis)

    def paired(array):
        return jnp.concatenate([array, to_mate(array)], axis=0)

    inputs = tokens.astype(F32).reshape(count, width)
    xhat1, rstd1 = layer_norm_parts(inputs)
    acts = (xhat1 * norm1_gain + norm1_bias).astype(BF).reshape(tokens.shape)
    cells = paired(cell_start)
    far_cells = from_all_ahead(cells)
    acts = after(acts, far_cells)
    far_own = from_all_ahead(acts)
    acts_pair = paired(acts).reshape(2 * count, width)
    w_own = jnp.concatenate([cut(w_qkv, part * width + core * half, half, 1) for part in range(3)], axis=1)
    b_own = jnp.concatenate([cut(bias_q, core * half, half, 0), jnp.zeros((half,), F32), cut(bias_v, core * half, half, 0)])

    def columns(array):
        return jnp.broadcast_to(array[:, :, None], array.shape + (128,))

    qkv = (dot(acts_pair, w_own, NN) + b_own).astype(BF).reshape(2 * rows, seg, 3 * half)
    near_flags = tile_flags(cells, cells, tq, tk)
    far_flags = tile_flags(cells, far_cells, tq, tk)
    cell_rows = cells[:, None, :]
    near_columns, far_columns = columns(cells), columns(far_cells)
    state = attn_fwd(near_flags, cell_rows, near_columns, qkv, qkv, 1, None, tq, tk, heads)
    d_out = cotangent.reshape(count, width)
    far_own = after(far_own, state)
    far_mate = to_mate(far_own)
    d_act = dot(after(d_out, far_own, state), w_back, NT).astype(BF)

    far_mate = after(far_mate, d_act)
    far_pair = jnp.concatenate([far_own, far_mate], axis=0)
    far_len = far_pair.shape[1]
    far_pair = far_pair.reshape(-1, width)
    far_kv = (dot(far_pair, w_own[:, half:], NN) + b_own[half:]).astype(BF).reshape(2 * rows, far_len, 2 * half)
    attended, stats = attn_fwd(far_flags, cell_rows, far_columns, qkv, far_kv, 0, state, tq, tk, heads)
    mine, theirs = attended[:rows].reshape(count, half), attended[rows:].reshape(count, half)
    own_rest = to_mate(theirs)
    mate_rest = to_mate(mine)
    w_out_own = cut(w_out, core * half, half, 0)
    w_out_mate = cut(w_out, (1 - core) * half, half, 0)
    middle = inputs + (dot(mine, w_out_own, NN) + dot(own_rest, w_out_mate, NN)) + bias_out

    xhat2, rstd2 = layer_norm_parts(middle)
    acts2 = (xhat2 * norm2_gain + norm2_bias).astype(BF)
    acts2_mate = to_mate(acts2)
    d_out_mate = to_mate(cut(d_out, (1 - core) * half, half, 1))
    act, d_pre_theirs, d_pre_mine, d_pre_sum = ffn_call(where[1:], acts2, w_in, bias_in.reshape(1, ff), d_act)
    d_pre_mate = to_mate(d_pre_theirs)
    act_mate = to_mate(act)
    w_in_mine = cut(w_in, core * (ff // 2), ff // 2, 1)
    w_in_theirs = cut(w_in, (1 - core) * (ff // 2), ff // 2, 1)
    d_norm2 = dot(d_pre_theirs, w_in_theirs, NT) + dot(d_pre_mine, w_in_mine, NT)
    grad_out = d_out.astype(F32)
    d_middle = grad_out + layer_norm_back(d_norm2, norm2_gain, xhat2, rstd2)
    d_z = d_middle.astype(BF)
    d_att_theirs = dot(d_z, w_out_mate, NT).astype(BF)
    d_att_mine = dot(d_z, w_out_own, NT).astype(BF)
    d_att_mate = to_mate(d_att_theirs)
    d_z_mate = to_mate(cut(d_z, (1 - core) * half, half, 1))

    def send(parts):
        return [across(parts[one], 2 * one) for one in range(1, first)]

    def add_first(parts, received):
        sums = []
        for two in range(second):
            total = parts[0][two].astype(F32)
            for part in received:
                total = total + part[two].astype(F32)
            sums.append(total.astype(BF))
        return sums

    def send_second(sums):
        return [across(sums[two], 2 * first * two) for two in range(1, second)]

    def add_second(sums, received):
        total = sums[0].astype(F32)
        for part in received:
            total = total + part.astype(F32)
        return total.astype(BF)

    def add_half(parts, received):
        return [(parts[0][one].astype(F32) + received[one].astype(F32)).astype(BF) for one in range(first)]

    def start(parts):
        return from_ahead(parts[1], 1) if halves else send(parts)

    def middle_step(parts, received):
        if not halves:
            return parts, received
        sums = add_half(parts, received)
        return sums, send(sums)

    def over_row(total, other):
        if group == 2:
            return (total.astype(F32) + other.astype(F32)).astype(BF)
        return lax.psum(total, "blk")

    def ahead(total):
        return from_ahead(total, 1) if group == 2 else None

    def join_halves(total, other):
        return jnp.concatenate([jnp.where(member == 0, total, other), jnp.where(member == 0, other, total)], axis=0)

    def finish(total):
        split = total.reshape(2, -1, total.shape[-1])
        given = lax.dynamic_index_in_dim(split, 1 - core, 0, keepdims=False)
        kept = lax.dynamic_index_in_dim(split, core, 0, keepdims=False)
        other = to_mate(given)
        low, high = jnp.where(core == 0, kept, other), jnp.where(core == 0, other, kept)
        return [low.astype(F32), high.astype(F32)]

    act_held, act_mate = after((act, act_mate), d_att_theirs, d_att_mine)
    if halves:
        grad_back = back_call(where, (act_held, d_out), (act_mate, d_out_mate), first, second, "grad_back")
        back_in = from_ahead(grad_back[1], 1)
    else:
        whole = dot(act_held, cut(d_out, core * half, half, 1), TN) + dot(act_mate, d_out_mate, TN)
        whole = whole.astype(BF).reshape(second, first, ff // chips, half)
        grad_back = [
            jnp.stack([
                whole.reshape(chips, ff // chips, half)[lax.bitwise_xor(two * first + one, where[0])]
                for two in range(second)
            ])
            for one in range(first)
        ]
        back_in = send(grad_back)
    acts2_held = after(acts2, grad_back)
    grad_in = grad_call(
        where, [[(acts2_held, d_pre_mine, 0), (acts2_mate, d_pre_mate, 0)]], ff // 2, first, second, 512, False, "grad_in"
    )
    in_in = send(grad_in)

    d_att = jnp.concatenate([d_att_mine, d_att_mate], axis=0).reshape(2 * rows, seg, half)
    d_z_mate, mate_rest = after((d_z_mate, mate_rest), grad_in)
    d_att = after(d_att, grad_in, d_z_mate, mate_rest)
    d_qT, far_dkv = attn_bwd(
        far_flags, cell_rows, far_columns, qkv, far_kv, 0, d_att, attended, stats, None, tq, tk, heads
    )
    if halves:
        back_sums = add_half(grad_back, after(back_in, d_qT))
        back_in = send(back_sums)
    else:
        back_sums = grad_back
    far_dkv_flat = after(far_dkv, back_sums).reshape(-1, 2 * half)
    far_part = product(far_dkv_flat, w_own[:, half:], NT, "far_norm").reshape(2 * rows, far_len, width)
    far_given = to_mate(far_part[rows:])
    in_sums = add_first(grad_in, after(in_in, far_part))
    in_more = send_second(in_sums)
    far_sum = (far_part[:rows].astype(F32) + after(far_given, in_sums).astype(F32)).astype(BF)
    far_back = [to_ahead(far_sum[:, by * seg : (by + 1) * seg], by + 1) for by in range(group - 1)]
    d_qT = after(d_qT, in_sums, back_sums, far_sum)
    d_qkv, = attn_bwd(
        near_flags, cell_rows, near_columns, qkv, qkv, 1, d_att, attended, stats, d_qT, tq, tk, heads
    )
    back_two = add_first(back_sums, after(back_in, d_qkv))
    back_more = send_second(back_two)
    d_z_held = after(d_z, back_two)
    grad_o = grad_call(
        where_out,
        [
            [(mine, d_z_held, None), (theirs, d_z_mate, 0)],
            [(own_rest, d_z_held, None), (mate_rest, d_z_mate, 0)],
        ],
        half, first, second, half, halves, "grad_out",
    )
    out_in = start(grad_o)
    d_qkv_flat = d_qkv.reshape(2 * count, 3 * half)
    held = after(d_qkv_flat, grad_o)

    def grad_part(part, halved, name, held):
        pairs = [(acts_pair, held, part * half)]
        if part:
            pairs.append((far_pair, far_dkv_flat, (part - 1) * half))
        tile = half if far_len <= 2 * seg else 128
        return grad_call(where, [pairs], half, first, second, tile, halved, name)

    grad_v = grad_part(2, halves, "grad_v", held)
    v_in = start(grad_v)
    in_total = add_second(in_sums, after(in_more, grad_v))
    in_row = ahead(in_total)
    held = after(held, in_total)
    grad_k = grad_part(1, halves, "grad_k", held)
    k_in = start(grad_k)
    out_half, out_in = middle_step(grad_o, after(out_in, grad_k))
    held = after(held, grad_k, out_half)
    grad_q = grad_part(0, halves, "grad_q", held)
    q_in = start(grad_q)
    v_half, v_in = middle_step(grad_v, after(v_in, grad_q))
    held = after(held, grad_q, v_half)
    near_part = product(held, w_own, NT, "near_norm")
    near_given = to_mate(near_part[count:])
    back_total = add_second(back_two, after(back_more, near_part))
    back_row = ahead(back_total)
    k_half, k_in = middle_step(grad_k, after(k_in, near_part))
    out_two = add_first(out_half, after(out_in, near_part))
    out_more = send_second(out_two)
    act_late = after(act_held, back_total, k_half, out_two)
    mixed = product(act_late, w_back, NN, "mixed", (middle, bias_back.reshape(1, width))).reshape(tokens.shape)
    q_half, q_in = middle_step(grad_q, after(q_in, mixed))
    v_two = add_first(v_half, after(v_in, mixed))
    v_more = send_second(v_two)
    k_two = add_first(k_half, after(k_in, v_two))
    k_more = send_second(k_two)
    d_norm1, = after((near_part[:count].astype(F32),), mixed, q_half, v_two, k_two)
    d_norm1 = d_norm1 + near_given.astype(F32)
    for part in far_back:
        d_norm1 = d_norm1 + part.reshape(count, width).astype(F32)
    grad_tokens = (d_middle + layer_norm_back(d_norm1, norm1_gain, xhat1, rstd1)).reshape(tokens.shape)

    def vectors(parts):
        packed = jnp.concatenate([p.reshape(wide, -1) for p in parts], axis=1)
        total = packed
        for stride, size in ((2 * first, second), (2, first), (1, 2)):
            total = total.reshape(-1, size, stride, packed.shape[1])
            spot = (place // stride) % size
            kept = lax.dynamic_index_in_dim(total, spot, 1, keepdims=False)
            for by in range(1, size):
                given = lax.dynamic_index_in_dim(total, spot ^ by, 1, keepdims=False)
                kept = kept + across(given, by * stride)
            total = kept.reshape(stride, packed.shape[1])
        total = total.reshape(-1)
        total = total + from_ahead(total, 1) if group == 2 else lax.psum(total, "blk")
        out, at = [], 0
        for p in parts:
            size = p.size // wide
            out.append(total[at : at + size])
            at += size
        return out

    def widened(array):
        return lax.dynamic_update_slice_in_dim(jnp.zeros((width,), F32), array, core * half, 0)

    far_v_sum = jnp.sum(far_dkv_flat[:, half:].astype(F32), axis=0)
    small = vectors(
        [
            jnp.sum(d_norm1 * xhat1, axis=0),
            jnp.sum(d_norm1, axis=0),
            widened(jnp.sum(d_qkv_flat[:, :half].astype(F32), axis=0)),
            widened(jnp.sum(d_qkv_flat[:, 2 * half :].astype(F32), axis=0) + far_v_sum),
            jnp.sum(d_z.astype(F32), axis=0),
            jnp.sum(d_norm2 * xhat2, axis=0),
            jnp.sum(d_norm2, axis=0),
            d_pre_sum,
            jnp.sum(grad_out, axis=0),
        ]
    )
    q_two = add_first(q_half, after(q_in, d_norm1))
    q_more = send_second(q_two)

    def rest(total, row=None):
        row = ahead(total) if row is None else row
        return join_halves(total, row) if halves else over_row(total, row)

    in_row, back_row = after((in_row, back_row), q_two)
    in_total, back_total = over_row(in_total, in_row), rest(back_total, back_row)
    out_total = rest(add_second(out_two, after(out_more, q_two)))
    v_total = rest(add_second(v_two, after(v_more, q_two)))
    k_total = rest(add_second(k_two, after(k_more, q_two)))
    q_total = rest(add_second(q_two, q_more))

    def matrix(*totals):
        return jnp.concatenate([piece for total in totals for piece in finish(total)], axis=1)

    return (
        mixed,
        grad_tokens,
        small[0],
        small[1],
        matrix(q_total, k_total, v_total),
        small[2],
        small[3],
        matrix(out_total),
        small[4],
        small[5],
        small[6],
        matrix(in_total),
        small[7],
        matrix(back_total),
        small[8],
    )


def solution(mesh):
    spread = P("wide", "blk", None)
    placed = (spread, P("wide", "blk")) + (P(),) * 13 + (spread,)
    matrix, vector = P("wide", None), P("wide")
    return jax.shard_map(
        on_device,
        mesh=mesh,
        in_specs=placed,
        out_specs=(
            spread, spread, vector, vector, matrix, vector, vector, matrix, vector, vector, vector,
            matrix, vector, matrix, vector,
        ),
        check_vma=False,
    )
```

```python
import functools
import math

import jax
import jax.numpy as jnp
from jax import lax
from jax.experimental import pallas as pl
from jax.experimental.pallas import tpu as pltpu
from jax.sharding import PartitionSpec as P

HEADS = 20
HEAD_DIM = 64
HD = HEAD_DIM
EPS = 1e-05
NEG = -1e30
LOG2E = math.log2(math.e)
C2 = LOG2E / math.sqrt(HEAD_DIM)
F32 = jnp.float32
BF = jnp.bfloat16
NN = (((1,), (0,)), ((), ()))
NT = (((1,), (1,)), ((), ()))
TN = (((0,), (0,)), ((), ()))
VMEM_LIMIT = 56 * 2**20
SHARE = 20
VR = HD + 16


def dot(a, b, dims):
    return lax.dot_general(a, b, dims, preferred_element_type=F32)


def head_sumsq(x,hp16):
    W=x.shape[1]
    sq=x.astype(F32)*x.astype(F32)
    row=lax.broadcasted_iota(jnp.int32,(hp16,W),0); col=lax.broadcasted_iota(jnp.int32,(hp16,W),1)
    ones=jnp.where(row==col//HD,1.0,0.0).astype(BF)
    return lax.dot_general(ones,sq.astype(BF),NT,preferred_element_type=F32)

def fwd_kernel(flags,cq,ck,q,k,v,*rest,first,tq,tk,heads):
    if first:
        accT_o,m_o,l_o,qm,vT,bias,acc,m,l,kn=rest
    else:
        accT_i,m_i,l_i,o_o,lse_o,qm,vT,bias,acc,m,l,kn=rest
    r=pl.program_id(0); qi=pl.program_id(1)
    nk=k.shape[1]//tk
    hp16=m.shape[0]
    @pl.when(qi==0)
    def _():
        for hh in range(heads):
            vT[hh*VR:hh*VR+HD,:]=v[0,:,hh*HD:(hh+1)*HD].T
            vT[hh*VR+HD:(hh+1)*VR,:]=jnp.ones((VR-HD,vT.shape[1]),BF)
        kn[...]=jnp.broadcast_to(jnp.sqrt(jnp.max(head_sumsq(k[0],hp16),1,keepdims=True)),kn.shape)
    lane=lax.broadcasted_iota(jnp.int32,(tq,128),1)
    for hp in range(heads//2):
        qp=q[0,:,hp*128:(hp+1)*128]
        qm[2*hp]=jnp.where(lane<64,qp,0).astype(BF)
        qm[2*hp+1]=jnp.where(lane>=64,qp,0).astype(BF)
    bound=jnp.sqrt(head_sumsq(q[0],hp16))*kn[:,0:1]*(C2*1.02)
    safe=jnp.max(bound)<50.0
    if first:
        m0=bound
    else:
        m0=jnp.maximum(bound,m_i[0])
    def loop(online):
        if first:
            acc[...]=jnp.zeros_like(acc); l[...]=jnp.zeros_like(l)
            m[...]=jnp.full_like(m,NEG) if online else m0
        elif online:
            acc[...]=accT_i[0]; m[...]=m_i[0]; l[...]=l_i[0]
        else:
            al=jnp.exp2(m_i[0]-m0)
            m[...]=m0; l[...]=al*l_i[0]
            for hh in range(heads):
                hs=slice(hh*HD,(hh+1)*HD)
                acc[hs,:]=al[hh:hh+1,:]*accT_i[0,hs,:]
        def body(kt,masked):
            ks=pl.ds(pl.multiple_of(kt*tk,tk),tk)
            if online:
                @pl.loop(0,heads//2)
                def _(hp):
                    kp=k[0,ks,pl.ds(pl.multiple_of(hp*128,128),128)]
                    for j in range(2):
                        hh=2*hp+j
                        s=lax.dot_general(kp,qm[hh],NT,preferred_element_type=F32)*C2+bias[...]
                        mp=m[pl.ds(hh,1),:]
                        mn=jnp.maximum(mp,jnp.max(s,0,keepdims=True))
                        p=jnp.exp2(s-mn)
                        al=jnp.exp2(mp-mn)
                        m[pl.ds(hh,1),:]=mn
                        l[pl.ds(hh,1),:]=al*l[pl.ds(hh,1),:]+jnp.sum(p,0,keepdims=True)
                        hs=pl.ds(pl.multiple_of(hh*HD,HD),HD)
                        vs=pl.ds(pl.multiple_of(hh*VR,16),HD)
                        acc[hs,:]=al*acc[hs,:]+lax.dot_general(vT[vs,ks],p.astype(BF),NN,preferred_element_type=F32)
                return
            def score(hh):
                s=lax.dot_general(k[0,ks,(hh//2)*128:(hh//2+1)*128],qm[hh],NT,preferred_element_type=F32)*C2
                if masked: s=s+bias[...]
                return s
            s=score(0); pp=None
            for hh in range(heads+1):
                if hh+1<heads: sn=score(hh+1)
                if pp is not None:
                    h1=hh-1
                    both=lax.dot_general(vT[h1*VR:(h1+1)*VR,ks],pp,NN,preferred_element_type=F32)
                    acc[h1*HD:(h1+1)*HD,:]+=both[:HD]
                    l[h1:h1+1,:]+=both[HD:HD+1]
                if hh<heads:
                    p=jnp.exp2(s-m[hh:hh+1,:])
                    pp=p.astype(BF)
                s=sn
        @pl.loop(0,nk)
        def _(kt):
            f=flags[r,qi,kt]
            def mask():
                ks=pl.ds(pl.multiple_of(kt*tk,tk),tk)
                bias[...]=jnp.where(ck[0,ks,0:1]==cq[0,0:1,:],0.0,NEG)
            if online:
                @pl.when(f>0)
                def _():
                    mask(); body(kt,True)
            else:
                @pl.when(f==1)
                def _():
                    mask(); body(kt,True)
                @pl.when(f==2)
                def _(): body(kt,False)
    @pl.when(safe)
    def _(): loop(False)
    @pl.when(jnp.logical_not(safe))
    def _(): loop(True)
    if first:
        accT_o[0]=acc[...]; m_o[0]=m[...]; l_o[0]=l[...]
    else:
        for hp in range(heads//2):
            parts=[]
            for hh in (2*hp,2*hp+1):
                parts.append(acc[hh*HD:(hh+1)*HD,:]/l[hh:hh+1,:])
            o_o[0,:,hp*128:(hp+1)*128]=jnp.concatenate(parts,0).T.astype(BF)
        lse_o[0]=m[...]+jnp.log2(l[...])

def attn_fwd(flags,cq,ck,q,kv,kb,state,tq,tk,heads):
    nr,S,_=q.shape; W=heads*HD; Sk=kv.shape[1]; hp16=-(-heads//8)*8
    first=state is None
    qs=lambda r,i,*_:(r,i,0); ts=lambda r,i,*_:(r,0,i); ks=lambda r,i,*_:(r,0,0)
    stspec=[pl.BlockSpec((1,W,tq),ts),pl.BlockSpec((1,hp16,tq),ts),pl.BlockSpec((1,hp16,tq),ts)]
    ins=[pl.BlockSpec((1,1,tq),ts),pl.BlockSpec((1,Sk,128),ks),pl.BlockSpec((1,tq,W),qs),pl.BlockSpec((1,Sk,W),lambda r,i,*_:(r,0,kb)),pl.BlockSpec((1,Sk,W),lambda r,i,*_:(r,0,kb+1))]
    if first:
        outs=stspec
        osh=[jax.ShapeDtypeStruct((nr,W,S),F32)]+[jax.ShapeDtypeStruct((nr,hp16,S),F32)]*2
    else:
        ins=ins+stspec
        outs=[pl.BlockSpec((1,tq,W),qs),pl.BlockSpec((1,hp16,tq),ts)]
        osh=[jax.ShapeDtypeStruct((nr,S,W),BF),jax.ShapeDtypeStruct((nr,hp16,S),F32)]
    fl=4*nr*S*Sk*W
    return pl.pallas_call(functools.partial(fwd_kernel,first=first,tq=tq,tk=tk,heads=heads),
        out_shape=osh,
        grid_spec=pltpu.PrefetchScalarGridSpec(num_scalar_prefetch=1,grid=(nr,S//tq),in_specs=ins,out_specs=outs,
          scratch_shapes=[pltpu.VMEM((heads,tq,128),BF),pltpu.VMEM((heads*VR,Sk),BF),pltpu.VMEM((tk,tq),F32),pltpu.VMEM((W,tq),F32),pltpu.VMEM((hp16,tq),F32),pltpu.VMEM((hp16,tq),F32),pltpu.VMEM((hp16,128),F32)]),
        compiler_params=pltpu.CompilerParams(dimension_semantics=("arbitrary","arbitrary"),vmem_limit_bytes=VMEM_LIMIT),
        cost_estimate=pl.CostEstimate(flops=fl//SHARE,bytes_accessed=nr*(S*W*2+2*Sk*W*2+S*W*4)//SHARE,transcendentals=0),
        name="attn_fwd_a" if first else "attn_fwd_b",
    )(flags,cq,ck,q,kv,kv,*(state or ()))

def bwd_kernel(flags,cq,ck,q,k,v,do_own,do_mate,o,lse,*rest,spans,tq,tk):
    first=len(spans)==2
    if first:
        dqT_o,*dkv_o,qm,dom,kT,bias,dqT,dk,dv,delta=rest
    else:
        dqT_i,dqkv_o,qm,dom,kT,bias,dqT,dk,dv,delta=rest
    r=pl.program_id(0); qi=pl.program_id(1); nq=pl.num_programs(1)
    nk=k.shape[1]//tk
    low=spans[0][0]; heads=sum(b-a for a,b in spans)
    W=heads*HD; c0=low*HD
    @pl.when(qi==0)
    def _():
        kT[...]=k[0,:,c0:c0+W].T
        dk[...]=jnp.zeros_like(dk); dv[...]=jnp.zeros_like(dv)
    own=r<pl.num_programs(0)//2
    lane=lax.broadcasted_iota(jnp.int32,(tq,128),1)
    for hp in range(heads//2):
        c=slice(c0+hp*128,c0+(hp+1)*128)
        qp=q[0,:,c]*jnp.asarray(0.125,BF); dp_=jnp.where(own,do_own[0,:,c],do_mate[0,:,c])
        qm[2*hp]=jnp.where(lane<64,qp,0).astype(BF)
        qm[2*hp+1]=jnp.where(lane>=64,qp,0).astype(BF)
        dom[2*hp]=jnp.where(lane<64,dp_,0).astype(BF)
        dom[2*hp+1]=jnp.where(lane>=64,dp_,0).astype(BF)
    prod=jnp.where(own,do_own[0,:,c0:c0+W],do_mate[0,:,c0:c0+W]).astype(F32)*o[0,:,c0:c0+W].astype(F32)
    hi=prod.astype(BF); lo=(prod-hi.astype(F32)).astype(BF)
    n16=delta.shape[0]
    row=lax.broadcasted_iota(jnp.int32,(n16,W),0); col_=lax.broadcasted_iota(jnp.int32,(n16,W),1)
    ones=jnp.where(row==col_//HD,1.0,0.0).astype(BF)
    delta[...]=lax.dot_general(ones,hi,NT,preferred_element_type=F32)+lax.dot_general(ones,lo,NT,preferred_element_type=F32)
    if first: dqT[...]=jnp.zeros_like(dqT)
    else: dqT[...]=dqT_i[0,c0:c0+W,:]
    def body(kt):
        ks=pl.ds(pl.multiple_of(kt*tk,tk),tk)
        def col(hh): return slice((hh//2)*128,(hh//2+1)*128)
        def wide(hh): return slice(c0+(hh//2)*128,c0+(hh//2+1)*128)
        def score(hh):
            s=lax.dot_general(k[0,ks,wide(hh)],qm[hh],NT,preferred_element_type=F32)*LOG2E+bias[...]
            return s,lax.dot_general(v[0,ks,wide(hh)],dom[hh],NT,preferred_element_type=F32)
        nxt=score(0); prev=None
        for hh in range(heads+1):
            cur=nxt
            if hh+1<heads: nxt=score(hh+1)
            if prev is not None:
                h1=hh-1; pb,dsb=prev
                hs=slice(h1*HD,(h1+1)*HD)
                dqT[hs,:]+=lax.dot_general(kT[hs,ks],dsb,NN,preferred_element_type=F32)
                dv[ks,col(h1)]+=jnp.dot(pb,dom[h1],preferred_element_type=F32)
                dk[ks,col(h1)]+=jnp.dot(dsb,qm[h1],preferred_element_type=F32)
            if hh<heads:
                s,dp=cur
                at=low+hh
                p=jnp.exp2(s-lse[0,at:at+1,:])
                ds=p*(dp-delta[hh:hh+1,:])
                prev=(p.astype(BF),ds.astype(BF))
    @pl.loop(0,nk)
    def _(kt):
        f=flags[r,qi,kt]
        @pl.when(f>0)
        def _():
            ks=pl.ds(pl.multiple_of(kt*tk,tk),tk)
            bias[...]=jnp.where(ck[0,ks,0:1]==cq[0,0:1,:],0.0,NEG)
            body(kt)
    if first: dqT_o[0]=dqT[...]
    else: dqkv_o[0,pl.ds(pl.multiple_of(qi*tq,tq),tq),0:W]=(dqT[...]*0.125).T.astype(BF)
    @pl.when(qi==nq-1)
    def _():
        if first:
            for (a,b),out in zip(spans,dkv_o):
                n=(b-a)*HD; at=(a-low)*HD
                out[0,:,0:n]=dk[:,at:at+n].astype(BF); out[0,:,n:2*n]=dv[:,at:at+n].astype(BF)
        else:
            dqkv_o[0,:,W:2*W]=dk[...].astype(BF); dqkv_o[0,:,2*W:3*W]=dv[...].astype(BF)

def attn_bwd(flags,cq,ck,q,kv,kb,do,o,lse,dqT,tq,tk,full,spans,name):
    nr,S,_=q.shape; F=full*HD; Sk=kv.shape[1]; n16=lse.shape[1]
    heads=sum(b-a for a,b in spans); W=heads*HD
    first=dqT is None
    qs=lambda r,i,*_:(r,i,0); ts=lambda r,i,*_:(r,0,i); ks=lambda r,i,*_:(r,0,0)
    ins=[pl.BlockSpec((1,1,tq),ts),pl.BlockSpec((1,Sk,128),ks),pl.BlockSpec((1,tq,F),qs),pl.BlockSpec((1,Sk,F),lambda r,i,*_:(r,0,kb)),pl.BlockSpec((1,Sk,F),lambda r,i,*_:(r,0,kb+1)),
         pl.BlockSpec((1,tq,F),lambda r,i,*_:(jnp.minimum(r,nr//2-1),jnp.where(r<nr//2,i,S//tq-1),0)),
         pl.BlockSpec((1,tq,F),lambda r,i,*_:(jnp.maximum(r-nr//2,0),jnp.where(r<nr//2,0,i),0)),
         pl.BlockSpec((1,tq,F),qs),pl.BlockSpec((1,n16,tq),ts)]
    if first:
        widths=[2*(b-a)*HD for a,b in spans]
        outs=[pl.BlockSpec((1,F,tq),ts)]+[pl.BlockSpec((1,Sk,n),ks) for n in widths]
        osh=[jax.ShapeDtypeStruct((nr,F,S),F32)]+[jax.ShapeDtypeStruct((nr,Sk,n),BF) for n in widths]
        extra=()
    else:
        ins=ins+[pl.BlockSpec((1,F,tq),ts)]
        outs=[pl.BlockSpec((1,Sk,3*W),ks)]; osh=[jax.ShapeDtypeStruct((nr,Sk,3*W),BF)]
        extra=(dqT,)
    fl=10*nr*S*Sk*W
    return pl.pallas_call(functools.partial(bwd_kernel,spans=spans,tq=tq,tk=tk),
        out_shape=osh,
        grid_spec=pltpu.PrefetchScalarGridSpec(num_scalar_prefetch=1,grid=(nr,S//tq),in_specs=ins,out_specs=outs,
          scratch_shapes=[pltpu.VMEM((heads,tq,128),BF),pltpu.VMEM((heads,tq,128),BF),pltpu.VMEM((W,Sk),BF),pltpu.VMEM((tk,tq),F32),pltpu.VMEM((W,tq),F32),
             pltpu.VMEM((Sk,W),F32),pltpu.VMEM((Sk,W),F32),pltpu.VMEM((n16,tq),F32)]),
        compiler_params=pltpu.CompilerParams(dimension_semantics=("arbitrary","arbitrary"),vmem_limit_bytes=VMEM_LIMIT),
        cost_estimate=pl.CostEstimate(flops=fl//SHARE,bytes_accessed=nr*(3*S*W*2+4*Sk*W*2+S*W*4)//SHARE,transcendentals=0),
        name=name,
    )(flags,cq,ck,q,kv,kv,*do,o,lse,*extra)


def ffn_kernel(where, acts, w, b, d_act, *rest):
    act_o, d_pre_o, sum_o = rest[-3:]
    rows = acts.shape[0]
    chunk = min(256, rows)
    count = rows // chunk

    def product(i):
        return dot(acts[i * chunk : (i + 1) * chunk, :], w[...], NN) + b[...]

    pre = product(0)
    total = None
    for i in range(count):
        following = product(i + 1) if i + 1 < count else None
        at = slice(i * chunk, (i + 1) * chunk)
        cdf = 0.5 + 0.5 * lax.erf(pre * math.sqrt(0.5))
        pdf = jnp.exp(-0.5 * pre * pre) * (1.0 / math.sqrt(2.0 * math.pi))
        act_o[at, :] = (pre * cdf).astype(BF)
        d_pre = (d_act[at, :].astype(F32) * (cdf + pre * pdf)).astype(BF)
        d_pre_o[at, :] = d_pre
        part = jnp.sum(d_pre.astype(F32), axis=0, keepdims=True)
        total = part if total is None else total + part
        pre = following
    sum_o[...] = total


def ffn_call(where, acts, w, b, d_act, earlier, name):
    rows, width = acts.shape
    ff = w.shape[1]
    tile = 512
    steps = ff // 2 // tile
    mine = bool(earlier)

    def place(i, where):
        return (where[1] if mine else 1 - where[1]) * steps + i

    col = lambda i, where: (0, place(i, where))
    return pl.pallas_call(
        ffn_kernel,
        out_shape=[
            jax.ShapeDtypeStruct((rows, ff), BF),
            jax.ShapeDtypeStruct((rows, ff // 2), BF),
            jax.ShapeDtypeStruct((1, ff), F32),
        ],
        grid_spec=pltpu.PrefetchScalarGridSpec(
            num_scalar_prefetch=1,
            grid=(steps,),
            in_specs=[
                pl.BlockSpec((rows, width), lambda i, where: (0, 0)),
                pl.BlockSpec((width, tile), col),
                pl.BlockSpec((1, tile), col),
                pl.BlockSpec((rows, tile), col),
            ]
            + [pl.BlockSpec(memory_space=pl.ANY)] * len(earlier),
            out_specs=[
                pl.BlockSpec((rows, tile), col),
                pl.BlockSpec((rows, tile), lambda i, where: (0, i)),
                pl.BlockSpec((1, tile), col),
            ],
        ),
        input_output_aliases={5: 0, 6: 2} if mine else {},
        compiler_params=pltpu.CompilerParams(vmem_limit_bytes=VMEM_LIMIT),
        cost_estimate=pl.CostEstimate(
            flops=rows * width * ff // SHARE,
            bytes_accessed=(2 * rows * width + width * ff + 3 * rows * ff) // SHARE,
            transcendentals=0,
        ),
        name=name,
    )(where, acts, w, b, d_act, *earlier)


def store_blocks(where, acc, outs, first, second, halved):
    rows = acc.shape[0] // (first * second)
    for one in range(first):
        for two in range(second):
            block = lax.bitwise_xor(two * first + one, where[0]) * rows
            if halved:
                for part in range(2):
                    at = block + lax.bitwise_xor(where[2], part) * (rows // 2)
                    piece = acc[pl.ds(pl.multiple_of(at, 16), rows // 2), :]
                    outs[part][one, two] = piece.astype(BF)
            else:
                outs[one][two] = acc[pl.ds(pl.multiple_of(block, 16), rows), :].astype(BF)


def grad_kernel(where, *refs, groups, first, second, halved, outs):
    acc = refs[-1]
    ins = refs[: sum(2 * g for g in groups)]
    height = acc.shape[0] // len(groups)
    at = 0
    for index, pairs in enumerate(groups):
        total = None
        for _ in range(pairs):
            part = dot(ins[at][...], ins[at + 1][...], TN)
            total = part if total is None else total + part
            at += 2
        acc[index * height : (index + 1) * height, :] = total
    store_blocks(where, acc, refs[-1 - outs : -1], first, second, halved)


def grad_call(where, groups, width, first, second, tile, halved, name, into=()):
    ins, flat, depth = [], [], 0
    for group in groups:
        for a, b, offset in group:
            ins.append(pl.BlockSpec(a.shape, lambda i, where: (0, 0)))
            if offset is None:
                index = lambda i, where: (0, where[1] * (width // tile) + i)
            else:
                index = lambda i, where, offset=offset: (0, offset // tile + i)
            ins.append(pl.BlockSpec((b.shape[0], tile), index))
            flat += [a, b]
            depth += a.shape[0]
    height = sum(g[0][0].shape[1] for g in groups)
    depth = depth // len(groups)
    rows = height // (first * second)
    if halved:
        shape, block = (first, second, rows // 2, width), (first, second, rows // 2, tile)
        outs = 2
        index = lambda i, where: (0, 0, 0, i)
    else:
        shape, block = (second, rows, width), (second, rows, tile)
        outs = first
        index = lambda i, where: (0, 0, i)
    if into:
        shape = into[0].shape
        row = shape[2] * 2 // rows - 1
        index = lambda i, where: (0, 0, row, i)
    return pl.pallas_call(
        functools.partial(
            grad_kernel, groups=[len(g) for g in groups], first=first, second=second, halved=halved, outs=outs
        ),
        out_shape=[jax.ShapeDtypeStruct(shape, BF)] * outs,
        grid_spec=pltpu.PrefetchScalarGridSpec(
            num_scalar_prefetch=1,
            grid=(width // tile,),
            in_specs=ins + [pl.BlockSpec(memory_space=pl.ANY)] * len(into),
            out_specs=[pl.BlockSpec(block, index)] * outs,
            scratch_shapes=[pltpu.VMEM((height, tile), F32)],
        ),
        input_output_aliases={1 + len(flat) + i: i for i in range(len(into))},
        compiler_params=pltpu.CompilerParams(vmem_limit_bytes=VMEM_LIMIT),
        cost_estimate=pl.CostEstimate(
            flops=2 * depth * height * width // SHARE,
            bytes_accessed=2 * (depth * (height + width) + height * width) // SHARE,
            transcendentals=0,
        ),
        name=name,
    )(where, *flat, *into)


def qkv_kernel(where, near_a, near_b, far_a, far_b, *refs, first, second, halved):
    *outs, sum_o, acc = refs
    acc[...] = dot(near_a[...], near_b[...], TN)
    sum_o[...] = jnp.sum(near_b[...].astype(F32), axis=0, keepdims=True)

    @pl.when(pl.program_id(0) > 0)
    def _():
        acc[...] += dot(far_a[...], far_b[...], TN)
        sum_o[...] += jnp.sum(far_b[...].astype(F32), axis=0, keepdims=True)

    store_blocks(where, acc, outs, first, second, halved)


def qkv_call(where, near, far, first, second, halved, name):
    (near_a, near_b), (far_a, far_b) = near, far
    height = near_a.shape[1]
    width = near_b.shape[1]
    tile = width // 3
    rows = height // (first * second)
    if halved:
        shape, block = (first, second, rows // 2, width), (first, second, rows // 2, tile)
        outs = 2
        index = lambda i, where: (0, 0, 0, i)
    else:
        shape, block = (second, rows, width), (second, rows, tile)
        outs = first
        index = lambda i, where: (0, 0, i)
    once = pl.Buffered(1)
    return pl.pallas_call(
        functools.partial(qkv_kernel, first=first, second=second, halved=halved),
        out_shape=[jax.ShapeDtypeStruct(shape, BF)] * outs + [jax.ShapeDtypeStruct((1, width), F32)],
        grid_spec=pltpu.PrefetchScalarGridSpec(
            num_scalar_prefetch=1,
            grid=(3,),
            in_specs=[
                pl.BlockSpec(near_a.shape, lambda i, where: (0, 0), pipeline_mode=once),
                pl.BlockSpec((near_b.shape[0], tile), lambda i, where: (0, i)),
                pl.BlockSpec(far_a.shape, lambda i, where: (0, 0), pipeline_mode=once),
                pl.BlockSpec((far_b.shape[0], tile), lambda i, where: (0, jnp.maximum(i - 1, 0))),
            ],
            out_specs=[pl.BlockSpec(block, index)] * outs + [pl.BlockSpec((1, tile), lambda i, where: (0, i))],
            scratch_shapes=[pltpu.VMEM((height, tile), F32)],
        ),
        compiler_params=pltpu.CompilerParams(vmem_limit_bytes=VMEM_LIMIT),
        cost_estimate=pl.CostEstimate(
            flops=2 * (near_a.shape[0] + far_a.shape[0]) * height * width // SHARE,
            bytes_accessed=2 * ((near_a.shape[0] + far_a.shape[0]) * (height + width) + height * width) // SHARE,
            transcendentals=0,
        ),
        name=name,
    )(where, near_a, near_b, far_a, far_b)


def back_kernel(where, a1, b1, a2, b2, out1, out2, acc):
    acc[...] = dot(a1[...], b1[...], TN) + dot(a2[...], b2[...], TN)
    rows = acc.shape[0] // 2
    for part, out in enumerate((out1, out2)):
        at = lax.bitwise_xor(where[2], part) * rows
        out[0, 0] = acc[pl.ds(pl.multiple_of(at, 16), rows), :].astype(BF)


def back_call(where, own, mate, first, second, extra, name):
    (a1, b1), (a2, b2) = own, mate
    tokens, ff = a1.shape
    rows = ff // (first * second)
    width = b2.shape[1] // 2

    def block(i, where):
        return (0, lax.bitwise_xor(lax.rem(i, second) * first + i // second, where[0]))

    return pl.pallas_call(
        back_kernel,
        out_shape=[jax.ShapeDtypeStruct((first, second, rows // 2 + extra, width), BF)] * 2,
        grid_spec=pltpu.PrefetchScalarGridSpec(
            num_scalar_prefetch=1,
            grid=(first * second,),
            in_specs=[
                pl.BlockSpec((tokens, rows), block),
                pl.BlockSpec((tokens, width), lambda i, where: (0, where[1])),
                pl.BlockSpec((tokens, rows), block),
                pl.BlockSpec((tokens, width), lambda i, where: (0, where[1])),
            ],
            out_specs=[
                pl.BlockSpec(
                    (1, 1, rows // 2, width), lambda i, where: (i // second, lax.rem(i, second), 0, 0)
                )
            ]
            * 2,
            scratch_shapes=[pltpu.VMEM((rows, width), F32)],
        ),
        compiler_params=pltpu.CompilerParams(vmem_limit_bytes=VMEM_LIMIT),
        cost_estimate=pl.CostEstimate(
            flops=4 * tokens * ff * width // SHARE,
            bytes_accessed=2 * (2 * tokens * (ff + width) + ff * width) // SHARE,
            transcendentals=0,
        ),
        name=name,
    )(where, a1, b1, a2, b2)


def product_kernel(*refs, dims, parts):
    total = dot(refs[0][...], refs[1][...], dims)
    for i in range(1, parts):
        total = total + dot(refs[2 * i][...], refs[2 * i + 1][...], dims)
    for term in refs[2 * parts : -1]:
        total = total + term[...]
    refs[-1][...] = total.astype(refs[-1].dtype)


def product(pairs, dims, name, terms=()):
    tile = 256
    turned = dims == NT
    rows = pairs[0][0].shape[0]
    width = pairs[0][1].shape[0 if turned else 1]
    ins, flat, depth = [], [], 0
    for a, b in pairs:
        ins.append(pl.BlockSpec(a.shape, lambda i: (0, 0), pipeline_mode=pl.Buffered(1)))
        if turned:
            ins.append(pl.BlockSpec((tile, b.shape[1]), lambda i: (i, 0)))
        else:
            ins.append(pl.BlockSpec((b.shape[0], tile), lambda i: (0, i)))
        flat += [a, b]
        depth += a.shape[1]
    return pl.pallas_call(
        functools.partial(product_kernel, dims=dims, parts=len(pairs)),
        out_shape=jax.ShapeDtypeStruct((rows, width), BF),
        grid=(width // tile,),
        in_specs=ins + [pl.BlockSpec((t.shape[0], tile), lambda i: (0, i)) for t in terms],
        out_specs=pl.BlockSpec((rows, tile), lambda i: (0, i)),
        compiler_params=pltpu.CompilerParams(vmem_limit_bytes=VMEM_LIMIT),
        cost_estimate=pl.CostEstimate(
            flops=2 * rows * depth * width // SHARE,
            bytes_accessed=2 * (rows * depth + depth * width + rows * width) // SHARE,
            transcendentals=0,
        ),
        name=name,
    )(*flat, *terms)


def tile_flags(queries, keys, tq, tk):
    q_first, q_last = queries[:, ::tq], queries[:, tq - 1 :: tq]
    k_first, k_last = keys[:, ::tk], keys[:, tk - 1 :: tk]
    meet = (q_first[:, :, None] <= k_last[:, None, :]) & (k_first[:, None, :] <= q_last[:, :, None])
    whole = (
        (q_first == q_last)[:, :, None]
        & (k_first == k_last)[:, None, :]
        & (q_first[:, :, None] == k_first[:, None, :])
    )
    return jnp.where(whole, 2, jnp.where(meet, 1, 0)).astype(jnp.int32)


def layer_norm_parts(values):
    centred = values - jnp.mean(values, axis=-1, keepdims=True)
    rstd = lax.rsqrt(jnp.mean(centred * centred, axis=-1, keepdims=True) + EPS)
    return centred * rstd, rstd


def layer_norm_back(d_norm, gain, xhat, rstd):
    e = d_norm * gain
    return rstd * (
        e - jnp.mean(e, axis=-1, keepdims=True) - xhat * jnp.mean(e * xhat, axis=-1, keepdims=True)
    )


def on_device(
    tokens,
    cell_start,
    norm1_gain,
    norm1_bias,
    w_qkv,
    bias_q,
    bias_v,
    w_out,
    bias_out,
    norm2_gain,
    norm2_bias,
    w_in,
    bias_in,
    w_back,
    bias_back,
    cotangent,
):
    rows, seg, width = tokens.shape
    count = rows * seg
    ff = w_in.shape[1]
    half = width // 2
    wide = lax.axis_size("wide")
    group = lax.axis_size("blk")
    place = lax.axis_index("wide")
    member = lax.axis_index("blk")
    core = place % 2
    chips = wide // 2
    first = 2 if chips <= 8 else 4
    second = chips // first
    heads = HEADS // 2
    early = 6
    spans = ((0, early), (early, heads))
    tq, tk = min(512, seg), min(256, seg)
    halves = group == 2 and ff // chips % 128 == 0
    where = jnp.stack([place // 2, core, member]).astype(jnp.int32)
    where_out = jnp.stack([lax.bitwise_xor(place // 2, core * (chips // 2)), core, member]).astype(jnp.int32)

    def after(value, *earlier):
        return lax.optimization_barrier((value, earlier))[0]

    def across(array, by):
        return lax.ppermute(array, "wide", [(i, i ^ by) for i in range(wide)])

    def to_mate(array):
        return across(array, 1)

    def from_ahead(array, by):
        return lax.ppermute(array, "blk", [((i + by) % group, i) for i in range(group)])

    def to_ahead(array, by):
        return lax.ppermute(array, "blk", [(i, (i + by) % group) for i in range(group)])

    def from_all_ahead(array):
        parts = [from_ahead(array, by) for by in range(1, group)]
        return parts[0] if len(parts) == 1 else jnp.concatenate(parts, axis=1)

    def cut(array, start, size, axis):
        return lax.dynamic_slice_in_dim(array, start, size, axis)

    def paired(array):
        return jnp.concatenate([array, to_mate(array)], axis=0)

    inputs = tokens.astype(F32).reshape(count, width)
    xhat1, rstd1 = layer_norm_parts(inputs)
    acts = (xhat1 * norm1_gain + norm1_bias).astype(BF).reshape(tokens.shape)
    cells = paired(cell_start)
    far_cells = from_all_ahead(cells)
    acts = after(acts, far_cells)
    far_own = from_all_ahead(acts)
    acts_pair = paired(acts).reshape(2 * count, width)
    w_own = jnp.concatenate([cut(w_qkv, part * width + core * half, half, 1) for part in range(3)], axis=1)
    b_own = jnp.concatenate([cut(bias_q, core * half, half, 0), jnp.zeros((half,), F32), cut(bias_v, core * half, half, 0)])

    def own_columns(span):
        return [w_own[:, part * half + span[0] * HD : part * half + span[1] * HD] for part in range(3)]

    w_early, w_late = (jnp.concatenate(own_columns(span), axis=1) for span in spans)

    def columns(array):
        return jnp.broadcast_to(array[:, :, None], array.shape + (128,))

    qkv = (dot(acts_pair, w_own, NN) + b_own).astype(BF).reshape(2 * rows, seg, 3 * half)
    near_flags = tile_flags(cells, cells, tq, tk)
    far_flags = tile_flags(cells, far_cells, tq, tk)
    cell_rows = cells[:, None, :]
    near_columns, far_columns = columns(cells), columns(far_cells)
    state = attn_fwd(near_flags, cell_rows, near_columns, qkv, qkv, 1, None, tq, tk, heads)
    d_out = cotangent.reshape(count, width)
    d_out_mate = to_mate(after(d_out, acts_pair))
    far_own = after(far_own, state)
    far_mate = to_mate(far_own)
    d_act = dot(after(d_out, far_own, state), w_back, NT).astype(BF)

    far_mate = after(far_mate, d_act)
    far_pair = jnp.concatenate([far_own, far_mate], axis=0)
    far_len = far_pair.shape[1]
    far_pair = far_pair.reshape(-1, width)
    far_kv = (dot(far_pair, w_own[:, half:], NN) + b_own[half:]).astype(BF).reshape(2 * rows, far_len, 2 * half)
    attended, stats = attn_fwd(far_flags, cell_rows, far_columns, qkv, far_kv, 0, state, tq, tk, heads)
    mine, theirs = attended[:rows].reshape(count, half), attended[rows:].reshape(count, half)
    own_rest = to_mate(theirs)
    mate_rest = to_mate(mine)
    w_out_own = cut(w_out, core * half, half, 0)
    w_out_mate = cut(w_out, (1 - core) * half, half, 0)
    middle = inputs + (dot(mine, w_out_own, NN) + dot(own_rest, w_out_mate, NN)) + bias_out

    xhat2, rstd2 = layer_norm_parts(middle)
    acts2 = (xhat2 * norm2_gain + norm2_bias).astype(BF)
    acts2_mate = to_mate(acts2)
    b_in = bias_in.reshape(1, ff)
    act_part, d_pre_theirs, sum_part = ffn_call(where, acts2, w_in, b_in, d_act, (), "ffn_theirs")
    d_pre_mate = to_mate(d_pre_theirs)
    act, d_pre_mine, d_pre_sum = ffn_call(where, acts2, w_in, b_in, d_act, (act_part, sum_part), "ffn_mine")
    act_mate = to_mate(act)
    w_in_mine = cut(w_in, core * (ff // 2), ff // 2, 1)
    w_in_theirs = cut(w_in, (1 - core) * (ff // 2), ff // 2, 1)
    d_norm2 = dot(d_pre_theirs, w_in_theirs, NT) + dot(d_pre_mine, w_in_mine, NT)
    grad_out = d_out.astype(F32)
    d_middle = grad_out + layer_norm_back(d_norm2, norm2_gain, xhat2, rstd2)
    d_z = d_middle.astype(BF)
    d_att_theirs = dot(d_z, w_out_mate, NT).astype(BF)
    d_att_mine = dot(d_z, w_out_own, NT).astype(BF)
    d_att_mate = to_mate(d_att_theirs)
    d_z_mate = to_mate(d_z)

    def send(parts):
        return [across(parts[one], 2 * one) for one in range(1, first)]

    def add_first(parts, received):
        sums = []
        for two in range(second):
            total = parts[0][two].astype(F32)
            for part in received:
                total = total + part[two].astype(F32)
            sums.append(total.astype(BF))
        return sums

    def send_second(sums):
        return [across(sums[two], 2 * first * two) for two in range(1, second)]

    def add_second(sums, received):
        total = sums[0].astype(F32)
        for part in received:
            total = total + part.astype(F32)
        return total.astype(BF)

    def start(parts):
        return from_ahead(parts[1], 1) if halves else send(parts)

    def middle_step(parts, received):
        if not halves:
            return parts, received
        sums = [(parts[0][one].astype(F32) + received[one].astype(F32)).astype(BF) for one in range(first)]
        return sums, send(sums)

    def ahead(total):
        return from_ahead(total, 1) if group == 2 else None

    def over_row(total, other):
        if group == 2:
            return (total.astype(F32) + other.astype(F32)).astype(BF)
        return lax.psum(total, "blk")

    def by_core(total, other, sizes):
        if halves:
            kept = jnp.where(member == core, total, other)
            return kept, jnp.where(member == core, other, total)
        total = over_row(total, other)
        parts, at = [], 0
        for size in sizes:
            parts.append(total[at : at + size].reshape(2, size // 2, total.shape[1]))
            at += size
        split = jnp.concatenate(parts, axis=1)
        return (lax.dynamic_index_in_dim(split, i, 0, keepdims=False) for i in (core, 1 - core))

    def swap(split):
        kept, given = split
        other = to_mate(given)
        return jnp.where(core == 0, kept, other).astype(F32), jnp.where(core == 0, other, kept).astype(F32)

    d_pre_held, d_pre_mate = after((d_pre_mine, d_pre_mate), d_att_theirs, d_att_mine)
    grad_in = grad_call(
        where, [[(acts2, d_pre_held, 0), (acts2_mate, d_pre_mate, 0)]], ff // 2, first, second, 512, False, "grad_in"
    )
    in_in = send(grad_in)
    act_held, act_mate, mate_rest, d_z_mate = after((act, act_mate, mate_rest, d_z_mate), grad_in)

    def grad_o(into):
        return grad_call(
            where_out,
            [
                [(mine, d_z, None), (theirs, d_z_mate, None)],
                [(own_rest, d_z, None), (mate_rest, d_z_mate, None)],
            ],
            half, first, second, half, halves, "grad_out", into,
        )

    back_rows, out_rows = ff // chips, width // chips
    if halves:
        grad_b = back_call(
            where, (act_held, d_out), (act_mate, d_out_mate), first, second, out_rows // 2, "grad_back"
        )
        grad_b = grad_o(tuple(grad_b))
    else:
        whole = dot(act_held, cut(d_out, core * half, half, 1), TN) + dot(act_mate, cut(d_out_mate, core * half, half, 1), TN)
        whole = whole.astype(BF).reshape(chips, back_rows, half)
        grad_b = [
            jnp.concatenate([
                jnp.stack([whole[lax.bitwise_xor(two * first + one, where[0])] for two in range(second)]), other
            ], axis=1)
            for one, other in enumerate(grad_o(()))
        ]
    b_in = start(grad_b)

    back_tq = min(256, seg)
    near_flags, far_flags = tile_flags(cells, cells, back_tq, tk), tile_flags(cells, far_cells, back_tq, tk)
    d_att = after((d_att_mine.reshape(rows, seg, half), d_att_mate.reshape(rows, seg, half)), grad_b)
    d_qT, far_early, far_late = attn_bwd(
        far_flags, cell_rows, far_columns, qkv, far_kv, 0, d_att, attended, stats, None, back_tq, tk, heads, spans, "attn_bwd_far"
    )
    in_sums = add_first(grad_in, after(in_in, d_qT))
    in_more = send_second(in_sums)
    far_early, far_late = after((far_early, far_late), in_sums)
    far_early, far_late = (f.reshape(-1, f.shape[-1]) for f in (far_early, far_late))
    n_early, n_late = early * HD, (heads - early) * HD
    far_part = product([(far_early, w_early[:, n_early:]), (far_late, w_late[:, n_late:])], NT, "far_norm")
    far_part = far_part.reshape(2 * rows, far_len, width)
    far_given = to_mate(far_part[rows:])
    far_sum = (far_part[:rows].astype(F32) + after(far_given, in_sums, far_part).astype(F32)).astype(BF)
    far_back = [to_ahead(far_sum[:, by * seg : (by + 1) * seg], by + 1) for by in range(group - 1)]
    d_qT = after(d_qT, far_sum)

    def near_back(span, name, *earlier):
        (out,) = attn_bwd(
            near_flags, cell_rows, near_columns, qkv, qkv, 1, d_att, attended, stats, after(d_qT, earlier), back_tq, tk, heads,
            (span,), name,
        )
        return out.reshape(2 * count, -1)

    near_early = near_back(spans[0], "attn_bwd_early")
    b_sums, b_in = middle_step(grad_b, after(b_in, near_early))
    in_total = add_second(in_sums, after(in_more, b_sums))
    in_row = ahead(in_total)
    near_early = after(near_early, b_sums, in_total)
    *grad_e, sum_e = qkv_call(where, (acts_pair, near_early), (far_pair, far_early), first, second, halves, "grad_early")
    grad_e, in_row, far_back = after((grad_e, in_row, far_back), grad_e)
    e_in = start(grad_e)
    near_late = near_back(spans[1], "attn_bwd_late", grad_e, far_back)
    b_two = add_first(b_sums, after(b_in, near_late))
    b_more = send_second(b_two)
    near_late = after(near_late, b_two)
    *grad_l, sum_l = qkv_call(where, (acts_pair, near_late), (far_pair, far_late), first, second, halves, "grad_late")
    l_in = start(grad_l)
    e_sums, e_in = middle_step(grad_e, after(e_in, grad_l))
    act_late = after(act_held, e_sums)
    mixed = product([(act_late, w_back)], NN, "mixed", (middle, bias_back.reshape(1, width))).reshape(tokens.shape)
    l_sums, l_in = middle_step(grad_l, after(l_in, mixed))
    b_total = add_second(b_two, after(b_more, l_sums))
    b_row = ahead(b_total)
    e_two = add_first(e_sums, after(e_in, b_total))
    e_more = send_second(e_two)
    near_part = product(
        [(after(near_early, l_sums, e_two), w_early), (near_late, w_late)], NT, "near_norm"
    )
    near_given = to_mate(near_part[count:])
    l_two = add_first(l_sums, after(l_in, near_part))
    e_total = add_second(e_two, after(e_more, l_two))
    l_more = send_second(l_two)
    e_row = ahead(e_total)
    (d_norm1,) = after((near_part[:count].astype(F32),), l_two, e_total)
    d_norm1 = d_norm1 + near_given.astype(F32)
    for part in far_back:
        d_norm1 = d_norm1 + part.reshape(count, width).astype(F32)
    grad_tokens = (d_middle + layer_norm_back(d_norm1, norm1_gain, xhat1, rstd1)).reshape(tokens.shape)

    def vectors(parts, *covers):
        packed = jnp.concatenate([p.reshape(wide, -1) for p in parts], axis=1)
        total = packed
        covers = iter(covers)
        for stride, size in ((2 * first, second), (2, first), (1, 2)):
            total = total.reshape(-1, size, stride, packed.shape[1])
            spot = (place // stride) % size
            kept = lax.dynamic_index_in_dim(total, spot, 1, keepdims=False)
            given = [
                across(lax.dynamic_index_in_dim(total, spot ^ by, 1, keepdims=False), by * stride)
                for by in range(1, size)
            ]
            given = after(given, next(covers))
            for part in given:
                kept = kept + part
            total = kept.reshape(stride, packed.shape[1])
        total = total.reshape(-1)
        total = total + after(from_ahead(total, 1), next(covers)) if group == 2 else lax.psum(total, "blk")
        out, at = [], 0
        for p in parts:
            size = p.size // wide
            out.append(total[at : at + size])
            at += size
        return out

    def widened(part):
        n = sum_e.shape[1] // 3, sum_l.shape[1] // 3
        own = jnp.concatenate([s[0, part * m : (part + 1) * m] for s, m in zip((sum_e, sum_l), n)])
        return lax.dynamic_update_slice_in_dim(jnp.zeros((width,), F32), own, core * half, 0)

    in_low, in_high = swap(by_core(after(in_total, d_norm1), in_row, [width // chips])) if not halves else (None, None)
    if halves:
        in_whole = over_row(after(in_total, d_norm1), in_row).reshape(2, -1, in_total.shape[1])
        in_low, in_high = swap([lax.dynamic_index_in_dim(in_whole, i, 0, keepdims=False) for i in (core, 1 - core)])
    b_low, b_high = swap(by_core(after(b_total, d_norm1), b_row, [back_rows, out_rows]))
    e_low, e_high = swap(by_core(e_total, e_row, [out_rows]))
    l_total = add_second(l_two, l_more)
    l_low, l_high = swap(by_core(l_total, ahead(l_total), [out_rows]))

    def part_columns(part):
        return [
            array[:, part * n : (part + 1) * n]
            for array, n in ((e_low, n_early), (l_low, n_late), (e_high, n_early), (l_high, n_late))
        ]

    share = ff // wide
    grad_w_in = jnp.concatenate([in_low, in_high], axis=1)
    grad_w_back = jnp.concatenate([b_low[:share], b_high[:share]], axis=1)
    grad_w_out = jnp.concatenate([b_low[share:], b_high[share:]], axis=1)
    small = vectors(
        [
            jnp.sum(d_norm1 * xhat1, axis=0),
            jnp.sum(d_norm1, axis=0),
            widened(0),
            widened(2),
            jnp.sum(d_z.astype(F32), axis=0),
            jnp.sum(d_norm2 * xhat2, axis=0),
            jnp.sum(d_norm2, axis=0),
            d_pre_sum,
            jnp.sum(grad_out, axis=0),
        ],
        grad_tokens,
        grad_w_in,
        grad_w_back,
        grad_w_out,
    )
    return (
        mixed,
        grad_tokens,
        small[0],
        small[1],
        jnp.concatenate([piece for part in range(3) for piece in part_columns(part)], axis=1),
        small[2],
        small[3],
        grad_w_out,
        small[4],
        small[5],
        small[6],
        grad_w_in,
        small[7],
        grad_w_back,
        small[8],
    )


def solution(mesh):
    spread = P("wide", "blk", None)
    placed = (spread, P("wide", "blk")) + (P(),) * 13 + (spread,)
    matrix, vector = P("wide", None), P("wide")
    return jax.shard_map(
        on_device,
        mesh=mesh,
        in_specs=placed,
        out_specs=(
            spread, spread, vector, vector, matrix, vector, vector, matrix, vector, vector, vector,
            matrix, vector, matrix, vector,
        ),
        check_vma=False,
    )
```

```python
import functools
import math

import jax
import jax.numpy as jnp
from jax import lax
from jax.experimental import pallas as pl
from jax.experimental.pallas import tpu as pltpu
from jax.sharding import PartitionSpec as P

HEADS = 20
HEAD_DIM = 64
HD = HEAD_DIM
EPS = 1e-05
NEG = -1e30
LOG2E = math.log2(math.e)
C2 = LOG2E / math.sqrt(HEAD_DIM)
F32 = jnp.float32
BF = jnp.bfloat16
NN = (((1,), (0,)), ((), ()))
NT = (((1,), (1,)), ((), ()))
TN = (((0,), (0,)), ((), ()))
VMEM_LIMIT = 56 * 2**20
SHARE = 1000
VR = HD + 16


def dot(a, b, dims):
    return lax.dot_general(a, b, dims, preferred_element_type=F32)


def head_sumsq(x,hp16):
    W=x.shape[1]
    sq=x.astype(F32)*x.astype(F32)
    row=lax.broadcasted_iota(jnp.int32,(hp16,W),0); col=lax.broadcasted_iota(jnp.int32,(hp16,W),1)
    ones=jnp.where(row==col//HD,1.0,0.0).astype(BF)
    return lax.dot_general(ones,sq.astype(BF),NT,preferred_element_type=F32)

def fwd_kernel(flags,cq,ck,q,k,v,*rest,first,tq,tk,heads):
    if first:
        accT_o,m_o,l_o,qm,vT,bias,acc,m,l,kn=rest
    else:
        accT_i,m_i,l_i,o_o,lse_o,qm,vT,bias,acc,m,l,kn=rest
    r=pl.program_id(0); qi=pl.program_id(1)
    nk=k.shape[1]//tk
    hp16=m.shape[0]
    @pl.when(qi==0)
    def _():
        for hh in range(heads):
            vT[hh*VR:hh*VR+HD,:]=v[0,:,hh*HD:(hh+1)*HD].T
            vT[hh*VR+HD:(hh+1)*VR,:]=jnp.ones((VR-HD,vT.shape[1]),BF)
        kn[...]=jnp.broadcast_to(jnp.sqrt(jnp.max(head_sumsq(k[0],hp16),1,keepdims=True)),kn.shape)
    lane=lax.broadcasted_iota(jnp.int32,(tq,128),1)
    for hp in range(heads//2):
        qp=q[0,:,hp*128:(hp+1)*128]
        qm[2*hp]=jnp.where(lane<64,qp,0).astype(BF)
        qm[2*hp+1]=jnp.where(lane>=64,qp,0).astype(BF)
    bound=jnp.sqrt(head_sumsq(q[0],hp16))*kn[:,0:1]*(C2*1.02)
    safe=jnp.max(bound)<50.0
    if first:
        m0=bound
    else:
        m0=jnp.maximum(bound,m_i[0])
    def loop(online):
        if first:
            acc[...]=jnp.zeros_like(acc); l[...]=jnp.zeros_like(l)
            m[...]=jnp.full_like(m,NEG) if online else m0
        elif online:
            acc[...]=accT_i[0]; m[...]=m_i[0]; l[...]=l_i[0]
        else:
            al=jnp.exp2(m_i[0]-m0)
            m[...]=m0; l[...]=al*l_i[0]
            for hh in range(heads):
                hs=slice(hh*HD,(hh+1)*HD)
                acc[hs,:]=al[hh:hh+1,:]*accT_i[0,hs,:]
        def body(kt,masked):
            ks=pl.ds(pl.multiple_of(kt*tk,tk),tk)
            if online:
                @pl.loop(0,heads//2)
                def _(hp):
                    kp=k[0,ks,pl.ds(pl.multiple_of(hp*128,128),128)]
                    for j in range(2):
                        hh=2*hp+j
                        s=lax.dot_general(kp,qm[hh],NT,preferred_element_type=F32)*C2+bias[...]
                        mp=m[pl.ds(hh,1),:]
                        mn=jnp.maximum(mp,jnp.max(s,0,keepdims=True))
                        p=jnp.exp2(s-mn)
                        al=jnp.exp2(mp-mn)
                        m[pl.ds(hh,1),:]=mn
                        l[pl.ds(hh,1),:]=al*l[pl.ds(hh,1),:]+jnp.sum(p,0,keepdims=True)
                        hs=pl.ds(pl.multiple_of(hh*HD,HD),HD)
                        vs=pl.ds(pl.multiple_of(hh*VR,16),HD)
                        acc[hs,:]=al*acc[hs,:]+lax.dot_general(vT[vs,ks],p.astype(BF),NN,preferred_element_type=F32)
                return
            def score(hh):
                s=lax.dot_general(k[0,ks,(hh//2)*128:(hh//2+1)*128],qm[hh],NT,preferred_element_type=F32)*C2
                if masked: s=s+bias[...]
                return s
            s=score(0); pp=None
            for hh in range(heads+1):
                if hh+1<heads: sn=score(hh+1)
                if pp is not None:
                    h1=hh-1
                    both=lax.dot_general(vT[h1*VR:(h1+1)*VR,ks],pp,NN,preferred_element_type=F32)
                    acc[h1*HD:(h1+1)*HD,:]+=both[:HD]
                    l[h1:h1+1,:]+=both[HD:HD+1]
                if hh<heads:
                    p=jnp.exp2(s-m[hh:hh+1,:])
                    pp=p.astype(BF)
                s=sn
        @pl.loop(0,nk)
        def _(kt):
            f=flags[r,qi,kt]
            def mask():
                ks=pl.ds(pl.multiple_of(kt*tk,tk),tk)
                bias[...]=jnp.where(ck[0,ks,0:1]==cq[0,0:1,:],0.0,NEG)
            if online:
                @pl.when(f>0)
                def _():
                    mask(); body(kt,True)
            else:
                @pl.when(f==1)
                def _():
                    mask(); body(kt,True)
                @pl.when(f==2)
                def _(): body(kt,False)
    @pl.when(safe)
    def _(): loop(False)
    @pl.when(jnp.logical_not(safe))
    def _(): loop(True)
    if first:
        accT_o[0]=acc[...]; m_o[0]=m[...]; l_o[0]=l[...]
    else:
        for hp in range(heads//2):
            parts=[]
            for hh in (2*hp,2*hp+1):
                parts.append(acc[hh*HD:(hh+1)*HD,:]/l[hh:hh+1,:])
            o_o[0,:,hp*128:(hp+1)*128]=jnp.concatenate(parts,0).T.astype(BF)
        lse_o[0]=m[...]+jnp.log2(l[...])

def attn_fwd(flags,cq,ck,q,kv,kb,state,tq,tk,heads):
    nr,S,_=q.shape; W=heads*HD; Sk=kv.shape[1]; hp16=-(-heads//8)*8
    first=state is None
    qs=lambda r,i,*_:(r,i,0); ts=lambda r,i,*_:(r,0,i); ks=lambda r,i,*_:(r,0,0)
    stspec=[pl.BlockSpec((1,W,tq),ts),pl.BlockSpec((1,hp16,tq),ts),pl.BlockSpec((1,hp16,tq),ts)]
    ins=[pl.BlockSpec((1,1,tq),ts),pl.BlockSpec((1,Sk,128),ks),pl.BlockSpec((1,tq,W),qs),pl.BlockSpec((1,Sk,W),lambda r,i,*_:(r,0,kb)),pl.BlockSpec((1,Sk,W),lambda r,i,*_:(r,0,kb+1))]
    if first:
        outs=stspec
        osh=[jax.ShapeDtypeStruct((nr,W,S),F32)]+[jax.ShapeDtypeStruct((nr,hp16,S),F32)]*2
    else:
        ins=ins+stspec
        outs=[pl.BlockSpec((1,tq,W),qs),pl.BlockSpec((1,hp16,tq),ts)]
        osh=[jax.ShapeDtypeStruct((nr,S,W),BF),jax.ShapeDtypeStruct((nr,hp16,S),F32)]
    fl=4*nr*S*Sk*W
    return pl.pallas_call(functools.partial(fwd_kernel,first=first,tq=tq,tk=tk,heads=heads),
        out_shape=osh,
        grid_spec=pltpu.PrefetchScalarGridSpec(num_scalar_prefetch=1,grid=(nr,S//tq),in_specs=ins,out_specs=outs,
          scratch_shapes=[pltpu.VMEM((heads,tq,128),BF),pltpu.VMEM((heads*VR,Sk),BF),pltpu.VMEM((tk,tq),F32),pltpu.VMEM((W,tq),F32),pltpu.VMEM((hp16,tq),F32),pltpu.VMEM((hp16,tq),F32),pltpu.VMEM((hp16,128),F32)]),
        compiler_params=pltpu.CompilerParams(dimension_semantics=("arbitrary","arbitrary"),vmem_limit_bytes=VMEM_LIMIT),
        cost_estimate=pl.CostEstimate(flops=fl//SHARE,bytes_accessed=nr*(S*W*2+2*Sk*W*2+S*W*4)//SHARE,transcendentals=0),
        name="attn_fwd_a" if first else "attn_fwd_b",
    )(flags,cq,ck,q,kv,kv,*(state or ()))

def bwd_kernel(flags,cq,ck,q,k,v,do_own,do_mate,o,lse,*rest,spans,tq,tk):
    first=len(spans)==2
    if first:
        dqT_o,*dkv_o,qm,dom,kT,bias,dqT,dk,dv,delta=rest
    else:
        dqT_i,dqkv_o,qm,dom,kT,bias,dqT,dk,dv,delta=rest
    r=pl.program_id(0); qi=pl.program_id(1); nq=pl.num_programs(1)
    nk=k.shape[1]//tk
    low=spans[0][0]; heads=sum(b-a for a,b in spans)
    W=heads*HD; c0=low*HD
    @pl.when(qi==0)
    def _():
        kT[...]=k[0,:,c0:c0+W].T
        dk[...]=jnp.zeros_like(dk); dv[...]=jnp.zeros_like(dv)
    own=r<pl.num_programs(0)//2
    lane=lax.broadcasted_iota(jnp.int32,(tq,128),1)
    for hp in range(heads//2):
        c=slice(c0+hp*128,c0+(hp+1)*128)
        qp=q[0,:,c]*jnp.asarray(0.125,BF); dp_=jnp.where(own,do_own[0,:,c],do_mate[0,:,c])
        qm[2*hp]=jnp.where(lane<64,qp,0).astype(BF)
        qm[2*hp+1]=jnp.where(lane>=64,qp,0).astype(BF)
        dom[2*hp]=jnp.where(lane<64,dp_,0).astype(BF)
        dom[2*hp+1]=jnp.where(lane>=64,dp_,0).astype(BF)
    prod=jnp.where(own,do_own[0,:,c0:c0+W],do_mate[0,:,c0:c0+W]).astype(F32)*o[0,:,c0:c0+W].astype(F32)
    hi=prod.astype(BF); lo=(prod-hi.astype(F32)).astype(BF)
    n16=delta.shape[0]
    row=lax.broadcasted_iota(jnp.int32,(n16,W),0); col_=lax.broadcasted_iota(jnp.int32,(n16,W),1)
    ones=jnp.where(row==col_//HD,1.0,0.0).astype(BF)
    delta[...]=lax.dot_general(ones,hi,NT,preferred_element_type=F32)+lax.dot_general(ones,lo,NT,preferred_element_type=F32)
    if first: dqT[...]=jnp.zeros_like(dqT)
    else: dqT[...]=dqT_i[0,c0:c0+W,:]
    def body(kt):
        ks=pl.ds(pl.multiple_of(kt*tk,tk),tk)
        def col(hh): return slice((hh//2)*128,(hh//2+1)*128)
        def wide(hh): return slice(c0+(hh//2)*128,c0+(hh//2+1)*128)
        def score(hh):
            s=lax.dot_general(k[0,ks,wide(hh)],qm[hh],NT,preferred_element_type=F32)*LOG2E+bias[...]
            return s,lax.dot_general(v[0,ks,wide(hh)],dom[hh],NT,preferred_element_type=F32)
        nxt=score(0); prev=None
        for hh in range(heads+1):
            cur=nxt
            if hh+1<heads: nxt=score(hh+1)
            if prev is not None:
                h1=hh-1; pb,dsb=prev
                hs=slice(h1*HD,(h1+1)*HD)
                dqT[hs,:]+=lax.dot_general(kT[hs,ks],dsb,NN,preferred_element_type=F32)
                dv[ks,col(h1)]+=jnp.dot(pb,dom[h1],preferred_element_type=F32)
                dk[ks,col(h1)]+=jnp.dot(dsb,qm[h1],preferred_element_type=F32)
            if hh<heads:
                s,dp=cur
                at=low+hh
                p=jnp.exp2(s-lse[0,at:at+1,:])
                ds=p*(dp-delta[hh:hh+1,:])
                prev=(p.astype(BF),ds.astype(BF))
    @pl.loop(0,nk)
    def _(kt):
        f=flags[r,qi,kt]
        @pl.when(f>0)
        def _():
            ks=pl.ds(pl.multiple_of(kt*tk,tk),tk)
            bias[...]=jnp.where(ck[0,ks,0:1]==cq[0,0:1,:],0.0,NEG)
            body(kt)
    if first: dqT_o[0]=dqT[...]
    else: dqkv_o[0,pl.ds(pl.multiple_of(qi*tq,tq),tq),0:W]=(dqT[...]*0.125).T.astype(BF)
    @pl.when(qi==nq-1)
    def _():
        if first:
            for (a,b),out in zip(spans,dkv_o):
                n=(b-a)*HD; at=(a-low)*HD
                out[0,:,0:n]=dk[:,at:at+n].astype(BF); out[0,:,n:2*n]=dv[:,at:at+n].astype(BF)
        else:
            dqkv_o[0,:,W:2*W]=dk[...].astype(BF); dqkv_o[0,:,2*W:3*W]=dv[...].astype(BF)

def attn_bwd(flags,cq,ck,q,kv,kb,do,o,lse,dqT,tq,tk,full,spans,name):
    nr,S,_=q.shape; F=full*HD; Sk=kv.shape[1]; n16=lse.shape[1]
    heads=sum(b-a for a,b in spans); W=heads*HD
    first=dqT is None
    qs=lambda r,i,*_:(r,i,0); ts=lambda r,i,*_:(r,0,i); ks=lambda r,i,*_:(r,0,0)
    ins=[pl.BlockSpec((1,1,tq),ts),pl.BlockSpec((1,Sk,128),ks),pl.BlockSpec((1,tq,F),qs),pl.BlockSpec((1,Sk,F),lambda r,i,*_:(r,0,kb)),pl.BlockSpec((1,Sk,F),lambda r,i,*_:(r,0,kb+1)),
         pl.BlockSpec((1,tq,F),lambda r,i,*_:(jnp.minimum(r,nr//2-1),jnp.where(r<nr//2,i,S//tq-1),0)),
         pl.BlockSpec((1,tq,F),lambda r,i,*_:(jnp.maximum(r-nr//2,0),jnp.where(r<nr//2,0,i),0)),
         pl.BlockSpec((1,tq,F),qs),pl.BlockSpec((1,n16,tq),ts)]
    if first:
        widths=[2*(b-a)*HD for a,b in spans]
        outs=[pl.BlockSpec((1,F,tq),ts)]+[pl.BlockSpec((1,Sk,n),ks) for n in widths]
        osh=[jax.ShapeDtypeStruct((nr,F,S),F32)]+[jax.ShapeDtypeStruct((nr,Sk,n),BF) for n in widths]
        extra=()
    else:
        ins=ins+[pl.BlockSpec((1,F,tq),ts)]
        outs=[pl.BlockSpec((1,Sk,3*W),ks)]; osh=[jax.ShapeDtypeStruct((nr,Sk,3*W),BF)]
        extra=(dqT,)
    fl=10*nr*S*Sk*W
    return pl.pallas_call(functools.partial(bwd_kernel,spans=spans,tq=tq,tk=tk),
        out_shape=osh,
        grid_spec=pltpu.PrefetchScalarGridSpec(num_scalar_prefetch=1,grid=(nr,S//tq),in_specs=ins,out_specs=outs,
          scratch_shapes=[pltpu.VMEM((heads,tq,128),BF),pltpu.VMEM((heads,tq,128),BF),pltpu.VMEM((W,Sk),BF),pltpu.VMEM((tk,tq),F32),pltpu.VMEM((W,tq),F32),
             pltpu.VMEM((Sk,W),F32),pltpu.VMEM((Sk,W),F32),pltpu.VMEM((n16,tq),F32)]),
        compiler_params=pltpu.CompilerParams(dimension_semantics=("arbitrary","arbitrary"),vmem_limit_bytes=VMEM_LIMIT),
        cost_estimate=pl.CostEstimate(flops=fl//SHARE,bytes_accessed=nr*(3*S*W*2+4*Sk*W*2+S*W*4)//SHARE,transcendentals=0),
        name=name,
    )(flags,cq,ck,q,kv,kv,*do,o,lse,*extra)


def ffn_kernel(where, acts, w, b, d_act, *rest):
    act_o, d_pre_o, sum_o = rest[-3:]
    rows = acts.shape[0]
    chunk = min(256, rows)
    count = rows // chunk

    def product(i):
        return dot(acts[i * chunk : (i + 1) * chunk, :], w[...], NN) + b[...]

    pre = product(0)
    total = None
    for i in range(count):
        following = product(i + 1) if i + 1 < count else None
        at = slice(i * chunk, (i + 1) * chunk)
        cdf = 0.5 + 0.5 * lax.erf(pre * math.sqrt(0.5))
        pdf = jnp.exp(-0.5 * pre * pre) * (1.0 / math.sqrt(2.0 * math.pi))
        act_o[at, :] = (pre * cdf).astype(BF)
        d_pre = (d_act[at, :].astype(F32) * (cdf + pre * pdf)).astype(BF)
        d_pre_o[at, :] = d_pre
        part = jnp.sum(d_pre.astype(F32), axis=0, keepdims=True)
        total = part if total is None else total + part
        pre = following
    sum_o[...] = total


def ffn_call(where, acts, w, b, d_act, earlier, name):
    rows, width = acts.shape
    ff = w.shape[1]
    tile = 512
    steps = ff // 2 // tile
    mine = bool(earlier)

    def place(i, where):
        return (where[1] if mine else 1 - where[1]) * steps + i

    col = lambda i, where: (0, place(i, where))
    return pl.pallas_call(
        ffn_kernel,
        out_shape=[
            jax.ShapeDtypeStruct((rows, ff), BF),
            jax.ShapeDtypeStruct((rows, ff // 2), BF),
            jax.ShapeDtypeStruct((1, ff), F32),
        ],
        grid_spec=pltpu.PrefetchScalarGridSpec(
            num_scalar_prefetch=1,
            grid=(steps,),
            in_specs=[
                pl.BlockSpec((rows, width), lambda i, where: (0, 0)),
                pl.BlockSpec((width, tile), col),
                pl.BlockSpec((1, tile), col),
                pl.BlockSpec((rows, tile), col),
            ]
            + [pl.BlockSpec(memory_space=pl.ANY)] * len(earlier),
            out_specs=[
                pl.BlockSpec((rows, tile), col),
                pl.BlockSpec((rows, tile), lambda i, where: (0, i)),
                pl.BlockSpec((1, tile), col),
            ],
        ),
        input_output_aliases={5: 0, 6: 2} if mine else {},
        compiler_params=pltpu.CompilerParams(vmem_limit_bytes=VMEM_LIMIT),
        cost_estimate=pl.CostEstimate(
            flops=rows * width * ff // SHARE,
            bytes_accessed=(2 * rows * width + width * ff + 3 * rows * ff) // SHARE,
            transcendentals=0,
        ),
        name=name,
    )(where, acts, w, b, d_act, *earlier)


def store_blocks(where, acc, outs, first, second, halved):
    rows = acc.shape[0] // (first * second)
    for one in range(first):
        for two in range(second):
            block = lax.bitwise_xor(two * first + one, where[0]) * rows
            if halved:
                for part in range(2):
                    at = block + lax.bitwise_xor(where[2], part) * (rows // 2)
                    piece = acc[pl.ds(pl.multiple_of(at, 16), rows // 2), :]
                    outs[part][one, two] = piece.astype(BF)
            else:
                outs[one][two] = acc[pl.ds(pl.multiple_of(block, 16), rows), :].astype(BF)


def grad_kernel(where, *refs, groups, first, second, halved, outs):
    acc = refs[-1]
    ins = refs[: sum(2 * g for g in groups)]
    height = acc.shape[0] // len(groups)
    at = 0
    for index, pairs in enumerate(groups):
        total = None
        for _ in range(pairs):
            part = dot(ins[at][...], ins[at + 1][...], TN)
            total = part if total is None else total + part
            at += 2
        acc[index * height : (index + 1) * height, :] = total
    store_blocks(where, acc, refs[-1 - outs : -1], first, second, halved)


def grad_call(where, groups, width, first, second, tile, halved, name, into=()):
    ins, flat, depth = [], [], 0
    for group in groups:
        for a, b, offset in group:
            ins.append(pl.BlockSpec(a.shape, lambda i, where: (0, 0)))
            if offset is None:
                index = lambda i, where: (0, where[1] * (width // tile) + i)
            else:
                index = lambda i, where, offset=offset: (0, offset // tile + i)
            ins.append(pl.BlockSpec((b.shape[0], tile), index))
            flat += [a, b]
            depth += a.shape[0]
    height = sum(g[0][0].shape[1] for g in groups)
    depth = depth // len(groups)
    rows = height // (first * second)
    if halved:
        shape, block = (first, second, rows // 2, width), (first, second, rows // 2, tile)
        outs = 2
        index = lambda i, where: (0, 0, 0, i)
    else:
        shape, block = (second, rows, width), (second, rows, tile)
        outs = first
        index = lambda i, where: (0, 0, i)
    if into:
        shape = into[0].shape
        row = shape[2] * 2 // rows - 1
        index = lambda i, where: (0, 0, row, i)
    return pl.pallas_call(
        functools.partial(
            grad_kernel, groups=[len(g) for g in groups], first=first, second=second, halved=halved, outs=outs
        ),
        out_shape=[jax.ShapeDtypeStruct(shape, BF)] * outs,
        grid_spec=pltpu.PrefetchScalarGridSpec(
            num_scalar_prefetch=1,
            grid=(width // tile,),
            in_specs=ins + [pl.BlockSpec(memory_space=pl.ANY)] * len(into),
            out_specs=[pl.BlockSpec(block, index)] * outs,
            scratch_shapes=[pltpu.VMEM((height, tile), F32)],
        ),
        input_output_aliases={1 + len(flat) + i: i for i in range(len(into))},
        compiler_params=pltpu.CompilerParams(vmem_limit_bytes=VMEM_LIMIT),
        cost_estimate=pl.CostEstimate(
            flops=2 * depth * height * width // SHARE,
            bytes_accessed=2 * (depth * (height + width) + height * width) // SHARE,
            transcendentals=0,
        ),
        name=name,
    )(where, *flat, *into)


def qkv_kernel(where, near_a, near_b, far_a, far_b, *refs, first, second, halved):
    *outs, sum_o, acc = refs
    acc[...] = dot(near_a[...], near_b[...], TN)
    sum_o[...] = jnp.sum(near_b[...].astype(F32), axis=0, keepdims=True)

    @pl.when(pl.program_id(0) > 0)
    def _():
        acc[...] += dot(far_a[...], far_b[...], TN)
        sum_o[...] += jnp.sum(far_b[...].astype(F32), axis=0, keepdims=True)

    store_blocks(where, acc, outs, first, second, halved)


def qkv_call(where, near, far, first, second, halved, name):
    (near_a, near_b), (far_a, far_b) = near, far
    height = near_a.shape[1]
    width = near_b.shape[1]
    tile = width // 3
    rows = height // (first * second)
    if halved:
        shape, block = (first, second, rows // 2, width), (first, second, rows // 2, tile)
        outs = 2
        index = lambda i, where: (0, 0, 0, i)
    else:
        shape, block = (second, rows, width), (second, rows, tile)
        outs = first
        index = lambda i, where: (0, 0, i)
    once = pl.Buffered(1)
    return pl.pallas_call(
        functools.partial(qkv_kernel, first=first, second=second, halved=halved),
        out_shape=[jax.ShapeDtypeStruct(shape, BF)] * outs + [jax.ShapeDtypeStruct((1, width), F32)],
        grid_spec=pltpu.PrefetchScalarGridSpec(
            num_scalar_prefetch=1,
            grid=(3,),
            in_specs=[
                pl.BlockSpec(near_a.shape, lambda i, where: (0, 0), pipeline_mode=once),
                pl.BlockSpec((near_b.shape[0], tile), lambda i, where: (0, i)),
                pl.BlockSpec(far_a.shape, lambda i, where: (0, 0), pipeline_mode=once),
                pl.BlockSpec((far_b.shape[0], tile), lambda i, where: (0, jnp.maximum(i - 1, 0))),
            ],
            out_specs=[pl.BlockSpec(block, index)] * outs + [pl.BlockSpec((1, tile), lambda i, where: (0, i))],
            scratch_shapes=[pltpu.VMEM((height, tile), F32)],
        ),
        compiler_params=pltpu.CompilerParams(vmem_limit_bytes=VMEM_LIMIT),
        cost_estimate=pl.CostEstimate(
            flops=2 * (near_a.shape[0] + far_a.shape[0]) * height * width // SHARE,
            bytes_accessed=2 * ((near_a.shape[0] + far_a.shape[0]) * (height + width) + height * width) // SHARE,
            transcendentals=0,
        ),
        name=name,
    )(where, near_a, near_b, far_a, far_b)


def back_kernel(where, a1, b1, a2, b2, out1, out2, acc):
    acc[...] = dot(a1[...], b1[...], TN) + dot(a2[...], b2[...], TN)
    rows = acc.shape[0] // 2
    for part, out in enumerate((out1, out2)):
        at = lax.bitwise_xor(where[2], part) * rows
        out[0, 0] = acc[pl.ds(pl.multiple_of(at, 16), rows), :].astype(BF)


def back_call(where, own, mate, first, second, extra, name):
    (a1, b1), (a2, b2) = own, mate
    tokens, ff = a1.shape
    rows = ff // (first * second)
    width = b2.shape[1] // 2

    def block(i, where):
        return (0, lax.bitwise_xor(lax.rem(i, second) * first + i // second, where[0]))

    return pl.pallas_call(
        back_kernel,
        out_shape=[jax.ShapeDtypeStruct((first, second, rows // 2 + extra, width), BF)] * 2,
        grid_spec=pltpu.PrefetchScalarGridSpec(
            num_scalar_prefetch=1,
            grid=(first * second,),
            in_specs=[
                pl.BlockSpec((tokens, rows), block),
                pl.BlockSpec((tokens, width), lambda i, where: (0, where[1])),
                pl.BlockSpec((tokens, rows), block),
                pl.BlockSpec((tokens, width), lambda i, where: (0, where[1])),
            ],
            out_specs=[
                pl.BlockSpec(
                    (1, 1, rows // 2, width), lambda i, where: (i // second, lax.rem(i, second), 0, 0)
                )
            ]
            * 2,
            scratch_shapes=[pltpu.VMEM((rows, width), F32)],
        ),
        compiler_params=pltpu.CompilerParams(vmem_limit_bytes=VMEM_LIMIT),
        cost_estimate=pl.CostEstimate(
            flops=4 * tokens * ff * width // SHARE,
            bytes_accessed=2 * (2 * tokens * (ff + width) + ff * width) // SHARE,
            transcendentals=0,
        ),
        name=name,
    )(where, a1, b1, a2, b2)


def product_kernel(*refs, dims, spans):
    parts = len(spans) if spans else 1
    total = None
    for i in range(parts):
        b = refs[parts]
        if spans:
            b = jnp.concatenate([b[:, low:high] for low, high in spans[i]], axis=1)
        else:
            b = b[...]
        part = dot(refs[i][...], b, dims)
        total = part if total is None else total + part
    for term in refs[parts + 1 : -1]:
        total = total + term[...]
    refs[-1][...] = total.astype(refs[-1].dtype)


def product(parts, b, dims, name, spans=None, terms=(), half=None):
    tile = 256
    turned = dims == NT
    rows = parts[0].shape[0] // (1 if half is None else 2)
    place = half or 0
    width = b.shape[0 if turned else 1]
    depth = sum(a.shape[1] for a in parts)
    ins = [
        pl.BlockSpec((rows, a.shape[1]), lambda i: (place, 0), pipeline_mode=pl.Buffered(1)) for a in parts
    ]
    if turned:
        ins.append(pl.BlockSpec((tile, b.shape[1]), lambda i: (i, 0)))
    else:
        ins.append(pl.BlockSpec((b.shape[0], tile), lambda i: (0, i)))
    return pl.pallas_call(
        functools.partial(product_kernel, dims=dims, spans=spans),
        out_shape=jax.ShapeDtypeStruct((rows, width), BF),
        grid=(width // tile,),
        in_specs=ins + [pl.BlockSpec((t.shape[0], tile), lambda i: (0, i)) for t in terms],
        out_specs=pl.BlockSpec((rows, tile), lambda i: (0, i)),
        compiler_params=pltpu.CompilerParams(vmem_limit_bytes=VMEM_LIMIT),
        cost_estimate=pl.CostEstimate(
            flops=2 * rows * depth * width // SHARE,
            bytes_accessed=2 * (rows * depth + depth * width + rows * width) // SHARE,
            transcendentals=0,
        ),
        name=name,
    )(*parts, b, *terms)


def tile_flags(queries, keys, tq, tk):
    q_first, q_last = queries[:, ::tq], queries[:, tq - 1 :: tq]
    k_first, k_last = keys[:, ::tk], keys[:, tk - 1 :: tk]
    meet = (q_first[:, :, None] <= k_last[:, None, :]) & (k_first[:, None, :] <= q_last[:, :, None])
    whole = (
        (q_first == q_last)[:, :, None]
        & (k_first == k_last)[:, None, :]
        & (q_first[:, :, None] == k_first[:, None, :])
    )
    return jnp.where(whole, 2, jnp.where(meet, 1, 0)).astype(jnp.int32)


def layer_norm_parts(values):
    centred = values - jnp.mean(values, axis=-1, keepdims=True)
    rstd = lax.rsqrt(jnp.mean(centred * centred, axis=-1, keepdims=True) + EPS)
    return centred * rstd, rstd


def layer_norm_back(d_norm, gain, xhat, rstd):
    e = d_norm * gain
    return rstd * (
        e - jnp.mean(e, axis=-1, keepdims=True) - xhat * jnp.mean(e * xhat, axis=-1, keepdims=True)
    )


def on_device(
    tokens,
    cell_start,
    norm1_gain,
    norm1_bias,
    w_qkv,
    bias_q,
    bias_v,
    w_out,
    bias_out,
    norm2_gain,
    norm2_bias,
    w_in,
    bias_in,
    w_back,
    bias_back,
    cotangent,
):
    rows, seg, width = tokens.shape
    count = rows * seg
    ff = w_in.shape[1]
    half = width // 2
    wide = lax.axis_size("wide")
    group = lax.axis_size("blk")
    place = lax.axis_index("wide")
    member = lax.axis_index("blk")
    core = place % 2
    chips = wide // 2
    first = 2 if chips <= 8 else 4
    second = chips // first
    heads = HEADS // 2
    early = 6
    spans = ((0, early), (early, heads))
    tq, tk = min(512, seg), min(256, seg)
    halves = group == 2 and ff // chips % 128 == 0
    where = jnp.stack([place // 2, core, member]).astype(jnp.int32)
    where_out = jnp.stack([lax.bitwise_xor(place // 2, core * (chips // 2)), core, member]).astype(jnp.int32)

    def after(value, *earlier):
        return lax.optimization_barrier((value, earlier))[0]

    def across(array, by):
        return lax.ppermute(array, "wide", [(i, i ^ by) for i in range(wide)])

    def to_mate(array):
        return across(array, 1)

    def from_ahead(array, by):
        return lax.ppermute(array, "blk", [((i + by) % group, i) for i in range(group)])

    def to_ahead(array, by):
        return lax.ppermute(array, "blk", [(i, (i + by) % group) for i in range(group)])

    def from_all_ahead(array):
        parts = [from_ahead(array, by) for by in range(1, group)]
        return parts[0] if len(parts) == 1 else jnp.concatenate(parts, axis=1)

    def cut(array, start, size, axis):
        return lax.dynamic_slice_in_dim(array, start, size, axis)

    def paired(array):
        return jnp.concatenate([array, to_mate(array)], axis=0)

    inputs = tokens.astype(F32).reshape(count, width)
    xhat1, rstd1 = layer_norm_parts(inputs)
    acts = (xhat1 * norm1_gain + norm1_bias).astype(BF).reshape(tokens.shape)
    cells = paired(cell_start)
    far_cells = from_all_ahead(cells)
    acts = after(acts, far_cells)
    far_own = from_all_ahead(acts)
    acts_pair = paired(acts).reshape(2 * count, width)
    w_own = jnp.concatenate([cut(w_qkv, part * width + core * half, half, 1) for part in range(3)], axis=1)
    b_own = jnp.concatenate([cut(bias_q, core * half, half, 0), jnp.zeros((half,), F32), cut(bias_v, core * half, half, 0)])

    def own_columns(span, parts):
        return tuple((part * half + span[0] * HD, part * half + span[1] * HD) for part in parts)

    near_spans = tuple(own_columns(span, (0, 1, 2)) for span in spans)
    far_spans = tuple(own_columns(span, (1, 2)) for span in spans)

    def columns(array):
        return jnp.broadcast_to(array[:, :, None], array.shape + (128,))

    qkv = (dot(acts_pair, w_own, NN) + b_own).astype(BF).reshape(2 * rows, seg, 3 * half)
    near_flags = tile_flags(cells, cells, tq, tk)
    far_flags = tile_flags(cells, far_cells, tq, tk)
    cell_rows = cells[:, None, :]
    near_columns, far_columns = columns(cells), columns(far_cells)
    state = attn_fwd(near_flags, cell_rows, near_columns, qkv, qkv, 1, None, tq, tk, heads)
    d_out = cotangent.reshape(count, width)
    d_out_mate = to_mate(after(d_out, acts_pair))
    far_own = after(far_own, state)
    far_mate = to_mate(far_own)
    d_act = dot(after(d_out, far_own, state, d_out_mate), w_back, NT).astype(BF)

    far_mate = after(far_mate, d_act)
    far_pair = jnp.concatenate([far_own, far_mate], axis=0)
    far_len = far_pair.shape[1]
    far_pair = far_pair.reshape(-1, width)
    far_kv = (dot(far_pair, w_own[:, half:], NN) + b_own[half:]).astype(BF).reshape(2 * rows, far_len, 2 * half)
    attended, stats = attn_fwd(far_flags, cell_rows, far_columns, qkv, far_kv, 0, state, tq, tk, heads)
    mine, theirs = attended[:rows].reshape(count, half), attended[rows:].reshape(count, half)
    own_rest = to_mate(theirs)
    mate_rest = to_mate(mine)
    w_out_own = cut(w_out, core * half, half, 0)
    w_out_mate = cut(w_out, (1 - core) * half, half, 0)
    middle = inputs + (dot(mine, w_out_own, NN) + dot(own_rest, w_out_mate, NN)) + bias_out

    xhat2, rstd2 = layer_norm_parts(middle)
    acts2 = (xhat2 * norm2_gain + norm2_bias).astype(BF)
    acts2_mate = to_mate(acts2)
    b_in = bias_in.reshape(1, ff)
    act_part, d_pre_theirs, sum_part = ffn_call(where, acts2, w_in, b_in, d_act, (), "ffn_theirs")
    d_pre_mate = to_mate(d_pre_theirs)
    act_part, acts2_mate, mate_rest = after((act_part, acts2_mate, mate_rest), d_pre_theirs)
    act, d_pre_mine, d_pre_sum = ffn_call(
        where, after(acts2, acts2_mate, mate_rest), w_in, b_in, d_act, (act_part, sum_part), "ffn_mine"
    )
    d_pre_mine, d_pre_mate = after((d_pre_mine, d_pre_mate), d_pre_sum)
    d_pre_theirs = after(d_pre_theirs, d_pre_mate)
    act_mate = to_mate(act)
    w_in_mine = cut(w_in, core * (ff // 2), ff // 2, 1)
    w_in_theirs = cut(w_in, (1 - core) * (ff // 2), ff // 2, 1)
    d_norm2 = dot(d_pre_theirs, w_in_theirs, NT) + dot(d_pre_mine, w_in_mine, NT)
    grad_out = d_out.astype(F32)
    d_middle = grad_out + layer_norm_back(d_norm2, norm2_gain, xhat2, rstd2)
    d_z = d_middle.astype(BF)
    d_att_theirs = dot(d_z, w_out_mate, NT).astype(BF)
    d_att_mine = dot(d_z, w_out_own, NT).astype(BF)
    d_att_mate = to_mate(d_att_theirs)
    d_z_mate = to_mate(d_z)

    def send(parts):
        return [across(parts[one], 2 * one) for one in range(1, first)]

    def add_first(parts, received):
        def added(at):
            total = parts[0][at].astype(F32)
            for part in received:
                total = total + part[at].astype(F32)
            return total.astype(BF)

        return added(slice(0, second // 2)), added(slice(second // 2, second))

    def send_second(pair):
        return across(pair[1], first * second)

    def add_second(pair, received):
        kept, got = pair[0].astype(F32), received.astype(F32)
        return tuple((kept[at] + got[at]).astype(BF) for at in range(2))

    def send_third(pair):
        return across(pair[1], 2 * first)

    def add_third(pair, received):
        return (pair[0].astype(F32) + received.astype(F32)).astype(BF)

    def start(parts):
        return from_ahead(parts[1], 1) if halves else send(parts)

    def middle_step(parts, received):
        if not halves:
            return parts, received
        sums = [(parts[0][one].astype(F32) + received[one].astype(F32)).astype(BF) for one in range(first)]
        return sums, send(sums)

    def ahead(total):
        return from_ahead(total, 1) if group == 2 else None

    def over_row(total, other):
        if group == 2:
            return (total.astype(F32) + other.astype(F32)).astype(BF)
        return lax.psum(total, "blk")

    def by_core(total, other, sizes):
        if halves:
            kept = jnp.where(member == core, total, other)
            return kept, jnp.where(member == core, other, total)
        total = over_row(total, other)
        parts, at = [], 0
        for size in sizes:
            parts.append(total[at : at + size].reshape(2, size // 2, total.shape[1]))
            at += size
        split = jnp.concatenate(parts, axis=1)
        return (lax.dynamic_index_in_dim(split, i, 0, keepdims=False) for i in (core, 1 - core))

    def swap(split):
        kept, given = split
        other = to_mate(given)
        return jnp.where(core == 0, kept, other).astype(F32), jnp.where(core == 0, other, kept).astype(F32)

    d_pre_held = after(d_pre_mine, d_att_theirs, d_att_mine)
    grad_in = grad_call(
        where, [[(acts2, d_pre_held, 0), (acts2_mate, d_pre_mate, 0)]], ff // 2, first, second, 512, False, "grad_in"
    )
    in_in = send(grad_in)
    act_held, act_mate, d_z_mate = after((act, act_mate, d_z_mate), grad_in)

    def grad_o(into):
        return grad_call(
            where_out,
            [
                [(mine, d_z, None), (theirs, d_z_mate, None)],
                [(own_rest, d_z, None), (mate_rest, d_z_mate, None)],
            ],
            half, first, second, half, halves, "grad_out", into,
        )

    back_rows, out_rows = ff // chips, width // chips
    if halves:
        grad_b = back_call(
            where, (act_held, d_out), (act_mate, d_out_mate), first, second, out_rows // 2, "grad_back"
        )
        grad_b = grad_o(tuple(grad_b))
    else:
        whole = dot(act_held, cut(d_out, core * half, half, 1), TN) + dot(act_mate, cut(d_out_mate, core * half, half, 1), TN)
        whole = whole.astype(BF).reshape(chips, back_rows, half)
        grad_b = [
            jnp.concatenate([
                jnp.stack([whole[lax.bitwise_xor(two * first + one, where[0])] for two in range(second)]), other
            ], axis=1)
            for one, other in enumerate(grad_o(()))
        ]
    b_in = start(grad_b)

    back_tq = min(256, seg)
    near_flags, far_flags = tile_flags(cells, cells, back_tq, tk), tile_flags(cells, far_cells, back_tq, tk)
    d_att = after((d_att_mine.reshape(rows, seg, half), d_att_mate.reshape(rows, seg, half)), grad_b)
    d_qT, far_early, far_late = attn_bwd(
        far_flags, cell_rows, far_columns, qkv, far_kv, 0, d_att, attended, stats, None, back_tq, tk, heads, spans, "attn_bwd_far"
    )
    in_sums = add_first(grad_in, after(in_in, d_qT))
    in_more = send_second(in_sums)
    far_early, far_late = after((far_early, far_late), in_sums)
    far_early, far_late = (f.reshape(-1, f.shape[-1]) for f in (far_early, far_late))
    n_early, n_late = early * HD, (heads - early) * HD
    far_theirs = product([far_early, far_late], w_own, NT, "far_norm_theirs", far_spans, half=1)
    far_given = to_mate(far_theirs)
    far_mine = product([after(far_early, far_theirs), far_late], w_own, NT, "far_norm_mine", far_spans, half=0)
    far_sum = (far_mine.astype(F32) + after(far_given, in_sums, far_mine).astype(F32)).astype(BF)
    far_sum = far_sum.reshape(rows, far_len, width)
    far_back = [to_ahead(far_sum[:, by * seg : (by + 1) * seg], by + 1) for by in range(group - 1)]
    d_qT = after(d_qT, far_sum)

    def near_back(span, name, *earlier):
        (out,) = attn_bwd(
            near_flags, cell_rows, near_columns, qkv, qkv, 1, d_att, attended, stats, after(d_qT, earlier), back_tq, tk, heads,
            (span,), name,
        )
        return out.reshape(2 * count, -1)

    near_early = near_back(spans[0], "attn_bwd_early")
    b_sums, b_in = middle_step(grad_b, after(b_in, near_early))
    in_two = add_second(in_sums, after(in_more, b_sums))
    in_last = send_third(in_two)
    near_early = after(near_early, b_sums, in_two)
    *grad_e, sum_e = qkv_call(where, (acts_pair, near_early), (far_pair, far_early), first, second, halves, "grad_early")
    in_total = add_third(in_two, after(in_last, grad_e))
    in_row = ahead(in_total)
    grad_e, far_back = after((grad_e, far_back), in_total)
    e_in = start(grad_e)
    near_late = near_back(spans[1], "attn_bwd_late", grad_e, far_back)
    b_two = add_first(b_sums, after(b_in, near_late))
    b_more = send_second(b_two)
    e_sums, e_in = middle_step(grad_e, after(e_in, b_two))
    in_row = after(in_row, e_sums)
    near_late = after(near_late, b_two, e_sums, in_row)
    *grad_l, sum_l = qkv_call(where, (acts_pair, near_late), (far_pair, far_late), first, second, halves, "grad_late")
    l_in = start(grad_l)
    near_held = after(near_early, grad_l)
    near_theirs = product([near_held, near_late], w_own, NT, "near_norm_theirs", near_spans, half=1)
    near_mine = product([after(near_held, near_theirs), near_late], w_own, NT, "near_norm_mine", near_spans, half=0)
    e_two = add_first(e_sums, after(e_in, near_mine))
    e_more = send_second(e_two)
    b_three = add_second(b_two, after(b_more, e_two))
    b_last = send_third(b_three)
    l_sums, l_in = middle_step(grad_l, after(l_in, b_three))
    near_given = to_mate(after(near_theirs, near_mine))
    act_late = after(act_held, e_two, b_three, l_sums)
    mixed = product([act_late], w_back, NN, "mixed", terms=(middle, bias_back.reshape(1, width))).reshape(tokens.shape)
    l_two = add_first(l_sums, after(l_in, mixed))
    l_more = send_second(l_two)
    e_three = add_second(e_two, after(e_more, l_two))
    e_last = send_third(e_three)
    b_total = add_third(b_three, after(b_last, e_three))
    b_row = ahead(b_total)
    near_mine, near_given = after((near_mine, near_given), l_two, e_three, b_total)
    d_norm1 = near_mine.astype(F32) + near_given.astype(F32)
    for part in far_back:
        d_norm1 = d_norm1 + part.reshape(count, width).astype(F32)
    norm1_sums = (jnp.sum(d_norm1 * xhat1, axis=0), jnp.sum(d_norm1, axis=0))
    e_total = add_third(e_three, after(e_last, norm1_sums))
    e_row = ahead(e_total)
    l_three = add_second(l_two, after(l_more, e_total))
    l_last = send_third(l_three)
    xhat1 = after(xhat1, l_three, e_total)
    grad_tokens = (d_middle + layer_norm_back(d_norm1, norm1_gain, xhat1, rstd1)).reshape(tokens.shape)

    def vectors(parts, *covers):
        packed = jnp.concatenate([p.reshape(wide, -1) for p in parts], axis=1)
        total = packed
        covers = iter(covers)
        for stride, size in ((2 * first, second), (2, first), (1, 2)):
            total = total.reshape(-1, size, stride, packed.shape[1])
            spot = (place // stride) % size
            kept = lax.dynamic_index_in_dim(total, spot, 1, keepdims=False)
            given = [
                across(lax.dynamic_index_in_dim(total, spot ^ by, 1, keepdims=False), by * stride)
                for by in range(1, size)
            ]
            given = after(given, next(covers))
            for part in given:
                kept = kept + part
            total = kept.reshape(stride, packed.shape[1])
        total = total.reshape(-1)
        total = total + after(from_ahead(total, 1), next(covers)) if group == 2 else lax.psum(total, "blk")
        out, at = [], 0
        for p in parts:
            size = p.size // wide
            out.append(total[at : at + size])
            at += size
        return out

    def widened(part):
        n = sum_e.shape[1] // 3, sum_l.shape[1] // 3
        own = jnp.concatenate([s[0, part * m : (part + 1) * m] for s, m in zip((sum_e, sum_l), n)])
        return lax.dynamic_update_slice_in_dim(jnp.zeros((width,), F32), own, core * half, 0)

    in_low, in_high = swap(by_core(after(in_total, grad_tokens), in_row, [width // chips])) if not halves else (None, None)
    if halves:
        in_whole = over_row(after(in_total, grad_tokens), in_row).reshape(2, -1, in_total.shape[1])
        in_low, in_high = swap([lax.dynamic_index_in_dim(in_whole, i, 0, keepdims=False) for i in (core, 1 - core)])
    b_low, b_high = swap(by_core(after(b_total, grad_tokens), b_row, [back_rows, out_rows]))
    e_low, e_high = swap(by_core(after(e_total, grad_tokens), e_row, [out_rows]))
    l_total = add_third(l_three, after(l_last, grad_tokens))
    l_low, l_high = swap(by_core(l_total, ahead(l_total), [out_rows]))

    def part_columns(part):
        return [
            array[:, part * n : (part + 1) * n]
            for array, n in ((e_low, n_early), (l_low, n_late), (e_high, n_early), (l_high, n_late))
        ]

    share = ff // wide
    grad_w_in = jnp.concatenate([in_low, in_high], axis=1)
    grad_w_back = jnp.concatenate([b_low[:share], b_high[:share]], axis=1)
    grad_w_out = jnp.concatenate([b_low[share:], b_high[share:]], axis=1)
    small = vectors(
        [
            *norm1_sums,
            widened(0),
            widened(2),
            jnp.sum(d_z.astype(F32), axis=0),
            jnp.sum(d_norm2 * xhat2, axis=0),
            jnp.sum(d_norm2, axis=0),
            d_pre_sum,
            jnp.sum(grad_out, axis=0),
        ],
        grad_tokens,
        grad_w_in,
        grad_w_back,
        grad_w_out,
    )
    return (
        mixed,
        grad_tokens,
        small[0],
        small[1],
        jnp.concatenate([piece for part in range(3) for piece in part_columns(part)], axis=1),
        small[2],
        small[3],
        grad_w_out,
        small[4],
        small[5],
        small[6],
        grad_w_in,
        small[7],
        grad_w_back,
        small[8],
    )


def solution(mesh):
    spread = P("wide", "blk", None)
    placed = (spread, P("wide", "blk")) + (P(),) * 13 + (spread,)
    matrix, vector = P("wide", None), P("wide")
    return jax.shard_map(
        on_device,
        mesh=mesh,
        in_specs=placed,
        out_specs=(
            spread, spread, vector, vector, matrix, vector, vector, matrix, vector, vector, vector,
            matrix, vector, matrix, vector,
        ),
        check_vma=False,
    )
```

```python
import functools
import math

import jax
import jax.numpy as jnp
from jax import lax
from jax.experimental import pallas as pl
from jax.experimental.pallas import tpu as pltpu
from jax.sharding import PartitionSpec as P

HEADS = 20
HEAD_DIM = 64
HD = HEAD_DIM
EPS = 1e-05
NEG = -1e30
LOG2E = math.log2(math.e)
C2 = LOG2E / math.sqrt(HEAD_DIM)
F32 = jnp.float32
BF = jnp.bfloat16
NN = (((1,), (0,)), ((), ()))
NT = (((1,), (1,)), ((), ()))
TN = (((0,), (0,)), ((), ()))
VMEM_LIMIT = 56 * 2**20
SHARE = 10
VR = HD + 16


def dot(a, b, dims):
    return lax.dot_general(a, b, dims, preferred_element_type=F32)


def head_sumsq(x,hp16):
    W=x.shape[1]
    sq=x.astype(F32)*x.astype(F32)
    row=lax.broadcasted_iota(jnp.int32,(hp16,W),0); col=lax.broadcasted_iota(jnp.int32,(hp16,W),1)
    ones=jnp.where(row==col//HD,1.0,0.0).astype(BF)
    return lax.dot_general(ones,sq.astype(BF),NT,preferred_element_type=F32)

def fwd_kernel(flags,cq,ck,q,k,v,*rest,first,tq,tk,heads):
    if first:
        accT_o,m_o,l_o,qm,vT,bias,acc,m,l,kn=rest
    else:
        accT_i,m_i,l_i,o_o,lse_o,qm,vT,bias,acc,m,l,kn=rest
    r=pl.program_id(0); qi=pl.program_id(1)
    nk=k.shape[1]//tk
    hp16=m.shape[0]
    @pl.when(qi==0)
    def _():
        for hh in range(heads):
            vT[hh*VR:hh*VR+HD,:]=v[0,:,hh*HD:(hh+1)*HD].T
            vT[hh*VR+HD:(hh+1)*VR,:]=jnp.ones((VR-HD,vT.shape[1]),BF)
        kn[...]=jnp.broadcast_to(jnp.sqrt(jnp.max(head_sumsq(k[0],hp16),1,keepdims=True)),kn.shape)
    lane=lax.broadcasted_iota(jnp.int32,(tq,128),1)
    for hp in range(heads//2):
        qp=q[0,:,hp*128:(hp+1)*128]
        qm[2*hp]=jnp.where(lane<64,qp,0).astype(BF)
        qm[2*hp+1]=jnp.where(lane>=64,qp,0).astype(BF)
    bound=jnp.sqrt(head_sumsq(q[0],hp16))*kn[:,0:1]*(C2*1.02)
    safe=jnp.max(bound)<50.0
    if first:
        m0=bound
    else:
        m0=jnp.maximum(bound,m_i[0])
    def loop(online):
        if first:
            acc[...]=jnp.zeros_like(acc); l[...]=jnp.zeros_like(l)
            m[...]=jnp.full_like(m,NEG) if online else m0
        elif online:
            acc[...]=accT_i[0]; m[...]=m_i[0]; l[...]=l_i[0]
        else:
            al=jnp.exp2(m_i[0]-m0)
            m[...]=m0; l[...]=al*l_i[0]
            for hh in range(heads):
                hs=slice(hh*HD,(hh+1)*HD)
                acc[hs,:]=al[hh:hh+1,:]*accT_i[0,hs,:]
        def body(kt,masked):
            ks=pl.ds(pl.multiple_of(kt*tk,tk),tk)
            if online:
                @pl.loop(0,heads//2)
                def _(hp):
                    kp=k[0,ks,pl.ds(pl.multiple_of(hp*128,128),128)]
                    for j in range(2):
                        hh=2*hp+j
                        s=lax.dot_general(kp,qm[hh],NT,preferred_element_type=F32)*C2+bias[...]
                        mp=m[pl.ds(hh,1),:]
                        mn=jnp.maximum(mp,jnp.max(s,0,keepdims=True))
                        p=jnp.exp2(s-mn)
                        al=jnp.exp2(mp-mn)
                        m[pl.ds(hh,1),:]=mn
                        l[pl.ds(hh,1),:]=al*l[pl.ds(hh,1),:]+jnp.sum(p,0,keepdims=True)
                        hs=pl.ds(pl.multiple_of(hh*HD,HD),HD)
                        vs=pl.ds(pl.multiple_of(hh*VR,16),HD)
                        acc[hs,:]=al*acc[hs,:]+lax.dot_general(vT[vs,ks],p.astype(BF),NN,preferred_element_type=F32)
                return
            def score(hh):
                s=lax.dot_general(k[0,ks,(hh//2)*128:(hh//2+1)*128],qm[hh],NT,preferred_element_type=F32)*C2
                if masked: s=s+bias[...]
                return s
            s=score(0); pp=None
            for hh in range(heads+1):
                if hh+1<heads: sn=score(hh+1)
                if pp is not None:
                    h1=hh-1
                    both=lax.dot_general(vT[h1*VR:(h1+1)*VR,ks],pp,NN,preferred_element_type=F32)
                    acc[h1*HD:(h1+1)*HD,:]+=both[:HD]
                    l[h1:h1+1,:]+=both[HD:HD+1]
                if hh<heads:
                    p=jnp.exp2(s-m[hh:hh+1,:])
                    pp=p.astype(BF)
                s=sn
        @pl.loop(0,nk)
        def _(kt):
            f=flags[r,qi,kt]
            def mask():
                ks=pl.ds(pl.multiple_of(kt*tk,tk),tk)
                bias[...]=jnp.where(ck[0,ks,0:1]==cq[0,0:1,:],0.0,NEG)
            if online:
                @pl.when(f>0)
                def _():
                    mask(); body(kt,True)
            else:
                @pl.when(f==1)
                def _():
                    mask(); body(kt,True)
                @pl.when(f==2)
                def _(): body(kt,False)
    @pl.when(safe)
    def _(): loop(False)
    @pl.when(jnp.logical_not(safe))
    def _(): loop(True)
    if first:
        accT_o[0]=acc[...]; m_o[0]=m[...]; l_o[0]=l[...]
    else:
        for hp in range(heads//2):
            parts=[]
            for hh in (2*hp,2*hp+1):
                parts.append(acc[hh*HD:(hh+1)*HD,:]/l[hh:hh+1,:])
            o_o[0,:,hp*128:(hp+1)*128]=jnp.concatenate(parts,0).T.astype(BF)
        lse_o[0]=m[...]+jnp.log2(l[...])

def attn_fwd(flags,cq,ck,q,kv,kb,state,tq,tk,heads):
    nr,S,_=q.shape; W=heads*HD; Sk=kv.shape[1]; hp16=-(-heads//8)*8
    first=state is None
    qs=lambda r,i,*_:(r,i,0); ts=lambda r,i,*_:(r,0,i); ks=lambda r,i,*_:(r,0,0)
    stspec=[pl.BlockSpec((1,W,tq),ts),pl.BlockSpec((1,hp16,tq),ts),pl.BlockSpec((1,hp16,tq),ts)]
    ins=[pl.BlockSpec((1,1,tq),ts),pl.BlockSpec((1,Sk,128),ks),pl.BlockSpec((1,tq,W),qs),pl.BlockSpec((1,Sk,W),lambda r,i,*_:(r,0,kb)),pl.BlockSpec((1,Sk,W),lambda r,i,*_:(r,0,kb+1))]
    if first:
        outs=stspec
        osh=[jax.ShapeDtypeStruct((nr,W,S),F32)]+[jax.ShapeDtypeStruct((nr,hp16,S),F32)]*2
    else:
        ins=ins+stspec
        outs=[pl.BlockSpec((1,tq,W),qs),pl.BlockSpec((1,hp16,tq),ts)]
        osh=[jax.ShapeDtypeStruct((nr,S,W),BF),jax.ShapeDtypeStruct((nr,hp16,S),F32)]
    fl=4*nr*S*Sk*W
    return pl.pallas_call(functools.partial(fwd_kernel,first=first,tq=tq,tk=tk,heads=heads),
        out_shape=osh,
        grid_spec=pltpu.PrefetchScalarGridSpec(num_scalar_prefetch=1,grid=(nr,S//tq),in_specs=ins,out_specs=outs,
          scratch_shapes=[pltpu.VMEM((heads,tq,128),BF),pltpu.VMEM((heads*VR,Sk),BF),pltpu.VMEM((tk,tq),F32),pltpu.VMEM((W,tq),F32),pltpu.VMEM((hp16,tq),F32),pltpu.VMEM((hp16,tq),F32),pltpu.VMEM((hp16,128),F32)]),
        compiler_params=pltpu.CompilerParams(dimension_semantics=("arbitrary","arbitrary"),vmem_limit_bytes=VMEM_LIMIT),
        cost_estimate=pl.CostEstimate(flops=fl//SHARE,bytes_accessed=nr*(S*W*2+2*Sk*W*2+S*W*4)//SHARE,transcendentals=0),
        name="attn_fwd_a" if first else "attn_fwd_b",
    )(flags,cq,ck,q,kv,kv,*(state or ()))

def bwd_kernel(flags,cq,ck,q,k,v,do_own,do_mate,o,lse,*rest,spans,tq,tk):
    first=len(spans)==2
    if first:
        dqT_o,*dkv_o,qm,dom,kT,bias,dqT,dk,dv,delta=rest
    else:
        dqT_i,dqkv_o,qm,dom,kT,bias,dqT,dk,dv,delta=rest
    r=pl.program_id(0); qi=pl.program_id(1); nq=pl.num_programs(1)
    nk=k.shape[1]//tk
    low=spans[0][0]; heads=sum(b-a for a,b in spans)
    W=heads*HD; c0=low*HD
    @pl.when(qi==0)
    def _():
        kT[...]=k[0,:,c0:c0+W].T
        dk[...]=jnp.zeros_like(dk); dv[...]=jnp.zeros_like(dv)
    own=r<pl.num_programs(0)//2
    lane=lax.broadcasted_iota(jnp.int32,(tq,128),1)
    for hp in range(heads//2):
        c=slice(c0+hp*128,c0+(hp+1)*128)
        qp=q[0,:,c]*jnp.asarray(0.125,BF); dp_=jnp.where(own,do_own[0,:,c],do_mate[0,:,c])
        qm[2*hp]=jnp.where(lane<64,qp,0).astype(BF)
        qm[2*hp+1]=jnp.where(lane>=64,qp,0).astype(BF)
        dom[2*hp]=jnp.where(lane<64,dp_,0).astype(BF)
        dom[2*hp+1]=jnp.where(lane>=64,dp_,0).astype(BF)
    prod=jnp.where(own,do_own[0,:,c0:c0+W],do_mate[0,:,c0:c0+W]).astype(F32)*o[0,:,c0:c0+W].astype(F32)
    hi=prod.astype(BF); lo=(prod-hi.astype(F32)).astype(BF)
    n16=delta.shape[0]
    row=lax.broadcasted_iota(jnp.int32,(n16,W),0); col_=lax.broadcasted_iota(jnp.int32,(n16,W),1)
    ones=jnp.where(row==col_//HD,1.0,0.0).astype(BF)
    delta[...]=lax.dot_general(ones,hi,NT,preferred_element_type=F32)+lax.dot_general(ones,lo,NT,preferred_element_type=F32)
    if first: dqT[...]=jnp.zeros_like(dqT)
    else: dqT[...]=dqT_i[0,c0:c0+W,:]
    def body(kt):
        ks=pl.ds(pl.multiple_of(kt*tk,tk),tk)
        def col(hh): return slice((hh//2)*128,(hh//2+1)*128)
        def wide(hh): return slice(c0+(hh//2)*128,c0+(hh//2+1)*128)
        def score(hh):
            s=lax.dot_general(k[0,ks,wide(hh)],qm[hh],NT,preferred_element_type=F32)*LOG2E+bias[...]
            return s,lax.dot_general(v[0,ks,wide(hh)],dom[hh],NT,preferred_element_type=F32)
        nxt=score(0); prev=None
        for hh in range(heads+1):
            cur=nxt
            if hh+1<heads: nxt=score(hh+1)
            if prev is not None:
                h1=hh-1; pb,dsb=prev
                hs=slice(h1*HD,(h1+1)*HD)
                dqT[hs,:]+=lax.dot_general(kT[hs,ks],dsb,NN,preferred_element_type=F32)
                dv[ks,col(h1)]+=jnp.dot(pb,dom[h1],preferred_element_type=F32)
                dk[ks,col(h1)]+=jnp.dot(dsb,qm[h1],preferred_element_type=F32)
            if hh<heads:
                s,dp=cur
                at=low+hh
                p=jnp.exp2(s-lse[0,at:at+1,:])
                ds=p*(dp-delta[hh:hh+1,:])
                prev=(p.astype(BF),ds.astype(BF))
    @pl.loop(0,nk)
    def _(kt):
        f=flags[r,qi,kt]
        @pl.when(f>0)
        def _():
            ks=pl.ds(pl.multiple_of(kt*tk,tk),tk)
            bias[...]=jnp.where(ck[0,ks,0:1]==cq[0,0:1,:],0.0,NEG)
            body(kt)
    if first: dqT_o[0]=dqT[...]
    else: dqkv_o[0,pl.ds(pl.multiple_of(qi*tq,tq),tq),0:W]=(dqT[...]*0.125).T.astype(BF)
    @pl.when(qi==nq-1)
    def _():
        if first:
            for (a,b),out in zip(spans,dkv_o):
                n=(b-a)*HD; at=(a-low)*HD
                out[0,:,0:n]=dk[:,at:at+n].astype(BF); out[0,:,n:2*n]=dv[:,at:at+n].astype(BF)
        else:
            dqkv_o[0,:,W:2*W]=dk[...].astype(BF); dqkv_o[0,:,2*W:3*W]=dv[...].astype(BF)

def attn_bwd(flags,cq,ck,q,kv,kb,do,o,lse,dqT,tq,tk,full,spans,name):
    nr,S,_=q.shape; F=full*HD; Sk=kv.shape[1]; n16=lse.shape[1]
    heads=sum(b-a for a,b in spans); W=heads*HD
    first=dqT is None
    qs=lambda r,i,*_:(r,i,0); ts=lambda r,i,*_:(r,0,i); ks=lambda r,i,*_:(r,0,0)
    ins=[pl.BlockSpec((1,1,tq),ts),pl.BlockSpec((1,Sk,128),ks),pl.BlockSpec((1,tq,F),qs),pl.BlockSpec((1,Sk,F),lambda r,i,*_:(r,0,kb)),pl.BlockSpec((1,Sk,F),lambda r,i,*_:(r,0,kb+1)),
         pl.BlockSpec((1,tq,F),lambda r,i,*_:(jnp.minimum(r,nr//2-1),jnp.where(r<nr//2,i,S//tq-1),0)),
         pl.BlockSpec((1,tq,F),lambda r,i,*_:(jnp.maximum(r-nr//2,0),jnp.where(r<nr//2,0,i),0)),
         pl.BlockSpec((1,tq,F),qs),pl.BlockSpec((1,n16,tq),ts)]
    if first:
        widths=[2*(b-a)*HD for a,b in spans]
        outs=[pl.BlockSpec((1,F,tq),ts)]+[pl.BlockSpec((1,Sk,n),ks) for n in widths]
        osh=[jax.ShapeDtypeStruct((nr,F,S),F32)]+[jax.ShapeDtypeStruct((nr,Sk,n),BF) for n in widths]
        extra=()
    else:
        ins=ins+[pl.BlockSpec((1,F,tq),ts)]
        outs=[pl.BlockSpec((1,Sk,3*W),ks)]; osh=[jax.ShapeDtypeStruct((nr,Sk,3*W),BF)]
        extra=(dqT,)
    fl=10*nr*S*Sk*W
    return pl.pallas_call(functools.partial(bwd_kernel,spans=spans,tq=tq,tk=tk),
        out_shape=osh,
        grid_spec=pltpu.PrefetchScalarGridSpec(num_scalar_prefetch=1,grid=(nr,S//tq),in_specs=ins,out_specs=outs,
          scratch_shapes=[pltpu.VMEM((heads,tq,128),BF),pltpu.VMEM((heads,tq,128),BF),pltpu.VMEM((W,Sk),BF),pltpu.VMEM((tk,tq),F32),pltpu.VMEM((W,tq),F32),
             pltpu.VMEM((Sk,W),F32),pltpu.VMEM((Sk,W),F32),pltpu.VMEM((n16,tq),F32)]),
        compiler_params=pltpu.CompilerParams(dimension_semantics=("arbitrary","arbitrary"),vmem_limit_bytes=VMEM_LIMIT),
        cost_estimate=pl.CostEstimate(flops=fl//SHARE,bytes_accessed=nr*(3*S*W*2+4*Sk*W*2+S*W*4)//SHARE,transcendentals=0),
        name=name,
    )(flags,cq,ck,q,kv,kv,*do,o,lse,*extra)


def ffn_kernel(where, acts, w, b, d_act, *rest, last):
    step = pl.program_id(0)
    final = pl.num_programs(0) - 1
    rows, width = acts.shape
    chunk = min(256, rows)
    count = rows // chunk
    if last:
        ins, outs, scratch = rest[:7], rest[7:15], rest[15:]
        _, _, acc_i, middle_i, d_out_i, w_out_i, gain = ins
        act_o, d_pre_o, sum_o, mid_o, d_z_o, theirs_o, mine_o, sums_o = outs
        acc, part, middle, d_out, w_out, d_z, att, in_sem, out_sem = scratch
        loads = [
            pltpu.make_async_copy(source, target, in_sem.at[n])
            for n, (source, target) in enumerate(
                ((acc_i, part), (middle_i, middle), (d_out_i, d_out), (w_out_i, w_out))
            )
        ]

        @pl.when(step == 0)
        def _():
            for load in loads:
                load.start()
    else:
        act_o, d_pre_o, sum_o, acc = rest

    @pl.when(step == 0)
    def _():
        acc[...] = jnp.zeros_like(acc)

    def span(i):
        return slice(i * chunk, (i + 1) * chunk)

    def product(i):
        return dot(acts[span(i), :], w[...], NN) + b[...]

    pre = product(0)
    total, held = None, None
    for i in range(count + 1):
        following = product(i + 1) if i + 1 < count else None
        if held is not None:
            acc[span(i - 1), :] += dot(held, w[...], NT)
        if i < count:
            at = span(i)
            cdf = 0.5 + 0.5 * lax.erf(pre * math.sqrt(0.5))
            pdf = jnp.exp(-0.5 * pre * pre) * (1.0 / math.sqrt(2.0 * math.pi))
            act_o[at, :] = (pre * cdf).astype(BF)
            held = (d_act[at, :].astype(F32) * (cdf + pre * pdf)).astype(BF)
            d_pre_o[at, :] = held
            summed = jnp.sum(held.astype(F32), axis=0, keepdims=True)
            total = summed if total is None else total + summed
        pre = following
    sum_o[...] = total
    if not last:
        return

    @pl.when(step == final)
    def _():
        for load in loads:
            load.wait()
        half = width // 2
        sums, stores = None, []
        for i in range(count):
            at = span(i)
            d_norm = acc[at, :] + part[at, :]
            xhat, rstd = layer_norm_parts(middle[at, :])
            d_mid = d_out[at, :].astype(F32) + layer_norm_back(d_norm, gain[...], xhat, rstd)
            low = d_mid.astype(BF)
            part[at, :] = d_mid
            d_z[at, :] = low
            for side in range(2):
                first = pl.multiple_of(lax.bitwise_xor(where[1], 1 - side) * half, half)
                att[side, at, :] = dot(low, w_out[pl.ds(first, half), :], NT).astype(BF)
            new = [low.astype(F32), d_norm * xhat, d_norm]
            new = jnp.concatenate([jnp.sum(n, axis=0, keepdims=True) for n in new], axis=0)
            sums = new if sums is None else sums + new
            pairs = ((part, mid_o), (d_z, d_z_o), (att.at[0], theirs_o), (att.at[1], mine_o))
            for n, (source, target) in enumerate(pairs):
                store = pltpu.make_async_copy(
                    source.at[pl.ds(i * chunk, chunk)], target.at[pl.ds(i * chunk, chunk)], out_sem.at[4 * i + n]
                )
                store.start()
                stores.append(store)
        sums_o[0:3, :] = sums
        sums_o[3:8, :] = jnp.zeros((5, width), F32)
        for store in stores:
            store.wait()


def ffn_call(where, acts, w, b, d_act, earlier, name):
    rows, width = acts.shape
    ff = w.shape[1]
    tile = 512
    steps = ff // 2 // tile
    last = bool(earlier)
    chunk = min(256, rows)

    def place(i, where):
        return (where[1] if last else 1 - where[1]) * steps + i

    col = lambda i, where: (0, place(i, where))
    whole = pl.BlockSpec((rows, width), lambda i, where: (0, 0))
    anywhere = pl.BlockSpec(memory_space=pl.ANY)
    out_shape = [
        jax.ShapeDtypeStruct((rows, ff), BF),
        jax.ShapeDtypeStruct((rows, ff // 2), BF),
        jax.ShapeDtypeStruct((1, ff), F32),
    ]
    out_specs = [
        pl.BlockSpec((rows, tile), col),
        pl.BlockSpec((rows, tile), lambda i, where: (0, i)),
        pl.BlockSpec((1, tile), col),
    ]
    ins = [
        pl.BlockSpec((rows, width), lambda i, where: (0, 0), pipeline_mode=pl.Buffered(1)),
        pl.BlockSpec((width, tile), col),
        pl.BlockSpec((1, tile), col),
        pl.BlockSpec((rows, tile), col),
    ]
    scratch = []
    if last:
        ins += [anywhere] * 6 + [pl.BlockSpec((1, width), lambda i, where: (0, 0))]
        out_shape += [
            jax.ShapeDtypeStruct((rows, width), F32),
            jax.ShapeDtypeStruct((rows, width), BF),
            jax.ShapeDtypeStruct((rows, width // 2), BF),
            jax.ShapeDtypeStruct((rows, width // 2), BF),
            jax.ShapeDtypeStruct((8, width), F32),
        ]
        out_specs += [anywhere] * 4 + [pl.BlockSpec((8, width), lambda i, where: (0, 0))]
        scratch = [
            pltpu.VMEM((rows, width), F32),
            pltpu.VMEM((rows, width), F32),
            pltpu.VMEM((rows, width), F32),
            pltpu.VMEM((rows, width), BF),
            pltpu.VMEM((width, width), BF),
            pltpu.VMEM((rows, width), BF),
            pltpu.VMEM((2, rows, width // 2), BF),
            pltpu.SemaphoreType.DMA((4,)),
            pltpu.SemaphoreType.DMA((4 * (rows // chunk),)),
        ]
    else:
        out_shape.append(jax.ShapeDtypeStruct((rows, width), F32))
        out_specs.append(whole)
    return pl.pallas_call(
        functools.partial(ffn_kernel, last=last),
        out_shape=out_shape,
        grid_spec=pltpu.PrefetchScalarGridSpec(
            num_scalar_prefetch=1, grid=(steps,), in_specs=ins, out_specs=out_specs, scratch_shapes=scratch
        ),
        input_output_aliases={5: 0, 6: 2} if last else {},
        compiler_params=pltpu.CompilerParams(vmem_limit_bytes=VMEM_LIMIT),
        cost_estimate=pl.CostEstimate(
            flops=2 * rows * width * ff // SHARE,
            bytes_accessed=(2 * rows * width + width * ff + 3 * rows * ff) // SHARE,
            transcendentals=0,
        ),
        name=name,
    )(where, acts, w, b, d_act, *earlier)


def store_blocks(where, acc, outs, first, second, halved):
    rows = acc.shape[0] // (first * second)
    for one in range(first):
        for two in range(second):
            block = lax.bitwise_xor(two * first + one, where[0]) * rows
            if halved:
                for part in range(2):
                    at = block + lax.bitwise_xor(where[2], part) * (rows // 2)
                    piece = acc[pl.ds(pl.multiple_of(at, 16), rows // 2), :]
                    outs[part][one, two] = piece.astype(BF)
            else:
                outs[one][two] = acc[pl.ds(pl.multiple_of(block, 16), rows), :].astype(BF)


def grad_kernel(where, *refs, groups, first, second, halved, outs):
    acc = refs[-1]
    ins = refs[: sum(2 * g for g in groups)]
    height = acc.shape[0] // len(groups)
    at = 0
    for index, pairs in enumerate(groups):
        total = None
        for _ in range(pairs):
            part = dot(ins[at][...], ins[at + 1][...], TN)
            total = part if total is None else total + part
            at += 2
        acc[index * height : (index + 1) * height, :] = total
    store_blocks(where, acc, refs[-1 - outs : -1], first, second, halved)


def grad_call(where, groups, width, first, second, tile, halved, name, into=()):
    ins, flat, depth = [], [], 0
    for group in groups:
        for a, b, offset in group:
            ins.append(pl.BlockSpec(a.shape, lambda i, where: (0, 0)))
            if offset is None:
                index = lambda i, where: (0, where[1] * (width // tile) + i)
            else:
                index = lambda i, where, offset=offset: (0, offset // tile + i)
            ins.append(pl.BlockSpec((b.shape[0], tile), index))
            flat += [a, b]
            depth += a.shape[0]
    height = sum(g[0][0].shape[1] for g in groups)
    depth = depth // len(groups)
    rows = height // (first * second)
    if halved:
        shape, block = (first, second, rows // 2, width), (first, second, rows // 2, tile)
        outs = 2
        index = lambda i, where: (0, 0, 0, i)
    else:
        shape, block = (second, rows, width), (second, rows, tile)
        outs = first
        index = lambda i, where: (0, 0, i)
    if into:
        shape = into[0].shape
        row = shape[2] * 2 // rows - 1
        index = lambda i, where: (0, 0, row, i)
    return pl.pallas_call(
        functools.partial(
            grad_kernel, groups=[len(g) for g in groups], first=first, second=second, halved=halved, outs=outs
        ),
        out_shape=[jax.ShapeDtypeStruct(shape, BF)] * outs,
        grid_spec=pltpu.PrefetchScalarGridSpec(
            num_scalar_prefetch=1,
            grid=(width // tile,),
            in_specs=ins + [pl.BlockSpec(memory_space=pl.ANY)] * len(into),
            out_specs=[pl.BlockSpec(block, index)] * outs,
            scratch_shapes=[pltpu.VMEM((height, tile), F32)],
        ),
        input_output_aliases={1 + len(flat) + i: i for i in range(len(into))},
        compiler_params=pltpu.CompilerParams(vmem_limit_bytes=VMEM_LIMIT),
        cost_estimate=pl.CostEstimate(
            flops=2 * depth * height * width // SHARE,
            bytes_accessed=2 * (depth * (height + width) + height * width) // SHARE,
            transcendentals=0,
        ),
        name=name,
    )(where, *flat, *into)


def qkv_kernel(where, near_a, near_b, far_a, far_b, *refs, first, second, halved):
    *outs, sum_o, acc = refs
    acc[...] = dot(near_a[...], near_b[...], TN)
    sum_o[...] = jnp.sum(near_b[...].astype(F32), axis=0, keepdims=True)

    @pl.when(pl.program_id(0) > 0)
    def _():
        acc[...] += dot(far_a[...], far_b[...], TN)
        sum_o[...] += jnp.sum(far_b[...].astype(F32), axis=0, keepdims=True)

    store_blocks(where, acc, outs, first, second, halved)


def qkv_call(where, near, far, first, second, halved, name):
    (near_a, near_b), (far_a, far_b) = near, far
    height = near_a.shape[1]
    width = near_b.shape[1]
    tile = width // 3
    rows = height // (first * second)
    if halved:
        shape, block = (first, second, rows // 2, width), (first, second, rows // 2, tile)
        outs = 2
        index = lambda i, where: (0, 0, 0, i)
    else:
        shape, block = (second, rows, width), (second, rows, tile)
        outs = first
        index = lambda i, where: (0, 0, i)
    once = pl.Buffered(1)
    return pl.pallas_call(
        functools.partial(qkv_kernel, first=first, second=second, halved=halved),
        out_shape=[jax.ShapeDtypeStruct(shape, BF)] * outs + [jax.ShapeDtypeStruct((1, width), F32)],
        grid_spec=pltpu.PrefetchScalarGridSpec(
            num_scalar_prefetch=1,
            grid=(3,),
            in_specs=[
                pl.BlockSpec(near_a.shape, lambda i, where: (0, 0), pipeline_mode=once),
                pl.BlockSpec((near_b.shape[0], tile), lambda i, where: (0, i)),
                pl.BlockSpec(far_a.shape, lambda i, where: (0, 0), pipeline_mode=once),
                pl.BlockSpec((far_b.shape[0], tile), lambda i, where: (0, jnp.maximum(i - 1, 0))),
            ],
            out_specs=[pl.BlockSpec(block, index)] * outs + [pl.BlockSpec((1, tile), lambda i, where: (0, i))],
            scratch_shapes=[pltpu.VMEM((height, tile), F32)],
        ),
        compiler_params=pltpu.CompilerParams(vmem_limit_bytes=VMEM_LIMIT),
        cost_estimate=pl.CostEstimate(
            flops=2 * (near_a.shape[0] + far_a.shape[0]) * height * width // SHARE,
            bytes_accessed=2 * ((near_a.shape[0] + far_a.shape[0]) * (height + width) + height * width) // SHARE,
            transcendentals=0,
        ),
        name=name,
    )(where, near_a, near_b, far_a, far_b)


def back_kernel(where, a1, b1, a2, b2, out1, out2, acc):
    acc[...] = dot(a1[...], b1[...], TN) + dot(a2[...], b2[...], TN)
    rows = acc.shape[0] // 2
    for part, out in enumerate((out1, out2)):
        at = lax.bitwise_xor(where[2], part) * rows
        out[0, 0] = acc[pl.ds(pl.multiple_of(at, 16), rows), :].astype(BF)


def back_call(where, own, mate, first, second, extra, name):
    (a1, b1), (a2, b2) = own, mate
    tokens, ff = a1.shape
    rows = ff // (first * second)
    width = b2.shape[1] // 2

    def block(i, where):
        return (0, lax.bitwise_xor(lax.rem(i, second) * first + i // second, where[0]))

    return pl.pallas_call(
        back_kernel,
        out_shape=[jax.ShapeDtypeStruct((first, second, rows // 2 + extra, width), BF)] * 2,
        grid_spec=pltpu.PrefetchScalarGridSpec(
            num_scalar_prefetch=1,
            grid=(first * second,),
            in_specs=[
                pl.BlockSpec((tokens, rows), block),
                pl.BlockSpec((tokens, width), lambda i, where: (0, where[1])),
                pl.BlockSpec((tokens, rows), block),
                pl.BlockSpec((tokens, width), lambda i, where: (0, where[1])),
            ],
            out_specs=[
                pl.BlockSpec(
                    (1, 1, rows // 2, width), lambda i, where: (i // second, lax.rem(i, second), 0, 0)
                )
            ]
            * 2,
            scratch_shapes=[pltpu.VMEM((rows, width), F32)],
        ),
        compiler_params=pltpu.CompilerParams(vmem_limit_bytes=VMEM_LIMIT),
        cost_estimate=pl.CostEstimate(
            flops=4 * tokens * ff * width // SHARE,
            bytes_accessed=2 * (2 * tokens * (ff + width) + ff * width) // SHARE,
            transcendentals=0,
        ),
        name=name,
    )(where, a1, b1, a2, b2)


def product_kernel(*refs, dims, spans):
    parts = len(spans) if spans else 1
    total = None
    for i in range(parts):
        b = refs[parts]
        if spans:
            b = jnp.concatenate([b[:, low:high] for low, high in spans[i]], axis=1)
        else:
            b = b[...]
        part = dot(refs[i][...], b, dims)
        total = part if total is None else total + part
    for term in refs[parts + 1 : -1]:
        total = total + term[...]
    refs[-1][...] = total.astype(refs[-1].dtype)


def product(parts, b, dims, name, spans=None, terms=(), half=None):
    tile = 256 if sum(a.shape[1] for a in parts) > 2560 else 640
    turned = dims == NT
    rows = parts[0].shape[0] // (1 if half is None else 2)
    place = half or 0
    width = b.shape[0 if turned else 1]
    depth = sum(a.shape[1] for a in parts)
    ins = [
        pl.BlockSpec((rows, a.shape[1]), lambda i: (place, 0), pipeline_mode=pl.Buffered(1)) for a in parts
    ]
    if turned:
        ins.append(pl.BlockSpec((tile, b.shape[1]), lambda i: (i, 0)))
    else:
        ins.append(pl.BlockSpec((b.shape[0], tile), lambda i: (0, i)))
    return pl.pallas_call(
        functools.partial(product_kernel, dims=dims, spans=spans),
        out_shape=jax.ShapeDtypeStruct((rows, width), BF),
        grid=(width // tile,),
        in_specs=ins + [pl.BlockSpec((t.shape[0], tile), lambda i: (0, i)) for t in terms],
        out_specs=pl.BlockSpec((rows, tile), lambda i: (0, i)),
        compiler_params=pltpu.CompilerParams(vmem_limit_bytes=VMEM_LIMIT),
        cost_estimate=pl.CostEstimate(
            flops=2 * rows * depth * width // SHARE,
            bytes_accessed=2 * (rows * depth + depth * width + rows * width) // SHARE,
            transcendentals=0,
        ),
        name=name,
    )(*parts, b, *terms)


def tile_flags(queries, keys, tq, tk):
    q_first, q_last = queries[:, ::tq], queries[:, tq - 1 :: tq]
    k_first, k_last = keys[:, ::tk], keys[:, tk - 1 :: tk]
    meet = (q_first[:, :, None] <= k_last[:, None, :]) & (k_first[:, None, :] <= q_last[:, :, None])
    whole = (
        (q_first == q_last)[:, :, None]
        & (k_first == k_last)[:, None, :]
        & (q_first[:, :, None] == k_first[:, None, :])
    )
    return jnp.where(whole, 2, jnp.where(meet, 1, 0)).astype(jnp.int32)


def layer_norm_parts(values):
    centred = values - jnp.mean(values, axis=-1, keepdims=True)
    rstd = lax.rsqrt(jnp.mean(centred * centred, axis=-1, keepdims=True) + EPS)
    return centred * rstd, rstd


def layer_norm_back(d_norm, gain, xhat, rstd):
    e = d_norm * gain
    return rstd * (
        e - jnp.mean(e, axis=-1, keepdims=True) - xhat * jnp.mean(e * xhat, axis=-1, keepdims=True)
    )


def on_device(
    tokens,
    cell_start,
    norm1_gain,
    norm1_bias,
    w_qkv,
    bias_q,
    bias_v,
    w_out,
    bias_out,
    norm2_gain,
    norm2_bias,
    w_in,
    bias_in,
    w_back,
    bias_back,
    cotangent,
):
    rows, seg, width = tokens.shape
    count = rows * seg
    ff = w_in.shape[1]
    half = width // 2
    wide = lax.axis_size("wide")
    group = lax.axis_size("blk")
    place = lax.axis_index("wide")
    member = lax.axis_index("blk")
    core = place % 2
    chips = wide // 2
    first = 2 if chips <= 8 else 4
    second = chips // first
    heads = HEADS // 2
    early = 6
    spans = ((0, early), (early, heads))
    tq, tk = min(512, seg), min(256, seg)
    halves = group == 2 and ff // chips % 128 == 0
    where = jnp.stack([place // 2, core, member]).astype(jnp.int32)
    where_out = jnp.stack([lax.bitwise_xor(place // 2, core * (chips // 2)), core, member]).astype(jnp.int32)

    def after(value, *earlier):
        return lax.optimization_barrier((value, earlier))[0]

    def across(array, by):
        return lax.ppermute(array, "wide", [(i, i ^ by) for i in range(wide)])

    def to_mate(array):
        return across(array, 1)

    def from_ahead(array, by):
        return lax.ppermute(array, "blk", [((i + by) % group, i) for i in range(group)])

    def to_ahead(array, by):
        return lax.ppermute(array, "blk", [(i, (i + by) % group) for i in range(group)])

    def from_all_ahead(array):
        parts = [from_ahead(array, by) for by in range(1, group)]
        return parts[0] if len(parts) == 1 else jnp.concatenate(parts, axis=1)

    def cut(array, start, size, axis):
        return lax.dynamic_slice_in_dim(array, start, size, axis)

    def paired(array):
        return jnp.concatenate([array, to_mate(array)], axis=0)

    inputs = tokens.astype(F32).reshape(count, width)
    xhat1, rstd1 = layer_norm_parts(inputs)
    acts = (xhat1 * norm1_gain + norm1_bias).astype(BF).reshape(tokens.shape)
    cells = paired(cell_start)
    far_cells = from_all_ahead(cells)
    acts = after(acts, far_cells)
    far_own = from_all_ahead(acts)
    acts_pair = paired(acts).reshape(2 * count, width)
    w_own = jnp.concatenate([cut(w_qkv, part * width + core * half, half, 1) for part in range(3)], axis=1)
    b_own = jnp.concatenate([cut(bias_q, core * half, half, 0), jnp.zeros((half,), F32), cut(bias_v, core * half, half, 0)])

    def own_columns(span, parts):
        return tuple((part * half + span[0] * HD, part * half + span[1] * HD) for part in parts)

    near_spans = tuple(own_columns(span, (0, 1, 2)) for span in spans)
    far_spans = tuple(own_columns(span, (1, 2)) for span in spans)

    def columns(array):
        return jnp.broadcast_to(array[:, :, None], array.shape + (128,))

    qkv = (dot(acts_pair, w_own, NN) + b_own).astype(BF).reshape(2 * rows, seg, 3 * half)
    near_flags = tile_flags(cells, cells, tq, tk)
    far_flags = tile_flags(cells, far_cells, tq, tk)
    cell_rows = cells[:, None, :]
    near_columns, far_columns = columns(cells), columns(far_cells)
    state = attn_fwd(near_flags, cell_rows, near_columns, qkv, qkv, 1, None, tq, tk, heads)
    d_out = cotangent.reshape(count, width)
    d_out_mate = to_mate(after(d_out, acts_pair))
    far_own = after(far_own, state)
    far_mate = to_mate(far_own)
    d_act = dot(after(d_out, far_own, state, d_out_mate), w_back, NT).astype(BF)

    far_mate = after(far_mate, d_act)
    far_pair = jnp.concatenate([far_own, far_mate], axis=0)
    far_len = far_pair.shape[1]
    far_pair = far_pair.reshape(-1, width)
    far_kv = (dot(far_pair, w_own[:, half:], NN) + b_own[half:]).astype(BF).reshape(2 * rows, far_len, 2 * half)
    attended, stats = attn_fwd(far_flags, cell_rows, far_columns, qkv, far_kv, 0, state, tq, tk, heads)
    mine, theirs = attended[:rows].reshape(count, half), attended[rows:].reshape(count, half)
    own_rest = to_mate(theirs)
    mate_rest = to_mate(mine)
    w_out_own = cut(w_out, core * half, half, 0)
    w_out_mate = cut(w_out, (1 - core) * half, half, 0)
    middle = inputs + (dot(mine, w_out_own, NN) + dot(own_rest, w_out_mate, NN)) + bias_out

    xhat2, _ = layer_norm_parts(middle)
    acts2 = (xhat2 * norm2_gain + norm2_bias).astype(BF)
    acts2_mate = to_mate(acts2)
    b_in = bias_in.reshape(1, ff)
    act_part, d_pre_theirs, sum_part, norm_part = ffn_call(
        where, after(acts2, mate_rest), w_in, b_in, d_act, (), "ffn_theirs"
    )
    d_pre_mate = to_mate(d_pre_theirs)
    act, d_pre_mine, d_pre_sum, d_middle, d_z, d_att_theirs, d_att_mine, z_sums = ffn_call(
        where, acts2, w_in, b_in, d_act,
        (act_part, sum_part, norm_part, middle, d_out, w_out, norm2_gain.reshape(1, width)), "ffn_mine",
    )
    act_mate = to_mate(after(act, d_pre_mate, acts2_mate))
    grad_out = d_out.astype(F32)
    d_att_mate = to_mate(d_att_theirs)
    d_z_mate = to_mate(d_z)

    def send(parts):
        return [across(parts[one], 2 * one) for one in range(1, first)]

    def add_first(parts, received):
        def added(at):
            total = parts[0][at].astype(F32)
            for part in received:
                total = total + part[at].astype(F32)
            return total.astype(BF)

        return added(slice(0, second // 2)), added(slice(second // 2, second))

    def send_second(pair):
        return across(pair[1], first * second)

    def add_second(pair, received):
        kept, got = pair[0].astype(F32), received.astype(F32)
        return tuple((kept[at] + got[at]).astype(BF) for at in range(2))

    def send_third(pair):
        return across(pair[1], 2 * first)

    def add_third(pair, received):
        return (pair[0].astype(F32) + received.astype(F32)).astype(BF)

    def start(parts):
        return from_ahead(parts[1], 1) if halves else send(parts)

    def middle_step(parts, received):
        if not halves:
            return parts, received
        sums = [(parts[0][one].astype(F32) + received[one].astype(F32)).astype(BF) for one in range(first)]
        return sums, send(sums)

    def ahead(total):
        return from_ahead(total, 1) if group == 2 else None

    def over_row(total, other):
        if group == 2:
            return (total.astype(F32) + other.astype(F32)).astype(BF)
        return lax.psum(total, "blk")

    def by_core(total, other, sizes):
        if halves:
            kept = jnp.where(member == core, total, other)
            return kept, jnp.where(member == core, other, total)
        total = over_row(total, other)
        parts, at = [], 0
        for size in sizes:
            parts.append(total[at : at + size].reshape(2, size // 2, total.shape[1]))
            at += size
        split = jnp.concatenate(parts, axis=1)
        return (lax.dynamic_index_in_dim(split, i, 0, keepdims=False) for i in (core, 1 - core))

    def swap(split):
        kept, given = split
        other = to_mate(given)
        return jnp.where(core == 0, kept, other).astype(F32), jnp.where(core == 0, other, kept).astype(F32)

    d_pre_held = d_pre_mine
    grad_in = grad_call(
        where, [[(acts2, d_pre_held, 0), (acts2_mate, d_pre_mate, 0)]], ff // 2, first, second, 512, False, "grad_in"
    )
    in_in = send(grad_in)
    act_held, act_mate, d_z_mate = after((act, act_mate, d_z_mate), grad_in)

    def grad_o(into):
        return grad_call(
            where_out,
            [
                [(mine, d_z, None), (theirs, d_z_mate, None)],
                [(own_rest, d_z, None), (mate_rest, d_z_mate, None)],
            ],
            half, first, second, half, halves, "grad_out", into,
        )

    back_rows, out_rows = ff // chips, width // chips
    if halves:
        grad_b = back_call(
            where, (act_held, d_out), (act_mate, d_out_mate), first, second, out_rows // 2, "grad_back"
        )
        grad_b = grad_o(tuple(grad_b))
    else:
        whole = dot(act_held, cut(d_out, core * half, half, 1), TN) + dot(act_mate, cut(d_out_mate, core * half, half, 1), TN)
        whole = whole.astype(BF).reshape(chips, back_rows, half)
        grad_b = [
            jnp.concatenate([
                jnp.stack([whole[lax.bitwise_xor(two * first + one, where[0])] for two in range(second)]), other
            ], axis=1)
            for one, other in enumerate(grad_o(()))
        ]
    b_in = start(grad_b)

    back_tq = min(256, seg)
    near_flags, far_flags = tile_flags(cells, cells, back_tq, tk), tile_flags(cells, far_cells, back_tq, tk)
    d_att = after((d_att_mine.reshape(rows, seg, half), d_att_mate.reshape(rows, seg, half)), grad_b)
    d_qT, far_early, far_late = attn_bwd(
        far_flags, cell_rows, far_columns, qkv, far_kv, 0, d_att, attended, stats, None, back_tq, tk, heads, spans, "attn_bwd_far"
    )
    in_sums = add_first(grad_in, after(in_in, d_qT))
    in_more = send_second(in_sums)
    far_early, far_late = after((far_early, far_late), in_sums)
    far_early, far_late = (f.reshape(-1, f.shape[-1]) for f in (far_early, far_late))
    n_early, n_late = early * HD, (heads - early) * HD
    far_theirs = product([far_early, far_late], w_own, NT, "far_norm_theirs", far_spans, half=1)
    far_given = to_mate(far_theirs)
    far_mine = product([after(far_early, far_theirs), far_late], w_own, NT, "far_norm_mine", far_spans, half=0)
    far_sum = (far_mine.astype(F32) + after(far_given, in_sums, far_mine).astype(F32)).astype(BF)
    far_sum = far_sum.reshape(rows, far_len, width)
    far_back = [to_ahead(far_sum[:, by * seg : (by + 1) * seg], by + 1) for by in range(group - 1)]
    d_qT = after(d_qT, far_sum)

    def near_back(span, name, *earlier):
        (out,) = attn_bwd(
            near_flags, cell_rows, near_columns, qkv, qkv, 1, d_att, attended, stats, after(d_qT, earlier), back_tq, tk, heads,
            (span,), name,
        )
        return out.reshape(2 * count, -1)

    near_early = near_back(spans[0], "attn_bwd_early")
    b_sums, b_in = middle_step(grad_b, after(b_in, near_early))
    in_two = add_second(in_sums, after(in_more, b_sums))
    in_last = send_third(in_two)
    near_early = after(near_early, b_sums, in_two)
    *grad_e, sum_e = qkv_call(where, (acts_pair, near_early), (far_pair, far_early), first, second, halves, "grad_early")
    in_total = add_third(in_two, after(in_last, grad_e))
    in_row = ahead(in_total)
    grad_e, far_back = after((grad_e, far_back), in_total)
    e_in = start(grad_e)
    near_late = near_back(spans[1], "attn_bwd_late", grad_e, far_back)
    b_two = add_first(b_sums, after(b_in, near_late))
    b_more = send_second(b_two)
    e_sums, e_in = middle_step(grad_e, after(e_in, b_two))
    near_late = after(near_late, b_two, e_sums)
    *grad_l, sum_l = qkv_call(where, (acts_pair, near_late), (far_pair, far_late), first, second, halves, "grad_late")
    l_in = start(grad_l)
    near_held = after(near_early, grad_l)
    near_theirs = product([near_held, near_late], w_own, NT, "near_norm_theirs", near_spans, half=1)
    near_mine = product([after(near_held, near_theirs), near_late], w_own, NT, "near_norm_mine", near_spans, half=0)
    e_two = add_first(e_sums, after(e_in, near_mine))
    e_more = send_second(e_two)
    b_three = add_second(b_two, after(b_more, e_two))
    b_last = send_third(b_three)
    l_sums, l_in = middle_step(grad_l, after(l_in, b_three))
    near_given = to_mate(after(near_theirs, near_mine))
    in_row = after(in_row, near_mine)
    act_late = after(act_held, e_two, b_three, l_sums, in_row)
    mixed = product([act_late], w_back, NN, "mixed", terms=(middle, bias_back.reshape(1, width))).reshape(tokens.shape)
    l_two = add_first(l_sums, after(l_in, mixed))
    l_more = send_second(l_two)
    e_three = add_second(e_two, after(e_more, l_two))
    e_last = send_third(e_three)
    b_total = add_third(b_three, after(b_last, e_three))
    b_row = ahead(b_total)
    near_mine, near_given = after((near_mine, near_given), l_two, e_three, b_total)
    d_norm1 = near_mine.astype(F32) + near_given.astype(F32)
    for part in far_back:
        d_norm1 = d_norm1 + part.reshape(count, width).astype(F32)
    norm1_sums = (jnp.sum(d_norm1 * xhat1, axis=0), jnp.sum(d_norm1, axis=0))
    e_total = add_third(e_three, after(e_last, norm1_sums))
    e_row = ahead(e_total)
    l_three = add_second(l_two, after(l_more, e_total))
    l_last = send_third(l_three)
    xhat1 = after(xhat1, l_three, e_total)
    grad_tokens = (d_middle + layer_norm_back(d_norm1, norm1_gain, xhat1, rstd1)).reshape(tokens.shape)

    def vectors(parts, *covers):
        packed = jnp.concatenate([p.reshape(wide, -1) for p in parts], axis=1)
        total = packed
        covers = iter(covers)
        for stride, size in ((2 * first, second), (2, first), (1, 2)):
            total = total.reshape(-1, size, stride, packed.shape[1])
            spot = (place // stride) % size
            kept = lax.dynamic_index_in_dim(total, spot, 1, keepdims=False)
            given = [
                across(lax.dynamic_index_in_dim(total, spot ^ by, 1, keepdims=False), by * stride)
                for by in range(1, size)
            ]
            given = after(given, next(covers))
            for part in given:
                kept = kept + part
            total = kept.reshape(stride, packed.shape[1])
        total = total.reshape(-1)
        total = total + after(from_ahead(total, 1), next(covers)) if group == 2 else lax.psum(total, "blk")
        out, at = [], 0
        for p in parts:
            size = p.size // wide
            out.append(total[at : at + size])
            at += size
        return out

    def widened(part):
        n = sum_e.shape[1] // 3, sum_l.shape[1] // 3
        own = jnp.concatenate([s[0, part * m : (part + 1) * m] for s, m in zip((sum_e, sum_l), n)])
        return lax.dynamic_update_slice_in_dim(jnp.zeros((width,), F32), own, core * half, 0)

    in_low, in_high = swap(by_core(after(in_total, grad_tokens), in_row, [width // chips])) if not halves else (None, None)
    if halves:
        in_whole = over_row(after(in_total, grad_tokens), in_row).reshape(2, -1, in_total.shape[1])
        in_low, in_high = swap([lax.dynamic_index_in_dim(in_whole, i, 0, keepdims=False) for i in (core, 1 - core)])
    b_low, b_high = swap(by_core(after(b_total, grad_tokens), b_row, [back_rows, out_rows]))
    e_low, e_high = swap(by_core(after(e_total, grad_tokens), e_row, [out_rows]))
    l_total = add_third(l_three, after(l_last, grad_tokens))
    l_low, l_high = swap(by_core(l_total, ahead(l_total), [out_rows]))

    def part_columns(part):
        return [
            array[:, part * n : (part + 1) * n]
            for array, n in ((e_low, n_early), (l_low, n_late), (e_high, n_early), (l_high, n_late))
        ]

    share = ff // wide
    grad_w_in = jnp.concatenate([in_low, in_high], axis=1)
    grad_w_back = jnp.concatenate([b_low[:share], b_high[:share]], axis=1)
    grad_w_out = jnp.concatenate([b_low[share:], b_high[share:]], axis=1)
    small = vectors(
        [
            *norm1_sums,
            widened(0),
            widened(2),
            z_sums[0],
            z_sums[1],
            z_sums[2],
            d_pre_sum,
            jnp.sum(grad_out, axis=0),
        ],
        grad_tokens,
        grad_w_in,
        grad_w_back,
        grad_w_out,
    )
    return (
        mixed,
        grad_tokens,
        small[0],
        small[1],
        jnp.concatenate([piece for part in range(3) for piece in part_columns(part)], axis=1),
        small[2],
        small[3],
        grad_w_out,
        small[4],
        small[5],
        small[6],
        grad_w_in,
        small[7],
        grad_w_back,
        small[8],
    )


def solution(mesh):
    spread = P("wide", "blk", None)
    placed = (spread, P("wide", "blk")) + (P(),) * 13 + (spread,)
    matrix, vector = P("wide", None), P("wide")
    return jax.shard_map(
        on_device,
        mesh=mesh,
        in_specs=placed,
        out_specs=(
            spread, spread, vector, vector, matrix, vector, vector, matrix, vector, vector, vector,
            matrix, vector, matrix, vector,
        ),
        check_vma=False,
    )
```

```python
import functools
import math

import jax
import jax.numpy as jnp
from jax import lax
from jax.experimental import pallas as pl
from jax.experimental.pallas import tpu as pltpu
from jax.sharding import PartitionSpec as P

HEADS = 20
HEAD_DIM = 64
HD = HEAD_DIM
EPS = 1e-05
NEG = -1e30
LOG2E = math.log2(math.e)
C2 = LOG2E / math.sqrt(HEAD_DIM)
F32 = jnp.float32
BF = jnp.bfloat16
NN = (((1,), (0,)), ((), ()))
NT = (((1,), (1,)), ((), ()))
TN = (((0,), (0,)), ((), ()))
VMEM_LIMIT = 56 * 2**20


def room(mebibytes, rows):
    return mebibytes * 2**20 if rows <= 2048 else VMEM_LIMIT

SHARE = 10
VR = HD + 16


def dot(a, b, dims):
    return lax.dot_general(a, b, dims, preferred_element_type=F32)


def own_map(nr,last):
    return lambda r,i,*_:(jnp.minimum(r,nr//2-1),jnp.where(r<nr//2,i,last-1),0)

def mate_map(nr):
    return lambda r,i,*_:(jnp.maximum(r-nr//2,0),jnp.where(r<nr//2,0,i),0)

def head_sumsq(x,hp16):
    W=x.shape[1]
    sq=x.astype(F32)*x.astype(F32)
    row=lax.broadcasted_iota(jnp.int32,(hp16,W),0); col=lax.broadcasted_iota(jnp.int32,(hp16,W),1)
    ones=jnp.where(row==col//HD,1.0,0.0).astype(BF)
    return lax.dot_general(ones,sq.astype(BF),NT,preferred_element_type=F32)

def fwd_kernel(flags,cq,ck,q,k,v,*rest,first,tq,tk,heads):
    if first:
        accT_o,m_o,l_o,qm,vT,bias,acc,m,l,kn=rest
    else:
        accT_i,m_i,l_i,o_own,o_mate,lse_o,qm,vT,bias,acc,m,l,kn=rest
    r=pl.program_id(0); qi=pl.program_id(1)
    nk=k.shape[1]//tk
    hp16=m.shape[0]
    @pl.when(qi==0)
    def _():
        for hh in range(heads):
            vT[hh*VR:hh*VR+HD,:]=v[0,:,hh*HD:(hh+1)*HD].T
            vT[hh*VR+HD:(hh+1)*VR,:]=jnp.ones((VR-HD,vT.shape[1]),BF)
        kn[...]=jnp.broadcast_to(jnp.sqrt(jnp.max(head_sumsq(k[0],hp16),1,keepdims=True)),kn.shape)
    lane=lax.broadcasted_iota(jnp.int32,(tq,128),1)
    for hp in range(heads//2):
        qp=q[0,:,hp*128:(hp+1)*128]
        qm[2*hp]=jnp.where(lane<64,qp,0).astype(BF)
        qm[2*hp+1]=jnp.where(lane>=64,qp,0).astype(BF)
    bound=jnp.sqrt(head_sumsq(q[0],hp16))*kn[:,0:1]*(C2*1.02)
    safe=jnp.max(bound)<50.0
    if first:
        m0=bound
    else:
        m0=jnp.maximum(bound,m_i[0])
    def loop(online):
        if first:
            acc[...]=jnp.zeros_like(acc); l[...]=jnp.zeros_like(l)
            m[...]=jnp.full_like(m,NEG) if online else m0
        elif online:
            acc[...]=accT_i[0]; m[...]=m_i[0]; l[...]=l_i[0]
        else:
            al=jnp.exp2(m_i[0]-m0)
            m[...]=m0; l[...]=al*l_i[0]
            for hh in range(heads):
                hs=slice(hh*HD,(hh+1)*HD)
                acc[hs,:]=al[hh:hh+1,:]*accT_i[0,hs,:]
        def body(kt,masked):
            ks=pl.ds(pl.multiple_of(kt*tk,tk),tk)
            if online:
                @pl.loop(0,heads//2)
                def _(hp):
                    kp=k[0,ks,pl.ds(pl.multiple_of(hp*128,128),128)]
                    for j in range(2):
                        hh=2*hp+j
                        s=lax.dot_general(kp,qm[hh],NT,preferred_element_type=F32)*C2+bias[...]
                        mp=m[pl.ds(hh,1),:]
                        mn=jnp.maximum(mp,jnp.max(s,0,keepdims=True))
                        p=jnp.exp2(s-mn)
                        al=jnp.exp2(mp-mn)
                        m[pl.ds(hh,1),:]=mn
                        l[pl.ds(hh,1),:]=al*l[pl.ds(hh,1),:]+jnp.sum(p,0,keepdims=True)
                        hs=pl.ds(pl.multiple_of(hh*HD,HD),HD)
                        vs=pl.ds(pl.multiple_of(hh*VR,16),HD)
                        acc[hs,:]=al*acc[hs,:]+lax.dot_general(vT[vs,ks],p.astype(BF),NN,preferred_element_type=F32)
                return
            def score(hh):
                s=lax.dot_general(k[0,ks,(hh//2)*128:(hh//2+1)*128],qm[hh],NT,preferred_element_type=F32)*C2
                if masked: s=s+bias[...]
                return s
            s=score(0); pp=None
            for hh in range(heads+1):
                if hh+1<heads: sn=score(hh+1)
                if pp is not None:
                    h1=hh-1
                    both=lax.dot_general(vT[h1*VR:(h1+1)*VR,ks],pp,NN,preferred_element_type=F32)
                    acc[h1*HD:(h1+1)*HD,:]+=both[:HD]
                    l[h1:h1+1,:]+=both[HD:HD+1]
                if hh<heads:
                    p=jnp.exp2(s-m[hh:hh+1,:])
                    pp=p.astype(BF)
                s=sn
        @pl.loop(0,nk)
        def _(kt):
            f=flags[r,qi,kt]
            def mask():
                ks=pl.ds(pl.multiple_of(kt*tk,tk),tk)
                bias[...]=jnp.where(ck[0,ks,0:1]==cq[0,0:1,:],0.0,NEG)
            if online:
                @pl.when(f>0)
                def _():
                    mask(); body(kt,True)
            else:
                @pl.when(f==1)
                def _():
                    mask(); body(kt,True)
                @pl.when(f==2)
                def _(): body(kt,False)
    @pl.when(safe)
    def _(): loop(False)
    @pl.when(jnp.logical_not(safe))
    def _(): loop(True)
    if first:
        accT_o[0]=acc[...]; m_o[0]=m[...]; l_o[0]=l[...]
    else:
        for hp in range(heads//2):
            parts=[]
            for hh in (2*hp,2*hp+1):
                parts.append(acc[hh*HD:(hh+1)*HD,:]/l[hh:hh+1,:])
            low=jnp.concatenate(parts,0).T.astype(BF)
            @pl.when(r<pl.num_programs(0)//2)
            def _(): o_own[0,:,hp*128:(hp+1)*128]=low
            @pl.when(r>=pl.num_programs(0)//2)
            def _(): o_mate[0,:,hp*128:(hp+1)*128]=low
        lse_o[0]=m[...]+jnp.log2(l[...])

def attn_fwd(flags,cq,ck,q,kv,kb,state,tq,tk,heads):
    nr,S,_=q.shape; W=heads*HD; Sk=kv.shape[1]; hp16=-(-heads//8)*8
    first=state is None
    qs=lambda r,i,*_:(r,i,0); ts=lambda r,i,*_:(r,0,i); ks=lambda r,i,*_:(r,0,0)
    stspec=[pl.BlockSpec((1,W,tq),ts),pl.BlockSpec((1,hp16,tq),ts),pl.BlockSpec((1,hp16,tq),ts)]
    ins=[pl.BlockSpec((1,1,tq),ts),pl.BlockSpec((1,Sk,128),ks),pl.BlockSpec((1,tq,W),qs),pl.BlockSpec((1,Sk,W),lambda r,i,*_:(r,0,kb)),pl.BlockSpec((1,Sk,W),lambda r,i,*_:(r,0,kb+1))]
    if first:
        outs=stspec
        osh=[jax.ShapeDtypeStruct((nr,W,S),F32)]+[jax.ShapeDtypeStruct((nr,hp16,S),F32)]*2
    else:
        ins=ins+stspec
        outs=[pl.BlockSpec((1,tq,W),own_map(nr,S//tq)),pl.BlockSpec((1,tq,W),mate_map(nr)),pl.BlockSpec((1,hp16,tq),ts)]
        osh=[jax.ShapeDtypeStruct((nr//2,S,W),BF)]*2+[jax.ShapeDtypeStruct((nr,hp16,S),F32)]
    fl=4*nr*S*Sk*W
    return pl.pallas_call(functools.partial(fwd_kernel,first=first,tq=tq,tk=tk,heads=heads),
        out_shape=osh,
        grid_spec=pltpu.PrefetchScalarGridSpec(num_scalar_prefetch=1,grid=(nr,S//tq),in_specs=ins,out_specs=outs,
          scratch_shapes=[pltpu.VMEM((heads,tq,128),BF),pltpu.VMEM((heads*VR,Sk),BF),pltpu.VMEM((tk,tq),F32),pltpu.VMEM((W,tq),F32),pltpu.VMEM((hp16,tq),F32),pltpu.VMEM((hp16,tq),F32),pltpu.VMEM((hp16,128),F32)]),
        compiler_params=pltpu.CompilerParams(dimension_semantics=("arbitrary","arbitrary"),vmem_limit_bytes=room(20, nr * Sk)),
        cost_estimate=pl.CostEstimate(flops=fl//SHARE,bytes_accessed=nr*(S*W*2+2*Sk*W*2+S*W*4)//SHARE,transcendentals=0),
        name="attn_fwd_a" if first else "attn_fwd_b",
    )(flags,cq,ck,q,kv,kv,*(state or ()))

def bwd_kernel(flags,cq,ck,q,k,v,do_own,do_mate,o_own,o_mate,lse,*rest,spans,tq,tk):
    first=len(spans)==2
    if first:
        dqT_o,*dkv_o,qm,dom,kT,bias,dqT,dk,dv,delta=rest
    else:
        dqT_i,dqkv_o,qm,dom,kT,bias,dqT,dk,dv,delta=rest
    r=pl.program_id(0); qi=pl.program_id(1); nq=pl.num_programs(1)
    nk=k.shape[1]//tk
    low=spans[0][0]; heads=sum(b-a for a,b in spans)
    W=heads*HD; c0=low*HD
    @pl.when(qi==0)
    def _():
        kT[...]=k[0,:,c0:c0+W].T
        dk[...]=jnp.zeros_like(dk); dv[...]=jnp.zeros_like(dv)
    own=r<pl.num_programs(0)//2
    lane=lax.broadcasted_iota(jnp.int32,(tq,128),1)
    for hp in range(heads//2):
        c=slice(c0+hp*128,c0+(hp+1)*128)
        qp=q[0,:,c]*jnp.asarray(0.125,BF); dp_=jnp.where(own,do_own[0,:,c],do_mate[0,:,c])
        qm[2*hp]=jnp.where(lane<64,qp,0).astype(BF)
        qm[2*hp+1]=jnp.where(lane>=64,qp,0).astype(BF)
        dom[2*hp]=jnp.where(lane<64,dp_,0).astype(BF)
        dom[2*hp+1]=jnp.where(lane>=64,dp_,0).astype(BF)
    prod=jnp.where(own,do_own[0,:,c0:c0+W],do_mate[0,:,c0:c0+W]).astype(F32)*jnp.where(own,o_own[0,:,c0:c0+W],o_mate[0,:,c0:c0+W]).astype(F32)
    hi=prod.astype(BF); lo=(prod-hi.astype(F32)).astype(BF)
    n16=delta.shape[0]
    row=lax.broadcasted_iota(jnp.int32,(n16,W),0); col_=lax.broadcasted_iota(jnp.int32,(n16,W),1)
    ones=jnp.where(row==col_//HD,1.0,0.0).astype(BF)
    delta[...]=lax.dot_general(ones,hi,NT,preferred_element_type=F32)+lax.dot_general(ones,lo,NT,preferred_element_type=F32)
    if first: dqT[...]=jnp.zeros_like(dqT)
    else: dqT[...]=dqT_i[0,c0:c0+W,:]
    def body(kt):
        ks=pl.ds(pl.multiple_of(kt*tk,tk),tk)
        def col(hh): return slice((hh//2)*128,(hh//2+1)*128)
        def wide(hh): return slice(c0+(hh//2)*128,c0+(hh//2+1)*128)
        def score(hh):
            s=lax.dot_general(k[0,ks,wide(hh)],qm[hh],NT,preferred_element_type=F32)*LOG2E+bias[...]
            return s,lax.dot_general(v[0,ks,wide(hh)],dom[hh],NT,preferred_element_type=F32)
        nxt=score(0); prev=None
        for hh in range(heads+1):
            cur=nxt
            if hh+1<heads: nxt=score(hh+1)
            if prev is not None:
                h1=hh-1; pb,dsb=prev
                hs=slice(h1*HD,(h1+1)*HD)
                dqT[hs,:]+=lax.dot_general(kT[hs,ks],dsb,NN,preferred_element_type=F32)
                dv[ks,col(h1)]+=jnp.dot(pb,dom[h1],preferred_element_type=F32)
                dk[ks,col(h1)]+=jnp.dot(dsb,qm[h1],preferred_element_type=F32)
            if hh<heads:
                s,dp=cur
                at=low+hh
                p=jnp.exp2(s-lse[0,at:at+1,:])
                ds=p*(dp-delta[hh:hh+1,:])
                prev=(p.astype(BF),ds.astype(BF))
    @pl.loop(0,nk)
    def _(kt):
        f=flags[r,qi,kt]
        @pl.when(f>0)
        def _():
            ks=pl.ds(pl.multiple_of(kt*tk,tk),tk)
            bias[...]=jnp.where(ck[0,ks,0:1]==cq[0,0:1,:],0.0,NEG)
            body(kt)
    if first: dqT_o[0]=dqT[...]
    else: dqkv_o[0,pl.ds(pl.multiple_of(qi*tq,tq),tq),0:W]=(dqT[...]*0.125).T.astype(BF)
    @pl.when(qi==nq-1)
    def _():
        if first:
            for (a,b),out in zip(spans,dkv_o):
                n=(b-a)*HD; at=(a-low)*HD
                out[0,:,0:n]=dk[:,at:at+n].astype(BF); out[0,:,n:2*n]=dv[:,at:at+n].astype(BF)
        else:
            dqkv_o[0,:,W:2*W]=dk[...].astype(BF); dqkv_o[0,:,2*W:3*W]=dv[...].astype(BF)

def attn_bwd(flags,cq,ck,q,kv,kb,do,o,lse,dqT,tq,tk,full,spans,name):
    nr,S,_=q.shape; F=full*HD; Sk=kv.shape[1]; n16=lse.shape[1]
    heads=sum(b-a for a,b in spans); W=heads*HD
    first=dqT is None
    qs=lambda r,i,*_:(r,i,0); ts=lambda r,i,*_:(r,0,i); ks=lambda r,i,*_:(r,0,0)
    ins=[pl.BlockSpec((1,1,tq),ts),pl.BlockSpec((1,Sk,128),ks),pl.BlockSpec((1,tq,F),qs),pl.BlockSpec((1,Sk,F),lambda r,i,*_:(r,0,kb)),pl.BlockSpec((1,Sk,F),lambda r,i,*_:(r,0,kb+1)),
         *[pl.BlockSpec((1,tq,F),own_map(nr,S//tq)),pl.BlockSpec((1,tq,F),mate_map(nr))]*2,pl.BlockSpec((1,n16,tq),ts)]
    if first:
        widths=[2*(b-a)*HD for a,b in spans]
        outs=[pl.BlockSpec((1,F,tq),ts)]+[pl.BlockSpec((1,Sk,n),ks) for n in widths]
        osh=[jax.ShapeDtypeStruct((nr,F,S),F32)]+[jax.ShapeDtypeStruct((nr,Sk,n),BF) for n in widths]
        extra=()
    else:
        ins=ins+[pl.BlockSpec((1,F,tq),ts)]
        outs=[pl.BlockSpec((1,Sk,3*W),ks)]; osh=[jax.ShapeDtypeStruct((nr,Sk,3*W),BF)]
        extra=(dqT,)
    fl=10*nr*S*Sk*W
    return pl.pallas_call(functools.partial(bwd_kernel,spans=spans,tq=tq,tk=tk),
        out_shape=osh,
        grid_spec=pltpu.PrefetchScalarGridSpec(num_scalar_prefetch=1,grid=(nr,S//tq),in_specs=ins,out_specs=outs,
          scratch_shapes=[pltpu.VMEM((heads,tq,128),BF),pltpu.VMEM((heads,tq,128),BF),pltpu.VMEM((W,Sk),BF),pltpu.VMEM((tk,tq),F32),pltpu.VMEM((W,tq),F32),
             pltpu.VMEM((Sk,W),F32),pltpu.VMEM((Sk,W),F32),pltpu.VMEM((n16,tq),F32)]),
        compiler_params=pltpu.CompilerParams(dimension_semantics=("arbitrary","arbitrary"),vmem_limit_bytes=room(28, nr * Sk)),
        cost_estimate=pl.CostEstimate(flops=fl//SHARE,bytes_accessed=nr*(3*S*W*2+4*Sk*W*2+S*W*4)//SHARE,transcendentals=0),
        name=name,
    )(flags,cq,ck,q,kv,kv,*do,*o,lse,*extra)


def ffn_kernel(where, acts, w, b, d_act, *rest, last):
    step = pl.program_id(0)
    final = pl.num_programs(0) - 1
    rows, width = acts.shape
    chunk = min(256, rows)
    count = rows // chunk
    if last:
        ins, outs, scratch = rest[:7], rest[7:15], rest[15:]
        _, _, acc_i, middle_i, d_out_i, w_out_i, gain = ins
        act_o, d_pre_o, sum_o, mid_o, d_z_o, theirs_o, mine_o, sums_o = outs
        acc, part, middle, d_out, w_out, d_z, att, in_sem, out_sem = scratch
        loads = [
            pltpu.make_async_copy(source, target, in_sem.at[n])
            for n, (source, target) in enumerate(
                ((acc_i, part), (middle_i, middle), (d_out_i, d_out), (w_out_i, w_out))
            )
        ]

        @pl.when(step == 0)
        def _():
            for load in loads:
                load.start()
    else:
        act_o, d_pre_o, sum_o, acc = rest

    @pl.when(step == 0)
    def _():
        acc[...] = jnp.zeros_like(acc)

    def span(i):
        return slice(i * chunk, (i + 1) * chunk)

    def product(i):
        return dot(acts[span(i), :], w[...], NN) + b[...]

    pre = product(0)
    total, held = None, None
    for i in range(count + 1):
        following = product(i + 1) if i + 1 < count else None
        if held is not None:
            acc[span(i - 1), :] += dot(held, w[...], NT)
        if i < count:
            at = span(i)
            cdf = 0.5 + 0.5 * lax.erf(pre * math.sqrt(0.5))
            pdf = jnp.exp(-0.5 * pre * pre) * (1.0 / math.sqrt(2.0 * math.pi))
            act_o[at, :] = (pre * cdf).astype(BF)
            held = (d_act[at, :].astype(F32) * (cdf + pre * pdf)).astype(BF)
            d_pre_o[at, :] = held
            summed = jnp.sum(held.astype(F32), axis=0, keepdims=True)
            total = summed if total is None else total + summed
        pre = following
    sum_o[...] = total
    if not last:
        return

    @pl.when(step == final)
    def _():
        for load in loads:
            load.wait()
        half = width // 2
        sums, stores = None, []
        for i in range(count):
            at = span(i)
            d_norm = acc[at, :] + part[at, :]
            xhat, rstd = layer_norm_parts(middle[at, :])
            d_mid = d_out[at, :].astype(F32) + layer_norm_back(d_norm, gain[...], xhat, rstd)
            low = d_mid.astype(BF)
            part[at, :] = d_mid
            d_z[at, :] = low
            for side in range(2):
                first = pl.multiple_of(lax.bitwise_xor(where[1], 1 - side) * half, half)
                att[side, at, :] = dot(low, w_out[pl.ds(first, half), :], NT).astype(BF)
            new = [low.astype(F32), d_norm * xhat, d_norm]
            new = jnp.concatenate([jnp.sum(n, axis=0, keepdims=True) for n in new], axis=0)
            sums = new if sums is None else sums + new
            pairs = ((part, mid_o), (d_z, d_z_o), (att.at[0], theirs_o), (att.at[1], mine_o))
            for n, (source, target) in enumerate(pairs):
                store = pltpu.make_async_copy(
                    source.at[pl.ds(i * chunk, chunk)], target.at[pl.ds(i * chunk, chunk)], out_sem.at[4 * i + n]
                )
                store.start()
                stores.append(store)
        sums_o[0:3, :] = sums
        sums_o[3:8, :] = jnp.zeros((5, width), F32)
        for store in stores:
            store.wait()


def ffn_call(where, acts, w, b, d_act, earlier, name):
    rows, width = acts.shape
    ff = w.shape[1]
    tile = 512
    steps = ff // 2 // tile
    last = bool(earlier)
    chunk = min(256, rows)

    def place(i, where):
        return (where[1] if last else 1 - where[1]) * steps + i

    col = lambda i, where: (0, place(i, where))
    whole = pl.BlockSpec((rows, width), lambda i, where: (0, 0))
    anywhere = pl.BlockSpec(memory_space=pl.ANY)
    out_shape = [
        jax.ShapeDtypeStruct((rows, ff), BF),
        jax.ShapeDtypeStruct((rows, ff // 2), BF),
        jax.ShapeDtypeStruct((1, ff), F32),
    ]
    out_specs = [
        pl.BlockSpec((rows, tile), col),
        pl.BlockSpec((rows, tile), lambda i, where: (0, i)),
        pl.BlockSpec((1, tile), col),
    ]
    ins = [
        pl.BlockSpec((rows, width), lambda i, where: (0, 0), pipeline_mode=pl.Buffered(1)),
        pl.BlockSpec((width, tile), col),
        pl.BlockSpec((1, tile), col),
        pl.BlockSpec((rows, tile), col),
    ]
    scratch = []
    if last:
        ins += [anywhere] * 6 + [pl.BlockSpec((1, width), lambda i, where: (0, 0))]
        out_shape += [
            jax.ShapeDtypeStruct((rows, width), F32),
            jax.ShapeDtypeStruct((rows, width), BF),
            jax.ShapeDtypeStruct((rows, width // 2), BF),
            jax.ShapeDtypeStruct((rows, width // 2), BF),
            jax.ShapeDtypeStruct((8, width), F32),
        ]
        out_specs += [anywhere] * 4 + [pl.BlockSpec((8, width), lambda i, where: (0, 0))]
        scratch = [
            pltpu.VMEM((rows, width), F32),
            pltpu.VMEM((rows, width), F32),
            pltpu.VMEM((rows, width), F32),
            pltpu.VMEM((rows, width), BF),
            pltpu.VMEM((width, width), BF),
            pltpu.VMEM((rows, width), BF),
            pltpu.VMEM((2, rows, width // 2), BF),
            pltpu.SemaphoreType.DMA((4,)),
            pltpu.SemaphoreType.DMA((4 * (rows // chunk),)),
        ]
    else:
        out_shape.append(jax.ShapeDtypeStruct((rows, width), F32))
        out_specs.append(whole)
    return pl.pallas_call(
        functools.partial(ffn_kernel, last=last),
        out_shape=out_shape,
        grid_spec=pltpu.PrefetchScalarGridSpec(
            num_scalar_prefetch=1, grid=(steps,), in_specs=ins, out_specs=out_specs, scratch_shapes=scratch
        ),
        input_output_aliases={5: 0, 6: 2} if last else {},
        compiler_params=pltpu.CompilerParams(vmem_limit_bytes=room((52 if last else 22), rows)),
        cost_estimate=pl.CostEstimate(
            flops=2 * rows * width * ff // SHARE,
            bytes_accessed=(2 * rows * width + width * ff + 3 * rows * ff) // SHARE,
            transcendentals=0,
        ),
        name=name,
    )(where, acts, w, b, d_act, *earlier)


def store_blocks(where, acc, outs, first, second, halved):
    rows = acc.shape[0] // (first * second)
    for one in range(first):
        for two in range(second):
            block = lax.bitwise_xor(two * first + one, where[0]) * rows
            if halved:
                for part in range(2):
                    at = block + lax.bitwise_xor(where[2], part) * (rows // 2)
                    piece = acc[pl.ds(pl.multiple_of(at, 16), rows // 2), :]
                    outs[part][one, two] = piece.astype(BF)
            else:
                outs[one][two] = acc[pl.ds(pl.multiple_of(block, 16), rows), :].astype(BF)


def grad_kernel(where, *refs, groups, first, second, halved, outs):
    acc = refs[-1]
    ins = refs[: sum(2 * g for g in groups)]
    height = acc.shape[0] // len(groups)
    at = 0
    for index, pairs in enumerate(groups):
        total = None
        for _ in range(pairs):
            part = dot(ins[at][...], ins[at + 1][...], TN)
            total = part if total is None else total + part
            at += 2
        acc[index * height : (index + 1) * height, :] = total
    store_blocks(where, acc, refs[-1 - outs : -1], first, second, halved)


def grad_call(where, groups, width, first, second, tile, halved, name, into=()):
    ins, flat, depth = [], [], 0
    for group in groups:
        for a, b, offset in group:
            ins.append(pl.BlockSpec(a.shape, lambda i, where: (0, 0)))
            if offset is None:
                index = lambda i, where: (0, where[1] * (width // tile) + i)
            else:
                index = lambda i, where, offset=offset: (0, offset // tile + i)
            ins.append(pl.BlockSpec((b.shape[0], tile), index))
            flat += [a, b]
            depth += a.shape[0]
    height = sum(g[0][0].shape[1] for g in groups)
    depth = depth // len(groups)
    rows = height // (first * second)
    if halved:
        shape, block = (first, second, rows // 2, width), (first, second, rows // 2, tile)
        outs = 2
        index = lambda i, where: (0, 0, 0, i)
    else:
        shape, block = (second, rows, width), (second, rows, tile)
        outs = first
        index = lambda i, where: (0, 0, i)
    if into:
        shape = into[0].shape
        row = shape[2] * 2 // rows - 1
        index = lambda i, where: (0, 0, row, i)
    return pl.pallas_call(
        functools.partial(
            grad_kernel, groups=[len(g) for g in groups], first=first, second=second, halved=halved, outs=outs
        ),
        out_shape=[jax.ShapeDtypeStruct(shape, BF)] * outs,
        grid_spec=pltpu.PrefetchScalarGridSpec(
            num_scalar_prefetch=1,
            grid=(width // tile,),
            in_specs=ins + [pl.BlockSpec(memory_space=pl.ANY)] * len(into),
            out_specs=[pl.BlockSpec(block, index)] * outs,
            scratch_shapes=[pltpu.VMEM((height, tile), F32)],
        ),
        input_output_aliases={1 + len(flat) + i: i for i in range(len(into))},
        compiler_params=pltpu.CompilerParams(vmem_limit_bytes=room(22, depth)),
        cost_estimate=pl.CostEstimate(
            flops=2 * depth * height * width // SHARE,
            bytes_accessed=2 * (depth * (height + width) + height * width) // SHARE,
            transcendentals=0,
        ),
        name=name,
    )(where, *flat, *into)


def qkv_kernel(where, near_a, near_b, far_a, far_b, *refs, first, second, halved):
    *outs, sum_o, acc = refs
    acc[...] = dot(near_a[...], near_b[...], TN)
    sum_o[...] = jnp.sum(near_b[...].astype(F32), axis=0, keepdims=True)

    @pl.when(pl.program_id(0) > 0)
    def _():
        acc[...] += dot(far_a[...], far_b[...], TN)
        sum_o[...] += jnp.sum(far_b[...].astype(F32), axis=0, keepdims=True)

    store_blocks(where, acc, outs, first, second, halved)


def qkv_call(where, near, far, first, second, halved, name):
    (near_a, near_b), (far_a, far_b) = near, far
    height = near_a.shape[1]
    width = near_b.shape[1]
    tile = width // 3
    rows = height // (first * second)
    if halved:
        shape, block = (first, second, rows // 2, width), (first, second, rows // 2, tile)
        outs = 2
        index = lambda i, where: (0, 0, 0, i)
    else:
        shape, block = (second, rows, width), (second, rows, tile)
        outs = first
        index = lambda i, where: (0, 0, i)
    once = pl.Buffered(1)
    return pl.pallas_call(
        functools.partial(qkv_kernel, first=first, second=second, halved=halved),
        out_shape=[jax.ShapeDtypeStruct(shape, BF)] * outs + [jax.ShapeDtypeStruct((1, width), F32)],
        grid_spec=pltpu.PrefetchScalarGridSpec(
            num_scalar_prefetch=1,
            grid=(3,),
            in_specs=[
                pl.BlockSpec(near_a.shape, lambda i, where: (0, 0), pipeline_mode=once),
                pl.BlockSpec((near_b.shape[0], tile), lambda i, where: (0, i)),
                pl.BlockSpec(far_a.shape, lambda i, where: (0, 0), pipeline_mode=once),
                pl.BlockSpec((far_b.shape[0], tile), lambda i, where: (0, jnp.maximum(i - 1, 0))),
            ],
            out_specs=[pl.BlockSpec(block, index)] * outs + [pl.BlockSpec((1, tile), lambda i, where: (0, i))],
            scratch_shapes=[pltpu.VMEM((height, tile), F32)],
        ),
        compiler_params=pltpu.CompilerParams(vmem_limit_bytes=room(27, far[0].shape[0])),
        cost_estimate=pl.CostEstimate(
            flops=2 * (near_a.shape[0] + far_a.shape[0]) * height * width // SHARE,
            bytes_accessed=2 * ((near_a.shape[0] + far_a.shape[0]) * (height + width) + height * width) // SHARE,
            transcendentals=0,
        ),
        name=name,
    )(where, near_a, near_b, far_a, far_b)


def back_kernel(where, a1, b1, a2, b2, out1, out2, acc):
    acc[...] = dot(a1[...], b1[...], TN) + dot(a2[...], b2[...], TN)
    rows = acc.shape[0] // 2
    for part, out in enumerate((out1, out2)):
        at = lax.bitwise_xor(where[2], part) * rows
        out[0, 0] = acc[pl.ds(pl.multiple_of(at, 16), rows), :].astype(BF)


def back_call(where, own, mate, first, second, extra, name):
    (a1, b1), (a2, b2) = own, mate
    tokens, ff = a1.shape
    rows = ff // (first * second)
    width = b2.shape[1] // 2

    def block(i, where):
        return (0, lax.bitwise_xor(lax.rem(i, second) * first + i // second, where[0]))

    return pl.pallas_call(
        back_kernel,
        out_shape=[jax.ShapeDtypeStruct((first, second, rows // 2 + extra, width), BF)] * 2,
        grid_spec=pltpu.PrefetchScalarGridSpec(
            num_scalar_prefetch=1,
            grid=(first * second,),
            in_specs=[
                pl.BlockSpec((tokens, rows), block),
                pl.BlockSpec((tokens, width), lambda i, where: (0, where[1])),
                pl.BlockSpec((tokens, rows), block),
                pl.BlockSpec((tokens, width), lambda i, where: (0, where[1])),
            ],
            out_specs=[
                pl.BlockSpec(
                    (1, 1, rows // 2, width), lambda i, where: (i // second, lax.rem(i, second), 0, 0)
                )
            ]
            * 2,
            scratch_shapes=[pltpu.VMEM((rows, width), F32)],
        ),
        compiler_params=pltpu.CompilerParams(vmem_limit_bytes=room(16, own[0].shape[0])),
        cost_estimate=pl.CostEstimate(
            flops=4 * tokens * ff * width // SHARE,
            bytes_accessed=2 * (2 * tokens * (ff + width) + ff * width) // SHARE,
            transcendentals=0,
        ),
        name=name,
    )(where, a1, b1, a2, b2)


def own_kernel(where, w, out):
    out[...] = w[...]


def own_columns_call(where, w):
    depth, width = w.shape
    tile = width // 6
    return pl.pallas_call(
        own_kernel,
        out_shape=jax.ShapeDtypeStruct((depth, width // 2), w.dtype),
        grid_spec=pltpu.PrefetchScalarGridSpec(
            num_scalar_prefetch=1,
            grid=(2, 3),
            in_specs=[pl.BlockSpec((depth // 2, tile), lambda j, i, where: (j, 2 * i + where[1]))],
            out_specs=pl.BlockSpec((depth // 2, tile), lambda j, i, where: (j, i)),
        ),
        compiler_params=pltpu.CompilerParams(vmem_limit_bytes=12 * 2**20),
        cost_estimate=pl.CostEstimate(flops=0, bytes_accessed=2 * depth * width // SHARE, transcendentals=0),
        name="own_columns",
    )(where, w)


def product_kernel(*refs, dims, spans):
    parts = len(spans) if spans else 1
    total = None
    for i in range(parts):
        b = refs[parts]
        if spans:
            b = jnp.concatenate([b[:, low:high] for low, high in spans[i]], axis=1)
        else:
            b = b[...]
        part = dot(refs[i][...], b, dims)
        total = part if total is None else total + part
    for term in refs[parts + 1 : -1]:
        total = total + term[...]
    refs[-1][...] = total.astype(refs[-1].dtype)


def product(parts, b, dims, name, spans=None, terms=(), half=None):
    tile = 256 if sum(a.shape[1] for a in parts) > 2560 else 640
    turned = dims == NT
    rows = parts[0].shape[0] // (1 if half is None else 2)
    place = half or 0
    width = b.shape[0 if turned else 1]
    depth = sum(a.shape[1] for a in parts)
    ins = [
        pl.BlockSpec((rows, a.shape[1]), lambda i: (place, 0), pipeline_mode=pl.Buffered(1)) for a in parts
    ]
    if turned:
        ins.append(pl.BlockSpec((tile, b.shape[1]), lambda i: (i, 0)))
    else:
        ins.append(pl.BlockSpec((b.shape[0], tile), lambda i: (0, i)))
    return pl.pallas_call(
        functools.partial(product_kernel, dims=dims, spans=spans),
        out_shape=jax.ShapeDtypeStruct((rows, width), BF),
        grid=(width // tile,),
        in_specs=ins + [pl.BlockSpec((t.shape[0], tile), lambda i: (0, i)) for t in terms],
        out_specs=pl.BlockSpec((rows, tile), lambda i: (0, i)),
        compiler_params=pltpu.CompilerParams(vmem_limit_bytes=room(22, rows)),
        cost_estimate=pl.CostEstimate(
            flops=2 * rows * depth * width // SHARE,
            bytes_accessed=2 * (rows * depth + depth * width + rows * width) // SHARE,
            transcendentals=0,
        ),
        name=name,
    )(*parts, b, *terms)


def tile_flags(queries, keys, tq, tk):
    q_first, q_last = queries[:, ::tq], queries[:, tq - 1 :: tq]
    k_first, k_last = keys[:, ::tk], keys[:, tk - 1 :: tk]
    meet = (q_first[:, :, None] <= k_last[:, None, :]) & (k_first[:, None, :] <= q_last[:, :, None])
    whole = (
        (q_first == q_last)[:, :, None]
        & (k_first == k_last)[:, None, :]
        & (q_first[:, :, None] == k_first[:, None, :])
    )
    return jnp.where(whole, 2, jnp.where(meet, 1, 0)).astype(jnp.int32)


def layer_norm_parts(values):
    centred = values - jnp.mean(values, axis=-1, keepdims=True)
    rstd = lax.rsqrt(jnp.mean(centred * centred, axis=-1, keepdims=True) + EPS)
    return centred * rstd, rstd


def layer_norm_back(d_norm, gain, xhat, rstd):
    e = d_norm * gain
    return rstd * (
        e - jnp.mean(e, axis=-1, keepdims=True) - xhat * jnp.mean(e * xhat, axis=-1, keepdims=True)
    )


def on_device(
    tokens,
    cell_start,
    norm1_gain,
    norm1_bias,
    w_qkv,
    bias_q,
    bias_v,
    w_out,
    bias_out,
    norm2_gain,
    norm2_bias,
    w_in,
    bias_in,
    w_back,
    bias_back,
    cotangent,
):
    rows, seg, width = tokens.shape
    count = rows * seg
    ff = w_in.shape[1]
    half = width // 2
    wide = lax.axis_size("wide")
    group = lax.axis_size("blk")
    place = lax.axis_index("wide")
    member = lax.axis_index("blk")
    core = place % 2
    chips = wide // 2
    first = 2 if chips <= 8 else 4
    second = chips // first
    heads = HEADS // 2
    early = 6
    spans = ((0, early), (early, heads))
    tq, tk = min(512, seg), min(256, seg)
    halves = group == 2 and ff // chips % 128 == 0
    where = jnp.stack([place // 2, core, member]).astype(jnp.int32)
    where_out = jnp.stack([lax.bitwise_xor(place // 2, core * (chips // 2)), core, member]).astype(jnp.int32)

    def after(value, *earlier):
        return lax.optimization_barrier((value, earlier))[0]

    def across(array, by):
        return lax.ppermute(array, "wide", [(i, i ^ by) for i in range(wide)])

    def to_mate(array):
        return across(array, 1)

    def from_ahead(array, by):
        return lax.ppermute(array, "blk", [((i + by) % group, i) for i in range(group)])

    def to_ahead(array, by):
        return lax.ppermute(array, "blk", [(i, (i + by) % group) for i in range(group)])

    def from_all_ahead(array):
        parts = [from_ahead(array, by) for by in range(1, group)]
        return parts[0] if len(parts) == 1 else jnp.concatenate(parts, axis=1)

    def cut(array, start, size, axis):
        return lax.dynamic_slice_in_dim(array, start, size, axis)

    def paired(array):
        return jnp.concatenate([array, to_mate(array)], axis=0)

    inputs = tokens.astype(F32).reshape(count, width)
    xhat1, rstd1 = layer_norm_parts(inputs)
    acts = (xhat1 * norm1_gain + norm1_bias).astype(BF).reshape(tokens.shape)
    cells = paired(cell_start)
    far_cells = from_all_ahead(cells)
    acts = after(acts, far_cells)
    far_own = from_all_ahead(acts)
    acts_pair = paired(acts).reshape(2 * count, width)
    w_own = own_columns_call(where, w_qkv)
    b_own = jnp.concatenate([cut(bias_q, core * half, half, 0), jnp.zeros((half,), F32), cut(bias_v, core * half, half, 0)])

    def own_columns(span, parts):
        return tuple((part * half + span[0] * HD, part * half + span[1] * HD) for part in parts)

    near_spans = tuple(own_columns(span, (0, 1, 2)) for span in spans)
    far_spans = tuple(own_columns(span, (1, 2)) for span in spans)

    def columns(array):
        return jnp.broadcast_to(array[:, :, None], array.shape + (128,))

    qkv = (dot(acts_pair, w_own, NN) + b_own).astype(BF).reshape(2 * rows, seg, 3 * half)
    near_flags = tile_flags(cells, cells, tq, tk)
    far_flags = tile_flags(cells, far_cells, tq, tk)
    cell_rows = cells[:, None, :]
    near_columns, far_columns = columns(cells), columns(far_cells)
    state = attn_fwd(near_flags, cell_rows, near_columns, qkv, qkv, 1, None, tq, tk, heads)
    d_out = cotangent.reshape(count, width)
    d_out_mate = to_mate(after(d_out, acts_pair))
    far_own = after(far_own, state)
    far_mate = to_mate(far_own)
    d_act = dot(after(d_out, far_own, state, d_out_mate), w_back, NT).astype(BF)

    far_mate = after(far_mate, d_act)
    far_pair = jnp.concatenate([far_own, far_mate], axis=0)
    far_len = far_pair.shape[1]
    far_pair = far_pair.reshape(-1, width)
    far_kv = (dot(far_pair, w_own[:, half:], NN) + b_own[half:]).astype(BF).reshape(2 * rows, far_len, 2 * half)
    *attended, stats = attn_fwd(far_flags, cell_rows, far_columns, qkv, far_kv, 0, state, tq, tk, heads)
    mine, theirs = (part.reshape(count, half) for part in attended)
    own_rest = to_mate(theirs)
    mate_rest = to_mate(mine)
    w_out_own = cut(w_out, core * half, half, 0)
    w_out_mate = cut(w_out, (1 - core) * half, half, 0)
    middle = inputs + (dot(mine, w_out_own, NN) + dot(own_rest, w_out_mate, NN)) + bias_out

    xhat2, _ = layer_norm_parts(middle)
    acts2 = (xhat2 * norm2_gain + norm2_bias).astype(BF)
    acts2_mate = to_mate(acts2)
    b_in = bias_in.reshape(1, ff)
    act_part, d_pre_theirs, sum_part, norm_part = ffn_call(
        where, after(acts2, mate_rest), w_in, b_in, d_act, (), "ffn_theirs"
    )
    d_pre_mate = to_mate(d_pre_theirs)
    act, d_pre_mine, d_pre_sum, d_middle, d_z, d_att_theirs, d_att_mine, z_sums = ffn_call(
        where, acts2, w_in, b_in, d_act,
        (act_part, sum_part, norm_part, middle, d_out, w_out, norm2_gain.reshape(1, width)), "ffn_mine",
    )
    act_mate = to_mate(after(act, d_pre_mate, acts2_mate))
    grad_out = d_out.astype(F32)
    d_att_mate = to_mate(d_att_theirs)
    d_z_mate = to_mate(d_z)

    def send(parts):
        return [across(parts[one], 2 * one) for one in range(1, first)]

    def add_first(parts, received):
        def added(at):
            total = parts[0][at].astype(F32)
            for part in received:
                total = total + part[at].astype(F32)
            return total.astype(BF)

        return added(slice(0, second // 2)), added(slice(second // 2, second))

    def send_second(pair):
        return across(pair[1], first * second)

    def add_second(pair, received):
        return tuple((pair[0][at].astype(F32) + received[at].astype(F32)).astype(BF) for at in range(2))

    def send_third(pair):
        return across(pair[1], 2 * first)

    def add_third(pair, received):
        return (pair[0].astype(F32) + received.astype(F32)).astype(BF)

    def start(parts):
        return from_ahead(parts[1], 1) if halves else send(parts)

    def middle_step(parts, received):
        if not halves:
            return parts, received
        sums = [(parts[0][one].astype(F32) + received[one].astype(F32)).astype(BF) for one in range(first)]
        return sums, send(sums)

    def ahead(total):
        return from_ahead(total, 1) if group == 2 else None

    def over_row(total, other):
        if group == 2:
            return (total.astype(F32) + other.astype(F32)).astype(BF)
        return lax.psum(total, "blk")

    def by_core(total, other, sizes):
        if halves:
            kept = jnp.where(member == core, total, other)
            return kept, jnp.where(member == core, other, total)
        total = over_row(total, other)
        parts, at = [], 0
        for size in sizes:
            parts.append(total[at : at + size].reshape(2, size // 2, total.shape[1]))
            at += size
        split = jnp.concatenate(parts, axis=1)
        return (lax.dynamic_index_in_dim(split, i, 0, keepdims=False) for i in (core, 1 - core))

    def swap(split):
        kept, given = split
        other = to_mate(given)
        return jnp.where(core == 0, kept, other).astype(F32), jnp.where(core == 0, other, kept).astype(F32)

    d_pre_held = d_pre_mine
    grad_in = grad_call(
        where, [[(acts2, d_pre_held, 0), (acts2_mate, d_pre_mate, 0)]], ff // 2, first, second, 512, False, "grad_in"
    )
    in_in = send(grad_in)
    act_held, act_mate, d_z_mate = after((act, act_mate, d_z_mate), grad_in)

    def grad_o(into):
        return grad_call(
            where_out,
            [
                [(mine, d_z, None), (theirs, d_z_mate, None)],
                [(own_rest, d_z, None), (mate_rest, d_z_mate, None)],
            ],
            half, first, second, half, halves, "grad_out", into,
        )

    back_rows, out_rows = ff // chips, width // chips
    if halves:
        grad_b = back_call(
            where, (act_held, d_out), (act_mate, d_out_mate), first, second, out_rows // 2, "grad_back"
        )
        grad_b = grad_o(tuple(grad_b))
    else:
        whole = dot(act_held, cut(d_out, core * half, half, 1), TN) + dot(act_mate, cut(d_out_mate, core * half, half, 1), TN)
        whole = whole.astype(BF).reshape(chips, back_rows, half)
        grad_b = [
            jnp.concatenate([
                jnp.stack([whole[lax.bitwise_xor(two * first + one, where[0])] for two in range(second)]), other
            ], axis=1)
            for one, other in enumerate(grad_o(()))
        ]
    b_in = start(grad_b)

    back_tq = min(256, seg)
    near_flags, far_flags = tile_flags(cells, cells, back_tq, tk), tile_flags(cells, far_cells, back_tq, tk)
    d_att = after((d_att_mine.reshape(rows, seg, half), d_att_mate.reshape(rows, seg, half)), grad_b)
    d_qT, far_early, far_late = attn_bwd(
        far_flags, cell_rows, far_columns, qkv, far_kv, 0, d_att, attended, stats, None, back_tq, tk, heads, spans, "attn_bwd_far"
    )
    in_sums = add_first(grad_in, after(in_in, d_qT))
    in_more = send_second(in_sums)
    far_early, far_late = after((far_early, far_late), in_sums)
    far_early, far_late = (f.reshape(-1, f.shape[-1]) for f in (far_early, far_late))
    n_early, n_late = early * HD, (heads - early) * HD
    far_theirs = product([far_early, far_late], w_own, NT, "far_norm_theirs", far_spans, half=1)
    far_given = to_mate(far_theirs)
    far_mine = product([after(far_early, far_theirs), far_late], w_own, NT, "far_norm_mine", far_spans, half=0)
    far_sum = (far_mine.astype(F32) + after(far_given, in_sums, far_mine).astype(F32)).astype(BF)
    far_sum = far_sum.reshape(rows, far_len, width)
    far_back = [to_ahead(far_sum[:, by * seg : (by + 1) * seg], by + 1) for by in range(group - 1)]
    d_qT = after(d_qT, far_sum)

    def near_back(span, name, *earlier):
        (out,) = attn_bwd(
            near_flags, cell_rows, near_columns, qkv, qkv, 1, d_att, attended, stats, after(d_qT, earlier), back_tq, tk, heads,
            (span,), name,
        )
        return out.reshape(2 * count, -1)

    near_early = near_back(spans[0], "attn_bwd_early")
    b_sums, b_in = middle_step(grad_b, after(b_in, near_early))
    in_two = add_second(in_sums, after(in_more, b_sums))
    in_last = send_third(in_two)
    near_early = after(near_early, b_sums, in_two)
    *grad_e, sum_e = qkv_call(where, (acts_pair, near_early), (far_pair, far_early), first, second, halves, "grad_early")
    in_total = add_third(in_two, after(in_last, grad_e))
    in_row = ahead(in_total)
    grad_e, far_back = after((grad_e, far_back), in_total)
    e_in = start(grad_e)
    near_late = near_back(spans[1], "attn_bwd_late", grad_e, far_back)
    b_two = add_first(b_sums, after(b_in, near_late))
    b_more = send_second(b_two)
    e_sums, e_in = middle_step(grad_e, after(e_in, b_two))
    near_late = after(near_late, b_two, e_sums)
    *grad_l, sum_l = qkv_call(where, (acts_pair, near_late), (far_pair, far_late), first, second, halves, "grad_late")
    l_in = start(grad_l)
    near_held = after(near_early, grad_l)
    near_theirs = product([near_held, near_late], w_own, NT, "near_norm_theirs", near_spans, half=1)
    near_mine = product([after(near_held, near_theirs), near_late], w_own, NT, "near_norm_mine", near_spans, half=0)
    e_two = add_first(e_sums, after(e_in, near_mine))
    e_more = send_second(e_two)
    b_three = add_second(b_two, after(b_more, e_two))
    b_last = send_third(b_three)
    l_sums, l_in = middle_step(grad_l, after(l_in, b_three))
    near_given = to_mate(after(near_theirs, near_mine))
    in_row = after(in_row, near_mine)
    act_late = after(act_held, e_two, b_three, l_sums, in_row)
    mixed = product([act_late], w_back, NN, "mixed", terms=(middle, bias_back.reshape(1, width))).reshape(tokens.shape)
    l_two = add_first(l_sums, after(l_in, mixed))
    l_more = send_second(l_two)
    e_three = add_second(e_two, after(e_more, l_two))
    e_last = send_third(e_three)
    b_total = add_third(b_three, after(b_last, e_three))
    b_row = ahead(b_total)
    near_mine, near_given = after((near_mine, near_given), l_two, e_three, b_total)
    d_norm1 = near_mine.astype(F32) + near_given.astype(F32)
    for part in far_back:
        d_norm1 = d_norm1 + part.reshape(count, width).astype(F32)
    norm1_sums = (jnp.sum(d_norm1 * xhat1, axis=0), jnp.sum(d_norm1, axis=0))
    e_total = add_third(e_three, after(e_last, norm1_sums))
    e_row = ahead(e_total)
    l_three = add_second(l_two, after(l_more, e_total))
    l_last = send_third(l_three)
    xhat1 = after(xhat1, l_three, e_total)
    grad_tokens = (d_middle + layer_norm_back(d_norm1, norm1_gain, xhat1, rstd1)).reshape(tokens.shape)

    def vectors(parts, *covers):
        packed = jnp.concatenate([p.reshape(wide, -1) for p in parts], axis=1)
        total = packed
        covers = iter(covers)
        for stride, size in ((2 * first, second), (2, first), (1, 2)):
            total = total.reshape(-1, size, stride, packed.shape[1])
            spot = (place // stride) % size
            kept = lax.dynamic_index_in_dim(total, spot, 1, keepdims=False)
            given = [
                across(lax.dynamic_index_in_dim(total, spot ^ by, 1, keepdims=False), by * stride)
                for by in range(1, size)
            ]
            given = after(given, next(covers))
            for part in given:
                kept = kept + part
            total = kept.reshape(stride, packed.shape[1])
        total = total.reshape(-1)
        total = total + after(from_ahead(total, 1), next(covers)) if group == 2 else lax.psum(total, "blk")
        out, at = [], 0
        for p in parts:
            size = p.size // wide
            out.append(total[at : at + size])
            at += size
        return out

    def widened(part):
        n = sum_e.shape[1] // 3, sum_l.shape[1] // 3
        own = jnp.concatenate([s[0, part * m : (part + 1) * m] for s, m in zip((sum_e, sum_l), n)])
        return lax.dynamic_update_slice_in_dim(jnp.zeros((width,), F32), own, core * half, 0)

    in_low, in_high = swap(by_core(after(in_total, grad_tokens), in_row, [width // chips])) if not halves else (None, None)
    if halves:
        in_whole = over_row(after(in_total, grad_tokens), in_row).reshape(2, -1, in_total.shape[1])
        in_low, in_high = swap([lax.dynamic_index_in_dim(in_whole, i, 0, keepdims=False) for i in (core, 1 - core)])
    b_low, b_high = swap(by_core(after(b_total, grad_tokens), b_row, [back_rows, out_rows]))
    e_low, e_high = swap(by_core(after(e_total, grad_tokens), e_row, [out_rows]))
    l_total = add_third(l_three, after(l_last, grad_tokens))
    l_low, l_high = swap(by_core(l_total, ahead(l_total), [out_rows]))

    def part_columns(part):
        return [
            array[:, part * n : (part + 1) * n]
            for array, n in ((e_low, n_early), (l_low, n_late), (e_high, n_early), (l_high, n_late))
        ]

    share = ff // wide
    grad_w_in = jnp.concatenate([in_low, in_high], axis=1)
    grad_w_back = jnp.concatenate([b_low[:share], b_high[:share]], axis=1)
    grad_w_out = jnp.concatenate([b_low[share:], b_high[share:]], axis=1)
    small = vectors(
        [
            *norm1_sums,
            widened(0),
            widened(2),
            z_sums[0],
            z_sums[1],
            z_sums[2],
            d_pre_sum,
            jnp.sum(grad_out, axis=0),
        ],
        grad_tokens,
        grad_w_in,
        grad_w_back,
        grad_w_out,
    )
    return (
        mixed,
        grad_tokens,
        small[0],
        small[1],
        jnp.concatenate([piece for part in range(3) for piece in part_columns(part)], axis=1),
        small[2],
        small[3],
        grad_w_out,
        small[4],
        small[5],
        small[6],
        grad_w_in,
        small[7],
        grad_w_back,
        small[8],
    )


def solution(mesh):
    spread = P("wide", "blk", None)
    placed = (spread, P("wide", "blk")) + (P(),) * 13 + (spread,)
    matrix, vector = P("wide", None), P("wide")
    return jax.shard_map(
        on_device,
        mesh=mesh,
        in_specs=placed,
        out_specs=(
            spread, spread, vector, vector, matrix, vector, vector, matrix, vector, vector, vector,
            matrix, vector, matrix, vector,
        ),
        check_vma=False,
    )
```

```python
import functools
import math

import jax
import jax.numpy as jnp
from jax import lax
from jax.experimental import pallas as pl
from jax.experimental.pallas import tpu as pltpu
from jax.sharding import PartitionSpec as P

HEADS = 20
HEAD_DIM = 64
HD = HEAD_DIM
EPS = 1e-05
NEG = -1e30
LOG2E = math.log2(math.e)
C2 = LOG2E / math.sqrt(HEAD_DIM)
F32 = jnp.float32
BF = jnp.bfloat16
NN = (((1,), (0,)), ((), ()))
NT = (((1,), (1,)), ((), ()))
TN = (((0,), (0,)), ((), ()))
VMEM_LIMIT = 56 * 2**20
SHARE = 10
VR = HD + 16


def dot(a, b, dims):
    return lax.dot_general(a, b, dims, preferred_element_type=F32)


def own_map(nr,last):
    return lambda r,i,*_:(jnp.minimum(r,nr//2-1),jnp.where(r<nr//2,i,last-1),0)

def mate_map(nr):
    return lambda r,i,*_:(jnp.maximum(r-nr//2,0),jnp.where(r<nr//2,0,i),0)

def head_sumsq(x,hp16):
    W=x.shape[1]
    sq=x.astype(F32)*x.astype(F32)
    row=lax.broadcasted_iota(jnp.int32,(hp16,W),0); col=lax.broadcasted_iota(jnp.int32,(hp16,W),1)
    ones=jnp.where(row==col//HD,1.0,0.0).astype(BF)
    return lax.dot_general(ones,sq.astype(BF),NT,preferred_element_type=F32)

def fwd_kernel(flags,cq,ck,q,k,v,*rest,first,tq,tk,heads):
    if first:
        accT_o,m_o,l_o,qm,vT,bias,acc,m,l,kn=rest
    else:
        accT_i,m_i,l_i,o_own,o_mate,lse_o,qm,vT,bias,acc,m,l,kn=rest
    r=pl.program_id(0); qi=pl.program_id(1)
    nk=k.shape[1]//tk
    hp16=m.shape[0]
    @pl.when(qi==0)
    def _():
        for hh in range(heads):
            vT[hh*VR:hh*VR+HD,:]=v[0,:,hh*HD:(hh+1)*HD].T
            vT[hh*VR+HD:(hh+1)*VR,:]=jnp.ones((VR-HD,vT.shape[1]),BF)
        kn[...]=jnp.broadcast_to(jnp.sqrt(jnp.max(head_sumsq(k[0],hp16),1,keepdims=True)),kn.shape)
    lane=lax.broadcasted_iota(jnp.int32,(tq,128),1)
    for hp in range(heads//2):
        qp=q[0,:,hp*128:(hp+1)*128]
        qm[2*hp]=jnp.where(lane<64,qp,0).astype(BF)
        qm[2*hp+1]=jnp.where(lane>=64,qp,0).astype(BF)
    bound=jnp.sqrt(head_sumsq(q[0],hp16))*kn[:,0:1]*(C2*1.02)
    safe=jnp.max(bound)<50.0
    if first:
        m0=bound
    else:
        m0=jnp.maximum(bound,m_i[0])
    def loop(online):
        if first:
            acc[...]=jnp.zeros_like(acc); l[...]=jnp.zeros_like(l)
            m[...]=jnp.full_like(m,NEG) if online else m0
        elif online:
            acc[...]=accT_i[0]; m[...]=m_i[0]; l[...]=l_i[0]
        else:
            al=jnp.exp2(m_i[0]-m0)
            m[...]=m0; l[...]=al*l_i[0]
            for hh in range(heads):
                hs=slice(hh*HD,(hh+1)*HD)
                acc[hs,:]=al[hh:hh+1,:]*accT_i[0,hs,:]
        def body(kt,masked):
            ks=pl.ds(pl.multiple_of(kt*tk,tk),tk)
            if online:
                @pl.loop(0,heads//2)
                def _(hp):
                    kp=k[0,ks,pl.ds(pl.multiple_of(hp*128,128),128)]
                    for j in range(2):
                        hh=2*hp+j
                        s=lax.dot_general(kp,qm[hh],NT,preferred_element_type=F32)*C2+bias[...]
                        mp=m[pl.ds(hh,1),:]
                        mn=jnp.maximum(mp,jnp.max(s,0,keepdims=True))
                        p=jnp.exp2(s-mn)
                        al=jnp.exp2(mp-mn)
                        m[pl.ds(hh,1),:]=mn
                        l[pl.ds(hh,1),:]=al*l[pl.ds(hh,1),:]+jnp.sum(p,0,keepdims=True)
                        hs=pl.ds(pl.multiple_of(hh*HD,HD),HD)
                        vs=pl.ds(pl.multiple_of(hh*VR,16),HD)
                        acc[hs,:]=al*acc[hs,:]+lax.dot_general(vT[vs,ks],p.astype(BF),NN,preferred_element_type=F32)
                return
            def score(hh):
                s=lax.dot_general(k[0,ks,(hh//2)*128:(hh//2+1)*128],qm[hh],NT,preferred_element_type=F32)*C2
                if masked: s=s+bias[...]
                return s
            s=score(0); pp=None
            for hh in range(heads+1):
                if hh+1<heads: sn=score(hh+1)
                if pp is not None:
                    h1=hh-1
                    both=lax.dot_general(vT[h1*VR:(h1+1)*VR,ks],pp,NN,preferred_element_type=F32)
                    acc[h1*HD:(h1+1)*HD,:]+=both[:HD]
                    l[h1:h1+1,:]+=both[HD:HD+1]
                if hh<heads:
                    p=jnp.exp2(s-m[hh:hh+1,:])
                    pp=p.astype(BF)
                s=sn
        @pl.loop(0,nk)
        def _(kt):
            f=flags[r,qi,kt]
            def mask():
                ks=pl.ds(pl.multiple_of(kt*tk,tk),tk)
                bias[...]=jnp.where(ck[0,ks,0:1]==cq[0,0:1,:],0.0,NEG)
            if online:
                @pl.when(f>0)
                def _():
                    mask(); body(kt,True)
            else:
                @pl.when(f==1)
                def _():
                    mask(); body(kt,True)
                @pl.when(f==2)
                def _(): body(kt,False)
    @pl.when(safe)
    def _(): loop(False)
    @pl.when(jnp.logical_not(safe))
    def _(): loop(True)
    if first:
        accT_o[0]=acc[...]; m_o[0]=m[...]; l_o[0]=l[...]
    else:
        for hp in range(heads//2):
            parts=[]
            for hh in (2*hp,2*hp+1):
                parts.append(acc[hh*HD:(hh+1)*HD,:]/l[hh:hh+1,:])
            low=jnp.concatenate(parts,0).T.astype(BF)
            @pl.when(r<pl.num_programs(0)//2)
            def _(): o_own[0,:,hp*128:(hp+1)*128]=low
            @pl.when(r>=pl.num_programs(0)//2)
            def _(): o_mate[0,:,hp*128:(hp+1)*128]=low
        lse_o[0]=m[...]+jnp.log2(l[...])

def attn_fwd(flags,cq,ck,q,kv,kb,state,tq,tk,heads):
    nr,S,_=q.shape; W=heads*HD; Sk=kv.shape[1]; hp16=-(-heads//8)*8
    first=state is None
    qs=lambda r,i,*_:(r,i,0); ts=lambda r,i,*_:(r,0,i); ks=lambda r,i,*_:(r,0,0)
    stspec=[pl.BlockSpec((1,W,tq),ts),pl.BlockSpec((1,hp16,tq),ts),pl.BlockSpec((1,hp16,tq),ts)]
    ins=[pl.BlockSpec((1,1,tq),ts),pl.BlockSpec((1,Sk,128),ks),pl.BlockSpec((1,tq,W),qs),pl.BlockSpec((1,Sk,W),lambda r,i,*_:(r,0,kb)),pl.BlockSpec((1,Sk,W),lambda r,i,*_:(r,0,kb+1))]
    if first:
        outs=stspec
        osh=[jax.ShapeDtypeStruct((nr,W,S),F32)]+[jax.ShapeDtypeStruct((nr,hp16,S),F32)]*2
    else:
        ins=ins+stspec
        outs=[pl.BlockSpec((1,tq,W),own_map(nr,S//tq)),pl.BlockSpec((1,tq,W),mate_map(nr)),pl.BlockSpec((1,hp16,tq),ts)]
        osh=[jax.ShapeDtypeStruct((nr//2,S,W),BF)]*2+[jax.ShapeDtypeStruct((nr,hp16,S),F32)]
    fl=4*nr*S*Sk*W
    return pl.pallas_call(functools.partial(fwd_kernel,first=first,tq=tq,tk=tk,heads=heads),
        out_shape=osh,
        grid_spec=pltpu.PrefetchScalarGridSpec(num_scalar_prefetch=1,grid=(nr,S//tq),in_specs=ins,out_specs=outs,
          scratch_shapes=[pltpu.VMEM((heads,tq,128),BF),pltpu.VMEM((heads*VR,Sk),BF),pltpu.VMEM((tk,tq),F32),pltpu.VMEM((W,tq),F32),pltpu.VMEM((hp16,tq),F32),pltpu.VMEM((hp16,tq),F32),pltpu.VMEM((hp16,128),F32)]),
        compiler_params=pltpu.CompilerParams(dimension_semantics=("arbitrary","arbitrary"),vmem_limit_bytes=VMEM_LIMIT),
        cost_estimate=pl.CostEstimate(flops=fl//SHARE,bytes_accessed=nr*(S*W*2+2*Sk*W*2+S*W*4)//SHARE,transcendentals=0),
        name="attn_fwd_a" if first else "attn_fwd_b",
    )(flags,cq,ck,q,kv,kv,*(state or ()))

def bwd_kernel(flags,cq,ck,q,k,v,do_own,do_mate,o_own,o_mate,lse,*rest,spans,tq,tk):
    first=len(spans)==2
    if first:
        dqT_o,*dkv_o,qm,dom,kT,bias,dqT,dk,dv,delta=rest
    else:
        dqT_i,dqkv_o,qm,dom,kT,bias,dqT,dk,dv,delta=rest
    r=pl.program_id(0); qi=pl.program_id(1); nq=pl.num_programs(1)
    nk=k.shape[1]//tk
    low=spans[0][0]; heads=sum(b-a for a,b in spans)
    W=heads*HD; c0=low*HD
    @pl.when(qi==0)
    def _():
        kT[...]=k[0,:,c0:c0+W].T
        dk[...]=jnp.zeros_like(dk); dv[...]=jnp.zeros_like(dv)
    own=r<pl.num_programs(0)//2
    lane=lax.broadcasted_iota(jnp.int32,(tq,128),1)
    for hp in range(heads//2):
        c=slice(c0+hp*128,c0+(hp+1)*128)
        qp=q[0,:,c]*jnp.asarray(0.125,BF); dp_=jnp.where(own,do_own[0,:,c],do_mate[0,:,c])
        qm[2*hp]=jnp.where(lane<64,qp,0).astype(BF)
        qm[2*hp+1]=jnp.where(lane>=64,qp,0).astype(BF)
        dom[2*hp]=jnp.where(lane<64,dp_,0).astype(BF)
        dom[2*hp+1]=jnp.where(lane>=64,dp_,0).astype(BF)
    prod=jnp.where(own,do_own[0,:,c0:c0+W],do_mate[0,:,c0:c0+W]).astype(F32)*jnp.where(own,o_own[0,:,c0:c0+W],o_mate[0,:,c0:c0+W]).astype(F32)
    hi=prod.astype(BF); lo=(prod-hi.astype(F32)).astype(BF)
    n16=delta.shape[0]
    row=lax.broadcasted_iota(jnp.int32,(n16,W),0); col_=lax.broadcasted_iota(jnp.int32,(n16,W),1)
    ones=jnp.where(row==col_//HD,1.0,0.0).astype(BF)
    delta[...]=lax.dot_general(ones,hi,NT,preferred_element_type=F32)+lax.dot_general(ones,lo,NT,preferred_element_type=F32)
    if first: dqT[...]=jnp.zeros_like(dqT)
    else: dqT[...]=dqT_i[0,c0:c0+W,:]
    def body(kt):
        ks=pl.ds(pl.multiple_of(kt*tk,tk),tk)
        def col(hh): return slice((hh//2)*128,(hh//2+1)*128)
        def wide(hh): return slice(c0+(hh//2)*128,c0+(hh//2+1)*128)
        def score(hh):
            s=lax.dot_general(k[0,ks,wide(hh)],qm[hh],NT,preferred_element_type=F32)*LOG2E+bias[...]
            return s,lax.dot_general(v[0,ks,wide(hh)],dom[hh],NT,preferred_element_type=F32)
        nxt=score(0); prev=None
        for hh in range(heads+1):
            cur=nxt
            if hh+1<heads: nxt=score(hh+1)
            if prev is not None:
                h1=hh-1; pb,dsb=prev
                hs=slice(h1*HD,(h1+1)*HD)
                dqT[hs,:]+=lax.dot_general(kT[hs,ks],dsb,NN,preferred_element_type=F32)
                dv[ks,col(h1)]+=jnp.dot(pb,dom[h1],preferred_element_type=F32)
                dk[ks,col(h1)]+=jnp.dot(dsb,qm[h1],preferred_element_type=F32)
            if hh<heads:
                s,dp=cur
                at=low+hh
                p=jnp.exp2(s-lse[0,at:at+1,:])
                ds=p*(dp-delta[hh:hh+1,:])
                prev=(p.astype(BF),ds.astype(BF))
    @pl.loop(0,nk)
    def _(kt):
        f=flags[r,qi,kt]
        @pl.when(f>0)
        def _():
            ks=pl.ds(pl.multiple_of(kt*tk,tk),tk)
            bias[...]=jnp.where(ck[0,ks,0:1]==cq[0,0:1,:],0.0,NEG)
            body(kt)
    if first: dqT_o[0]=dqT[...]
    else: dqkv_o[0,pl.ds(pl.multiple_of(qi*tq,tq),tq),0:W]=(dqT[...]*0.125).T.astype(BF)
    @pl.when(qi==nq-1)
    def _():
        if first:
            for (a,b),out in zip(spans,dkv_o):
                n=(b-a)*HD; at=(a-low)*HD
                out[0,:,0:n]=dk[:,at:at+n].astype(BF); out[0,:,n:2*n]=dv[:,at:at+n].astype(BF)
        else:
            dqkv_o[0,:,W:2*W]=dk[...].astype(BF); dqkv_o[0,:,2*W:3*W]=dv[...].astype(BF)

def attn_bwd(flags,cq,ck,q,kv,kb,do,o,lse,dqT,tq,tk,full,spans,name):
    nr,S,_=q.shape; F=full*HD; Sk=kv.shape[1]; n16=lse.shape[1]
    heads=sum(b-a for a,b in spans); W=heads*HD
    first=dqT is None
    qs=lambda r,i,*_:(r,i,0); ts=lambda r,i,*_:(r,0,i); ks=lambda r,i,*_:(r,0,0)
    ins=[pl.BlockSpec((1,1,tq),ts),pl.BlockSpec((1,Sk,128),ks),pl.BlockSpec((1,tq,F),qs),pl.BlockSpec((1,Sk,F),lambda r,i,*_:(r,0,kb)),pl.BlockSpec((1,Sk,F),lambda r,i,*_:(r,0,kb+1)),
         *[pl.BlockSpec((1,tq,F),own_map(nr,S//tq)),pl.BlockSpec((1,tq,F),mate_map(nr))]*2,pl.BlockSpec((1,n16,tq),ts)]
    if first:
        widths=[2*(b-a)*HD for a,b in spans]
        outs=[pl.BlockSpec((1,F,tq),ts)]+[pl.BlockSpec((1,Sk,n),ks) for n in widths]
        osh=[jax.ShapeDtypeStruct((nr,F,S),F32)]+[jax.ShapeDtypeStruct((nr,Sk,n),BF) for n in widths]
        extra=()
    else:
        ins=ins+[pl.BlockSpec((1,F,tq),ts)]
        outs=[pl.BlockSpec((1,Sk,3*W),ks)]; osh=[jax.ShapeDtypeStruct((nr,Sk,3*W),BF)]
        extra=(dqT,)
    fl=10*nr*S*Sk*W
    return pl.pallas_call(functools.partial(bwd_kernel,spans=spans,tq=tq,tk=tk),
        out_shape=osh,
        grid_spec=pltpu.PrefetchScalarGridSpec(num_scalar_prefetch=1,grid=(nr,S//tq),in_specs=ins,out_specs=outs,
          scratch_shapes=[pltpu.VMEM((heads,tq,128),BF),pltpu.VMEM((heads,tq,128),BF),pltpu.VMEM((W,Sk),BF),pltpu.VMEM((tk,tq),F32),pltpu.VMEM((W,tq),F32),
             pltpu.VMEM((Sk,W),F32),pltpu.VMEM((Sk,W),F32),pltpu.VMEM((n16,tq),F32)]),
        compiler_params=pltpu.CompilerParams(dimension_semantics=("arbitrary","arbitrary"),vmem_limit_bytes=VMEM_LIMIT),
        cost_estimate=pl.CostEstimate(flops=fl//SHARE,bytes_accessed=nr*(3*S*W*2+4*Sk*W*2+S*W*4)//SHARE,transcendentals=0),
        name=name,
    )(flags,cq,ck,q,kv,kv,*do,*o,lse,*extra)


def ffn_kernel(where, acts, w, b, d_act, *rest, last):
    step = pl.program_id(0)
    final = pl.num_programs(0) - 1
    rows, width = acts.shape
    chunk = min(256, rows)
    count = rows // chunk
    if last:
        ins, outs, scratch = rest[:7], rest[7:15], rest[15:]
        _, _, acc_i, middle_i, d_out_i, w_out_i, gain = ins
        act_o, d_pre_o, sum_o, mid_o, d_z_o, theirs_o, mine_o, sums_o = outs
        acc, part, middle, d_out, w_out, d_z, att, in_sem, out_sem = scratch
        loads = [
            pltpu.make_async_copy(source, target, in_sem.at[n])
            for n, (source, target) in enumerate(
                ((acc_i, part), (middle_i, middle), (d_out_i, d_out), (w_out_i, w_out))
            )
        ]

        @pl.when(step == 0)
        def _():
            for load in loads:
                load.start()
    else:
        act_o, d_pre_o, sum_o, acc = rest

    @pl.when(step == 0)
    def _():
        acc[...] = jnp.zeros_like(acc)

    def span(i):
        return slice(i * chunk, (i + 1) * chunk)

    def product(i):
        return dot(acts[span(i), :], w[...], NN) + b[...]

    pre = product(0)
    total, held = None, None
    for i in range(count + 1):
        following = product(i + 1) if i + 1 < count else None
        if held is not None:
            acc[span(i - 1), :] += dot(held, w[...], NT)
        if i < count:
            at = span(i)
            cdf = 0.5 + 0.5 * lax.erf(pre * math.sqrt(0.5))
            pdf = jnp.exp(-0.5 * pre * pre) * (1.0 / math.sqrt(2.0 * math.pi))
            act_o[at, :] = (pre * cdf).astype(BF)
            held = (d_act[at, :].astype(F32) * (cdf + pre * pdf)).astype(BF)
            d_pre_o[at, :] = held
            summed = jnp.sum(held.astype(F32), axis=0, keepdims=True)
            total = summed if total is None else total + summed
        pre = following
    sum_o[...] = total
    if not last:
        return

    @pl.when(step == final)
    def _():
        for load in loads:
            load.wait()
        half = width // 2
        sums, stores = None, []
        for i in range(count):
            at = span(i)
            d_norm = acc[at, :] + part[at, :]
            xhat, rstd = layer_norm_parts(middle[at, :])
            d_mid = d_out[at, :].astype(F32) + layer_norm_back(d_norm, gain[...], xhat, rstd)
            low = d_mid.astype(BF)
            part[at, :] = d_mid
            d_z[at, :] = low
            for side in range(2):
                first = pl.multiple_of(lax.bitwise_xor(where[1], 1 - side) * half, half)
                att[side, at, :] = dot(low, w_out[pl.ds(first, half), :], NT).astype(BF)
            new = [low.astype(F32), d_norm * xhat, d_norm]
            new = jnp.concatenate([jnp.sum(n, axis=0, keepdims=True) for n in new], axis=0)
            sums = new if sums is None else sums + new
            pairs = ((part, mid_o), (d_z, d_z_o), (att.at[0], theirs_o), (att.at[1], mine_o))
            for n, (source, target) in enumerate(pairs):
                store = pltpu.make_async_copy(
                    source.at[pl.ds(i * chunk, chunk)], target.at[pl.ds(i * chunk, chunk)], out_sem.at[4 * i + n]
                )
                store.start()
                stores.append(store)
        sums_o[0:3, :] = sums
        sums_o[3:8, :] = jnp.zeros((5, width), F32)
        for store in stores:
            store.wait()


def ffn_call(where, acts, w, b, d_act, earlier, name):
    rows, width = acts.shape
    ff = w.shape[1]
    tile = 512
    steps = ff // 2 // tile
    last = bool(earlier)
    chunk = min(256, rows)

    def place(i, where):
        return (where[1] if last else 1 - where[1]) * steps + i

    col = lambda i, where: (0, place(i, where))
    whole = pl.BlockSpec((rows, width), lambda i, where: (0, 0))
    anywhere = pl.BlockSpec(memory_space=pl.ANY)
    out_shape = [
        jax.ShapeDtypeStruct((rows, ff), BF),
        jax.ShapeDtypeStruct((rows, ff // 2), BF),
        jax.ShapeDtypeStruct((1, ff), F32),
    ]
    out_specs = [
        pl.BlockSpec((rows, tile), col),
        pl.BlockSpec((rows, tile), lambda i, where: (0, i)),
        pl.BlockSpec((1, tile), col),
    ]
    ins = [
        pl.BlockSpec((rows, width), lambda i, where: (0, 0), pipeline_mode=pl.Buffered(1)),
        pl.BlockSpec((width, tile), col),
        pl.BlockSpec((1, tile), col),
        pl.BlockSpec((rows, tile), col),
    ]
    scratch = []
    if last:
        ins += [anywhere] * 6 + [pl.BlockSpec((1, width), lambda i, where: (0, 0))]
        out_shape += [
            jax.ShapeDtypeStruct((rows, width), F32),
            jax.ShapeDtypeStruct((rows, width), BF),
            jax.ShapeDtypeStruct((rows, width // 2), BF),
            jax.ShapeDtypeStruct((rows, width // 2), BF),
            jax.ShapeDtypeStruct((8, width), F32),
        ]
        out_specs += [anywhere] * 4 + [pl.BlockSpec((8, width), lambda i, where: (0, 0))]
        scratch = [
            pltpu.VMEM((rows, width), F32),
            pltpu.VMEM((rows, width), F32),
            pltpu.VMEM((rows, width), F32),
            pltpu.VMEM((rows, width), BF),
            pltpu.VMEM((width, width), BF),
            pltpu.VMEM((rows, width), BF),
            pltpu.VMEM((2, rows, width // 2), BF),
            pltpu.SemaphoreType.DMA((4,)),
            pltpu.SemaphoreType.DMA((4 * (rows // chunk),)),
        ]
    else:
        out_shape.append(jax.ShapeDtypeStruct((rows, width), F32))
        out_specs.append(whole)
    return pl.pallas_call(
        functools.partial(ffn_kernel, last=last),
        out_shape=out_shape,
        grid_spec=pltpu.PrefetchScalarGridSpec(
            num_scalar_prefetch=1, grid=(steps,), in_specs=ins, out_specs=out_specs, scratch_shapes=scratch
        ),
        input_output_aliases={5: 0, 6: 2} if last else {},
        compiler_params=pltpu.CompilerParams(vmem_limit_bytes=VMEM_LIMIT),
        cost_estimate=pl.CostEstimate(
            flops=2 * rows * width * ff // SHARE,
            bytes_accessed=(2 * rows * width + width * ff + 3 * rows * ff) // SHARE,
            transcendentals=0,
        ),
        name=name,
    )(where, acts, w, b, d_act, *earlier)


def store_blocks(where, acc, outs, first, second, halved):
    rows = acc.shape[0] // (first * second)
    for one in range(first):
        for two in range(second):
            block = lax.bitwise_xor(two * first + one, where[0]) * rows
            if halved:
                for part in range(2):
                    at = block + lax.bitwise_xor(where[2], part) * (rows // 2)
                    piece = acc[pl.ds(pl.multiple_of(at, 16), rows // 2), :]
                    outs[part][one, two] = piece.astype(BF)
            else:
                outs[one][two] = acc[pl.ds(pl.multiple_of(block, 16), rows), :].astype(BF)


def grad_kernel(where, *refs, groups, first, second, halved, outs):
    acc = refs[-1]
    ins = refs[: sum(2 * g for g in groups)]
    height = acc.shape[0] // len(groups)
    at = 0
    for index, pairs in enumerate(groups):
        total = None
        for _ in range(pairs):
            part = dot(ins[at][...], ins[at + 1][...], TN)
            total = part if total is None else total + part
            at += 2
        acc[index * height : (index + 1) * height, :] = total
    store_blocks(where, acc, refs[-1 - outs : -1], first, second, halved)


def grad_call(where, groups, width, first, second, tile, halved, name, into=()):
    ins, flat, depth = [], [], 0
    for group in groups:
        for a, b, offset in group:
            ins.append(pl.BlockSpec(a.shape, lambda i, where: (0, 0)))
            if offset is None:
                index = lambda i, where: (0, where[1] * (width // tile) + i)
            else:
                index = lambda i, where, offset=offset: (0, offset // tile + i)
            ins.append(pl.BlockSpec((b.shape[0], tile), index))
            flat += [a, b]
            depth += a.shape[0]
    height = sum(g[0][0].shape[1] for g in groups)
    depth = depth // len(groups)
    rows = height // (first * second)
    if halved:
        shape, block = (first, second, rows // 2, width), (first, second, rows // 2, tile)
        outs = 2
        index = lambda i, where: (0, 0, 0, i)
    else:
        shape, block = (second, rows, width), (second, rows, tile)
        outs = first
        index = lambda i, where: (0, 0, i)
    if into:
        shape = into[0].shape
        row = shape[2] * 2 // rows - 1
        index = lambda i, where: (0, 0, row, i)
    return pl.pallas_call(
        functools.partial(
            grad_kernel, groups=[len(g) for g in groups], first=first, second=second, halved=halved, outs=outs
        ),
        out_shape=[jax.ShapeDtypeStruct(shape, BF)] * outs,
        grid_spec=pltpu.PrefetchScalarGridSpec(
            num_scalar_prefetch=1,
            grid=(width // tile,),
            in_specs=ins + [pl.BlockSpec(memory_space=pl.ANY)] * len(into),
            out_specs=[pl.BlockSpec(block, index)] * outs,
            scratch_shapes=[pltpu.VMEM((height, tile), F32)],
        ),
        input_output_aliases={1 + len(flat) + i: i for i in range(len(into))},
        compiler_params=pltpu.CompilerParams(vmem_limit_bytes=VMEM_LIMIT),
        cost_estimate=pl.CostEstimate(
            flops=2 * depth * height * width // SHARE,
            bytes_accessed=2 * (depth * (height + width) + height * width) // SHARE,
            transcendentals=0,
        ),
        name=name,
    )(where, *flat, *into)


def qkv_kernel(where, near_a, near_b, far_a, far_b, *refs, first, second, halved):
    *outs, sum_o, acc = refs
    acc[...] = dot(near_a[...], near_b[...], TN)
    sum_o[...] = jnp.sum(near_b[...].astype(F32), axis=0, keepdims=True)

    @pl.when(pl.program_id(0) > 0)
    def _():
        acc[...] += dot(far_a[...], far_b[...], TN)
        sum_o[...] += jnp.sum(far_b[...].astype(F32), axis=0, keepdims=True)

    store_blocks(where, acc, outs, first, second, halved)


def qkv_call(where, near, far, first, second, halved, name):
    (near_a, near_b), (far_a, far_b) = near, far
    height = near_a.shape[1]
    width = near_b.shape[1]
    tile = width // 3
    rows = height // (first * second)
    if halved:
        shape, block = (first, second, rows // 2, width), (first, second, rows // 2, tile)
        outs = 2
        index = lambda i, where: (0, 0, 0, i)
    else:
        shape, block = (second, rows, width), (second, rows, tile)
        outs = first
        index = lambda i, where: (0, 0, i)
    once = pl.Buffered(1)
    return pl.pallas_call(
        functools.partial(qkv_kernel, first=first, second=second, halved=halved),
        out_shape=[jax.ShapeDtypeStruct(shape, BF)] * outs + [jax.ShapeDtypeStruct((1, width), F32)],
        grid_spec=pltpu.PrefetchScalarGridSpec(
            num_scalar_prefetch=1,
            grid=(3,),
            in_specs=[
                pl.BlockSpec(near_a.shape, lambda i, where: (0, 0), pipeline_mode=once),
                pl.BlockSpec((near_b.shape[0], tile), lambda i, where: (0, i)),
                pl.BlockSpec(far_a.shape, lambda i, where: (0, 0), pipeline_mode=once),
                pl.BlockSpec((far_b.shape[0], tile), lambda i, where: (0, jnp.maximum(i - 1, 0))),
            ],
            out_specs=[pl.BlockSpec(block, index)] * outs + [pl.BlockSpec((1, tile), lambda i, where: (0, i))],
            scratch_shapes=[pltpu.VMEM((height, tile), F32)],
        ),
        compiler_params=pltpu.CompilerParams(vmem_limit_bytes=VMEM_LIMIT),
        cost_estimate=pl.CostEstimate(
            flops=2 * (near_a.shape[0] + far_a.shape[0]) * height * width // SHARE,
            bytes_accessed=2 * ((near_a.shape[0] + far_a.shape[0]) * (height + width) + height * width) // SHARE,
            transcendentals=0,
        ),
        name=name,
    )(where, near_a, near_b, far_a, far_b)


def back_kernel(where, a1, b1, a2, b2, out1, out2, acc):
    acc[...] = dot(a1[...], b1[...], TN) + dot(a2[...], b2[...], TN)
    rows = acc.shape[0] // 2
    for part, out in enumerate((out1, out2)):
        at = lax.bitwise_xor(where[2], part) * rows
        out[0, 0] = acc[pl.ds(pl.multiple_of(at, 16), rows), :].astype(BF)


def back_call(where, own, mate, first, second, extra, name):
    (a1, b1), (a2, b2) = own, mate
    tokens, ff = a1.shape
    rows = ff // (first * second)
    width = b2.shape[1] // 2

    def block(i, where):
        return (0, lax.bitwise_xor(lax.rem(i, second) * first + i // second, where[0]))

    return pl.pallas_call(
        back_kernel,
        out_shape=[jax.ShapeDtypeStruct((first, second, rows // 2 + extra, width), BF)] * 2,
        grid_spec=pltpu.PrefetchScalarGridSpec(
            num_scalar_prefetch=1,
            grid=(first * second,),
            in_specs=[
                pl.BlockSpec((tokens, rows), block),
                pl.BlockSpec((tokens, width), lambda i, where: (0, where[1])),
                pl.BlockSpec((tokens, rows), block),
                pl.BlockSpec((tokens, width), lambda i, where: (0, where[1])),
            ],
            out_specs=[
                pl.BlockSpec(
                    (1, 1, rows // 2, width), lambda i, where: (i // second, lax.rem(i, second), 0, 0)
                )
            ]
            * 2,
            scratch_shapes=[pltpu.VMEM((rows, width), F32)],
        ),
        compiler_params=pltpu.CompilerParams(vmem_limit_bytes=VMEM_LIMIT),
        cost_estimate=pl.CostEstimate(
            flops=4 * tokens * ff * width // SHARE,
            bytes_accessed=2 * (2 * tokens * (ff + width) + ff * width) // SHARE,
            transcendentals=0,
        ),
        name=name,
    )(where, a1, b1, a2, b2)


def pack_kernel(where, in_mine, in_row, b_mine, b_row, q_mine, q_row, *outs):
    core, member = where[1], where[2]
    half = outs[0].shape[1]
    rows = in_mine.shape[0] // 2
    blocks, thirds = in_mine.shape[1] // half, q_mine.shape[1] // half
    for side, out in enumerate(outs):
        at = pl.ds(pl.multiple_of(lax.bitwise_xor(core, side) * rows, 16), rows)
        whole = (in_mine[at, :].astype(F32) + in_row[at, :].astype(F32)).astype(BF)
        for i in range(blocks):
            out[i * rows : (i + 1) * rows, :] = whole[:, i * half : (i + 1) * half]
        mine = lax.bitwise_xor(core, side) == member
        first = blocks * rows
        out[first : first + b_mine.shape[0], :] = jnp.where(mine, b_mine[...], b_row[...])
        first += b_mine.shape[0]
        q = jnp.where(mine, q_mine[...], q_row[...])
        for i in range(thirds):
            out[first + i * rows : first + (i + 1) * rows, :] = q[:, i * half : (i + 1) * half]


def pack_call(where, in_pair, b_pair, q_pair):
    half = b_pair[0].shape[1]
    rows = in_pair[0].shape[0] // 2
    height = rows * (in_pair[0].shape[1] + q_pair[0].shape[1]) // half + b_pair[0].shape[0]
    return pl.pallas_call(
        pack_kernel,
        out_shape=[jax.ShapeDtypeStruct((height, half), BF)] * 2,
        grid_spec=pltpu.PrefetchScalarGridSpec(
            num_scalar_prefetch=1,
            grid=(1,),
            in_specs=[
                pl.BlockSpec(a.shape, lambda i, where: (0, 0)) for pair in (in_pair, b_pair, q_pair) for a in pair
            ],
            out_specs=[pl.BlockSpec((height, half), lambda i, where: (0, 0))] * 2,
        ),
        compiler_params=pltpu.CompilerParams(vmem_limit_bytes=20 * 2**20),
        cost_estimate=pl.CostEstimate(flops=0, bytes_accessed=8 * height * half // SHARE, transcendentals=0),
        name="pack",
    )(where, *in_pair, *b_pair, *q_pair)


def unpack_kernel(where, kept, other, in_o, back_o, out_o, qkv_o, *, groups):
    core = where[1]
    half = kept.shape[1]
    rows, share = in_o.shape[0], back_o.shape[0]
    for side in range(2):
        own = (core == side).astype(F32)
        whole = jnp.where(own > 0.5, kept[...], other[...]).astype(F32)
        at = 0
        for i in range(in_o.shape[1] // 2 // half):
            first = side * (in_o.shape[1] // 2) + i * half
            in_o[:, first : first + half] = whole[at : at + rows]
            at += rows
        back_o[:, side * half : (side + 1) * half] = whole[at : at + share]
        at += share
        out_o[:, side * half : (side + 1) * half] = whole[at : at + rows]
        at += rows
        line = jnp.concatenate([whole[at + i * rows : at + (i + 1) * rows] for i in range(3)], axis=1)
        start, place = 0, 0
        for n in groups:
            for part in range(3):
                to = part * 2 * half + side * half + place
                qkv_o[:, to : to + n] = line[:, start + part * n : start + (part + 1) * n]
            start, place = start + 3 * n, place + n


def unpack_call(where, kept, other, shapes, groups):
    return pl.pallas_call(
        functools.partial(unpack_kernel, groups=groups),
        out_shape=[jax.ShapeDtypeStruct(shape, F32) for shape in shapes],
        grid_spec=pltpu.PrefetchScalarGridSpec(
            num_scalar_prefetch=1,
            grid=(1,),
            in_specs=[pl.BlockSpec(kept.shape, lambda i, where: (0, 0))] * 2,
            out_specs=[pl.BlockSpec(shape, lambda i, where: (0, 0)) for shape in shapes],
        ),
        compiler_params=pltpu.CompilerParams(vmem_limit_bytes=24 * 2**20),
        cost_estimate=pl.CostEstimate(flops=0, bytes_accessed=12 * kept.size // SHARE, transcendentals=0),
        name="unpack",
    )(where, kept, other)


def own_kernel(where, w, out):
    out[...] = w[...]


def own_columns_call(where, w):
    depth, width = w.shape
    tile = width // 6
    return pl.pallas_call(
        own_kernel,
        out_shape=jax.ShapeDtypeStruct((depth, width // 2), w.dtype),
        grid_spec=pltpu.PrefetchScalarGridSpec(
            num_scalar_prefetch=1,
            grid=(2, 3),
            in_specs=[pl.BlockSpec((depth // 2, tile), lambda j, i, where: (j, 2 * i + where[1]))],
            out_specs=pl.BlockSpec((depth // 2, tile), lambda j, i, where: (j, i)),
        ),
        compiler_params=pltpu.CompilerParams(vmem_limit_bytes=12 * 2**20),
        cost_estimate=pl.CostEstimate(flops=0, bytes_accessed=2 * depth * width // SHARE, transcendentals=0),
        name="own_columns",
    )(where, w)


def product_kernel(*refs, dims, spans):
    parts = len(spans) if spans else 1
    total = None
    for i in range(parts):
        b = refs[parts]
        if spans:
            b = jnp.concatenate([b[:, low:high] for low, high in spans[i]], axis=1)
        else:
            b = b[...]
        part = dot(refs[i][...], b, dims)
        total = part if total is None else total + part
    for term in refs[parts + 1 : -1]:
        total = total + term[...]
    refs[-1][...] = total.astype(refs[-1].dtype)


def product(parts, b, dims, name, spans=None, terms=(), half=None):
    tile = 256 if sum(a.shape[1] for a in parts) > 2560 else 640
    turned = dims == NT
    rows = parts[0].shape[0] // (1 if half is None else 2)
    place = half or 0
    width = b.shape[0 if turned else 1]
    depth = sum(a.shape[1] for a in parts)
    out_spec, steps = pl.BlockSpec((rows, tile), lambda i: (0, i)), width // tile
    ins = [
        pl.BlockSpec((rows, a.shape[1]), lambda i: (place, 0), pipeline_mode=pl.Buffered(1)) for a in parts
    ]
    if spans:
        steps = rows // 256
        ins = [pl.BlockSpec((256, a.shape[1]), lambda i: (place * steps + i, 0)) for a in parts]
        ins.append(pl.BlockSpec(b.shape, lambda i: (0, 0), pipeline_mode=pl.Buffered(1)))
        out_spec = pl.BlockSpec((256, width), lambda i: (i, 0))
    elif turned:
        ins.append(pl.BlockSpec((tile, b.shape[1]), lambda i: (i, 0)))
    else:
        ins.append(pl.BlockSpec((b.shape[0], tile), lambda i: (0, i)))
    return pl.pallas_call(
        functools.partial(product_kernel, dims=dims, spans=spans),
        out_shape=jax.ShapeDtypeStruct((rows, width), BF),
        grid=(steps,),
        in_specs=ins + [pl.BlockSpec((t.shape[0], tile), lambda i: (0, i)) for t in terms],
        out_specs=out_spec,
        compiler_params=pltpu.CompilerParams(vmem_limit_bytes=VMEM_LIMIT),
        cost_estimate=pl.CostEstimate(
            flops=2 * rows * depth * width // SHARE,
            bytes_accessed=2 * (rows * depth + depth * width + rows * width) // SHARE,
            transcendentals=0,
        ),
        name=name,
    )(*parts, b, *terms)


def tile_flags(queries, keys, tq, tk):
    q_first, q_last = queries[:, ::tq], queries[:, tq - 1 :: tq]
    k_first, k_last = keys[:, ::tk], keys[:, tk - 1 :: tk]
    meet = (q_first[:, :, None] <= k_last[:, None, :]) & (k_first[:, None, :] <= q_last[:, :, None])
    whole = (
        (q_first == q_last)[:, :, None]
        & (k_first == k_last)[:, None, :]
        & (q_first[:, :, None] == k_first[:, None, :])
    )
    return jnp.where(whole, 2, jnp.where(meet, 1, 0)).astype(jnp.int32)


def layer_norm_parts(values):
    centred = values - jnp.mean(values, axis=-1, keepdims=True)
    rstd = lax.rsqrt(jnp.mean(centred * centred, axis=-1, keepdims=True) + EPS)
    return centred * rstd, rstd


def layer_norm_back(d_norm, gain, xhat, rstd):
    e = d_norm * gain
    return rstd * (
        e - jnp.mean(e, axis=-1, keepdims=True) - xhat * jnp.mean(e * xhat, axis=-1, keepdims=True)
    )


def on_device(
    tokens,
    cell_start,
    norm1_gain,
    norm1_bias,
    w_qkv,
    bias_q,
    bias_v,
    w_out,
    bias_out,
    norm2_gain,
    norm2_bias,
    w_in,
    bias_in,
    w_back,
    bias_back,
    cotangent,
):
    rows, seg, width = tokens.shape
    count = rows * seg
    ff = w_in.shape[1]
    half = width // 2
    wide = lax.axis_size("wide")
    group = lax.axis_size("blk")
    place = lax.axis_index("wide")
    member = lax.axis_index("blk")
    core = place % 2
    chips = wide // 2
    first = 2 if chips <= 8 else 4
    second = chips // first
    heads = HEADS // 2
    early = 6
    spans = ((0, early), (early, heads))
    tq, tk = min(512, seg), min(256, seg)
    halves = group == 2 and ff // chips % 128 == 0
    where = jnp.stack([place // 2, core, member]).astype(jnp.int32)
    where_out = jnp.stack([lax.bitwise_xor(place // 2, core * (chips // 2)), core, member]).astype(jnp.int32)

    def after(value, *earlier):
        return lax.optimization_barrier((value, earlier))[0]

    def across(array, by):
        return lax.ppermute(array, "wide", [(i, i ^ by) for i in range(wide)])

    def to_mate(array):
        return across(array, 1)

    def from_ahead(array, by):
        return lax.ppermute(array, "blk", [((i + by) % group, i) for i in range(group)])

    def to_ahead(array, by):
        return lax.ppermute(array, "blk", [(i, (i + by) % group) for i in range(group)])

    def from_all_ahead(array):
        parts = [from_ahead(array, by) for by in range(1, group)]
        return parts[0] if len(parts) == 1 else jnp.concatenate(parts, axis=1)

    def cut(array, start, size, axis):
        return lax.dynamic_slice_in_dim(array, start, size, axis)

    def paired(array):
        return jnp.concatenate([array, to_mate(array)], axis=0)

    inputs = tokens.astype(F32).reshape(count, width)
    xhat1, rstd1 = layer_norm_parts(inputs)
    acts = (xhat1 * norm1_gain + norm1_bias).astype(BF).reshape(tokens.shape)
    cells = paired(cell_start)
    far_cells = from_all_ahead(cells)
    acts = after(acts, far_cells)
    far_own = from_all_ahead(acts)
    acts_pair = paired(acts).reshape(2 * count, width)
    w_own = own_columns_call(where, w_qkv)
    b_own = jnp.concatenate([cut(bias_q, core * half, half, 0), jnp.zeros((half,), F32), cut(bias_v, core * half, half, 0)])

    def own_columns(span, parts):
        return tuple((part * half + span[0] * HD, part * half + span[1] * HD) for part in parts)

    near_spans = tuple(own_columns(span, (0, 1, 2)) for span in spans)
    far_spans = tuple(own_columns(span, (1, 2)) for span in spans)

    def columns(array):
        return jnp.broadcast_to(array[:, :, None], array.shape + (128,))

    qkv = (dot(acts_pair, w_own, NN) + b_own).astype(BF).reshape(2 * rows, seg, 3 * half)
    near_flags = tile_flags(cells, cells, tq, tk)
    far_flags = tile_flags(cells, far_cells, tq, tk)
    cell_rows = cells[:, None, :]
    near_columns, far_columns = columns(cells), columns(far_cells)
    state = attn_fwd(near_flags, cell_rows, near_columns, qkv, qkv, 1, None, tq, tk, heads)
    d_out = cotangent.reshape(count, width)
    d_out_mate = to_mate(after(d_out, acts_pair))
    far_own = after(far_own, state)
    far_mate = to_mate(far_own)
    d_act = dot(after(d_out, far_own, state, d_out_mate), w_back, NT).astype(BF)

    far_mate = after(far_mate, d_act)
    far_pair = jnp.concatenate([far_own, far_mate], axis=0)
    far_len = far_pair.shape[1]
    far_pair = far_pair.reshape(-1, width)
    far_kv = (dot(far_pair, w_own[:, half:], NN) + b_own[half:]).astype(BF).reshape(2 * rows, far_len, 2 * half)
    *attended, stats = attn_fwd(far_flags, cell_rows, far_columns, qkv, far_kv, 0, state, tq, tk, heads)
    mine, theirs = (part.reshape(count, half) for part in attended)
    own_rest = to_mate(theirs)
    mate_rest = to_mate(mine)
    w_out_own = cut(w_out, core * half, half, 0)
    w_out_mate = cut(w_out, (1 - core) * half, half, 0)
    middle = inputs + (dot(mine, w_out_own, NN) + dot(own_rest, w_out_mate, NN)) + bias_out

    xhat2, _ = layer_norm_parts(middle)
    acts2 = (xhat2 * norm2_gain + norm2_bias).astype(BF)
    acts2_mate = to_mate(acts2)
    b_in = bias_in.reshape(1, ff)
    act_part, d_pre_theirs, sum_part, norm_part = ffn_call(
        where, after(acts2, mate_rest), w_in, b_in, d_act, (), "ffn_theirs"
    )
    d_pre_mate = to_mate(d_pre_theirs)
    act, d_pre_mine, d_pre_sum, d_middle, d_z, d_att_theirs, d_att_mine, z_sums = ffn_call(
        where, acts2, w_in, b_in, d_act,
        (act_part, sum_part, norm_part, middle, d_out, w_out, norm2_gain.reshape(1, width)), "ffn_mine",
    )
    act_mate = to_mate(after(act, d_pre_mate, acts2_mate))
    grad_out = d_out.astype(F32)
    d_att_mate = to_mate(d_att_theirs)
    d_z_mate = to_mate(d_z)

    def send(parts):
        return [across(parts[one], 2 * one) for one in range(1, first)]

    def add_first(parts, received):
        def added(at):
            total = parts[0][at].astype(F32)
            for part in received:
                total = total + part[at].astype(F32)
            return total.astype(BF)

        return added(slice(0, second // 2)), added(slice(second // 2, second))

    def send_second(pair):
        return across(pair[1], first * second)

    def add_second(pair, received):
        return tuple((pair[0][at].astype(F32) + received[at].astype(F32)).astype(BF) for at in range(2))

    def send_third(pair):
        return across(pair[1], 2 * first)

    def add_third(pair, received):
        return (pair[0].astype(F32) + received.astype(F32)).astype(BF)

    def start(parts):
        return from_ahead(parts[1], 1) if halves else send(parts)

    def middle_step(parts, received):
        if not halves:
            return parts, received
        sums = [(parts[0][one].astype(F32) + received[one].astype(F32)).astype(BF) for one in range(first)]
        return sums, send(sums)

    def ahead(total):
        return from_ahead(total, 1) if group == 2 else None

    def over_row(total, other):
        if group == 2:
            return (total.astype(F32) + other.astype(F32)).astype(BF)
        return lax.psum(total, "blk")

    def by_core(total):
        split = total.reshape(2, -1, total.shape[-1])
        return [lax.dynamic_index_in_dim(split, i, 0, keepdims=False) for i in (core, 1 - core)]

    def joined(total, other, sizes):
        total = over_row(total, other)
        parts, at = [], 0
        for size in sizes:
            parts.append(by_core(total[at : at + size]))
            at += size
        return [jnp.concatenate(part, axis=0) for part in zip(*parts)]

    def in_blocks(array):
        return [array[:, at : at + half] for at in range(0, array.shape[1], half)]

    d_pre_held = d_pre_mine
    grad_in = grad_call(
        where, [[(acts2, d_pre_held, 0), (acts2_mate, d_pre_mate, 0)]], ff // 2, first, second, 512, False, "grad_in"
    )
    in_in = send(grad_in)
    act_held, act_mate, d_z_mate = after((act, act_mate, d_z_mate), grad_in)

    def grad_o(into):
        return grad_call(
            where_out,
            [
                [(mine, d_z, None), (theirs, d_z_mate, None)],
                [(own_rest, d_z, None), (mate_rest, d_z_mate, None)],
            ],
            half, first, second, half, halves, "grad_out", into,
        )

    back_rows, out_rows = ff // chips, width // chips
    if halves:
        grad_b = back_call(
            where, (act_held, d_out), (act_mate, d_out_mate), first, second, out_rows // 2, "grad_back"
        )
        grad_b = grad_o(tuple(grad_b))
    else:
        whole = dot(act_held, cut(d_out, core * half, half, 1), TN) + dot(act_mate, cut(d_out_mate, core * half, half, 1), TN)
        whole = whole.astype(BF).reshape(chips, back_rows, half)
        grad_b = [
            jnp.concatenate([
                jnp.stack([whole[lax.bitwise_xor(two * first + one, where[0])] for two in range(second)]), other
            ], axis=1)
            for one, other in enumerate(grad_o(()))
        ]
    b_in = start(grad_b)

    back_tq = min(256, seg)
    near_flags, far_flags = tile_flags(cells, cells, back_tq, tk), tile_flags(cells, far_cells, back_tq, tk)
    d_att = after((d_att_mine.reshape(rows, seg, half), d_att_mate.reshape(rows, seg, half)), grad_b)
    d_qT, far_early, far_late = attn_bwd(
        far_flags, cell_rows, far_columns, qkv, far_kv, 0, d_att, attended, stats, None, back_tq, tk, heads, spans, "attn_bwd_far"
    )
    in_sums = add_first(grad_in, after(in_in, d_qT))
    in_more = send_second(in_sums)
    far_early, far_late = after((far_early, far_late), in_sums)
    far_early, far_late = (f.reshape(-1, f.shape[-1]) for f in (far_early, far_late))
    n_early, n_late = early * HD, (heads - early) * HD
    far_theirs = product([far_early, far_late], w_own, NT, "far_norm_theirs", far_spans, half=1)
    far_given = to_mate(far_theirs)
    far_mine = product([after(far_early, far_theirs), far_late], w_own, NT, "far_norm_mine", far_spans, half=0)
    far_sum = (far_mine.astype(F32) + after(far_given, in_sums, far_mine).astype(F32)).astype(BF)
    far_sum = far_sum.reshape(rows, far_len, width)
    far_back = [to_ahead(far_sum[:, by * seg : (by + 1) * seg], by + 1) for by in range(group - 1)]
    d_qT = after(d_qT, far_sum)

    def near_back(span, name, *earlier):
        (out,) = attn_bwd(
            near_flags, cell_rows, near_columns, qkv, qkv, 1, d_att, attended, stats, after(d_qT, earlier), back_tq, tk, heads,
            (span,), name,
        )
        return out.reshape(2 * count, -1)

    near_early = near_back(spans[0], "attn_bwd_early")
    b_sums, b_in = middle_step(grad_b, after(b_in, near_early))
    in_two = add_second(in_sums, after(in_more, b_sums))
    in_last = send_third(in_two)
    near_early = after(near_early, b_sums, in_two)
    *grad_e, sum_e = qkv_call(where, (acts_pair, near_early), (far_pair, far_early), first, second, halves, "grad_early")
    in_total = add_third(in_two, after(in_last, grad_e))
    in_row = ahead(in_total)
    grad_e, far_back = after((grad_e, far_back), in_total)
    e_in = start(grad_e)
    near_late = near_back(spans[1], "attn_bwd_late", grad_e, far_back)
    b_two = add_first(b_sums, after(b_in, near_late))
    b_more = send_second(b_two)
    e_sums, e_in = middle_step(grad_e, after(e_in, b_two))
    near_late = after(near_late, b_two, e_sums)
    *grad_l, sum_l = qkv_call(where, (acts_pair, near_late), (far_pair, far_late), first, second, halves, "grad_late")
    l_in = start(grad_l)
    near_held = after(near_early, grad_l)
    near_theirs = product([near_held, near_late], w_own, NT, "near_norm_theirs", near_spans, half=1)
    near_mine = product([after(near_held, near_theirs), near_late], w_own, NT, "near_norm_mine", near_spans, half=0)
    e_two = add_first(e_sums, after(e_in, near_mine))
    e_more = send_second(e_two)
    b_three = add_second(b_two, after(b_more, e_two))
    b_last = send_third(b_three)
    l_sums, l_in = middle_step(grad_l, after(l_in, b_three))
    near_given = to_mate(after(near_theirs, near_mine))
    in_row = after(in_row, near_mine)
    act_late = after(act_held, e_two, b_three, l_sums, in_row)
    mixed = product([act_late], w_back, NN, "mixed", terms=(middle, bias_back.reshape(1, width))).reshape(tokens.shape)
    l_two = add_first(l_sums, after(l_in, mixed))
    l_more = send_second(l_two)
    e_three = add_second(e_two, after(e_more, l_two))
    e_last = send_third(e_three)
    b_total = add_third(b_three, after(b_last, e_three))
    b_row = ahead(b_total)
    near_mine, near_given = after((near_mine, near_given), l_two, e_three, b_total)
    d_norm1 = near_mine.astype(F32) + near_given.astype(F32)
    for part in far_back:
        d_norm1 = d_norm1 + part.reshape(count, width).astype(F32)
    norm1_sums = (jnp.sum(d_norm1 * xhat1, axis=0), jnp.sum(d_norm1, axis=0))
    def vector_stage(total, stride, size):
        total = total.reshape(-1, size, stride, total.shape[-1])
        spot = (place // stride) % size
        kept = lax.dynamic_index_in_dim(total, spot, 1, keepdims=False)
        for by in range(1, size):
            kept = kept + across(lax.dynamic_index_in_dim(total, spot ^ by, 1, keepdims=False), by * stride)
        return kept.reshape(stride, -1)

    def widened(part):
        n = sum_e.shape[1] // 3, sum_l.shape[1] // 3
        own = jnp.concatenate([s[0, part * m : (part + 1) * m] for s, m in zip((sum_e, sum_l), n)])
        return lax.dynamic_update_slice_in_dim(jnp.zeros((width,), F32), own, core * half, 0)

    parts = [
        *norm1_sums,
        widened(0),
        widened(2),
        z_sums[0],
        z_sums[1],
        z_sums[2],
        d_pre_sum,
        jnp.sum(grad_out, axis=0),
    ]
    totals = vector_stage(jnp.concatenate([part.reshape(wide, -1) for part in parts], axis=1), 2 * first, second)
    e_total = add_third(e_three, after(e_last, norm1_sums))
    l_three = add_second(l_two, after(l_more, e_total))
    l_last = send_third(l_three)
    xhat1 = after(xhat1, l_three, e_total, totals)
    totals = vector_stage(totals, 2, first)
    grad_tokens = (d_middle + layer_norm_back(d_norm1, norm1_gain, xhat1, rstd1)).reshape(tokens.shape)

    l_total = add_third(l_three, after(l_last, grad_tokens, totals))
    totals = vector_stage(totals, 1, 2).reshape(-1)
    qkv_total = jnp.concatenate([e_total, l_total], axis=1)
    qkv_row = ahead(qkv_total)
    in_total, b_total = after((in_total, b_total), grad_tokens, totals)
    totals = totals + from_ahead(totals, 1) if group == 2 else lax.psum(totals, "blk")
    if halves:
        kept, given = pack_call(where, (in_total, in_row), (b_total, b_row), (qkv_total, qkv_row))
    else:
        in_parts = by_core(over_row(in_total, in_row))
        b_parts = joined(b_total, b_row, [back_rows, out_rows])
        qkv_parts = joined(qkv_total, qkv_row, [out_rows])
        kept, given = (
            jnp.concatenate(in_blocks(i) + [b] + in_blocks(q), axis=0)
            for i, b, q in zip(in_parts, b_parts, qkv_parts)
        )
    other = after(to_mate(given), totals)
    share = ff // wide
    own_rows = width // wide
    in_count = ff // 2 // half

    def rows_of(array, first_row, size):
        return array[first_row : first_row + size]

    def blocks_of(array, first_row, count):
        return [rows_of(array, first_row + i * own_rows, own_rows) for i in range(count)]

    if halves:
        shapes = [(own_rows, ff), (share, width), (own_rows, width), (own_rows, 3 * width)]
        grad_w_in, grad_w_back, grad_w_out, grad_w_qkv = unpack_call(where, kept, other, shapes, (n_early, n_late))
    else:
        low, high = (jnp.where(core == side, kept, other).astype(F32) for side in range(2))
        b_at = in_count * own_rows
        q_at = b_at + share + own_rows

        def part_columns(part):
            columns = []
            for side in (low, high):
                wide_rows = jnp.concatenate(blocks_of(side, q_at, 3), axis=1)
                for start, n in ((0, n_early), (3 * n_early, n_late)):
                    columns.append(wide_rows[:, start + part * n : start + (part + 1) * n])
            return columns

        grad_w_in = jnp.concatenate([b for side in (low, high) for b in blocks_of(side, 0, in_count)], axis=1)
        grad_w_back = jnp.concatenate([rows_of(side, b_at, share) for side in (low, high)], axis=1)
        grad_w_out = jnp.concatenate([rows_of(side, b_at + share, own_rows) for side in (low, high)], axis=1)
        grad_w_qkv = jnp.concatenate([piece for part in range(3) for piece in part_columns(part)], axis=1)

    small, at = [], 0
    for part in parts:
        size = part.size // wide
        small.append(totals[at : at + size])
        at += size

    return (
        mixed,
        grad_tokens,
        small[0],
        small[1],
        grad_w_qkv,
        small[2],
        small[3],
        grad_w_out,
        small[4],
        small[5],
        small[6],
        grad_w_in,
        small[7],
        grad_w_back,
        small[8],
    )


def solution(mesh):
    spread = P("wide", "blk", None)
    placed = (spread, P("wide", "blk")) + (P(),) * 13 + (spread,)
    matrix, vector = P("wide", None), P("wide")
    return jax.shard_map(
        on_device,
        mesh=mesh,
        in_specs=placed,
        out_specs=(
            spread, spread, vector, vector, matrix, vector, vector, matrix, vector, vector, vector,
            matrix, vector, matrix, vector,
        ),
        check_vma=False,
    )
```

```python
import functools
import math

import jax
import jax.numpy as jnp
from jax import lax
from jax.experimental import pallas as pl
from jax.experimental.pallas import tpu as pltpu
from jax.sharding import PartitionSpec as P

HEADS = 20
HEAD_DIM = 64
HD = HEAD_DIM
EPS = 1e-05
NEG = -1e30
LOG2E = math.log2(math.e)
C2 = LOG2E / math.sqrt(HEAD_DIM)
F32 = jnp.float32
BF = jnp.bfloat16
NN = (((1,), (0,)), ((), ()))
NT = (((1,), (1,)), ((), ()))
TN = (((0,), (0,)), ((), ()))
VMEM_LIMIT = 56 * 2**20
SHARE = 10
VR = HD + 16


def dot(a, b, dims):
    return lax.dot_general(a, b, dims, preferred_element_type=F32)


def own_map(nr,last):
    return lambda r,i,*_:(jnp.minimum(r,nr//2-1),jnp.where(r<nr//2,i,last-1),0)

def mate_map(nr):
    return lambda r,i,*_:(jnp.maximum(r-nr//2,0),jnp.where(r<nr//2,0,i),0)

def head_sumsq(x,hp16):
    W=x.shape[1]
    sq=x.astype(F32)*x.astype(F32)
    row=lax.broadcasted_iota(jnp.int32,(hp16,W),0); col=lax.broadcasted_iota(jnp.int32,(hp16,W),1)
    ones=jnp.where(row==col//HD,1.0,0.0).astype(BF)
    return lax.dot_general(ones,sq.astype(BF),NT,preferred_element_type=F32)

def fwd_kernel(flags,cq,ck,q,k,v,*rest,first,tq,tk,heads):
    if first:
        accT_o,m_o,l_o,qm,vT,bias,acc,m,l,kn=rest
    else:
        accT_i,m_i,l_i,o_own,o_mate,lse_o,qm,vT,bias,acc,m,l,kn=rest
    r=pl.program_id(0); qi=pl.program_id(1)
    nk=k.shape[1]//tk
    hp16=m.shape[0]
    @pl.when(qi==0)
    def _():
        for hh in range(heads):
            vT[hh*VR:hh*VR+HD,:]=v[0,:,hh*HD:(hh+1)*HD].T
            vT[hh*VR+HD:(hh+1)*VR,:]=jnp.ones((VR-HD,vT.shape[1]),BF)
        kn[...]=jnp.broadcast_to(jnp.sqrt(jnp.max(head_sumsq(k[0],hp16),1,keepdims=True)),kn.shape)
    lane=lax.broadcasted_iota(jnp.int32,(tq,128),1)
    for hp in range(heads//2):
        qp=q[0,:,hp*128:(hp+1)*128]
        qm[2*hp]=jnp.where(lane<64,qp,0).astype(BF)
        qm[2*hp+1]=jnp.where(lane>=64,qp,0).astype(BF)
    bound=jnp.sqrt(head_sumsq(q[0],hp16))*kn[:,0:1]*(C2*1.02)
    safe=jnp.max(bound)<50.0
    if first:
        m0=bound
    else:
        m0=jnp.maximum(bound,m_i[0])
    def loop(online):
        if first:
            acc[...]=jnp.zeros_like(acc); l[...]=jnp.zeros_like(l)
            m[...]=jnp.full_like(m,NEG) if online else m0
        elif online:
            acc[...]=accT_i[0]; m[...]=m_i[0]; l[...]=l_i[0]
        else:
            al=jnp.exp2(m_i[0]-m0)
            m[...]=m0; l[...]=al*l_i[0]
            for hh in range(heads):
                hs=slice(hh*HD,(hh+1)*HD)
                acc[hs,:]=al[hh:hh+1,:]*accT_i[0,hs,:]
        def body(kt,masked):
            ks=pl.ds(pl.multiple_of(kt*tk,tk),tk)
            if online:
                @pl.loop(0,heads//2)
                def _(hp):
                    kp=k[0,ks,pl.ds(pl.multiple_of(hp*128,128),128)]
                    for j in range(2):
                        hh=2*hp+j
                        s=lax.dot_general(kp,qm[hh],NT,preferred_element_type=F32)*C2+bias[...]
                        mp=m[pl.ds(hh,1),:]
                        mn=jnp.maximum(mp,jnp.max(s,0,keepdims=True))
                        p=jnp.exp2(s-mn)
                        al=jnp.exp2(mp-mn)
                        m[pl.ds(hh,1),:]=mn
                        l[pl.ds(hh,1),:]=al*l[pl.ds(hh,1),:]+jnp.sum(p,0,keepdims=True)
                        hs=pl.ds(pl.multiple_of(hh*HD,HD),HD)
                        vs=pl.ds(pl.multiple_of(hh*VR,16),HD)
                        acc[hs,:]=al*acc[hs,:]+lax.dot_general(vT[vs,ks],p.astype(BF),NN,preferred_element_type=F32)
                return
            def score(hh):
                s=lax.dot_general(k[0,ks,(hh//2)*128:(hh//2+1)*128],qm[hh],NT,preferred_element_type=F32)*C2
                if masked: s=s+bias[...]
                return s
            s=score(0); pp=None
            for hh in range(heads+1):
                if hh+1<heads: sn=score(hh+1)
                if pp is not None:
                    h1=hh-1
                    both=lax.dot_general(vT[h1*VR:(h1+1)*VR,ks],pp,NN,preferred_element_type=F32)
                    acc[h1*HD:(h1+1)*HD,:]+=both[:HD]
                    l[h1:h1+1,:]+=both[HD:HD+1]
                if hh<heads:
                    p=jnp.exp2(s-m[hh:hh+1,:])
                    pp=p.astype(BF)
                s=sn
        @pl.loop(0,nk)
        def _(kt):
            f=flags[r,qi,kt]
            def mask():
                ks=pl.ds(pl.multiple_of(kt*tk,tk),tk)
                bias[...]=jnp.where(ck[0,ks,0:1]==cq[0,0:1,:],0.0,NEG)
            if online:
                @pl.when(f>0)
                def _():
                    mask(); body(kt,True)
            else:
                @pl.when(f==1)
                def _():
                    mask(); body(kt,True)
                @pl.when(f==2)
                def _(): body(kt,False)
    @pl.when(safe)
    def _(): loop(False)
    @pl.when(jnp.logical_not(safe))
    def _(): loop(True)
    if first:
        accT_o[0]=acc[...]; m_o[0]=m[...]; l_o[0]=l[...]
    else:
        for hp in range(heads//2):
            parts=[]
            for hh in (2*hp,2*hp+1):
                parts.append(acc[hh*HD:(hh+1)*HD,:]/l[hh:hh+1,:])
            low=jnp.concatenate(parts,0).T.astype(BF)
            @pl.when(r<pl.num_programs(0)//2)
            def _(): o_own[0,:,hp*128:(hp+1)*128]=low
            @pl.when(r>=pl.num_programs(0)//2)
            def _(): o_mate[0,:,hp*128:(hp+1)*128]=low
        lse_o[0]=m[...]+jnp.log2(l[...])

def attn_fwd(flags,cq,ck,q,kv,kb,state,tq,tk,heads):
    nr,S,_=q.shape; W=heads*HD; Sk=kv.shape[1]; hp16=-(-heads//8)*8
    first=state is None
    qs=lambda r,i,*_:(r,i,0); ts=lambda r,i,*_:(r,0,i); ks=lambda r,i,*_:(r,0,0)
    stspec=[pl.BlockSpec((1,W,tq),ts),pl.BlockSpec((1,hp16,tq),ts),pl.BlockSpec((1,hp16,tq),ts)]
    ins=[pl.BlockSpec((1,1,tq),ts),pl.BlockSpec((1,Sk,128),ks),pl.BlockSpec((1,tq,W),qs),pl.BlockSpec((1,Sk,W),lambda r,i,*_:(r,0,kb)),pl.BlockSpec((1,Sk,W),lambda r,i,*_:(r,0,kb+1))]
    if first:
        outs=stspec
        osh=[jax.ShapeDtypeStruct((nr,W,S),F32)]+[jax.ShapeDtypeStruct((nr,hp16,S),F32)]*2
    else:
        ins=ins+stspec
        outs=[pl.BlockSpec((1,tq,W),own_map(nr,S//tq)),pl.BlockSpec((1,tq,W),mate_map(nr)),pl.BlockSpec((1,hp16,tq),ts)]
        osh=[jax.ShapeDtypeStruct((nr//2,S,W),BF)]*2+[jax.ShapeDtypeStruct((nr,hp16,S),F32)]
    fl=4*nr*S*Sk*W
    return pl.pallas_call(functools.partial(fwd_kernel,first=first,tq=tq,tk=tk,heads=heads),
        out_shape=osh,
        grid_spec=pltpu.PrefetchScalarGridSpec(num_scalar_prefetch=1,grid=(nr,S//tq),in_specs=ins,out_specs=outs,
          scratch_shapes=[pltpu.VMEM((heads,tq,128),BF),pltpu.VMEM((heads*VR,Sk),BF),pltpu.VMEM((tk,tq),F32),pltpu.VMEM((W,tq),F32),pltpu.VMEM((hp16,tq),F32),pltpu.VMEM((hp16,tq),F32),pltpu.VMEM((hp16,128),F32)]),
        compiler_params=pltpu.CompilerParams(dimension_semantics=("arbitrary","arbitrary"),vmem_limit_bytes=VMEM_LIMIT),
        cost_estimate=pl.CostEstimate(flops=fl//SHARE,bytes_accessed=nr*(S*W*2+2*Sk*W*2+S*W*4)//SHARE,transcendentals=0),
        name="attn_fwd_a" if first else "attn_fwd_b",
    )(flags,cq,ck,q,kv,kv,*(state or ()))

def bwd_kernel(flags,cq,ck,q,k,v,do_own,do_mate,o_own,o_mate,lse,*rest,spans,tq,tk):
    first=len(spans)==2
    if first:
        dqT_o,*dkv_o,qm,dom,kT,bias,dqT,dk,dv,delta=rest
    else:
        dqT_i,dqkv_o,qm,dom,kT,bias,dqT,dk,dv,delta=rest
    r=pl.program_id(0); qi=pl.program_id(1); nq=pl.num_programs(1)
    nk=k.shape[1]//tk
    low=spans[0][0]; heads=sum(b-a for a,b in spans)
    W=heads*HD; c0=low*HD
    @pl.when(qi==0)
    def _():
        kT[...]=k[0,:,c0:c0+W].T
        dk[...]=jnp.zeros_like(dk); dv[...]=jnp.zeros_like(dv)
    own=r<pl.num_programs(0)//2
    lane=lax.broadcasted_iota(jnp.int32,(tq,128),1)
    for hp in range(heads//2):
        c=slice(c0+hp*128,c0+(hp+1)*128)
        qp=q[0,:,c]*jnp.asarray(0.125,BF); dp_=jnp.where(own,do_own[0,:,c],do_mate[0,:,c])
        qm[2*hp]=jnp.where(lane<64,qp,0).astype(BF)
        qm[2*hp+1]=jnp.where(lane>=64,qp,0).astype(BF)
        dom[2*hp]=jnp.where(lane<64,dp_,0).astype(BF)
        dom[2*hp+1]=jnp.where(lane>=64,dp_,0).astype(BF)
    prod=jnp.where(own,do_own[0,:,c0:c0+W],do_mate[0,:,c0:c0+W]).astype(F32)*jnp.where(own,o_own[0,:,c0:c0+W],o_mate[0,:,c0:c0+W]).astype(F32)
    hi=prod.astype(BF); lo=(prod-hi.astype(F32)).astype(BF)
    n16=delta.shape[0]
    row=lax.broadcasted_iota(jnp.int32,(n16,W),0); col_=lax.broadcasted_iota(jnp.int32,(n16,W),1)
    ones=jnp.where(row==col_//HD,1.0,0.0).astype(BF)
    delta[...]=lax.dot_general(ones,hi,NT,preferred_element_type=F32)+lax.dot_general(ones,lo,NT,preferred_element_type=F32)
    if first: dqT[...]=jnp.zeros_like(dqT)
    else: dqT[...]=dqT_i[0,c0:c0+W,:]
    def body(kt):
        ks=pl.ds(pl.multiple_of(kt*tk,tk),tk)
        def col(hh): return slice((hh//2)*128,(hh//2+1)*128)
        def wide(hh): return slice(c0+(hh//2)*128,c0+(hh//2+1)*128)
        def score(hh):
            s=lax.dot_general(k[0,ks,wide(hh)],qm[hh],NT,preferred_element_type=F32)*LOG2E+bias[...]
            return s,lax.dot_general(v[0,ks,wide(hh)],dom[hh],NT,preferred_element_type=F32)
        nxt=score(0); prev=None
        for hh in range(heads+1):
            cur=nxt
            if hh+1<heads: nxt=score(hh+1)
            if prev is not None:
                h1=hh-1; pb,dsb=prev
                hs=slice(h1*HD,(h1+1)*HD)
                dqT[hs,:]+=lax.dot_general(kT[hs,ks],dsb,NN,preferred_element_type=F32)
                dv[ks,col(h1)]+=jnp.dot(pb,dom[h1],preferred_element_type=F32)
                dk[ks,col(h1)]+=jnp.dot(dsb,qm[h1],preferred_element_type=F32)
            if hh<heads:
                s,dp=cur
                at=low+hh
                p=jnp.exp2(s-lse[0,at:at+1,:])
                ds=p*(dp-delta[hh:hh+1,:])
                prev=(p.astype(BF),ds.astype(BF))
    @pl.loop(0,nk)
    def _(kt):
        f=flags[r,qi,kt]
        @pl.when(f>0)
        def _():
            ks=pl.ds(pl.multiple_of(kt*tk,tk),tk)
            bias[...]=jnp.where(ck[0,ks,0:1]==cq[0,0:1,:],0.0,NEG)
            body(kt)
    if first: dqT_o[0]=dqT[...]
    else: dqkv_o[0,pl.ds(pl.multiple_of(qi*tq,tq),tq),0:W]=(dqT[...]*0.125).T.astype(BF)
    @pl.when(qi==nq-1)
    def _():
        if first:
            for (a,b),out in zip(spans,dkv_o):
                n=(b-a)*HD; at=(a-low)*HD
                out[0,:,0:n]=dk[:,at:at+n].astype(BF); out[0,:,n:2*n]=dv[:,at:at+n].astype(BF)
        else:
            dqkv_o[0,:,W:2*W]=dk[...].astype(BF); dqkv_o[0,:,2*W:3*W]=dv[...].astype(BF)

def attn_bwd(flags,cq,ck,q,kv,kb,do,o,lse,dqT,tq,tk,full,spans,name):
    nr,S,_=q.shape; F=full*HD; Sk=kv.shape[1]; n16=lse.shape[1]
    heads=sum(b-a for a,b in spans); W=heads*HD
    first=dqT is None
    qs=lambda r,i,*_:(r,i,0); ts=lambda r,i,*_:(r,0,i); ks=lambda r,i,*_:(r,0,0)
    ins=[pl.BlockSpec((1,1,tq),ts),pl.BlockSpec((1,Sk,128),ks),pl.BlockSpec((1,tq,F),qs),pl.BlockSpec((1,Sk,F),lambda r,i,*_:(r,0,kb)),pl.BlockSpec((1,Sk,F),lambda r,i,*_:(r,0,kb+1)),
         *[pl.BlockSpec((1,tq,F),own_map(nr,S//tq)),pl.BlockSpec((1,tq,F),mate_map(nr))]*2,pl.BlockSpec((1,n16,tq),ts)]
    if first:
        widths=[2*(b-a)*HD for a,b in spans]
        outs=[pl.BlockSpec((1,F,tq),ts)]+[pl.BlockSpec((1,Sk,n),ks) for n in widths]
        osh=[jax.ShapeDtypeStruct((nr,F,S),F32)]+[jax.ShapeDtypeStruct((nr,Sk,n),BF) for n in widths]
        extra=()
    else:
        ins=ins+[pl.BlockSpec((1,F,tq),ts)]
        outs=[pl.BlockSpec((1,Sk,3*W),ks)]; osh=[jax.ShapeDtypeStruct((nr,Sk,3*W),BF)]
        extra=(dqT,)
    fl=10*nr*S*Sk*W
    return pl.pallas_call(functools.partial(bwd_kernel,spans=spans,tq=tq,tk=tk),
        out_shape=osh,
        grid_spec=pltpu.PrefetchScalarGridSpec(num_scalar_prefetch=1,grid=(nr,S//tq),in_specs=ins,out_specs=outs,
          scratch_shapes=[pltpu.VMEM((heads,tq,128),BF),pltpu.VMEM((heads,tq,128),BF),pltpu.VMEM((W,Sk),BF),pltpu.VMEM((tk,tq),F32),pltpu.VMEM((W,tq),F32),
             pltpu.VMEM((Sk,W),F32),pltpu.VMEM((Sk,W),F32),pltpu.VMEM((n16,tq),F32)]),
        compiler_params=pltpu.CompilerParams(dimension_semantics=("arbitrary","arbitrary"),vmem_limit_bytes=VMEM_LIMIT),
        cost_estimate=pl.CostEstimate(flops=fl//SHARE,bytes_accessed=nr*(3*S*W*2+4*Sk*W*2+S*W*4)//SHARE,transcendentals=0),
        name=name,
    )(flags,cq,ck,q,kv,kv,*do,*o,lse,*extra)


def ffn_kernel(where, acts, w, b, d_act, *rest, last):
    step = pl.program_id(0)
    final = pl.num_programs(0) - 1
    rows, width = acts.shape
    chunk = min(256, rows)
    count = rows // chunk
    if last:
        ins, outs, scratch = rest[:7], rest[7:15], rest[15:]
        _, _, acc_i, middle_i, d_out_i, w_out_i, gain = ins
        act_o, d_pre_o, sum_o, mid_o, d_z_o, theirs_o, mine_o, sums_o = outs
        acc, part, middle, d_out, w_out, d_z, att, in_sem, out_sem = scratch
        loads = [
            pltpu.make_async_copy(source, target, in_sem.at[n])
            for n, (source, target) in enumerate(
                ((acc_i, part), (middle_i, middle), (d_out_i, d_out), (w_out_i, w_out))
            )
        ]

        @pl.when(step == 0)
        def _():
            for load in loads:
                load.start()
    else:
        act_o, d_pre_o, sum_o, acc = rest

    @pl.when(step == 0)
    def _():
        acc[...] = jnp.zeros_like(acc)

    def span(i):
        return slice(i * chunk, (i + 1) * chunk)

    def product(i):
        return dot(acts[span(i), :], w[...], NN) + b[...]

    pre = product(0)
    total, held = None, None
    for i in range(count + 1):
        following = product(i + 1) if i + 1 < count else None
        if held is not None:
            acc[span(i - 1), :] += dot(held, w[...], NT)
        if i < count:
            at = span(i)
            cdf = 0.5 + 0.5 * lax.erf(pre * math.sqrt(0.5))
            pdf = jnp.exp(-0.5 * pre * pre) * (1.0 / math.sqrt(2.0 * math.pi))
            act_o[at, :] = (pre * cdf).astype(BF)
            held = (d_act[at, :].astype(F32) * (cdf + pre * pdf)).astype(BF)
            d_pre_o[at, :] = held
            summed = jnp.sum(held.astype(F32), axis=0, keepdims=True)
            total = summed if total is None else total + summed
        pre = following
    sum_o[...] = total
    if not last:
        return

    @pl.when(step == final)
    def _():
        for load in loads:
            load.wait()
        half = width // 2
        sums, stores = None, []
        for i in range(count):
            at = span(i)
            d_norm = acc[at, :] + part[at, :]
            xhat, rstd = layer_norm_parts(middle[at, :])
            d_mid = d_out[at, :].astype(F32) + layer_norm_back(d_norm, gain[...], xhat, rstd)
            low = d_mid.astype(BF)
            part[at, :] = d_mid
            d_z[at, :] = low
            for side in range(2):
                first = pl.multiple_of(lax.bitwise_xor(where[1], 1 - side) * half, half)
                att[side, at, :] = dot(low, w_out[pl.ds(first, half), :], NT).astype(BF)
            new = [low.astype(F32), d_norm * xhat, d_norm]
            new = jnp.concatenate([jnp.sum(n, axis=0, keepdims=True) for n in new], axis=0)
            sums = new if sums is None else sums + new
            pairs = ((part, mid_o), (d_z, d_z_o), (att.at[0], theirs_o), (att.at[1], mine_o))
            for n, (source, target) in enumerate(pairs):
                store = pltpu.make_async_copy(
                    source.at[pl.ds(i * chunk, chunk)], target.at[pl.ds(i * chunk, chunk)], out_sem.at[4 * i + n]
                )
                store.start()
                stores.append(store)
        sums_o[0:3, :] = sums
        sums_o[3:8, :] = jnp.zeros((5, width), F32)
        for store in stores:
            store.wait()


def ffn_call(where, acts, w, b, d_act, earlier, name):
    rows, width = acts.shape
    ff = w.shape[1]
    tile = 512
    steps = ff // 2 // tile
    last = bool(earlier)
    chunk = min(256, rows)

    def place(i, where):
        return (where[1] if last else 1 - where[1]) * steps + i

    col = lambda i, where: (0, place(i, where))
    whole = pl.BlockSpec((rows, width), lambda i, where: (0, 0))
    anywhere = pl.BlockSpec(memory_space=pl.ANY)
    out_shape = [
        jax.ShapeDtypeStruct((rows, ff), BF),
        jax.ShapeDtypeStruct((rows, ff // 2), BF),
        jax.ShapeDtypeStruct((1, ff), F32),
    ]
    out_specs = [
        pl.BlockSpec((rows, tile), col),
        pl.BlockSpec((rows, tile), lambda i, where: (0, i)),
        pl.BlockSpec((1, tile), col),
    ]
    ins = [
        pl.BlockSpec((rows, width), lambda i, where: (0, 0), pipeline_mode=pl.Buffered(1)),
        pl.BlockSpec((width, tile), col),
        pl.BlockSpec((1, tile), col),
        pl.BlockSpec((rows, tile), col),
    ]
    scratch = []
    if last:
        ins += [anywhere] * 6 + [pl.BlockSpec((1, width), lambda i, where: (0, 0))]
        out_shape += [
            jax.ShapeDtypeStruct((rows, width), F32),
            jax.ShapeDtypeStruct((rows, width), BF),
            jax.ShapeDtypeStruct((rows, width // 2), BF),
            jax.ShapeDtypeStruct((rows, width // 2), BF),
            jax.ShapeDtypeStruct((8, width), F32),
        ]
        out_specs += [anywhere] * 4 + [pl.BlockSpec((8, width), lambda i, where: (0, 0))]
        scratch = [
            pltpu.VMEM((rows, width), F32),
            pltpu.VMEM((rows, width), F32),
            pltpu.VMEM((rows, width), F32),
            pltpu.VMEM((rows, width), BF),
            pltpu.VMEM((width, width), BF),
            pltpu.VMEM((rows, width), BF),
            pltpu.VMEM((2, rows, width // 2), BF),
            pltpu.SemaphoreType.DMA((4,)),
            pltpu.SemaphoreType.DMA((4 * (rows // chunk),)),
        ]
    else:
        out_shape.append(jax.ShapeDtypeStruct((rows, width), F32))
        out_specs.append(whole)
    return pl.pallas_call(
        functools.partial(ffn_kernel, last=last),
        out_shape=out_shape,
        grid_spec=pltpu.PrefetchScalarGridSpec(
            num_scalar_prefetch=1, grid=(steps,), in_specs=ins, out_specs=out_specs, scratch_shapes=scratch
        ),
        input_output_aliases={5: 0, 6: 2} if last else {},
        compiler_params=pltpu.CompilerParams(vmem_limit_bytes=VMEM_LIMIT),
        cost_estimate=pl.CostEstimate(
            flops=2 * rows * width * ff // SHARE,
            bytes_accessed=(2 * rows * width + width * ff + 3 * rows * ff) // SHARE,
            transcendentals=0,
        ),
        name=name,
    )(where, acts, w, b, d_act, *earlier)


def store_blocks(where, acc, outs, first, second, halved):
    rows = acc.shape[0] // (first * second)
    for one in range(first):
        for two in range(second):
            block = lax.bitwise_xor(two * first + one, where[0]) * rows
            if halved:
                for part in range(2):
                    at = block + lax.bitwise_xor(where[2], part) * (rows // 2)
                    piece = acc[pl.ds(pl.multiple_of(at, 16), rows // 2), :]
                    outs[part][one, two] = piece.astype(BF)
            else:
                outs[one][two] = acc[pl.ds(pl.multiple_of(block, 16), rows), :].astype(BF)


def grad_kernel(where, *refs, groups, first, second, halved, outs):
    acc = refs[-1]
    ins = refs[: sum(2 * g for g in groups)]
    height = acc.shape[0] // len(groups)
    at = 0
    for index, pairs in enumerate(groups):
        total = None
        for _ in range(pairs):
            part = dot(ins[at][...], ins[at + 1][...], TN)
            total = part if total is None else total + part
            at += 2
        acc[index * height : (index + 1) * height, :] = total
    store_blocks(where, acc, refs[-1 - outs : -1], first, second, halved)


def grad_call(where, groups, width, first, second, tile, halved, name, into=()):
    ins, flat, depth = [], [], 0
    for group in groups:
        for a, b, offset in group:
            ins.append(pl.BlockSpec(a.shape, lambda i, where: (0, 0)))
            if offset is None:
                index = lambda i, where: (0, where[1] * (width // tile) + i)
            else:
                index = lambda i, where, offset=offset: (0, offset // tile + i)
            ins.append(pl.BlockSpec((b.shape[0], tile), index))
            flat += [a, b]
            depth += a.shape[0]
    height = sum(g[0][0].shape[1] for g in groups)
    depth = depth // len(groups)
    rows = height // (first * second)
    if halved:
        shape, block = (first, second, rows // 2, width), (first, second, rows // 2, tile)
        outs = 2
        index = lambda i, where: (0, 0, 0, i)
    else:
        shape, block = (second, rows, width), (second, rows, tile)
        outs = first
        index = lambda i, where: (0, 0, i)
    if into:
        shape = into[0].shape
        row = shape[2] * 2 // rows - 1
        index = lambda i, where: (0, 0, row, i)
    return pl.pallas_call(
        functools.partial(
            grad_kernel, groups=[len(g) for g in groups], first=first, second=second, halved=halved, outs=outs
        ),
        out_shape=[jax.ShapeDtypeStruct(shape, BF)] * outs,
        grid_spec=pltpu.PrefetchScalarGridSpec(
            num_scalar_prefetch=1,
            grid=(width // tile,),
            in_specs=ins + [pl.BlockSpec(memory_space=pl.ANY)] * len(into),
            out_specs=[pl.BlockSpec(block, index)] * outs,
            scratch_shapes=[pltpu.VMEM((height, tile), F32)],
        ),
        input_output_aliases={1 + len(flat) + i: i for i in range(len(into))},
        compiler_params=pltpu.CompilerParams(vmem_limit_bytes=VMEM_LIMIT),
        cost_estimate=pl.CostEstimate(
            flops=2 * depth * height * width // SHARE,
            bytes_accessed=2 * (depth * (height + width) + height * width) // SHARE,
            transcendentals=0,
        ),
        name=name,
    )(where, *flat, *into)


def qkv_kernel(where, near_a, near_b, far_a, far_b, *refs, first, second, halved):
    *outs, sum_o, acc = refs
    acc[...] = dot(near_a[...], near_b[...], TN)
    sum_o[...] = jnp.sum(near_b[...].astype(F32), axis=0, keepdims=True)

    @pl.when(pl.program_id(0) > 0)
    def _():
        acc[...] += dot(far_a[...], far_b[...], TN)
        sum_o[...] += jnp.sum(far_b[...].astype(F32), axis=0, keepdims=True)

    store_blocks(where, acc, outs, first, second, halved)


def qkv_call(where, near, far, first, second, halved, name):
    (near_a, near_b), (far_a, far_b) = near, far
    height = near_a.shape[1]
    width = near_b.shape[1]
    tile = width // 3
    rows = height // (first * second)
    if halved:
        shape, block = (first, second, rows // 2, width), (first, second, rows // 2, tile)
        outs = 2
        index = lambda i, where: (0, 0, 0, i)
    else:
        shape, block = (second, rows, width), (second, rows, tile)
        outs = first
        index = lambda i, where: (0, 0, i)
    once = pl.Buffered(1)
    return pl.pallas_call(
        functools.partial(qkv_kernel, first=first, second=second, halved=halved),
        out_shape=[jax.ShapeDtypeStruct(shape, BF)] * outs + [jax.ShapeDtypeStruct((1, width), F32)],
        grid_spec=pltpu.PrefetchScalarGridSpec(
            num_scalar_prefetch=1,
            grid=(3,),
            in_specs=[
                pl.BlockSpec(near_a.shape, lambda i, where: (0, 0), pipeline_mode=once),
                pl.BlockSpec((near_b.shape[0], tile), lambda i, where: (0, i)),
                pl.BlockSpec(far_a.shape, lambda i, where: (0, 0), pipeline_mode=once),
                pl.BlockSpec((far_b.shape[0], tile), lambda i, where: (0, jnp.maximum(i - 1, 0))),
            ],
            out_specs=[pl.BlockSpec(block, index)] * outs + [pl.BlockSpec((1, tile), lambda i, where: (0, i))],
            scratch_shapes=[pltpu.VMEM((height, tile), F32)],
        ),
        compiler_params=pltpu.CompilerParams(vmem_limit_bytes=VMEM_LIMIT),
        cost_estimate=pl.CostEstimate(
            flops=2 * (near_a.shape[0] + far_a.shape[0]) * height * width // SHARE,
            bytes_accessed=2 * ((near_a.shape[0] + far_a.shape[0]) * (height + width) + height * width) // SHARE,
            transcendentals=0,
        ),
        name=name,
    )(where, near_a, near_b, far_a, far_b)


def back_kernel(where, a1, b1, a2, b2, out1, out2, acc):
    acc[...] = dot(a1[...], b1[...], TN) + dot(a2[...], b2[...], TN)
    rows = acc.shape[0] // 2
    for part, out in enumerate((out1, out2)):
        at = lax.bitwise_xor(where[2], part) * rows
        out[0, 0] = acc[pl.ds(pl.multiple_of(at, 16), rows), :].astype(BF)


def back_call(where, own, mate, first, second, extra, name):
    (a1, b1), (a2, b2) = own, mate
    tokens, ff = a1.shape
    rows = ff // (first * second)
    width = b2.shape[1] // 2

    def block(i, where):
        return (0, lax.bitwise_xor(lax.rem(i, second) * first + i // second, where[0]))

    return pl.pallas_call(
        back_kernel,
        out_shape=[jax.ShapeDtypeStruct((first, second, rows // 2 + extra, width), BF)] * 2,
        grid_spec=pltpu.PrefetchScalarGridSpec(
            num_scalar_prefetch=1,
            grid=(first * second,),
            in_specs=[
                pl.BlockSpec((tokens, rows), block),
                pl.BlockSpec((tokens, width), lambda i, where: (0, where[1])),
                pl.BlockSpec((tokens, rows), block),
                pl.BlockSpec((tokens, width), lambda i, where: (0, where[1])),
            ],
            out_specs=[
                pl.BlockSpec(
                    (1, 1, rows // 2, width), lambda i, where: (i // second, lax.rem(i, second), 0, 0)
                )
            ]
            * 2,
            scratch_shapes=[pltpu.VMEM((rows, width), F32)],
        ),
        compiler_params=pltpu.CompilerParams(vmem_limit_bytes=VMEM_LIMIT),
        cost_estimate=pl.CostEstimate(
            flops=4 * tokens * ff * width // SHARE,
            bytes_accessed=2 * (2 * tokens * (ff + width) + ff * width) // SHARE,
            transcendentals=0,
        ),
        name=name,
    )(where, a1, b1, a2, b2)


def first_norm_kernel(tokens, d_middle, gain, *rest):
    parts, (out, sums) = rest[:-2], rest[-2:]
    d_norm = parts[0][...].astype(F32)
    for part in parts[1:]:
        d_norm = d_norm + part[...].astype(F32)
    xhat, rstd = layer_norm_parts(tokens[...].astype(F32))
    out[...] = d_middle[...] + layer_norm_back(d_norm, gain[...], xhat, rstd)
    new = jnp.concatenate(
        [jnp.sum(d_norm * xhat, axis=0, keepdims=True), jnp.sum(d_norm, axis=0, keepdims=True)], axis=0
    )

    @pl.when(pl.program_id(0) == 0)
    def _():
        sums[...] = jnp.zeros_like(sums)

    sums[0:2, :] += new


def first_norm_call(tokens, d_middle, gain, parts):
    rows, width = tokens.shape
    block = pl.BlockSpec((128, width), lambda i: (i, 0))
    return pl.pallas_call(
        first_norm_kernel,
        out_shape=[jax.ShapeDtypeStruct((rows, width), F32), jax.ShapeDtypeStruct((8, width), F32)],
        grid=(rows // 128,),
        in_specs=[block, block, pl.BlockSpec((1, width), lambda i: (0, 0))] + [block] * len(parts),
        out_specs=[block, pl.BlockSpec((8, width), lambda i: (0, 0))],
        compiler_params=pltpu.CompilerParams(vmem_limit_bytes=VMEM_LIMIT),
        cost_estimate=pl.CostEstimate(
            flops=20 * rows * width // SHARE, bytes_accessed=20 * rows * width // SHARE, transcendentals=0
        ),
        name="first_norm",
    )(tokens, d_middle, gain, *parts)


def pack_kernel(where, in_mine, in_row, b_mine, b_row, q_mine, q_row, *outs):
    core, member = where[1], where[2]
    half = outs[0].shape[1]
    rows = in_mine.shape[0] // 2
    blocks, thirds = in_mine.shape[1] // half, q_mine.shape[1] // half
    for side, out in enumerate(outs):
        at = pl.ds(pl.multiple_of(lax.bitwise_xor(core, side) * rows, 16), rows)
        whole = (in_mine[at, :].astype(F32) + in_row[at, :].astype(F32)).astype(BF)
        for i in range(blocks):
            out[i * rows : (i + 1) * rows, :] = whole[:, i * half : (i + 1) * half]
        mine = lax.bitwise_xor(core, side) == member
        first = blocks * rows
        out[first : first + b_mine.shape[0], :] = jnp.where(mine, b_mine[...], b_row[...])
        first += b_mine.shape[0]
        q = jnp.where(mine, q_mine[...], q_row[...])
        for i in range(thirds):
            out[first + i * rows : first + (i + 1) * rows, :] = q[:, i * half : (i + 1) * half]


def pack_call(where, in_pair, b_pair, q_pair):
    half = b_pair[0].shape[1]
    rows = in_pair[0].shape[0] // 2
    height = rows * (in_pair[0].shape[1] + q_pair[0].shape[1]) // half + b_pair[0].shape[0]
    return pl.pallas_call(
        pack_kernel,
        out_shape=[jax.ShapeDtypeStruct((height, half), BF)] * 2,
        grid_spec=pltpu.PrefetchScalarGridSpec(
            num_scalar_prefetch=1,
            grid=(1,),
            in_specs=[
                pl.BlockSpec(a.shape, lambda i, where: (0, 0)) for pair in (in_pair, b_pair, q_pair) for a in pair
            ],
            out_specs=[pl.BlockSpec((height, half), lambda i, where: (0, 0))] * 2,
        ),
        compiler_params=pltpu.CompilerParams(vmem_limit_bytes=20 * 2**20),
        cost_estimate=pl.CostEstimate(flops=0, bytes_accessed=8 * height * half // SHARE, transcendentals=0),
        name="pack",
    )(where, *in_pair, *b_pair, *q_pair)


def unpack_kernel(where, kept, other, in_o, back_o, out_o, qkv_o, *, groups):
    core = where[1]
    half = kept.shape[1]
    rows, share = in_o.shape[0], back_o.shape[0]
    for side in range(2):
        own = (core == side).astype(F32)
        whole = jnp.where(own > 0.5, kept[...], other[...]).astype(F32)
        at = 0
        for i in range(in_o.shape[1] // 2 // half):
            first = side * (in_o.shape[1] // 2) + i * half
            in_o[:, first : first + half] = whole[at : at + rows]
            at += rows
        back_o[:, side * half : (side + 1) * half] = whole[at : at + share]
        at += share
        out_o[:, side * half : (side + 1) * half] = whole[at : at + rows]
        at += rows
        line = jnp.concatenate([whole[at + i * rows : at + (i + 1) * rows] for i in range(3)], axis=1)
        start, place = 0, 0
        for n in groups:
            for part in range(3):
                to = part * 2 * half + side * half + place
                qkv_o[:, to : to + n] = line[:, start + part * n : start + (part + 1) * n]
            start, place = start + 3 * n, place + n


def unpack_call(where, kept, other, shapes, groups):
    return pl.pallas_call(
        functools.partial(unpack_kernel, groups=groups),
        out_shape=[jax.ShapeDtypeStruct(shape, F32) for shape in shapes],
        grid_spec=pltpu.PrefetchScalarGridSpec(
            num_scalar_prefetch=1,
            grid=(1,),
            in_specs=[pl.BlockSpec(kept.shape, lambda i, where: (0, 0))] * 2,
            out_specs=[pl.BlockSpec(shape, lambda i, where: (0, 0)) for shape in shapes],
        ),
        compiler_params=pltpu.CompilerParams(vmem_limit_bytes=24 * 2**20),
        cost_estimate=pl.CostEstimate(flops=0, bytes_accessed=12 * kept.size // SHARE, transcendentals=0),
        name="unpack",
    )(where, kept, other)


def own_kernel(where, w, out):
    out[...] = w[...]


def own_columns_call(where, w):
    depth, width = w.shape
    tile = width // 6
    return pl.pallas_call(
        own_kernel,
        out_shape=jax.ShapeDtypeStruct((depth, width // 2), w.dtype),
        grid_spec=pltpu.PrefetchScalarGridSpec(
            num_scalar_prefetch=1,
            grid=(2, 3),
            in_specs=[pl.BlockSpec((depth // 2, tile), lambda j, i, where: (j, 2 * i + where[1]))],
            out_specs=pl.BlockSpec((depth // 2, tile), lambda j, i, where: (j, i)),
        ),
        compiler_params=pltpu.CompilerParams(vmem_limit_bytes=VMEM_LIMIT),
        cost_estimate=pl.CostEstimate(flops=0, bytes_accessed=2 * depth * width // SHARE, transcendentals=0),
        name="own_columns",
    )(where, w)


def product_kernel(*refs, dims, spans):
    parts = len(spans) if spans else 1
    total = None
    if spans:
        cuts, refs = refs[-parts:], refs[:-parts]

        @pl.when(pl.program_id(0) == 0)
        def _():
            for i in range(parts):
                at = 0
                for low, high in spans[i]:
                    cuts[i][:, at : at + high - low] = refs[parts][:, low:high]
                    at += high - low

    else:
        cuts = [refs[parts]]
    for i in range(parts):
        part = dot(refs[i][...], cuts[i][...], dims)
        total = part if total is None else total + part
    for term in refs[parts + 1 : -1]:
        total = total + term[...]
    refs[-1][...] = total.astype(refs[-1].dtype)


def product(parts, b, dims, name, spans=None, terms=(), half=None):
    tile = 256 if sum(a.shape[1] for a in parts) > 2560 else 640
    turned = dims == NT
    rows = parts[0].shape[0] // (1 if half is None else 2)
    place = half or 0
    width = b.shape[0 if turned else 1]
    depth = sum(a.shape[1] for a in parts)
    out_spec, steps = pl.BlockSpec((rows, tile), lambda i: (0, i)), width // tile
    ins = [
        pl.BlockSpec((rows, a.shape[1]), lambda i: (place, 0), pipeline_mode=pl.Buffered(1)) for a in parts
    ]
    if spans:
        steps = rows // 256
        ins = [pl.BlockSpec((256, a.shape[1]), lambda i: (place * steps + i, 0)) for a in parts]
        ins.append(pl.BlockSpec(b.shape, lambda i: (0, 0), pipeline_mode=pl.Buffered(1)))
        out_spec = pl.BlockSpec((256, width), lambda i: (i, 0))
    elif turned:
        ins.append(pl.BlockSpec((tile, b.shape[1]), lambda i: (i, 0)))
    else:
        ins.append(pl.BlockSpec((b.shape[0], tile), lambda i: (0, i)))
    return pl.pallas_call(
        functools.partial(product_kernel, dims=dims, spans=spans),
        out_shape=jax.ShapeDtypeStruct((rows, width), BF),
        grid=(steps,),
        in_specs=ins + [pl.BlockSpec((t.shape[0], tile), lambda i: (0, i)) for t in terms],
        out_specs=out_spec,
        scratch_shapes=[pltpu.VMEM((width, a.shape[1]), BF) for a in parts] if spans else [],
        compiler_params=pltpu.CompilerParams(vmem_limit_bytes=VMEM_LIMIT),
        cost_estimate=pl.CostEstimate(
            flops=2 * rows * depth * width // SHARE,
            bytes_accessed=2 * (rows * depth + depth * width + rows * width) // SHARE,
            transcendentals=0,
        ),
        name=name,
    )(*parts, b, *terms)


def tile_flags(queries, keys, tq, tk):
    q_first, q_last = queries[:, ::tq], queries[:, tq - 1 :: tq]
    k_first, k_last = keys[:, ::tk], keys[:, tk - 1 :: tk]
    meet = (q_first[:, :, None] <= k_last[:, None, :]) & (k_first[:, None, :] <= q_last[:, :, None])
    whole = (
        (q_first == q_last)[:, :, None]
        & (k_first == k_last)[:, None, :]
        & (q_first[:, :, None] == k_first[:, None, :])
    )
    return jnp.where(whole, 2, jnp.where(meet, 1, 0)).astype(jnp.int32)


def layer_norm_parts(values):
    centred = values - jnp.mean(values, axis=-1, keepdims=True)
    rstd = lax.rsqrt(jnp.mean(centred * centred, axis=-1, keepdims=True) + EPS)
    return centred * rstd, rstd


def layer_norm_back(d_norm, gain, xhat, rstd):
    e = d_norm * gain
    return rstd * (
        e - jnp.mean(e, axis=-1, keepdims=True) - xhat * jnp.mean(e * xhat, axis=-1, keepdims=True)
    )


def on_device(
    tokens,
    cell_start,
    norm1_gain,
    norm1_bias,
    w_qkv,
    bias_q,
    bias_v,
    w_out,
    bias_out,
    norm2_gain,
    norm2_bias,
    w_in,
    bias_in,
    w_back,
    bias_back,
    cotangent,
):
    rows, seg, width = tokens.shape
    count = rows * seg
    ff = w_in.shape[1]
    half = width // 2
    wide = lax.axis_size("wide")
    group = lax.axis_size("blk")
    place = lax.axis_index("wide")
    member = lax.axis_index("blk")
    core = place % 2
    chips = wide // 2
    first = 2 if chips <= 8 else 4
    second = chips // first
    heads = HEADS // 2
    early = 6
    spans = ((0, early), (early, heads))
    tq, tk = min(512, seg), min(256, seg)
    halves = group == 2 and ff // chips % 128 == 0
    where = jnp.stack([place // 2, core, member]).astype(jnp.int32)
    where_out = jnp.stack([lax.bitwise_xor(place // 2, core * (chips // 2)), core, member]).astype(jnp.int32)

    def after(value, *earlier):
        return lax.optimization_barrier((value, earlier))[0]

    def across(array, by):
        return lax.ppermute(array, "wide", [(i, i ^ by) for i in range(wide)])

    def to_mate(array):
        return across(array, 1)

    def from_ahead(array, by):
        return lax.ppermute(array, "blk", [((i + by) % group, i) for i in range(group)])

    def to_ahead(array, by):
        return lax.ppermute(array, "blk", [(i, (i + by) % group) for i in range(group)])

    def from_all_ahead(array):
        parts = [from_ahead(array, by) for by in range(1, group)]
        return parts[0] if len(parts) == 1 else jnp.concatenate(parts, axis=1)

    def cut(array, start, size, axis):
        return lax.dynamic_slice_in_dim(array, start, size, axis)

    def paired(array):
        return jnp.concatenate([array, to_mate(array)], axis=0)

    inputs = tokens.astype(F32).reshape(count, width)
    xhat1, rstd1 = layer_norm_parts(inputs)
    acts = (xhat1 * norm1_gain + norm1_bias).astype(BF).reshape(tokens.shape)
    cells = paired(cell_start)
    far_cells = from_all_ahead(cells)
    acts = after(acts, far_cells)
    far_own = from_all_ahead(acts)
    acts_pair = paired(acts).reshape(2 * count, width)
    w_own = own_columns_call(where, w_qkv)
    b_own = jnp.concatenate([cut(bias_q, core * half, half, 0), jnp.zeros((half,), F32), cut(bias_v, core * half, half, 0)])

    def own_columns(span, parts):
        return tuple((part * half + span[0] * HD, part * half + span[1] * HD) for part in parts)

    near_spans = tuple(own_columns(span, (0, 1, 2)) for span in spans)
    far_spans = tuple(own_columns(span, (1, 2)) for span in spans)

    def columns(array):
        return jnp.broadcast_to(array[:, :, None], array.shape + (128,))

    qkv = (dot(acts_pair, w_own, NN) + b_own).astype(BF).reshape(2 * rows, seg, 3 * half)
    near_flags = tile_flags(cells, cells, tq, tk)
    far_flags = tile_flags(cells, far_cells, tq, tk)
    cell_rows = cells[:, None, :]
    near_columns, far_columns = columns(cells), columns(far_cells)
    state = attn_fwd(near_flags, cell_rows, near_columns, qkv, qkv, 1, None, tq, tk, heads)
    d_out = cotangent.reshape(count, width)
    d_out_mate = to_mate(after(d_out, acts_pair))
    far_own = after(far_own, state)
    far_mate = to_mate(far_own)
    d_act = dot(after(d_out, far_own, state, d_out_mate), w_back, NT).astype(BF)

    far_mate = after(far_mate, d_act)
    far_pair = jnp.concatenate([far_own, far_mate], axis=0)
    far_len = far_pair.shape[1]
    far_pair = far_pair.reshape(-1, width)
    far_kv = (dot(far_pair, w_own[:, half:], NN) + b_own[half:]).astype(BF).reshape(2 * rows, far_len, 2 * half)
    *attended, stats = attn_fwd(far_flags, cell_rows, far_columns, qkv, far_kv, 0, state, tq, tk, heads)
    mine, theirs = (part.reshape(count, half) for part in attended)
    own_rest = to_mate(theirs)
    mate_rest = to_mate(mine)
    w_out_own = cut(w_out, core * half, half, 0)
    w_out_mate = cut(w_out, (1 - core) * half, half, 0)
    middle = inputs + (dot(mine, w_out_own, NN) + dot(own_rest, w_out_mate, NN)) + bias_out

    xhat2, _ = layer_norm_parts(middle)
    acts2 = (xhat2 * norm2_gain + norm2_bias).astype(BF)
    acts2_mate = to_mate(acts2)
    b_in = bias_in.reshape(1, ff)
    act_part, d_pre_theirs, sum_part, norm_part = ffn_call(
        where, after(acts2, mate_rest), w_in, b_in, d_act, (), "ffn_theirs"
    )
    d_pre_mate = to_mate(d_pre_theirs)
    act, d_pre_mine, d_pre_sum, d_middle, d_z, d_att_theirs, d_att_mine, z_sums = ffn_call(
        where, acts2, w_in, b_in, d_act,
        (act_part, sum_part, norm_part, middle, d_out, w_out, norm2_gain.reshape(1, width)), "ffn_mine",
    )
    act_mate = to_mate(after(act, d_pre_mate, acts2_mate))
    grad_out = d_out.astype(F32)
    d_att_mate = to_mate(d_att_theirs)
    d_z_mate = to_mate(d_z)

    def send(parts):
        return [across(parts[one], 2 * one) for one in range(1, first)]

    def add_first(parts, received):
        def added(at):
            total = parts[0][at].astype(F32)
            for part in received:
                total = total + part[at].astype(F32)
            return total.astype(BF)

        return added(slice(0, second // 2)), added(slice(second // 2, second))

    def send_second(pair):
        return across(pair[1], first * second)

    def add_second(pair, received):
        return tuple((pair[0][at].astype(F32) + received[at].astype(F32)).astype(BF) for at in range(2))

    def send_third(pair):
        return across(pair[1], 2 * first)

    def add_third(pair, received):
        return (pair[0].astype(F32) + received.astype(F32)).astype(BF)

    def start(parts):
        return from_ahead(parts[1], 1) if halves else send(parts)

    def middle_step(parts, received):
        if not halves:
            return parts, received
        sums = [(parts[0][one].astype(F32) + received[one].astype(F32)).astype(BF) for one in range(first)]
        return sums, send(sums)

    def ahead(total):
        return from_ahead(total, 1) if group == 2 else None

    def over_row(total, other):
        if group == 2:
            return (total.astype(F32) + other.astype(F32)).astype(BF)
        return lax.psum(total, "blk")

    def by_core(total):
        split = total.reshape(2, -1, total.shape[-1])
        return [lax.dynamic_index_in_dim(split, i, 0, keepdims=False) for i in (core, 1 - core)]

    def joined(total, other, sizes):
        total = over_row(total, other)
        parts, at = [], 0
        for size in sizes:
            parts.append(by_core(total[at : at + size]))
            at += size
        return [jnp.concatenate(part, axis=0) for part in zip(*parts)]

    def in_blocks(array):
        return [array[:, at : at + half] for at in range(0, array.shape[1], half)]

    d_pre_held = d_pre_mine
    grad_in = grad_call(
        where, [[(acts2, d_pre_held, 0), (acts2_mate, d_pre_mate, 0)]], ff // 2, first, second, 512, False, "grad_in"
    )
    in_in = send(grad_in)
    act_held, act_mate, d_z_mate = after((act, act_mate, d_z_mate), grad_in)

    def grad_o(into):
        return grad_call(
            where_out,
            [
                [(mine, d_z, None), (theirs, d_z_mate, None)],
                [(own_rest, d_z, None), (mate_rest, d_z_mate, None)],
            ],
            half, first, second, half, halves, "grad_out", into,
        )

    back_rows, out_rows = ff // chips, width // chips
    if halves:
        grad_b = back_call(
            where, (act_held, d_out), (act_mate, d_out_mate), first, second, out_rows // 2, "grad_back"
        )
        grad_b = grad_o(tuple(grad_b))
    else:
        whole = dot(act_held, cut(d_out, core * half, half, 1), TN) + dot(act_mate, cut(d_out_mate, core * half, half, 1), TN)
        whole = whole.astype(BF).reshape(chips, back_rows, half)
        grad_b = [
            jnp.concatenate([
                jnp.stack([whole[lax.bitwise_xor(two * first + one, where[0])] for two in range(second)]), other
            ], axis=1)
            for one, other in enumerate(grad_o(()))
        ]
    b_in = start(grad_b)

    back_tq = min(256, seg)
    near_flags, far_flags = tile_flags(cells, cells, back_tq, tk), tile_flags(cells, far_cells, back_tq, tk)
    d_att = after((d_att_mine.reshape(rows, seg, half), d_att_mate.reshape(rows, seg, half)), grad_b)
    d_qT, far_early, far_late = attn_bwd(
        far_flags, cell_rows, far_columns, qkv, far_kv, 0, d_att, attended, stats, None, back_tq, tk, heads, spans, "attn_bwd_far"
    )
    in_sums = add_first(grad_in, after(in_in, d_qT))
    in_more = send_second(in_sums)
    far_early, far_late = after((far_early, far_late), in_sums)
    far_early, far_late = (f.reshape(-1, f.shape[-1]) for f in (far_early, far_late))
    n_early, n_late = early * HD, (heads - early) * HD
    far_theirs = product([far_early, far_late], w_own, NT, "far_norm_theirs", far_spans, half=1)
    far_given = to_mate(far_theirs)
    far_mine = product([after(far_early, far_theirs), far_late], w_own, NT, "far_norm_mine", far_spans, half=0)
    far_sum = (far_mine.astype(F32) + after(far_given, in_sums, far_mine).astype(F32)).astype(BF)
    far_sum = far_sum.reshape(rows, far_len, width)
    far_back = [to_ahead(far_sum[:, by * seg : (by + 1) * seg], by + 1) for by in range(group - 1)]
    d_qT = after(d_qT, far_sum)

    def near_back(span, name, *earlier):
        (out,) = attn_bwd(
            near_flags, cell_rows, near_columns, qkv, qkv, 1, d_att, attended, stats, after(d_qT, earlier), back_tq, tk, heads,
            (span,), name,
        )
        return out.reshape(2 * count, -1)

    near_early = near_back(spans[0], "attn_bwd_early")
    b_sums, b_in = middle_step(grad_b, after(b_in, near_early))
    in_two = add_second(in_sums, after(in_more, b_sums))
    in_last = send_third(in_two)
    near_early = after(near_early, b_sums, in_two)
    *grad_e, sum_e = qkv_call(where, (acts_pair, near_early), (far_pair, far_early), first, second, halves, "grad_early")
    in_total = add_third(in_two, after(in_last, grad_e))
    in_row = ahead(in_total)
    grad_e, far_back = after((grad_e, far_back), in_total)
    e_in = start(grad_e)
    near_late = near_back(spans[1], "attn_bwd_late", grad_e, far_back)
    b_two = add_first(b_sums, after(b_in, near_late))
    b_more = send_second(b_two)
    e_sums, e_in = middle_step(grad_e, after(e_in, b_two))
    near_late = after(near_late, b_two, e_sums)
    *grad_l, sum_l = qkv_call(where, (acts_pair, near_late), (far_pair, far_late), first, second, halves, "grad_late")
    l_in = start(grad_l)
    near_held = after(near_early, grad_l)
    near_theirs = product([near_held, near_late], w_own, NT, "near_norm_theirs", near_spans, half=1)
    near_mine = product([after(near_held, near_theirs), near_late], w_own, NT, "near_norm_mine", near_spans, half=0)
    e_two = add_first(e_sums, after(e_in, near_mine))
    e_more = send_second(e_two)
    b_three = add_second(b_two, after(b_more, e_two))
    b_last = send_third(b_three)
    l_sums, l_in = middle_step(grad_l, after(l_in, b_three))
    near_given = to_mate(after(near_theirs, near_mine))
    in_row = after(in_row, near_mine)
    act_late = after(act_held, e_two, b_three, l_sums, in_row)
    mixed = product([act_late], w_back, NN, "mixed", terms=(middle, bias_back.reshape(1, width))).reshape(tokens.shape)
    l_two = add_first(l_sums, after(l_in, mixed))
    l_more = send_second(l_two)
    e_three = add_second(e_two, after(e_more, l_two))
    e_last = send_third(e_three)
    b_total = add_third(b_three, after(b_last, e_three))
    b_row = ahead(b_total)
    near_mine, near_given = after((near_mine, near_given), l_two, e_three, b_total)
    grad_tokens, norm1_sums = first_norm_call(
        tokens.reshape(count, width), d_middle, norm1_gain.reshape(1, width),
        [near_mine, near_given, *(part.reshape(count, width) for part in far_back)],
    )
    grad_tokens = grad_tokens.reshape(tokens.shape)

    def vector_stage(total, stride, size):
        total = total.reshape(-1, size, stride, total.shape[-1])
        spot = (place // stride) % size
        kept = lax.dynamic_index_in_dim(total, spot, 1, keepdims=False)
        for by in range(1, size):
            kept = kept + across(lax.dynamic_index_in_dim(total, spot ^ by, 1, keepdims=False), by * stride)
        return kept.reshape(stride, -1)

    def widened(part):
        n = sum_e.shape[1] // 3, sum_l.shape[1] // 3
        own = jnp.concatenate([s[0, part * m : (part + 1) * m] for s, m in zip((sum_e, sum_l), n)])
        return lax.dynamic_update_slice_in_dim(jnp.zeros((width,), F32), own, core * half, 0)

    parts = [
        norm1_sums[0],
        norm1_sums[1],
        widened(0),
        widened(2),
        z_sums[0],
        z_sums[1],
        z_sums[2],
        d_pre_sum,
        jnp.sum(grad_out, axis=0),
    ]
    totals = vector_stage(jnp.concatenate([part.reshape(wide, -1) for part in parts], axis=1), 2 * first, second)
    e_total = add_third(e_three, after(e_last, norm1_sums))
    l_three = add_second(l_two, after(l_more, e_total))
    l_last = send_third(l_three)
    totals = vector_stage(totals, 2, first)

    l_total = add_third(l_three, after(l_last, totals))
    totals = vector_stage(totals, 1, 2).reshape(-1)
    qkv_total = jnp.concatenate([e_total, l_total], axis=1)
    qkv_row = ahead(qkv_total)
    in_total, b_total = after((in_total, b_total), grad_tokens, totals)
    totals = totals + from_ahead(totals, 1) if group == 2 else lax.psum(totals, "blk")
    if halves:
        kept, given = pack_call(where, (in_total, in_row), (b_total, b_row), (qkv_total, qkv_row))
    else:
        in_parts = by_core(over_row(in_total, in_row))
        b_parts = joined(b_total, b_row, [back_rows, out_rows])
        qkv_parts = joined(qkv_total, qkv_row, [out_rows])
        kept, given = (
            jnp.concatenate(in_blocks(i) + [b] + in_blocks(q), axis=0)
            for i, b, q in zip(in_parts, b_parts, qkv_parts)
        )
    other = after(to_mate(given), totals)
    share = ff // wide
    own_rows = width // wide
    in_count = ff // 2 // half

    def rows_of(array, first_row, size):
        return array[first_row : first_row + size]

    def blocks_of(array, first_row, count):
        return [rows_of(array, first_row + i * own_rows, own_rows) for i in range(count)]

    if halves:
        shapes = [(own_rows, ff), (share, width), (own_rows, width), (own_rows, 3 * width)]
        grad_w_in, grad_w_back, grad_w_out, grad_w_qkv = unpack_call(where, kept, other, shapes, (n_early, n_late))
    else:
        low, high = (jnp.where(core == side, kept, other).astype(F32) for side in range(2))
        b_at = in_count * own_rows
        q_at = b_at + share + own_rows

        def part_columns(part):
            columns = []
            for side in (low, high):
                wide_rows = jnp.concatenate(blocks_of(side, q_at, 3), axis=1)
                for start, n in ((0, n_early), (3 * n_early, n_late)):
                    columns.append(wide_rows[:, start + part * n : start + (part + 1) * n])
            return columns

        grad_w_in = jnp.concatenate([b for side in (low, high) for b in blocks_of(side, 0, in_count)], axis=1)
        grad_w_back = jnp.concatenate([rows_of(side, b_at, share) for side in (low, high)], axis=1)
        grad_w_out = jnp.concatenate([rows_of(side, b_at + share, own_rows) for side in (low, high)], axis=1)
        grad_w_qkv = jnp.concatenate([piece for part in range(3) for piece in part_columns(part)], axis=1)

    small, at = [], 0
    for part in parts:
        size = part.size // wide
        small.append(totals[at : at + size])
        at += size

    return (
        mixed,
        grad_tokens,
        small[0],
        small[1],
        grad_w_qkv,
        small[2],
        small[3],
        grad_w_out,
        small[4],
        small[5],
        small[6],
        grad_w_in,
        small[7],
        grad_w_back,
        small[8],
    )


def solution(mesh):
    spread = P("wide", "blk", None)
    placed = (spread, P("wide", "blk")) + (P(),) * 13 + (spread,)
    matrix, vector = P("wide", None), P("wide")
    return jax.shard_map(
        on_device,
        mesh=mesh,
        in_specs=placed,
        out_specs=(
            spread, spread, vector, vector, matrix, vector, vector, matrix, vector, vector, vector,
            matrix, vector, matrix, vector,
        ),
        check_vma=False,
    )
```

```python
import functools
import math

import jax
import jax.numpy as jnp
from jax import lax
from jax.experimental import pallas as pl
from jax.experimental.pallas import tpu as pltpu
from jax.sharding import PartitionSpec as P

HEADS = 20
HEAD_DIM = 64
HD = HEAD_DIM
EPS = 1e-05
NEG = -1e30
LOG2E = math.log2(math.e)
C2 = LOG2E / math.sqrt(HEAD_DIM)
F32 = jnp.float32
BF = jnp.bfloat16
NN = (((1,), (0,)), ((), ()))
NT = (((1,), (1,)), ((), ()))
TN = (((0,), (0,)), ((), ()))
VMEM_LIMIT = 56 * 2**20
SHARE = 10
VR = HD + 16


def dot(a, b, dims):
    return lax.dot_general(a, b, dims, preferred_element_type=F32)


def own_map(nr,last):
    return lambda r,i,*_:(jnp.minimum(r,nr//2-1),jnp.where(r<nr//2,i,last-1),0)

def mate_map(nr):
    return lambda r,i,*_:(jnp.maximum(r-nr//2,0),jnp.where(r<nr//2,0,i),0)

def head_sumsq(x,hp16):
    W=x.shape[1]
    sq=x.astype(F32)*x.astype(F32)
    row=lax.broadcasted_iota(jnp.int32,(hp16,W),0); col=lax.broadcasted_iota(jnp.int32,(hp16,W),1)
    ones=jnp.where(row==col//HD,1.0,0.0).astype(BF)
    return lax.dot_general(ones,sq.astype(BF),NT,preferred_element_type=F32)

def fwd_kernel(flags,cq,ck,q,k,v,*rest,first,tq,tk,heads):
    if first:
        accT_o,m_o,l_o,qm,vT,bias,acc,m,l,kn=rest
    else:
        accT_i,m_i,l_i,o_own,o_mate,lse_o,qm,vT,bias,acc,m,l,kn=rest
    r=pl.program_id(0); qi=pl.program_id(1)
    nk=k.shape[1]//tk
    hp16=m.shape[0]
    @pl.when(qi==0)
    def _():
        for hh in range(heads):
            vT[hh*VR:hh*VR+HD,:]=v[0,:,hh*HD:(hh+1)*HD].T
            vT[hh*VR+HD:(hh+1)*VR,:]=jnp.ones((VR-HD,vT.shape[1]),BF)
        kn[...]=jnp.broadcast_to(jnp.sqrt(jnp.max(head_sumsq(k[0],hp16),1,keepdims=True)),kn.shape)
    lane=lax.broadcasted_iota(jnp.int32,(tq,128),1)
    for hp in range(heads//2):
        qp=q[0,:,hp*128:(hp+1)*128]
        qm[2*hp]=jnp.where(lane<64,qp,0).astype(BF)
        qm[2*hp+1]=jnp.where(lane>=64,qp,0).astype(BF)
    bound=jnp.sqrt(head_sumsq(q[0],hp16))*kn[:,0:1]*(C2*1.02)
    safe=jnp.max(bound)<50.0
    if first:
        m0=bound
    else:
        m0=jnp.maximum(bound,m_i[0])
    def loop(online):
        if first:
            acc[...]=jnp.zeros_like(acc); l[...]=jnp.zeros_like(l)
            m[...]=jnp.full_like(m,NEG) if online else m0
        elif online:
            acc[...]=accT_i[0]; m[...]=m_i[0]; l[...]=l_i[0]
        else:
            al=jnp.exp2(m_i[0]-m0)
            m[...]=m0; l[...]=al*l_i[0]
            for hh in range(heads):
                hs=slice(hh*HD,(hh+1)*HD)
                acc[hs,:]=al[hh:hh+1,:]*accT_i[0,hs,:]
        def body(kt,masked):
            ks=pl.ds(pl.multiple_of(kt*tk,tk),tk)
            if online:
                @pl.loop(0,heads//2)
                def _(hp):
                    kp=k[0,ks,pl.ds(pl.multiple_of(hp*128,128),128)]
                    for j in range(2):
                        hh=2*hp+j
                        s=lax.dot_general(kp,qm[hh],NT,preferred_element_type=F32)*C2+bias[...]
                        mp=m[pl.ds(hh,1),:]
                        mn=jnp.maximum(mp,jnp.max(s,0,keepdims=True))
                        p=jnp.exp2(s-mn)
                        al=jnp.exp2(mp-mn)
                        m[pl.ds(hh,1),:]=mn
                        l[pl.ds(hh,1),:]=al*l[pl.ds(hh,1),:]+jnp.sum(p,0,keepdims=True)
                        hs=pl.ds(pl.multiple_of(hh*HD,HD),HD)
                        vs=pl.ds(pl.multiple_of(hh*VR,16),HD)
                        acc[hs,:]=al*acc[hs,:]+lax.dot_general(vT[vs,ks],p.astype(BF),NN,preferred_element_type=F32)
                return
            def score(hh):
                s=lax.dot_general(k[0,ks,(hh//2)*128:(hh//2+1)*128],qm[hh],NT,preferred_element_type=F32)*C2
                if masked: s=s+bias[...]
                return s
            s=score(0); pp=None
            for hh in range(heads+1):
                if hh+1<heads: sn=score(hh+1)
                if pp is not None:
                    h1=hh-1
                    both=lax.dot_general(vT[h1*VR:(h1+1)*VR,ks],pp,NN,preferred_element_type=F32)
                    acc[h1*HD:(h1+1)*HD,:]+=both[:HD]
                    l[h1:h1+1,:]+=both[HD:HD+1]
                if hh<heads:
                    p=jnp.exp2(s-m[hh:hh+1,:])
                    pp=p.astype(BF)
                s=sn
        @pl.loop(0,nk)
        def _(kt):
            f=flags[r,qi,kt]
            def mask():
                ks=pl.ds(pl.multiple_of(kt*tk,tk),tk)
                bias[...]=jnp.where(ck[0,ks,0:1]==cq[0,0:1,:],0.0,NEG)
            if online:
                @pl.when(f>0)
                def _():
                    mask(); body(kt,True)
            else:
                @pl.when(f==1)
                def _():
                    mask(); body(kt,True)
                @pl.when(f==2)
                def _(): body(kt,False)
    @pl.when(safe)
    def _(): loop(False)
    @pl.when(jnp.logical_not(safe))
    def _(): loop(True)
    if first:
        accT_o[0]=acc[...]; m_o[0]=m[...]; l_o[0]=l[...]
    else:
        for hp in range(heads//2):
            parts=[]
            for hh in (2*hp,2*hp+1):
                parts.append(acc[hh*HD:(hh+1)*HD,:]/l[hh:hh+1,:])
            low=jnp.concatenate(parts,0).T.astype(BF)
            @pl.when(r<pl.num_programs(0)//2)
            def _(): o_own[0,:,hp*128:(hp+1)*128]=low
            @pl.when(r>=pl.num_programs(0)//2)
            def _(): o_mate[0,:,hp*128:(hp+1)*128]=low
        lse_o[0]=m[...]+jnp.log2(l[...])

def attn_fwd(flags,cq,ck,q,kv,kb,state,tq,tk,heads):
    nr,S,_=q.shape; W=heads*HD; Sk=kv.shape[1]; hp16=-(-heads//8)*8
    first=state is None
    qs=lambda r,i,*_:(r,i,0); ts=lambda r,i,*_:(r,0,i); ks=lambda r,i,*_:(r,0,0)
    stspec=[pl.BlockSpec((1,W,tq),ts),pl.BlockSpec((1,hp16,tq),ts),pl.BlockSpec((1,hp16,tq),ts)]
    ins=[pl.BlockSpec((1,1,tq),ts),pl.BlockSpec((1,Sk,128),ks),pl.BlockSpec((1,tq,W),qs),pl.BlockSpec((1,Sk,W),lambda r,i,*_:(r,0,kb)),pl.BlockSpec((1,Sk,W),lambda r,i,*_:(r,0,kb+1))]
    if first:
        outs=stspec
        osh=[jax.ShapeDtypeStruct((nr,W,S),F32)]+[jax.ShapeDtypeStruct((nr,hp16,S),F32)]*2
    else:
        ins=ins+stspec
        outs=[pl.BlockSpec((1,tq,W),own_map(nr,S//tq)),pl.BlockSpec((1,tq,W),mate_map(nr)),pl.BlockSpec((1,hp16,tq),ts)]
        osh=[jax.ShapeDtypeStruct((nr//2,S,W),BF)]*2+[jax.ShapeDtypeStruct((nr,hp16,S),F32)]
    fl=4*nr*S*Sk*W
    return pl.pallas_call(functools.partial(fwd_kernel,first=first,tq=tq,tk=tk,heads=heads),
        out_shape=osh,
        grid_spec=pltpu.PrefetchScalarGridSpec(num_scalar_prefetch=1,grid=(nr,S//tq),in_specs=ins,out_specs=outs,
          scratch_shapes=[pltpu.VMEM((heads,tq,128),BF),pltpu.VMEM((heads*VR,Sk),BF),pltpu.VMEM((tk,tq),F32),pltpu.VMEM((W,tq),F32),pltpu.VMEM((hp16,tq),F32),pltpu.VMEM((hp16,tq),F32),pltpu.VMEM((hp16,128),F32)]),
        compiler_params=pltpu.CompilerParams(dimension_semantics=("arbitrary","arbitrary"),vmem_limit_bytes=VMEM_LIMIT),
        cost_estimate=pl.CostEstimate(flops=fl//SHARE,bytes_accessed=nr*(S*W*2+2*Sk*W*2+S*W*4)//SHARE,transcendentals=0),
        name="attn_fwd_a" if first else "attn_fwd_b",
    )(flags,cq,ck,q,kv,kv,*(state or ()))

def bwd_kernel(flags,cq,ck,q,k,v,do_own,do_mate,o_own,o_mate,lse,*rest,spans,tq,tk):
    first=len(spans)==2
    if first:
        dqT_o,*dkv_o,qm,dom,kT,bias,dqT,dk,dv,delta=rest
    else:
        dqT_i,dqkv_o,qm,dom,kT,bias,dqT,dk,dv,delta=rest
    r=pl.program_id(0); qi=pl.program_id(1); nq=pl.num_programs(1)
    nk=k.shape[1]//tk
    low=spans[0][0]; heads=sum(b-a for a,b in spans)
    W=heads*HD; c0=low*HD
    @pl.when(qi==0)
    def _():
        kT[...]=k[0,:,c0:c0+W].T
        dk[...]=jnp.zeros_like(dk); dv[...]=jnp.zeros_like(dv)
    own=r<pl.num_programs(0)//2
    lane=lax.broadcasted_iota(jnp.int32,(tq,128),1)
    for hp in range(heads//2):
        c=slice(c0+hp*128,c0+(hp+1)*128)
        qp=q[0,:,c]*jnp.asarray(0.125,BF); dp_=jnp.where(own,do_own[0,:,c],do_mate[0,:,c])
        qm[2*hp]=jnp.where(lane<64,qp,0).astype(BF)
        qm[2*hp+1]=jnp.where(lane>=64,qp,0).astype(BF)
        dom[2*hp]=jnp.where(lane<64,dp_,0).astype(BF)
        dom[2*hp+1]=jnp.where(lane>=64,dp_,0).astype(BF)
    prod=jnp.where(own,do_own[0,:,c0:c0+W],do_mate[0,:,c0:c0+W]).astype(F32)*jnp.where(own,o_own[0,:,c0:c0+W],o_mate[0,:,c0:c0+W]).astype(F32)
    hi=prod.astype(BF); lo=(prod-hi.astype(F32)).astype(BF)
    n16=delta.shape[0]
    row=lax.broadcasted_iota(jnp.int32,(n16,W),0); col_=lax.broadcasted_iota(jnp.int32,(n16,W),1)
    ones=jnp.where(row==col_//HD,1.0,0.0).astype(BF)
    delta[...]=lax.dot_general(ones,hi,NT,preferred_element_type=F32)+lax.dot_general(ones,lo,NT,preferred_element_type=F32)
    if first: dqT[...]=jnp.zeros_like(dqT)
    else: dqT[...]=dqT_i[0,c0:c0+W,:]
    def body(kt):
        ks=pl.ds(pl.multiple_of(kt*tk,tk),tk)
        def col(hh): return slice((hh//2)*128,(hh//2+1)*128)
        def wide(hh): return slice(c0+(hh//2)*128,c0+(hh//2+1)*128)
        def score(hh):
            s=lax.dot_general(k[0,ks,wide(hh)],qm[hh],NT,preferred_element_type=F32)*LOG2E+bias[...]
            return s,lax.dot_general(v[0,ks,wide(hh)],dom[hh],NT,preferred_element_type=F32)
        nxt=score(0); prev=None
        for hh in range(heads+1):
            cur=nxt
            if hh+1<heads: nxt=score(hh+1)
            if prev is not None:
                h1=hh-1; pb,dsb=prev
                hs=slice(h1*HD,(h1+1)*HD)
                dqT[hs,:]+=lax.dot_general(kT[hs,ks],dsb,NN,preferred_element_type=F32)
                dv[ks,col(h1)]+=jnp.dot(pb,dom[h1],preferred_element_type=F32)
                dk[ks,col(h1)]+=jnp.dot(dsb,qm[h1],preferred_element_type=F32)
            if hh<heads:
                s,dp=cur
                at=low+hh
                p=jnp.exp2(s-lse[0,at:at+1,:])
                ds=p*(dp-delta[hh:hh+1,:])
                prev=(p.astype(BF),ds.astype(BF))
    @pl.loop(0,nk)
    def _(kt):
        f=flags[r,qi,kt]
        @pl.when(f>0)
        def _():
            ks=pl.ds(pl.multiple_of(kt*tk,tk),tk)
            bias[...]=jnp.where(ck[0,ks,0:1]==cq[0,0:1,:],0.0,NEG)
            body(kt)
    if first: dqT_o[0]=dqT[...]
    else: dqkv_o[0,pl.ds(pl.multiple_of(qi*tq,tq),tq),0:W]=(dqT[...]*0.125).T.astype(BF)
    @pl.when(qi==nq-1)
    def _():
        if first:
            for (a,b),out in zip(spans,dkv_o):
                n=(b-a)*HD; at=(a-low)*HD
                out[0,:,0:n]=dk[:,at:at+n].astype(BF); out[0,:,n:2*n]=dv[:,at:at+n].astype(BF)
        else:
            dqkv_o[0,:,W:2*W]=dk[...].astype(BF); dqkv_o[0,:,2*W:3*W]=dv[...].astype(BF)

def attn_bwd(flags,cq,ck,q,kv,kb,do,o,lse,dqT,tq,tk,full,spans,name):
    nr,S,_=q.shape; F=full*HD; Sk=kv.shape[1]; n16=lse.shape[1]
    heads=sum(b-a for a,b in spans); W=heads*HD
    first=dqT is None
    qs=lambda r,i,*_:(r,i,0); ts=lambda r,i,*_:(r,0,i); ks=lambda r,i,*_:(r,0,0)
    ins=[pl.BlockSpec((1,1,tq),ts),pl.BlockSpec((1,Sk,128),ks),pl.BlockSpec((1,tq,F),qs),pl.BlockSpec((1,Sk,F),lambda r,i,*_:(r,0,kb)),pl.BlockSpec((1,Sk,F),lambda r,i,*_:(r,0,kb+1)),
         *[pl.BlockSpec((1,tq,F),own_map(nr,S//tq)),pl.BlockSpec((1,tq,F),mate_map(nr))]*2,pl.BlockSpec((1,n16,tq),ts)]
    if first:
        widths=[2*(b-a)*HD for a,b in spans]
        outs=[pl.BlockSpec((1,F,tq),ts)]+[pl.BlockSpec((1,Sk,n),ks) for n in widths]
        osh=[jax.ShapeDtypeStruct((nr,F,S),F32)]+[jax.ShapeDtypeStruct((nr,Sk,n),BF) for n in widths]
        extra=()
    else:
        ins=ins+[pl.BlockSpec((1,F,tq),ts)]
        outs=[pl.BlockSpec((1,Sk,3*W),ks)]; osh=[jax.ShapeDtypeStruct((nr,Sk,3*W),BF)]
        extra=(dqT,)
    fl=10*nr*S*Sk*W
    return pl.pallas_call(functools.partial(bwd_kernel,spans=spans,tq=tq,tk=tk),
        out_shape=osh,
        grid_spec=pltpu.PrefetchScalarGridSpec(num_scalar_prefetch=1,grid=(nr,S//tq),in_specs=ins,out_specs=outs,
          scratch_shapes=[pltpu.VMEM((heads,tq,128),BF),pltpu.VMEM((heads,tq,128),BF),pltpu.VMEM((W,Sk),BF),pltpu.VMEM((tk,tq),F32),pltpu.VMEM((W,tq),F32),
             pltpu.VMEM((Sk,W),F32),pltpu.VMEM((Sk,W),F32),pltpu.VMEM((n16,tq),F32)]),
        compiler_params=pltpu.CompilerParams(dimension_semantics=("arbitrary","arbitrary"),vmem_limit_bytes=VMEM_LIMIT),
        cost_estimate=pl.CostEstimate(flops=fl//SHARE,bytes_accessed=nr*(3*S*W*2+4*Sk*W*2+S*W*4)//SHARE,transcendentals=0),
        name=name,
    )(flags,cq,ck,q,kv,kv,*do,*o,lse,*extra)


def ffn_kernel(where, acts, w, b, d_act, *rest, last):
    step = pl.program_id(0)
    final = pl.num_programs(0) - 1
    rows, width = acts.shape
    chunk = min(256, rows)
    count = rows // chunk
    if last:
        ins, outs, scratch = rest[:7], rest[7:15], rest[15:]
        _, _, acc_i, middle_i, d_out_i, w_out_i, gain = ins
        act_o, d_pre_o, sum_o, mid_o, d_z_o, theirs_o, mine_o, sums_o = outs
        acc, part, middle, d_out, w_out, d_z, att, in_sem, out_sem = scratch
        loads = [
            pltpu.make_async_copy(source, target, in_sem.at[n])
            for n, (source, target) in enumerate(
                ((acc_i, part), (middle_i, middle), (d_out_i, d_out), (w_out_i, w_out))
            )
        ]

        @pl.when(step == 0)
        def _():
            for load in loads:
                load.start()
    else:
        act_o, d_pre_o, sum_o, acc = rest

    @pl.when(step == 0)
    def _():
        acc[...] = jnp.zeros_like(acc)

    def span(i):
        return slice(i * chunk, (i + 1) * chunk)

    def product(i):
        return dot(acts[span(i), :], w[...], NN) + b[...]

    pre = product(0)
    total, held = None, None
    for i in range(count + 1):
        following = product(i + 1) if i + 1 < count else None
        if held is not None:
            acc[span(i - 1), :] += dot(held, w[...], NT)
        if i < count:
            at = span(i)
            cdf = 0.5 + 0.5 * lax.erf(pre * math.sqrt(0.5))
            pdf = jnp.exp(-0.5 * pre * pre) * (1.0 / math.sqrt(2.0 * math.pi))
            act_o[at, :] = (pre * cdf).astype(BF)
            held = (d_act[at, :].astype(F32) * (cdf + pre * pdf)).astype(BF)
            d_pre_o[at, :] = held
            summed = jnp.sum(held.astype(F32), axis=0, keepdims=True)
            total = summed if total is None else total + summed
        pre = following
    sum_o[...] = total
    if not last:
        return

    @pl.when(step == final)
    def _():
        for load in loads:
            load.wait()
        half = width // 2
        sums, stores = None, []
        for i in range(count):
            at = span(i)
            d_norm = acc[at, :] + part[at, :]
            xhat, rstd = layer_norm_parts(middle[at, :])
            d_mid = d_out[at, :].astype(F32) + layer_norm_back(d_norm, gain[...], xhat, rstd)
            low = d_mid.astype(BF)
            part[at, :] = d_mid
            d_z[at, :] = low
            for side in range(2):
                first = pl.multiple_of(lax.bitwise_xor(where[1], 1 - side) * half, half)
                att[side, at, :] = dot(low, w_out[pl.ds(first, half), :], NT).astype(BF)
            new = [low.astype(F32), d_norm * xhat, d_norm]
            new = jnp.concatenate([jnp.sum(n, axis=0, keepdims=True) for n in new], axis=0)
            sums = new if sums is None else sums + new
            pairs = ((part, mid_o), (d_z, d_z_o), (att.at[0], theirs_o), (att.at[1], mine_o))
            for n, (source, target) in enumerate(pairs):
                store = pltpu.make_async_copy(
                    source.at[pl.ds(i * chunk, chunk)], target.at[pl.ds(i * chunk, chunk)], out_sem.at[4 * i + n]
                )
                store.start()
                stores.append(store)
        sums_o[0:3, :] = sums
        sums_o[3:8, :] = jnp.zeros((5, width), F32)
        for store in stores:
            store.wait()


def ffn_call(where, acts, w, b, d_act, earlier, name):
    rows, width = acts.shape
    ff = w.shape[1]
    tile = 512
    steps = ff // 2 // tile
    last = bool(earlier)
    chunk = min(256, rows)

    def place(i, where):
        return (where[1] if last else 1 - where[1]) * steps + i

    col = lambda i, where: (0, place(i, where))
    whole = pl.BlockSpec((rows, width), lambda i, where: (0, 0))
    anywhere = pl.BlockSpec(memory_space=pl.ANY)
    out_shape = [
        jax.ShapeDtypeStruct((rows, ff), BF),
        jax.ShapeDtypeStruct((rows, ff // 2), BF),
        jax.ShapeDtypeStruct((1, ff), F32),
    ]
    out_specs = [
        pl.BlockSpec((rows, tile), col),
        pl.BlockSpec((rows, tile), lambda i, where: (0, i)),
        pl.BlockSpec((1, tile), col),
    ]
    ins = [
        pl.BlockSpec((rows, width), lambda i, where: (0, 0), pipeline_mode=pl.Buffered(1)),
        pl.BlockSpec((width, tile), col),
        pl.BlockSpec((1, tile), col),
        pl.BlockSpec((rows, tile), col),
    ]
    scratch = []
    if last:
        ins += [anywhere] * 6 + [pl.BlockSpec((1, width), lambda i, where: (0, 0))]
        out_shape += [
            jax.ShapeDtypeStruct((rows, width), F32),
            jax.ShapeDtypeStruct((rows, width), BF),
            jax.ShapeDtypeStruct((rows, width // 2), BF),
            jax.ShapeDtypeStruct((rows, width // 2), BF),
            jax.ShapeDtypeStruct((8, width), F32),
        ]
        out_specs += [anywhere] * 4 + [pl.BlockSpec((8, width), lambda i, where: (0, 0))]
        scratch = [
            pltpu.VMEM((rows, width), F32),
            pltpu.VMEM((rows, width), F32),
            pltpu.VMEM((rows, width), F32),
            pltpu.VMEM((rows, width), BF),
            pltpu.VMEM((width, width), BF),
            pltpu.VMEM((rows, width), BF),
            pltpu.VMEM((2, rows, width // 2), BF),
            pltpu.SemaphoreType.DMA((4,)),
            pltpu.SemaphoreType.DMA((4 * (rows // chunk),)),
        ]
    else:
        out_shape.append(jax.ShapeDtypeStruct((rows, width), F32))
        out_specs.append(whole)
    return pl.pallas_call(
        functools.partial(ffn_kernel, last=last),
        out_shape=out_shape,
        grid_spec=pltpu.PrefetchScalarGridSpec(
            num_scalar_prefetch=1, grid=(steps,), in_specs=ins, out_specs=out_specs, scratch_shapes=scratch
        ),
        input_output_aliases={5: 0, 6: 2} if last else {},
        compiler_params=pltpu.CompilerParams(vmem_limit_bytes=VMEM_LIMIT),
        cost_estimate=pl.CostEstimate(
            flops=2 * rows * width * ff // SHARE,
            bytes_accessed=(2 * rows * width + width * ff + 3 * rows * ff) // SHARE,
            transcendentals=0,
        ),
        name=name,
    )(where, acts, w, b, d_act, *earlier)


def store_blocks(where, acc, outs, first, second, halved):
    rows = acc.shape[0] // (first * second)
    for one in range(first):
        for two in range(second):
            block = lax.bitwise_xor(two * first + one, where[0]) * rows
            if halved:
                for part in range(2):
                    at = block + lax.bitwise_xor(where[2], part) * (rows // 2)
                    piece = acc[pl.ds(pl.multiple_of(at, 16), rows // 2), :]
                    outs[part][one, two] = piece.astype(BF)
            else:
                outs[one][two] = acc[pl.ds(pl.multiple_of(block, 16), rows), :].astype(BF)


def grad_kernel(where, *refs, groups, first, second, halved, outs):
    acc = refs[-1]
    ins = refs[: sum(2 * g for g in groups)]
    height = acc.shape[0] // len(groups)
    at = 0
    for index, pairs in enumerate(groups):
        total = None
        for _ in range(pairs):
            part = dot(ins[at][...], ins[at + 1][...], TN)
            total = part if total is None else total + part
            at += 2
        acc[index * height : (index + 1) * height, :] = total
    store_blocks(where, acc, refs[-1 - outs : -1], first, second, halved)


def grad_call(where, groups, width, first, second, tile, halved, name, into=()):
    ins, flat, depth = [], [], 0
    for group in groups:
        for a, b, offset in group:
            ins.append(pl.BlockSpec(a.shape, lambda i, where: (0, 0)))
            if offset is None:
                index = lambda i, where: (0, where[1] * (width // tile) + i)
            else:
                index = lambda i, where, offset=offset: (0, offset // tile + i)
            ins.append(pl.BlockSpec((b.shape[0], tile), index))
            flat += [a, b]
            depth += a.shape[0]
    height = sum(g[0][0].shape[1] for g in groups)
    depth = depth // len(groups)
    rows = height // (first * second)
    if halved:
        shape, block = (first, second, rows // 2, width), (first, second, rows // 2, tile)
        outs = 2
        index = lambda i, where: (0, 0, 0, i)
    else:
        shape, block = (second, rows, width), (second, rows, tile)
        outs = first
        index = lambda i, where: (0, 0, i)
    if into:
        shape = into[0].shape
        row = shape[2] * 2 // rows - 1
        index = lambda i, where: (0, 0, row, i)
    return pl.pallas_call(
        functools.partial(
            grad_kernel, groups=[len(g) for g in groups], first=first, second=second, halved=halved, outs=outs
        ),
        out_shape=[jax.ShapeDtypeStruct(shape, BF)] * outs,
        grid_spec=pltpu.PrefetchScalarGridSpec(
            num_scalar_prefetch=1,
            grid=(width // tile,),
            in_specs=ins + [pl.BlockSpec(memory_space=pl.ANY)] * len(into),
            out_specs=[pl.BlockSpec(block, index)] * outs,
            scratch_shapes=[pltpu.VMEM((height, tile), F32)],
        ),
        input_output_aliases={1 + len(flat) + i: i for i in range(len(into))},
        compiler_params=pltpu.CompilerParams(vmem_limit_bytes=VMEM_LIMIT),
        cost_estimate=pl.CostEstimate(
            flops=2 * depth * height * width // SHARE,
            bytes_accessed=2 * (depth * (height + width) + height * width) // SHARE,
            transcendentals=0,
        ),
        name=name,
    )(where, *flat, *into)


def qkv_kernel(where, near_a, near_b, far_a, far_b, *refs, first, second, halved):
    *outs, sum_o, acc = refs
    acc[...] = dot(near_a[...], near_b[...], TN)
    sum_o[...] = jnp.sum(near_b[...].astype(F32), axis=0, keepdims=True)

    @pl.when(pl.program_id(0) > 0)
    def _():
        acc[...] += dot(far_a[...], far_b[...], TN)
        sum_o[...] += jnp.sum(far_b[...].astype(F32), axis=0, keepdims=True)

    store_blocks(where, acc, outs, first, second, halved)


def qkv_call(where, near, far, first, second, halved, name):
    (near_a, near_b), (far_a, far_b) = near, far
    height = near_a.shape[1]
    width = near_b.shape[1]
    tile = width // 3
    rows = height // (first * second)
    if halved:
        shape, block = (first, second, rows // 2, width), (first, second, rows // 2, tile)
        outs = 2
        index = lambda i, where: (0, 0, 0, i)
    else:
        shape, block = (second, rows, width), (second, rows, tile)
        outs = first
        index = lambda i, where: (0, 0, i)
    once = pl.Buffered(1)
    return pl.pallas_call(
        functools.partial(qkv_kernel, first=first, second=second, halved=halved),
        out_shape=[jax.ShapeDtypeStruct(shape, BF)] * outs + [jax.ShapeDtypeStruct((1, width), F32)],
        grid_spec=pltpu.PrefetchScalarGridSpec(
            num_scalar_prefetch=1,
            grid=(3,),
            in_specs=[
                pl.BlockSpec(near_a.shape, lambda i, where: (0, 0), pipeline_mode=once),
                pl.BlockSpec((near_b.shape[0], tile), lambda i, where: (0, i)),
                pl.BlockSpec(far_a.shape, lambda i, where: (0, 0), pipeline_mode=once),
                pl.BlockSpec((far_b.shape[0], tile), lambda i, where: (0, jnp.maximum(i - 1, 0))),
            ],
            out_specs=[pl.BlockSpec(block, index)] * outs + [pl.BlockSpec((1, tile), lambda i, where: (0, i))],
            scratch_shapes=[pltpu.VMEM((height, tile), F32)],
        ),
        compiler_params=pltpu.CompilerParams(vmem_limit_bytes=VMEM_LIMIT),
        cost_estimate=pl.CostEstimate(
            flops=2 * (near_a.shape[0] + far_a.shape[0]) * height * width // SHARE,
            bytes_accessed=2 * ((near_a.shape[0] + far_a.shape[0]) * (height + width) + height * width) // SHARE,
            transcendentals=0,
        ),
        name=name,
    )(where, near_a, near_b, far_a, far_b)


def back_kernel(where, a1, b1, a2, b2, out1, out2, acc):
    acc[...] = dot(a1[...], b1[...], TN) + dot(a2[...], b2[...], TN)
    rows = acc.shape[0] // 2
    for part, out in enumerate((out1, out2)):
        at = lax.bitwise_xor(where[2], part) * rows
        out[0, 0] = acc[pl.ds(pl.multiple_of(at, 16), rows), :].astype(BF)


def back_call(where, own, mate, first, second, extra, name):
    (a1, b1), (a2, b2) = own, mate
    tokens, ff = a1.shape
    rows = ff // (first * second)
    width = b2.shape[1] // 2

    def block(i, where):
        return (0, lax.bitwise_xor(lax.rem(i, second) * first + i // second, where[0]))

    return pl.pallas_call(
        back_kernel,
        out_shape=[jax.ShapeDtypeStruct((first, second, rows // 2 + extra, width), BF)] * 2,
        grid_spec=pltpu.PrefetchScalarGridSpec(
            num_scalar_prefetch=1,
            grid=(first * second,),
            in_specs=[
                pl.BlockSpec((tokens, rows), block),
                pl.BlockSpec((tokens, width), lambda i, where: (0, where[1])),
                pl.BlockSpec((tokens, rows), block),
                pl.BlockSpec((tokens, width), lambda i, where: (0, where[1])),
            ],
            out_specs=[
                pl.BlockSpec(
                    (1, 1, rows // 2, width), lambda i, where: (i // second, lax.rem(i, second), 0, 0)
                )
            ]
            * 2,
            scratch_shapes=[pltpu.VMEM((rows, width), F32)],
        ),
        compiler_params=pltpu.CompilerParams(vmem_limit_bytes=VMEM_LIMIT),
        cost_estimate=pl.CostEstimate(
            flops=4 * tokens * ff * width // SHARE,
            bytes_accessed=2 * (2 * tokens * (ff + width) + ff * width) // SHARE,
            transcendentals=0,
        ),
        name=name,
    )(where, a1, b1, a2, b2)


def first_norm_kernel(tokens, d_middle, gain, *rest):
    parts, (out, sums) = rest[:-2], rest[-2:]
    d_norm = parts[0][...].astype(F32)
    for part in parts[1:]:
        d_norm = d_norm + part[...].astype(F32)
    xhat, rstd = layer_norm_parts(tokens[...].astype(F32))
    out[...] = d_middle[...] + layer_norm_back(d_norm, gain[...], xhat, rstd)
    new = jnp.concatenate(
        [jnp.sum(d_norm * xhat, axis=0, keepdims=True), jnp.sum(d_norm, axis=0, keepdims=True)], axis=0
    )

    @pl.when(pl.program_id(0) == 0)
    def _():
        sums[...] = jnp.zeros_like(sums)

    sums[0:2, :] += new


def first_norm_call(tokens, d_middle, gain, parts):
    rows, width = tokens.shape
    block = pl.BlockSpec((128, width), lambda i: (i, 0))
    return pl.pallas_call(
        first_norm_kernel,
        out_shape=[jax.ShapeDtypeStruct((rows, width), F32), jax.ShapeDtypeStruct((8, width), F32)],
        grid=(rows // 128,),
        in_specs=[block, block, pl.BlockSpec((1, width), lambda i: (0, 0))] + [block] * len(parts),
        out_specs=[block, pl.BlockSpec((8, width), lambda i: (0, 0))],
        compiler_params=pltpu.CompilerParams(vmem_limit_bytes=VMEM_LIMIT),
        cost_estimate=pl.CostEstimate(
            flops=20 * rows * width // SHARE, bytes_accessed=20 * rows * width // SHARE, transcendentals=0
        ),
        name="first_norm",
    )(tokens, d_middle, gain, *parts)


def pack_kernel(where, in_mine, in_row, b_mine, b_row, q_mine, q_row, *outs):
    core, member = where[1], where[2]
    half = outs[0].shape[1]
    rows = in_mine.shape[0] // 2
    blocks, thirds = in_mine.shape[1] // half, q_mine.shape[1] // half
    for side, out in enumerate(outs):
        at = pl.ds(pl.multiple_of(lax.bitwise_xor(core, side) * rows, 16), rows)
        whole = (in_mine[at, :].astype(F32) + in_row[at, :].astype(F32)).astype(BF)
        for i in range(blocks):
            out[i * rows : (i + 1) * rows, :] = whole[:, i * half : (i + 1) * half]
        mine = lax.bitwise_xor(core, side) == member
        first = blocks * rows
        out[first : first + b_mine.shape[0], :] = jnp.where(mine, b_mine[...], b_row[...])
        first += b_mine.shape[0]
        q = jnp.where(mine, q_mine[...], q_row[...])
        for i in range(thirds):
            out[first + i * rows : first + (i + 1) * rows, :] = q[:, i * half : (i + 1) * half]


def pack_call(where, in_pair, b_pair, q_pair):
    half = b_pair[0].shape[1]
    rows = in_pair[0].shape[0] // 2
    height = rows * (in_pair[0].shape[1] + q_pair[0].shape[1]) // half + b_pair[0].shape[0]
    return pl.pallas_call(
        pack_kernel,
        out_shape=[jax.ShapeDtypeStruct((height, half), BF)] * 2,
        grid_spec=pltpu.PrefetchScalarGridSpec(
            num_scalar_prefetch=1,
            grid=(1,),
            in_specs=[
                pl.BlockSpec(a.shape, lambda i, where: (0, 0)) for pair in (in_pair, b_pair, q_pair) for a in pair
            ],
            out_specs=[pl.BlockSpec((height, half), lambda i, where: (0, 0))] * 2,
        ),
        compiler_params=pltpu.CompilerParams(vmem_limit_bytes=20 * 2**20),
        cost_estimate=pl.CostEstimate(flops=0, bytes_accessed=8 * height * half // SHARE, transcendentals=0),
        name="pack",
    )(where, *in_pair, *b_pair, *q_pair)


def unpack_kernel(where, kept, other, in_o, back_o, out_o, qkv_o, *, groups):
    core = where[1]
    half = kept.shape[1]
    rows, share = in_o.shape[0], back_o.shape[0]
    for side in range(2):
        own = (core == side).astype(F32)
        whole = jnp.where(own > 0.5, kept[...], other[...]).astype(F32)
        at = 0
        for i in range(in_o.shape[1] // 2 // half):
            first = side * (in_o.shape[1] // 2) + i * half
            in_o[:, first : first + half] = whole[at : at + rows]
            at += rows
        back_o[:, side * half : (side + 1) * half] = whole[at : at + share]
        at += share
        out_o[:, side * half : (side + 1) * half] = whole[at : at + rows]
        at += rows
        line = jnp.concatenate([whole[at + i * rows : at + (i + 1) * rows] for i in range(3)], axis=1)
        start, place = 0, 0
        for n in groups:
            for part in range(3):
                to = part * 2 * half + side * half + place
                qkv_o[:, to : to + n] = line[:, start + part * n : start + (part + 1) * n]
            start, place = start + 3 * n, place + n


def unpack_call(where, kept, other, shapes, groups):
    return pl.pallas_call(
        functools.partial(unpack_kernel, groups=groups),
        out_shape=[jax.ShapeDtypeStruct(shape, F32) for shape in shapes],
        grid_spec=pltpu.PrefetchScalarGridSpec(
            num_scalar_prefetch=1,
            grid=(1,),
            in_specs=[pl.BlockSpec(kept.shape, lambda i, where: (0, 0))] * 2,
            out_specs=[pl.BlockSpec(shape, lambda i, where: (0, 0)) for shape in shapes],
        ),
        compiler_params=pltpu.CompilerParams(vmem_limit_bytes=24 * 2**20),
        cost_estimate=pl.CostEstimate(flops=0, bytes_accessed=12 * kept.size // SHARE, transcendentals=0),
        name="unpack",
    )(where, kept, other)


def own_kernel(where, w, out, sems):
    width = w.shape[1] // 6
    copies = []
    for part in range(3):
        first = pl.multiple_of((2 * part + where[1]) * width, 128)
        copies.append(
            pltpu.make_async_copy(
                w.at[:, pl.ds(first, width)], out.at[:, pl.ds(part * width, width)], sems.at[part]
            )
        )
    for copy in copies:
        copy.start()
    for copy in copies:
        copy.wait()


def own_columns_call(where, w):
    depth, width = w.shape
    return pl.pallas_call(
        own_kernel,
        out_shape=jax.ShapeDtypeStruct((depth, width // 2), w.dtype),
        grid_spec=pltpu.PrefetchScalarGridSpec(
            num_scalar_prefetch=1,
            grid=(1,),
            in_specs=[pl.BlockSpec(memory_space=pl.ANY)],
            out_specs=pl.BlockSpec(memory_space=pl.ANY),
            scratch_shapes=[pltpu.SemaphoreType.DMA((3,))],
        ),
        compiler_params=pltpu.CompilerParams(vmem_limit_bytes=VMEM_LIMIT),
        cost_estimate=pl.CostEstimate(flops=0, bytes_accessed=2 * depth * width // SHARE, transcendentals=0),
        name="own_columns",
    )(where, w)


def product_kernel(*refs, dims, spans):
    parts = len(spans) if spans else 1
    total = None
    if spans:
        cuts, refs = refs[-parts:], refs[:-parts]

        @pl.when(pl.program_id(0) == 0)
        def _():
            for i in range(parts):
                at = 0
                for low, high in spans[i]:
                    cuts[i][:, at : at + high - low] = refs[parts][:, low:high]
                    at += high - low

    else:
        cuts = [refs[parts]]
    for i in range(parts):
        part = dot(refs[i][...], cuts[i][...], dims)
        total = part if total is None else total + part
    for term in refs[parts + 1 : -1]:
        total = total + term[...]
    refs[-1][...] = total.astype(refs[-1].dtype)


def product(parts, b, dims, name, spans=None, terms=(), half=None):
    tile = 256 if sum(a.shape[1] for a in parts) > 2560 else 640
    turned = dims == NT
    rows = parts[0].shape[0] // (1 if half is None else 2)
    place = half or 0
    width = b.shape[0 if turned else 1]
    depth = sum(a.shape[1] for a in parts)
    out_spec, steps = pl.BlockSpec((rows, tile), lambda i: (0, i)), width // tile
    ins = [
        pl.BlockSpec((rows, a.shape[1]), lambda i: (place, 0), pipeline_mode=pl.Buffered(1)) for a in parts
    ]
    if spans:
        steps = rows // 256
        ins = [pl.BlockSpec((256, a.shape[1]), lambda i: (place * steps + i, 0)) for a in parts]
        ins.append(pl.BlockSpec(b.shape, lambda i: (0, 0), pipeline_mode=pl.Buffered(1)))
        out_spec = pl.BlockSpec((256, width), lambda i: (i, 0))
    elif turned:
        ins.append(pl.BlockSpec((tile, b.shape[1]), lambda i: (i, 0)))
    else:
        ins.append(pl.BlockSpec((b.shape[0], tile), lambda i: (0, i)))
    return pl.pallas_call(
        functools.partial(product_kernel, dims=dims, spans=spans),
        out_shape=jax.ShapeDtypeStruct((rows, width), BF),
        grid=(steps,),
        in_specs=ins + [pl.BlockSpec((t.shape[0], tile), lambda i: (0, i)) for t in terms],
        out_specs=out_spec,
        scratch_shapes=[pltpu.VMEM((width, a.shape[1]), BF) for a in parts] if spans else [],
        compiler_params=pltpu.CompilerParams(vmem_limit_bytes=VMEM_LIMIT),
        cost_estimate=pl.CostEstimate(
            flops=2 * rows * depth * width // SHARE,
            bytes_accessed=2 * (rows * depth + depth * width + rows * width) // SHARE,
            transcendentals=0,
        ),
        name=name,
    )(*parts, b, *terms)


def tile_flags(queries, keys, tq, tk):
    q_first, q_last = queries[:, ::tq], queries[:, tq - 1 :: tq]
    k_first, k_last = keys[:, ::tk], keys[:, tk - 1 :: tk]
    meet = (q_first[:, :, None] <= k_last[:, None, :]) & (k_first[:, None, :] <= q_last[:, :, None])
    whole = (
        (q_first == q_last)[:, :, None]
        & (k_first == k_last)[:, None, :]
        & (q_first[:, :, None] == k_first[:, None, :])
    )
    return jnp.where(whole, 2, jnp.where(meet, 1, 0)).astype(jnp.int32)


def layer_norm_parts(values):
    centred = values - jnp.mean(values, axis=-1, keepdims=True)
    rstd = lax.rsqrt(jnp.mean(centred * centred, axis=-1, keepdims=True) + EPS)
    return centred * rstd, rstd


def layer_norm_back(d_norm, gain, xhat, rstd):
    e = d_norm * gain
    return rstd * (
        e - jnp.mean(e, axis=-1, keepdims=True) - xhat * jnp.mean(e * xhat, axis=-1, keepdims=True)
    )


def on_device(
    tokens,
    cell_start,
    norm1_gain,
    norm1_bias,
    w_qkv,
    bias_q,
    bias_v,
    w_out,
    bias_out,
    norm2_gain,
    norm2_bias,
    w_in,
    bias_in,
    w_back,
    bias_back,
    cotangent,
):
    rows, seg, width = tokens.shape
    count = rows * seg
    ff = w_in.shape[1]
    half = width // 2
    wide = lax.axis_size("wide")
    group = lax.axis_size("blk")
    place = lax.axis_index("wide")
    member = lax.axis_index("blk")
    core = place % 2
    chips = wide // 2
    first = 2 if chips <= 8 else 4
    second = chips // first
    heads = HEADS // 2
    early = 6
    spans = ((0, early), (early, heads))
    tq, tk = min(512, seg), min(256, seg)
    halves = group == 2 and ff // chips % 128 == 0
    where = jnp.stack([place // 2, core, member]).astype(jnp.int32)
    where_out = jnp.stack([lax.bitwise_xor(place // 2, core * (chips // 2)), core, member]).astype(jnp.int32)

    def after(value, *earlier):
        return lax.optimization_barrier((value, earlier))[0]

    def across(array, by):
        return lax.ppermute(array, "wide", [(i, i ^ by) for i in range(wide)])

    def to_mate(array):
        return across(array, 1)

    def from_ahead(array, by):
        return lax.ppermute(array, "blk", [((i + by) % group, i) for i in range(group)])

    def to_ahead(array, by):
        return lax.ppermute(array, "blk", [(i, (i + by) % group) for i in range(group)])

    def from_all_ahead(array):
        parts = [from_ahead(array, by) for by in range(1, group)]
        return parts[0] if len(parts) == 1 else jnp.concatenate(parts, axis=1)

    def cut(array, start, size, axis):
        return lax.dynamic_slice_in_dim(array, start, size, axis)

    def paired(array):
        return jnp.concatenate([array, to_mate(array)], axis=0)

    inputs = tokens.astype(F32).reshape(count, width)
    xhat1, rstd1 = layer_norm_parts(inputs)
    acts = (xhat1 * norm1_gain + norm1_bias).astype(BF).reshape(tokens.shape)
    cells = paired(cell_start)
    far_cells = from_all_ahead(cells)
    acts = after(acts, far_cells)
    far_own = from_all_ahead(acts)
    acts_pair = paired(acts).reshape(2 * count, width)
    w_own = own_columns_call(where, w_qkv)
    b_own = jnp.concatenate([cut(bias_q, core * half, half, 0), jnp.zeros((half,), F32), cut(bias_v, core * half, half, 0)])

    def own_columns(span, parts):
        return tuple((part * half + span[0] * HD, part * half + span[1] * HD) for part in parts)

    near_spans = tuple(own_columns(span, (0, 1, 2)) for span in spans)
    far_spans = tuple(own_columns(span, (1, 2)) for span in spans)

    def columns(array):
        return jnp.broadcast_to(array[:, :, None], array.shape + (128,))

    qkv = (dot(acts_pair, w_own, NN) + b_own).astype(BF).reshape(2 * rows, seg, 3 * half)
    near_flags = tile_flags(cells, cells, tq, tk)
    far_flags = tile_flags(cells, far_cells, tq, tk)
    cell_rows = cells[:, None, :]
    near_columns, far_columns = columns(cells), columns(far_cells)
    state = attn_fwd(near_flags, cell_rows, near_columns, qkv, qkv, 1, None, tq, tk, heads)
    d_out = cotangent.reshape(count, width)
    d_out_mate = to_mate(after(d_out, acts_pair))
    far_own = after(far_own, state)
    far_mate = to_mate(far_own)
    d_act = dot(after(d_out, far_own, state, d_out_mate), w_back, NT).astype(BF)

    far_mate = after(far_mate, d_act)
    far_pair = jnp.concatenate([far_own, far_mate], axis=0)
    far_len = far_pair.shape[1]
    far_pair = far_pair.reshape(-1, width)
    far_kv = (dot(far_pair, w_own[:, half:], NN) + b_own[half:]).astype(BF).reshape(2 * rows, far_len, 2 * half)
    *attended, stats = attn_fwd(far_flags, cell_rows, far_columns, qkv, far_kv, 0, state, tq, tk, heads)
    mine, theirs = (part.reshape(count, half) for part in attended)
    own_rest = to_mate(theirs)
    mate_rest = to_mate(mine)
    w_out_own = cut(w_out, core * half, half, 0)
    w_out_mate = cut(w_out, (1 - core) * half, half, 0)
    middle = inputs + (dot(mine, w_out_own, NN) + dot(own_rest, w_out_mate, NN)) + bias_out

    xhat2, _ = layer_norm_parts(middle)
    acts2 = (xhat2 * norm2_gain + norm2_bias).astype(BF)
    acts2_mate = to_mate(acts2)
    b_in = bias_in.reshape(1, ff)
    act_part, d_pre_theirs, sum_part, norm_part = ffn_call(
        where, after(acts2, mate_rest), w_in, b_in, d_act, (), "ffn_theirs"
    )
    d_pre_mate = to_mate(d_pre_theirs)
    act, d_pre_mine, d_pre_sum, d_middle, d_z, d_att_theirs, d_att_mine, z_sums = ffn_call(
        where, acts2, w_in, b_in, d_act,
        (act_part, sum_part, norm_part, middle, d_out, w_out, norm2_gain.reshape(1, width)), "ffn_mine",
    )
    act_mate = to_mate(after(act, d_pre_mate, acts2_mate))
    grad_out = d_out.astype(F32)
    d_att_mate = to_mate(d_att_theirs)
    d_z_mate = to_mate(d_z)

    def send(parts):
        return [across(parts[one], 2 * one) for one in range(1, first)]

    def add_first(parts, received):
        def added(at):
            total = parts[0][at].astype(F32)
            for part in received:
                total = total + part[at].astype(F32)
            return total.astype(BF)

        return added(slice(0, second // 2)), added(slice(second // 2, second))

    def send_second(pair):
        return across(pair[1], first * second)

    def add_second(pair, received):
        return tuple((pair[0][at].astype(F32) + received[at].astype(F32)).astype(BF) for at in range(2))

    def send_third(pair):
        return across(pair[1], 2 * first)

    def add_third(pair, received):
        return (pair[0].astype(F32) + received.astype(F32)).astype(BF)

    def start(parts):
        return from_ahead(parts[1], 1) if halves else send(parts)

    def middle_step(parts, received):
        if not halves:
            return parts, received
        sums = [(parts[0][one].astype(F32) + received[one].astype(F32)).astype(BF) for one in range(first)]
        return sums, send(sums)

    def ahead(total):
        return from_ahead(total, 1) if group == 2 else None

    def over_row(total, other):
        if group == 2:
            return (total.astype(F32) + other.astype(F32)).astype(BF)
        return lax.psum(total, "blk")

    def by_core(total):
        split = total.reshape(2, -1, total.shape[-1])
        return [lax.dynamic_index_in_dim(split, i, 0, keepdims=False) for i in (core, 1 - core)]

    def joined(total, other, sizes):
        total = over_row(total, other)
        parts, at = [], 0
        for size in sizes:
            parts.append(by_core(total[at : at + size]))
            at += size
        return [jnp.concatenate(part, axis=0) for part in zip(*parts)]

    def in_blocks(array):
        return [array[:, at : at + half] for at in range(0, array.shape[1], half)]

    d_pre_held = d_pre_mine
    grad_in = grad_call(
        where, [[(acts2, d_pre_held, 0), (acts2_mate, d_pre_mate, 0)]], ff // 2, first, second, 512, False, "grad_in"
    )
    in_in = send(grad_in)
    act_held, act_mate, d_z_mate = after((act, act_mate, d_z_mate), grad_in)

    def grad_o(into):
        return grad_call(
            where_out,
            [
                [(mine, d_z, None), (theirs, d_z_mate, None)],
                [(own_rest, d_z, None), (mate_rest, d_z_mate, None)],
            ],
            half, first, second, half, halves, "grad_out", into,
        )

    back_rows, out_rows = ff // chips, width // chips
    if halves:
        grad_b = back_call(
            where, (act_held, d_out), (act_mate, d_out_mate), first, second, out_rows // 2, "grad_back"
        )
        grad_b = grad_o(tuple(grad_b))
    else:
        whole = dot(act_held, cut(d_out, core * half, half, 1), TN) + dot(act_mate, cut(d_out_mate, core * half, half, 1), TN)
        whole = whole.astype(BF).reshape(chips, back_rows, half)
        grad_b = [
            jnp.concatenate([
                jnp.stack([whole[lax.bitwise_xor(two * first + one, where[0])] for two in range(second)]), other
            ], axis=1)
            for one, other in enumerate(grad_o(()))
        ]
    b_in = start(grad_b)

    back_tq = min(256, seg)
    near_flags, far_flags = tile_flags(cells, cells, back_tq, tk), tile_flags(cells, far_cells, back_tq, tk)
    d_att = after((d_att_mine.reshape(rows, seg, half), d_att_mate.reshape(rows, seg, half)), grad_b)
    d_qT, far_early, far_late = attn_bwd(
        far_flags, cell_rows, far_columns, qkv, far_kv, 0, d_att, attended, stats, None, back_tq, tk, heads, spans, "attn_bwd_far"
    )
    in_sums = add_first(grad_in, after(in_in, d_qT))
    in_more = send_second(in_sums)
    far_early, far_late = after((far_early, far_late), in_sums)
    far_early, far_late = (f.reshape(-1, f.shape[-1]) for f in (far_early, far_late))
    n_early, n_late = early * HD, (heads - early) * HD
    far_theirs = product([far_early, far_late], w_own, NT, "far_norm_theirs", far_spans, half=1)
    far_given = to_mate(far_theirs)
    far_mine = product([after(far_early, far_theirs), far_late], w_own, NT, "far_norm_mine", far_spans, half=0)
    far_sum = (far_mine.astype(F32) + after(far_given, in_sums, far_mine).astype(F32)).astype(BF)
    far_sum = far_sum.reshape(rows, far_len, width)
    far_back = [to_ahead(far_sum[:, by * seg : (by + 1) * seg], by + 1) for by in range(group - 1)]
    d_qT = after(d_qT, far_sum)

    def near_back(span, name, *earlier):
        (out,) = attn_bwd(
            near_flags, cell_rows, near_columns, qkv, qkv, 1, d_att, attended, stats, after(d_qT, earlier), back_tq, tk, heads,
            (span,), name,
        )
        return out.reshape(2 * count, -1)

    near_early = near_back(spans[0], "attn_bwd_early")
    b_sums, b_in = middle_step(grad_b, after(b_in, near_early))
    in_two = add_second(in_sums, after(in_more, b_sums))
    in_last = send_third(in_two)
    near_early = after(near_early, b_sums, in_two)
    *grad_e, sum_e = qkv_call(where, (acts_pair, near_early), (far_pair, far_early), first, second, halves, "grad_early")
    in_total = add_third(in_two, after(in_last, grad_e))
    in_row = ahead(in_total)
    grad_e, far_back = after((grad_e, far_back), in_total)
    e_in = start(grad_e)
    near_late = near_back(spans[1], "attn_bwd_late", grad_e, far_back)
    b_two = add_first(b_sums, after(b_in, near_late))
    b_more = send_second(b_two)
    e_sums, e_in = middle_step(grad_e, after(e_in, b_two))
    near_late = after(near_late, b_two, e_sums)
    *grad_l, sum_l = qkv_call(where, (acts_pair, near_late), (far_pair, far_late), first, second, halves, "grad_late")
    l_in = start(grad_l)
    near_held = after(near_early, grad_l)
    near_theirs = product([near_held, near_late], w_own, NT, "near_norm_theirs", near_spans, half=1)
    near_mine = product([after(near_held, near_theirs), near_late], w_own, NT, "near_norm_mine", near_spans, half=0)
    e_two = add_first(e_sums, after(e_in, near_mine))
    e_more = send_second(e_two)
    b_three = add_second(b_two, after(b_more, e_two))
    b_last = send_third(b_three)
    l_sums, l_in = middle_step(grad_l, after(l_in, b_three))
    near_given = to_mate(after(near_theirs, near_mine))
    in_row = after(in_row, near_mine)
    act_late = after(act_held, e_two, b_three, l_sums, in_row)
    mixed = product([act_late], w_back, NN, "mixed", terms=(middle, bias_back.reshape(1, width))).reshape(tokens.shape)
    l_two = add_first(l_sums, after(l_in, mixed))
    l_more = send_second(l_two)
    e_three = add_second(e_two, after(e_more, l_two))
    e_last = send_third(e_three)
    b_total = add_third(b_three, after(b_last, e_three))
    b_row = ahead(b_total)
    near_mine, near_given = after((near_mine, near_given), l_two, e_three, b_total)
    grad_tokens, norm1_sums = first_norm_call(
        tokens.reshape(count, width), d_middle, norm1_gain.reshape(1, width),
        [near_mine, near_given, *(part.reshape(count, width) for part in far_back)],
    )
    grad_tokens = grad_tokens.reshape(tokens.shape)

    def vector_stage(total, stride, size):
        total = total.reshape(-1, size, stride, total.shape[-1])
        spot = (place // stride) % size
        kept = lax.dynamic_index_in_dim(total, spot, 1, keepdims=False)
        for by in range(1, size):
            kept = kept + across(lax.dynamic_index_in_dim(total, spot ^ by, 1, keepdims=False), by * stride)
        return kept.reshape(stride, -1)

    def widened(part):
        n = sum_e.shape[1] // 3, sum_l.shape[1] // 3
        own = jnp.concatenate([s[0, part * m : (part + 1) * m] for s, m in zip((sum_e, sum_l), n)])
        return lax.dynamic_update_slice_in_dim(jnp.zeros((width,), F32), own, core * half, 0)

    parts = [
        norm1_sums[0],
        norm1_sums[1],
        widened(0),
        widened(2),
        z_sums[0],
        z_sums[1],
        z_sums[2],
        d_pre_sum,
        jnp.sum(grad_out, axis=0),
    ]
    totals = vector_stage(jnp.concatenate([part.reshape(wide, -1) for part in parts], axis=1), 2 * first, second)
    e_total = add_third(e_three, after(e_last, norm1_sums))
    l_three = add_second(l_two, after(l_more, e_total))
    l_last = send_third(l_three)
    totals = vector_stage(totals, 2, first)

    l_total = add_third(l_three, after(l_last, totals))
    totals = vector_stage(totals, 1, 2).reshape(-1)
    qkv_total = jnp.concatenate([e_total, l_total], axis=1)
    qkv_row = ahead(qkv_total)
    in_total, b_total = after((in_total, b_total), grad_tokens, totals)
    totals = totals + from_ahead(totals, 1) if group == 2 else lax.psum(totals, "blk")
    if halves:
        kept, given = pack_call(where, (in_total, in_row), (b_total, b_row), (qkv_total, qkv_row))
    else:
        in_parts = by_core(over_row(in_total, in_row))
        b_parts = joined(b_total, b_row, [back_rows, out_rows])
        qkv_parts = joined(qkv_total, qkv_row, [out_rows])
        kept, given = (
            jnp.concatenate(in_blocks(i) + [b] + in_blocks(q), axis=0)
            for i, b, q in zip(in_parts, b_parts, qkv_parts)
        )
    other = after(to_mate(given), totals)
    share = ff // wide
    own_rows = width // wide
    in_count = ff // 2 // half

    def rows_of(array, first_row, size):
        return array[first_row : first_row + size]

    def blocks_of(array, first_row, count):
        return [rows_of(array, first_row + i * own_rows, own_rows) for i in range(count)]

    if halves:
        shapes = [(own_rows, ff), (share, width), (own_rows, width), (own_rows, 3 * width)]
        grad_w_in, grad_w_back, grad_w_out, grad_w_qkv = unpack_call(where, kept, other, shapes, (n_early, n_late))
    else:
        low, high = (jnp.where(core == side, kept, other).astype(F32) for side in range(2))
        b_at = in_count * own_rows
        q_at = b_at + share + own_rows

        def part_columns(part):
            columns = []
            for side in (low, high):
                wide_rows = jnp.concatenate(blocks_of(side, q_at, 3), axis=1)
                for start, n in ((0, n_early), (3 * n_early, n_late)):
                    columns.append(wide_rows[:, start + part * n : start + (part + 1) * n])
            return columns

        grad_w_in = jnp.concatenate([b for side in (low, high) for b in blocks_of(side, 0, in_count)], axis=1)
        grad_w_back = jnp.concatenate([rows_of(side, b_at, share) for side in (low, high)], axis=1)
        grad_w_out = jnp.concatenate([rows_of(side, b_at + share, own_rows) for side in (low, high)], axis=1)
        grad_w_qkv = jnp.concatenate([piece for part in range(3) for piece in part_columns(part)], axis=1)

    small, at = [], 0
    for part in parts:
        size = part.size // wide
        small.append(totals[at : at + size])
        at += size

    return (
        mixed,
        grad_tokens,
        small[0],
        small[1],
        grad_w_qkv,
        small[2],
        small[3],
        grad_w_out,
        small[4],
        small[5],
        small[6],
        grad_w_in,
        small[7],
        grad_w_back,
        small[8],
    )


def solution(mesh):
    spread = P("wide", "blk", None)
    placed = (spread, P("wide", "blk")) + (P(),) * 13 + (spread,)
    matrix, vector = P("wide", None), P("wide")
    return jax.shard_map(
        on_device,
        mesh=mesh,
        in_specs=placed,
        out_specs=(
            spread, spread, vector, vector, matrix, vector, vector, matrix, vector, vector, vector,
            matrix, vector, matrix, vector,
        ),
        check_vma=False,
    )
```
